32 devices in a mesh: row: 16 (over z, y, core), col: 2 (over x).
Axes of the slice: x: 2, y: 2, z: 4, core: 2. Of those that a mesh axis runs over, the one named last changes fastest.
Arguments:
- tokens: bfloat16 [8192, 512], P('row', 'col'), may hold values from -6 to 6
- prev_logits: bfloat16 [8, 8192, 1024], P('col', 'row'), may hold values from -5 to 5
- doc_lengths: int32 [1, 33], replicated, may hold values from 1 to 512, as said below
- qkv_weight: bfloat16 [3, 512, 512], P(None, 'row', 'col'), may hold values from -0.25 to 0.25
- qv_bias: float32 [2, 512], P(None, 'col'), may hold values from -3 to 3
- out_weight: bfloat16 [512, 512], P('col', 'row'), may hold values from -2 to 2
- out_bias: float32 [2, 512], P(None, 'col'), may hold values from -2 to 2
- up_weight: bfloat16 [512, 2048], P('row', 'col'), may hold values from -0.25 to 0.25
- up_bias: float32 [2048], P('col'), may hold values from -3 to 3
- down_weight: bfloat16 [2048, 512], P('col', 'row'), may hold values from -0.125 to 0.125
- norm_gain: float32 [2, 512], P(None, 'col'), may hold values from 0.25 to 1.75
- norm_shift: float32 [2, 512], P(None, 'col'), may hold values from -2 to 2
- out_grad: bfloat16 [8192, 512], P('row', 'col'), may hold values from -6 to 6
- logit_grad: bfloat16 [8, 8192, 1024], P('col', 'row'), may hold values from -5 to 5
Outputs:
- output: bfloat16 [8192, 512], P('row', 'col')
- new_logits: bfloat16 [8, 8192, 1024], P('col', 'row')
- tokens_grad: bfloat16 [8192, 512], P('row', 'col')
- prev_grad: bfloat16 [8, 8192, 1024], P('col', 'row')
- qkv_weight_grad: float32 [3, 512, 512], P(None, 'row', 'col')
- qv_bias_grad: float32 [2, 512], P(None, 'col')
- out_weight_grad: float32 [512, 512], P('col', 'row')
- out_bias_grad: float32 [2, 512], P(None, 'col')
- up_weight_grad: float32 [512, 2048], P('row', 'col')
- up_bias_grad: float32 [2048], P('col')
- down_weight_grad: float32 [2048, 512], P('col', 'row')
- norm_gain_grad: float32 [2, 512], P(None, 'col')
- norm_shift_grad: float32 [2, 512], P(None, 'col')
The draws below stay inside these ranges and needn't reach their ends.
Inputs may be any that keep to these rules, and one draw needn't show every extreme that they name: Each row of doc_lengths sums to 8192, its longest document has exactly 512 tokens, and every nonzero multiple of 512 below 8192 lies inside a document with at least 128 of its tokens on each side of that position.
All inputs are finite; a program needn't handle non-finite values.
Results may differ from the reference program's by a relative error of at most 0.02.
Values may be sent and summed in bfloat16 or wider, within the bound.
No kernel may reach another device: no remote copies, remote signals or barrier semaphores. Data moves between devices by JAX's collectives and lax.ppermute only.
A program may use at most 128 MiB of HBM per device.

```python
import jax
import jax.numpy as jnp
from jax import lax

D = 512
HEADS = 8
HEAD_DIM = 64
FF = 2048
MAXDOC = 512
TOKENS = 8192
SEQ = 8192
NDOCS = 33
HD = 512
BAND = 1024


def draw_doc_lengths(key, part):
    periods = TOKENS // MAXDOC
    quarter = MAXDOC // 4
    count = 2 * periods
    base = jax.random.randint(jax.random.fold_in(key, 11), (count,), 0, quarter, dtype=jnp.int32)
    marks = jax.random.randint(jax.random.fold_in(key, 23), (count,), 0, 2, dtype=jnp.int32)
    raised = jax.random.randint(jax.random.fold_in(key, 37), (count,), 0, quarter, dtype=jnp.int32)
    before = jnp.concatenate([jnp.zeros((1,), jnp.int32), marks[:-1]])
    boosted = marks * (1 - before)
    high = (quarter + raised) * boosted
    high_left = jnp.concatenate([jnp.zeros((1,), jnp.int32), high[:-1]])
    high_right = jnp.concatenate([high[1:], jnp.zeros((1,), jnp.int32)])
    limit = 2 * quarter - 1 - jnp.maximum(high_left, high_right)
    extras = jnp.where(boosted > 0, high, jnp.minimum(base, limit)).astype(jnp.int32)
    forced = jnp.array([0, quarter, quarter, 0, 2 * quarter - 1, 0], jnp.int32)
    extras = jnp.concatenate([forced, extras[6:]])
    lower_off = extras[0::2]
    upper_off = extras[1::2]
    starts_period = jnp.arange(periods, dtype=jnp.int32) * MAXDOC
    lower_bound = starts_period + quarter + lower_off
    upper_bound = starts_period + 3 * quarter - upper_off
    bounds = jnp.stack([lower_bound, upper_bound], 1).reshape(-1)
    ends = jnp.concatenate([bounds, jnp.array([TOKENS], jnp.int32)])
    begins = jnp.concatenate([jnp.array([0], jnp.int32), bounds])
    return (ends - begins).astype(jnp.int32).reshape(1, NDOCS)


def steps_of(own_key, shape, shards, low, top_value):
    level, own = 1.0, jax.random.fold_in(own_key, 6)
    for position, blocks in shards:
        steps = jnp.exp(jax.random.uniform(jax.random.fold_in(own, position), (blocks,), jnp.float32, low / len(shards), top_value / len(shards)))
        level = level * jnp.repeat(steps, shape[position] // blocks).reshape([-1 if axis == position else 1 for axis in range(len(shape))])
    return level


def normal_values(rng, shape, width, most, pieces=(), kind=jnp.bfloat16):
    values = jax.random.normal(rng, shape, jnp.float32) * width
    if len(pieces) > 0:
        values = steps_of(rng, shape, pieces, -0.22, 0.18) * values
    return jnp.clip(values, min=-most, max=most).astype(kind)


def setup_inputs(seed: int = 0) -> dict:
    splits = jax.random.split(jax.random.key(seed), 15)
    tokens = normal_values(splits[0], (TOKENS, D), 1.0, 6.0, ((0, 16), (1, 2)))
    prev_logits = normal_values(splits[1], (HEADS, TOKENS, BAND), 1.0, 5.0, ((0, 2), (1, 16)))
    doc_lengths = draw_doc_lengths(jax.random.fold_in(splits[14], 71), 0)
    qkv_weight = normal_values(splits[3], (3, D, HD), D ** -0.5, 0.25, ((1, 16), (2, 2)))
    qv_bias = normal_values(splits[4], (2, HD), 0.5, 3.0, ((1, 2),), jnp.float32)
    out_weight = normal_values(splits[5], (HD, D), (max(HD * 16 // (2 * MAXDOC), 1)) ** -0.5, 2.0, ((0, 2), (1, 16)))
    out_bias = normal_values(splits[6], (2, D), 0.3, 2.0, ((1, 2),), jnp.float32)
    up_weight = normal_values(splits[7], (D, FF), D ** -0.5, 0.25, ((0, 16), (1, 2)))
    up_bias = normal_values(splits[8], (FF,), 0.5, 3.0, ((0, 2),), jnp.float32)
    down_weight = normal_values(splits[9], (FF, D), FF ** -0.5, 0.125, ((0, 2), (1, 16)))
    norm_gain = jnp.clip(1.0 + 0.15 * jax.random.normal(splits[10], (2, D), jnp.float32), 0.25, 1.75)
    norm_shift = normal_values(splits[11], (2, D), 0.3, 2.0, ((1, 2),), jnp.float32)
    out_grad = normal_values(splits[12], (TOKENS, D), 1.0, 6.0, ((0, 16), (1, 2)))
    logit_grad = normal_values(splits[13], (HEADS, TOKENS, BAND), 1.0, 5.0, ((0, 2), (1, 16)))
    return dict(tokens=tokens, prev_logits=prev_logits, doc_lengths=doc_lengths, qkv_weight=qkv_weight, qv_bias=qv_bias, out_weight=out_weight, out_bias=out_bias, up_weight=up_weight, up_bias=up_bias, down_weight=down_weight, norm_gain=norm_gain, norm_shift=norm_shift, out_grad=out_grad, logit_grad=logit_grad)


EPSILON = 1e-05
MASKED_SCORE = -1e+30
HIGHEST = lax.Precision.HIGHEST

@jax.custom_vjp
def low(v):
    return lax.optimization_barrier(v.astype(jnp.bfloat16)).astype(jnp.float32)

@jax.custom_vjp
def low_back(v):
    return v

def low_keep(v):
    return (low(v), None)

def low_pass(kept, grad):
    return (grad,)

def back_keep(v):
    return (v, None)

def back_low(kept, grad):
    return (low(grad),)
low.defvjp(low_keep, low_pass)
low_back.defvjp(back_keep, back_low)

def to_band(dense_block, band_width):
    leading = dense_block.shape[:-2]
    rows_count = dense_block.shape[-2]
    key_span = dense_block.shape[-1]
    flattened = dense_block.reshape(leading + (rows_count * key_span,))
    flattened = jnp.concatenate([flattened, jnp.zeros(leading + (rows_count,), dense_block.dtype)], -1)
    return flattened.reshape(leading + (rows_count, key_span + 1))[..., :band_width]

def to_dense(banded, key_span):
    leading = banded.shape[:-2]
    rows_count = banded.shape[-2]
    band_width = banded.shape[-1]
    padded = jnp.pad(banded, [(0, 0)] * (banded.ndim - 1) + [(0, key_span + 1 - band_width)])
    flattened = padded.reshape(leading + (rows_count * (key_span + 1),))[..., :rows_count * key_span]
    return flattened.reshape(leading + (rows_count, key_span))

def segment_ids(doc_lengths, token_count):
    positions = jnp.arange(token_count + 2 * MAXDOC, dtype=jnp.int32) - MAXDOC
    doc_ends = (jnp.cumsum(doc_lengths, 1).astype(jnp.int32) + SEQ * jnp.arange(doc_lengths.shape[0], dtype=jnp.int32)[:, None]).reshape(-1)
    segment = lax.optimization_barrier(jnp.sum((doc_ends[None, :] <= positions[:, None]).astype(jnp.int32), 1)).astype(jnp.int32)
    return jnp.where((positions >= 0) & (positions < token_count), segment, -1)

def layer_norm(hidden, gain, shift):
    mean_rows = lax.optimization_barrier(jnp.mean(hidden, -1, keepdims=True))
    inverse_std = lax.rsqrt(lax.optimization_barrier(jnp.mean(hidden * hidden, -1, keepdims=True)) - mean_rows * mean_rows + EPSILON)
    return (hidden - mean_rows) * inverse_std * gain + shift

def attend(queries, keys, values, previous, segment):
    token_count = queries.shape[0]
    block_rows = min(512, token_count)
    band_width = 2 * MAXDOC
    key_span = block_rows + band_width
    query_heads = queries.reshape(token_count, HEADS, HEAD_DIM)
    key_heads = jnp.pad(keys, ((MAXDOC, MAXDOC), (0, 0))).reshape(token_count + band_width, HEADS, HEAD_DIM)
    value_heads = jnp.pad(values, ((MAXDOC, MAXDOC), (0, 0))).reshape(token_count + band_width, HEADS, HEAD_DIM)

    def one_block(block_index):
        anchor = block_index * block_rows
        block_queries = lax.dynamic_slice_in_dim(query_heads, anchor, block_rows, 0)
        block_keys = lax.dynamic_slice_in_dim(key_heads, anchor, key_span, 0)
        block_values = lax.dynamic_slice_in_dim(value_heads, anchor, key_span, 0)
        block_prev = lax.dynamic_slice_in_dim(previous, anchor, block_rows, 1)
        query_segment = lax.dynamic_slice_in_dim(segment, anchor + MAXDOC, block_rows, 0)
        key_segment = lax.dynamic_slice_in_dim(segment, anchor, key_span, 0)
        dense_block = jnp.einsum('qhe,khe->hqk', block_queries, block_keys, precision=HIGHEST)
        scores = low_back(to_band(dense_block, band_width) * HEAD_DIM ** (-0.5) + block_prev)
        same = jnp.where(query_segment[:, None] == key_segment[None, :], 1.0, 0.0)
        allowed = to_band(same, band_width) > 0.5
        new_block = jnp.where(allowed, scores, 0.0)
        probabilities = jax.nn.softmax(jnp.where(allowed, scores, MASKED_SCORE), axis=-1)
        spread = to_dense(low(probabilities), key_span)
        outputs = jnp.einsum('hqk,khe->qhe', spread, block_values, precision=HIGHEST)
        return (outputs.reshape(block_rows, HEADS * HEAD_DIM), new_block)
    outputs, new_logits = lax.map(jax.checkpoint(one_block), jnp.arange(token_count // block_rows, dtype=jnp.int32))
    new_logits = jnp.transpose(new_logits, (1, 0, 2, 3)).reshape(HEADS, token_count, band_width)
    return (outputs.reshape(token_count, HEADS * HEAD_DIM), new_logits)

def reference(tokens, prev_logits, doc_lengths, qkv_weight, qv_bias, out_weight, out_bias, up_weight, up_bias, down_weight, norm_gain, norm_shift, out_grad, logit_grad):
    token_count = tokens.shape[0]
    segment = segment_ids(doc_lengths, token_count)

    def forward(inputs, previous, weight_qkv, bias_qv, weight_out, bias_out, weight_up, bias_up, weight_down, gains, shifts):
        qkv_sums = jnp.einsum('td,sdo->sto', inputs, weight_qkv, precision=HIGHEST)
        queries = low_back(low(qkv_sums[0] + bias_qv[0]))
        keys = low_back(low(qkv_sums[1]))
        values = low_back(low(qkv_sums[2] + bias_qv[1]))
        attended, new_logits = attend(queries, keys, values, previous, segment)
        attended = low_back(low(attended))
        attn_branch = low_back(jnp.dot(attended, weight_out, precision=HIGHEST) + bias_out[0])
        upper = layer_norm(inputs + attn_branch, gains[0], shifts[0])
        hidden_pre = low_back(jnp.dot(low(upper), weight_up, precision=HIGHEST) + bias_up)
        activation = low(jax.nn.gelu(hidden_pre, approximate=False))
        ffn_branch = low_back(jnp.dot(activation, weight_down, precision=HIGHEST) + bias_out[1])
        output = layer_norm(upper + ffn_branch, gains[1], shifts[1])
        return (output, new_logits)
    (output, new_logits), pullback = jax.vjp(forward, tokens.astype(jnp.float32), prev_logits.astype(jnp.float32), qkv_weight.astype(jnp.float32), qv_bias, out_weight.astype(jnp.float32), out_bias, up_weight.astype(jnp.float32), up_bias, down_weight.astype(jnp.float32), norm_gain, norm_shift)
    gradients = pullback((out_grad.astype(jnp.float32), logit_grad.astype(jnp.float32)))
    return (output.astype(jnp.bfloat16), new_logits.astype(jnp.bfloat16), gradients[0].astype(jnp.bfloat16), gradients[1].astype(jnp.bfloat16), gradients[2], gradients[3], gradients[4], gradients[5], gradients[6], gradients[7], gradients[8], gradients[9], gradients[10])
```

```python
import functools

import jax
import jax.numpy as jnp
from jax import lax
from jax.experimental import pallas as pl
from jax.experimental.pallas import tpu as pltpu
from jax.sharding import PartitionSpec as P

D = 512
HEAD_DIM = 64
MAXDOC = 512
BAND = 2 * MAXDOC
BLOCK = 128
WINDOW = BAND + BLOCK
HALO = MAXDOC - 128
PAD = MAXDOC - HALO

EPSILON = 1e-05
MASKED_SCORE = -1e30
ERF_RATE = 0.7071067811865476
DENSITY_RATE = 0.3989422804014327

F32 = jnp.float32
BF16 = jnp.bfloat16
SMEM = pltpu.MemorySpace.SMEM
VMEM_LIMIT = 48 << 20


def dot_nn(a, b):
    return lax.dot_general(a, b, (((1,), (0,)), ((), ())), preferred_element_type=F32)


def dot_nt(a, b):
    return lax.dot_general(a, b, (((1,), (1,)), ((), ())), preferred_element_type=F32)


def dot_tn(a, b):
    return lax.dot_general(a, b, (((0,), (0,)), ((), ())), preferred_element_type=F32)


def params():
    return pltpu.CompilerParams(
        dimension_semantics=("arbitrary",), vmem_limit_bytes=VMEM_LIMIT
    )


def cost(flops, moved, special=0):
    return pl.CostEstimate(flops=flops, bytes_accessed=moved, transcendentals=special)


def whole(shape):
    return pl.BlockSpec(shape, lambda b: (0,) * len(shape))


def rows(width, height=BLOCK):
    return pl.BlockSpec((height, width), lambda b: (b, 0))


def heads_block(heads, width):
    return pl.BlockSpec((heads, BLOCK, width), lambda b: (0, b, 0))


def struct(shape, dtype):
    return jax.ShapeDtypeStruct(shape, dtype)


def segment_of(positions, lengths_ref, token_count):
    sequences, documents = lengths_ref.shape
    found = jnp.zeros(positions.shape, jnp.int32)
    end = jnp.int32(0)
    for sequence in range(sequences):
        for document in range(documents):
            end = end + lengths_ref[sequence, document]
            found = found + (positions >= end).astype(jnp.int32)
    return jnp.where((positions >= 0) & (positions < token_count), found, -1)


def dense_kernel(fill, token_count, lengths_ref, base_ref, band_ref, dense_ref):
    first = base_ref[0] + pl.program_id(0) * BLOCK
    query = first + lax.broadcasted_iota(jnp.int32, (BLOCK, 1), 0)
    key = first - MAXDOC + lax.broadcasted_iota(jnp.int32, (1, WINDOW), 1)
    same = segment_of(query, lengths_ref, token_count) == segment_of(
        key, lengths_ref, token_count
    )
    for head in range(band_ref.shape[0]):
        wide = jnp.concatenate(
            [band_ref[head].astype(F32), jnp.zeros((BLOCK, BLOCK), F32)], 1
        )
        turned = pltpu.roll(wide, 0, 1, stride=1, stride_axis=0)
        dense_ref[head] = jnp.where(same, turned, fill).astype(BF16)


def to_dense(banded, lengths, base, fill, token_count):
    heads, count, _ = banded.shape
    return pl.pallas_call(
        functools.partial(dense_kernel, fill, token_count),
        grid=(count // BLOCK,),
        in_specs=[
            pl.BlockSpec(memory_space=SMEM),
            pl.BlockSpec(memory_space=SMEM),
            heads_block(heads, BAND),
        ],
        out_specs=heads_block(heads, WINDOW),
        out_shape=struct((heads, count, WINDOW), BF16),
        compiler_params=params(),
        cost_estimate=cost(heads * count * WINDOW * 8, heads * count * (BAND + WINDOW) * 2),
        name="to_dense",
    )(lengths, base, banded)


def band_kernel(masked, dense_ref, band_ref):
    lane = lax.broadcasted_iota(jnp.int32, (BLOCK, BLOCK), 1)
    row = lax.broadcasted_iota(jnp.int32, (BLOCK, BLOCK), 0)
    source = (lane + row) & (BLOCK - 1)
    near = lane + row < BLOCK
    for head in range(band_ref.shape[0]):
        pieces = []
        for place in range(WINDOW // BLOCK):
            piece = dense_ref[head, :, place * BLOCK : (place + 1) * BLOCK].astype(F32)
            if masked:
                piece = jnp.where(piece < 0.5 * MASKED_SCORE, 0.0, piece)
            pieces.append(jnp.take_along_axis(piece, source, axis=1))
        for place in range(BAND // BLOCK):
            band_ref[head, :, place * BLOCK : (place + 1) * BLOCK] = jnp.where(
                near, pieces[place], pieces[place + 1]
            ).astype(BF16)


def to_band(dense, masked):
    heads, count, _ = dense.shape
    return pl.pallas_call(
        functools.partial(band_kernel, masked),
        grid=(count // BLOCK,),
        in_specs=[heads_block(heads, WINDOW)],
        out_specs=heads_block(heads, BAND),
        out_shape=struct((heads, count, BAND), BF16),
        compiler_params=params(),
        cost_estimate=cost(heads * count * WINDOW * 8, heads * count * (BAND + WINDOW) * 2),
        name="to_band",
    )(dense)


def head_split(block, size):
    if size == 1:
        return block
    lane = lax.broadcasted_iota(jnp.int32, block.shape, 1)
    return jnp.concatenate(
        [
            jnp.where((lane >= h * HEAD_DIM) & (lane < (h + 1) * HEAD_DIM), block, 0)
            for h in range(size)
        ],
        0,
    )


def head_join(stacked, size):
    if size == 1:
        return stacked
    height = stacked.shape[0] // size
    joined = stacked[:height]
    lane = lax.broadcasted_iota(jnp.int32, joined.shape, 1)
    for h in range(1, size):
        joined = jnp.where(lane >= h * HEAD_DIM, stacked[h * height : (h + 1) * height], joined)
    return joined


def forward_kernel(
    slot_ref, token_ref, low_ref, high_ref, near_ref, far_ref, bias_ref, prev_ref,
    score_ref, prob_ref, attended_ref, query_ref, key_ref, value_ref, weight_ref,
):
    step = pl.program_id(0)
    half, _, depth, width = near_ref.shape
    count = token_ref.shape[0]
    heads = prev_ref.shape[0]
    size = min(2, heads)
    span = size * HEAD_DIM

    @pl.when(step == 0)
    def _():
        for place in range(2 * half):
            slot = slot_ref[place]

            @pl.when(slot < half)
            def _():
                weight_ref[:, place * depth : (place + 1) * depth, :] = near_ref[slot]

            @pl.when(slot >= half)
            def _():
                weight_ref[:, place * depth : (place + 1) * depth, :] = far_ref[slot - half]

        low_rows, high_rows = low_ref[...], high_ref[...]
        own = token_ref[...]
        empty = jnp.zeros((PAD, width), BF16)
        query = (dot_nn(own, weight_ref[0]) + bias_ref[0:1, :]).astype(BF16)
        query_ref[...] = query * jnp.asarray(HEAD_DIM ** (-0.5), BF16)
        for out_ref, which in ((key_ref, 1), (value_ref, 2)):
            shift = bias_ref[1:2, :] if which == 2 else 0.0
            weight = weight_ref[which]
            out_ref[0:PAD, :] = empty
            out_ref[PAD:MAXDOC, :] = (dot_nn(low_rows, weight) + shift).astype(BF16)
            out_ref[MAXDOC : MAXDOC + count, :] = (dot_nn(own, weight) + shift).astype(BF16)
            out_ref[MAXDOC + count : MAXDOC + count + HALO, :] = (
                dot_nn(high_rows, weight) + shift
            ).astype(BF16)
            out_ref[MAXDOC + count + HALO :, :] = empty

    start = pl.multiple_of(step * BLOCK, BLOCK)
    for group in range(heads // size):
        lanes = slice(group * span, (group + 1) * span)
        query = head_split(query_ref[pl.ds(start, BLOCK), lanes], size)
        dense = dot_nt(query, key_ref[pl.ds(start, WINDOW), lanes])
        weights = []
        for h in range(size):
            head = group * size + h
            score = dense[h * BLOCK : (h + 1) * BLOCK] + prev_ref[head].astype(F32)
            score_ref[head] = score.astype(BF16)
            peak = jnp.max(score, -1, keepdims=True)
            grown = jnp.exp(score - peak)
            total = jnp.sum(grown, -1, keepdims=True)
            prob = (grown * (1.0 / total)).astype(BF16)
            prob_ref[head] = prob
            weights.append(prob)
        mixed = dot_nn(jnp.concatenate(weights, 0), value_ref[pl.ds(start, WINDOW), lanes])
        attended_ref[:, lanes] = head_join(mixed, size).astype(BF16)


def attend_forward(slots, tokens, low, high, near, far, bias, prev):
    heads, count, _ = prev.shape
    half, _, depth, width = near.shape
    features = tokens.shape[1]
    extended = count + BAND
    flops = 2 * features * width * (3 * count + 4 * HALO) + 4 * heads * count * WINDOW * 128
    return pl.pallas_call(
        forward_kernel,
        grid=(count // BLOCK,),
        in_specs=[
            pl.BlockSpec(memory_space=SMEM),
            whole(tokens.shape),
            whole(low.shape),
            whole(high.shape),
            whole(near.shape),
            whole(far.shape),
            whole(bias.shape),
            heads_block(heads, WINDOW),
        ],
        out_specs=[
            heads_block(heads, WINDOW),
            heads_block(heads, WINDOW),
            rows(width),
            whole((count, width)),
            whole((extended, width)),
            whole((extended, width)),
            whole((3, features, width)),
        ],
        out_shape=[
            struct((heads, count, WINDOW), BF16),
            struct((heads, count, WINDOW), BF16),
            struct((count, width), BF16),
            struct((count, width), BF16),
            struct((extended, width), BF16),
            struct((extended, width), BF16),
            struct((3, features, width), BF16),
        ],
        compiler_params=params(),
        cost_estimate=cost(flops, heads * count * WINDOW * 6, heads * count * WINDOW),
        name="attend_forward",
    )(slots, tokens, low, high, near, far, bias, prev)


def backward_kernel(
    grad_ref, query_ref, key_ref, value_ref, prob_ref, logit_ref,
    prev_ref, query_grad_ref, key_grad_ref, value_grad_ref, key_sum, value_sum,
):
    step = pl.program_id(0)
    heads = prob_ref.shape[0]
    size = min(2, heads)
    span = size * HEAD_DIM

    @pl.when(step == 0)
    def _():
        key_sum[...] = jnp.zeros_like(key_sum)
        value_sum[...] = jnp.zeros_like(value_sum)

    start = pl.multiple_of(step * BLOCK, BLOCK)
    window = pl.ds(start, WINDOW)
    for group in range(heads // size):
        lanes = slice(group * span, (group + 1) * span)
        query = head_split(query_ref[:, lanes], size)
        grad = head_split(grad_ref[:, lanes], size)
        key = key_ref[window, lanes]
        prob_grad = dot_nt(grad, value_ref[window, lanes])
        probs, scores = [], []
        for h in range(size):
            head = group * size + h
            low = prob_ref[head]
            prob = low.astype(F32)
            slope = prob_grad[h * BLOCK : (h + 1) * BLOCK]
            inner = jnp.sum(prob * slope, -1, keepdims=True)
            score = (prob * (slope - inner) + logit_ref[head].astype(F32)).astype(BF16)
            prev_ref[head] = score
            probs.append(low)
            scores.append(score)
        stacked = jnp.concatenate(scores, 0)
        mixed = head_join(dot_nn(stacked, key), size) * HEAD_DIM ** (-0.5)
        query_grad_ref[:, lanes] = mixed.astype(BF16)
        key_sum[lanes, window] += dot_tn(query, stacked)
        value_sum[lanes, window] += dot_tn(grad, jnp.concatenate(probs, 0))

    @pl.when(step == pl.num_programs(0) - 1)
    def _():
        key_grad_ref[...] = key_sum[...].astype(BF16).T
        value_grad_ref[...] = value_sum[...].astype(BF16).T


def attend_backward(grad, query, key, value, prob, logit):
    heads, count, _ = prob.shape
    width = query.shape[1]
    extended = count + BAND
    return pl.pallas_call(
        backward_kernel,
        grid=(count // BLOCK,),
        in_specs=[
            rows(width),
            rows(width),
            whole((extended, width)),
            whole((extended, width)),
            heads_block(heads, WINDOW),
            heads_block(heads, WINDOW),
        ],
        out_specs=[
            heads_block(heads, WINDOW),
            rows(width),
            whole((extended, width)),
            whole((extended, width)),
        ],
        out_shape=[
            struct((heads, count, WINDOW), BF16),
            struct((count, width), BF16),
            struct((extended, width), BF16),
            struct((extended, width), BF16),
        ],
        scratch_shapes=[pltpu.VMEM((width, extended), F32), pltpu.VMEM((width, extended), F32)],
        compiler_params=params(),
        cost_estimate=cost(8 * heads * count * WINDOW * 128, heads * count * WINDOW * 6),
        name="attend_backward",
    )(grad, query, key, value, prob, logit)


def order_kernel(slot_ref, near_ref, far_ref, out_ref):
    half, depth, _ = near_ref.shape
    for place in range(2 * half):
        slot = slot_ref[place]

        @pl.when(slot < half)
        def _():
            out_ref[place * depth : (place + 1) * depth, :] = near_ref[slot]

        @pl.when(slot >= half)
        def _():
            out_ref[place * depth : (place + 1) * depth, :] = far_ref[slot - half]


def in_order(slots, near, far):
    half, depth, width = near.shape
    return pl.pallas_call(
        order_kernel,
        grid=(1,),
        in_specs=[pl.BlockSpec(memory_space=SMEM), whole(near.shape), whole(far.shape)],
        out_specs=whole((2 * half * depth, width)),
        out_shape=struct((2 * half * depth, width), BF16),
        compiler_params=params(),
        cost_estimate=cost(0, 4 * half * depth * width * 2),
        name="in_order",
    )(slots, near, far)


def mean_of(x):
    return jnp.sum(x, -1, keepdims=True) * (1.0 / D)


def normalized(hidden):
    mean = mean_of(hidden)
    inverse = lax.rsqrt(mean_of(hidden * hidden) - mean * mean + EPSILON)
    return (hidden - mean) * inverse, inverse


def norm_back(upstream, normed, inverse):
    return inverse * (upstream - mean_of(upstream) - normed * mean_of(upstream * normed))


def added(own_ref, other_ref, swap):
    other = other_ref[...]
    if swap:
        middle = other.shape[1] // 2
        other = jnp.concatenate([other[:, middle:], other[:, :middle]], 1)
    return own_ref[...].astype(F32) + other.astype(F32)


def first_kernel(
    hidden_units, own_ref, other_ref, token_ref, weight_ref, norm_ref, up_bias_ref,
    normed_ref, inverse_ref, upper_ref, act_ref, slope_ref, part_ref,
):
    width = own_ref.shape[1]
    features = token_ref.shape[1]
    branch = dot_nt(own_ref[...], weight_ref[:, :width]) + dot_nt(
        other_ref[...], weight_ref[:, width:features]
    )
    hidden = token_ref[...].astype(F32) + branch + norm_ref[4:5, :]
    normed, inverse = normalized(hidden)
    normed_ref[...] = normed
    inverse_ref[...] = inverse
    upper = (normed * norm_ref[0:1, :] + norm_ref[2:3, :]).astype(BF16)
    upper_ref[...] = upper
    pre = dot_nn(upper, weight_ref[:, features : features + hidden_units]) + up_bias_ref[...]
    share = 0.5 * (1.0 + lax.erf(pre * ERF_RATE))
    act = (pre * share).astype(BF16)
    act_ref[...] = act
    slope_ref[...] = (share + pre * jnp.exp(-0.5 * pre * pre) * DENSITY_RATE).astype(BF16)
    part_ref[...] = dot_nt(act, weight_ref[:, features + hidden_units :]).astype(BF16)


def feed_first(own, other, tokens, weight, norms, up_bias):
    count, features = tokens.shape
    width = own.shape[1]
    hidden_units = up_bias.shape[1]
    return pl.pallas_call(
        functools.partial(first_kernel, hidden_units),
        grid=(count // BLOCK,),
        in_specs=[
            rows(width),
            rows(other.shape[1]),
            rows(features),
            whole(weight.shape),
            whole(norms.shape),
            whole(up_bias.shape),
        ],
        out_specs=[
            rows(features),
            rows(1),
            rows(features),
            rows(hidden_units),
            rows(hidden_units),
            rows(features),
        ],
        out_shape=[
            struct((count, features), F32),
            struct((count, 1), F32),
            struct((count, features), BF16),
            struct((count, hidden_units), BF16),
            struct((count, hidden_units), BF16),
            struct((count, features), BF16),
        ],
        compiler_params=params(),
        cost_estimate=cost(
            2 * count * weight.size, 2 * weight.size + count * features * 12, count * hidden_units
        ),
        name="feed_first",
    )(own, other, tokens, weight, norms, up_bias)


def column_sum(ref, value):
    partial = jnp.sum(value, 0, keepdims=True)

    @pl.when(pl.program_id(0) == 0)
    def _():
        ref[...] = partial

    @pl.when(pl.program_id(0) > 0)
    def _():
        ref[...] += partial


def second_kernel(
    swap, hidden_units, part_ref, recv_ref, normed_ref, grad_ref, slope_ref, weight_ref, norm_ref,
    output_ref, res_ref, low_ref, hidden_ref, lower_ref,
    bias_sum, gain_sum, shift_sum, hidden_sum,
):
    own = output_ref.shape[1]
    features = part_ref.shape[1]
    upper = normed_ref[...] * norm_ref[0:1, :] + norm_ref[2:3, :]
    hidden = upper + added(part_ref, recv_ref, swap) + norm_ref[5:6, :]
    normed, inverse = normalized(hidden)
    output_ref[...] = (
        normed[:, :own] * norm_ref[1:2, :own] + norm_ref[3:4, :own]
    ).astype(BF16)
    grad = grad_ref[...].astype(F32)
    res = norm_back(grad * norm_ref[1:2, :], normed, inverse)
    res_ref[...] = res
    low = res.astype(BF16)
    low_ref[...] = low
    act_grad = dot_nn(low, weight_ref[:, features + hidden_units :])
    hidden_grad = (act_grad * slope_ref[...].astype(F32)).astype(BF16)
    hidden_ref[...] = hidden_grad
    lower_ref[...] = dot_nt(
        hidden_grad, weight_ref[:, features : features + hidden_units]
    ).astype(BF16)
    column_sum(bias_sum, low[:, :own].astype(F32))
    column_sum(gain_sum, grad[:, :own] * normed[:, :own])
    column_sum(shift_sum, grad[:, :own])
    column_sum(hidden_sum, hidden_grad.astype(F32))


def feed_second(swap, own, part, recv, normed, grad, slope, weight, norms):
    count, features = part.shape
    hidden_units = slope.shape[1]
    return pl.pallas_call(
        functools.partial(second_kernel, swap, hidden_units),
        grid=(count // BLOCK,),
        in_specs=[
            rows(features),
            rows(features),
            rows(features),
            rows(features),
            rows(hidden_units),
            whole(weight.shape),
            whole(norms.shape),
        ],
        out_specs=[
            rows(own),
            rows(features),
            rows(features),
            rows(hidden_units),
            rows(features),
            whole((1, own)),
            whole((1, own)),
            whole((1, own)),
            whole((1, hidden_units)),
        ],
        out_shape=[
            struct((count, own), BF16),
            struct((count, features), F32),
            struct((count, features), BF16),
            struct((count, hidden_units), BF16),
            struct((count, features), BF16),
            struct((1, own), F32),
            struct((1, own), F32),
            struct((1, own), F32),
            struct((1, hidden_units), F32),
        ],
        compiler_params=params(),
        cost_estimate=cost(
            4 * count * features * hidden_units, 2 * weight.size + count * features * 20
        ),
        name="feed_second",
    )(part, recv, normed, grad, slope, weight, norms)


def third_kernel(
    swap, part_ref, recv_ref, res_ref, normed_ref, inverse_ref, weight_ref, norm_ref,
    low_ref, attended_ref, own_ref, gain_sum, shift_sum, bias_sum,
):
    own = own_ref.shape[1]
    grad = added(part_ref, recv_ref, swap) + res_ref[...]
    normed = normed_ref[...]
    res = norm_back(grad * norm_ref[0:1, :], normed, inverse_ref[...])
    own_ref[...] = res[:, :own]
    low = res.astype(BF16)
    low_ref[...] = low
    attended_ref[...] = dot_nn(low, weight_ref[:, : attended_ref.shape[1]]).astype(BF16)
    column_sum(gain_sum, grad[:, :own] * normed[:, :own])
    column_sum(shift_sum, grad[:, :own])
    column_sum(bias_sum, low[:, :own].astype(F32))


def feed_third(swap, own, width, part, recv, res, normed, inverse, weight, norms):
    count, features = part.shape
    return pl.pallas_call(
        functools.partial(third_kernel, swap),
        grid=(count // BLOCK,),
        in_specs=[
            rows(features),
            rows(features),
            rows(features),
            rows(features),
            rows(1),
            whole((features, features)),
            whole(norms.shape),
        ],
        out_specs=[
            rows(features),
            rows(width),
            rows(own),
            whole((1, own)),
            whole((1, own)),
            whole((1, own)),
        ],
        out_shape=[
            struct((count, features), BF16),
            struct((count, width), BF16),
            struct((count, own), F32),
            struct((1, own), F32),
            struct((1, own), F32),
            struct((1, own), F32),
        ],
        compiler_params=params(),
        cost_estimate=cost(2 * count * features * width, count * features * 16),
        name="feed_third",
    )(part, recv, res, normed, inverse, weight, norms)


def spread_rows(block_ref, scratch, keep_ref, send_ref, which):
    half, _, depth, _ = keep_ref.shape
    for slot in range(2 * half):
        start = pl.multiple_of(block_ref[slot] * depth, depth)
        piece = scratch[pl.ds(start, depth), :]
        if slot < half:
            keep_ref[slot, which] = piece
        else:
            send_ref[slot - half, which] = piece.astype(BF16)


def feed_grad_kernel(
    block_ref, low_ref, act_ref, upper_ref, hidden_ref, keep_ref, send_ref, scratch
):
    scratch[...] = dot_tn(upper_ref[...], hidden_ref[...])
    spread_rows(block_ref, scratch, keep_ref, send_ref, 0)
    scratch[...] = dot_tn(low_ref[...], act_ref[...])
    spread_rows(block_ref, scratch, keep_ref, send_ref, 1)


def feed_grads(blocks, low, act, upper, hidden):
    count, features = low.shape
    units = act.shape[1]
    half = blocks.shape[0] // 2
    depth = features // (2 * half)
    chunk = min(256, units)
    column = pl.BlockSpec((count, chunk), lambda b: (0, b))
    result = pl.BlockSpec((half, 2, depth, chunk), lambda b: (0, 0, 0, b))
    return pl.pallas_call(
        feed_grad_kernel,
        grid=(units // chunk,),
        in_specs=[
            pl.BlockSpec(memory_space=SMEM),
            whole(low.shape),
            column,
            whole(upper.shape),
            column,
        ],
        out_specs=[result, result],
        out_shape=[
            struct((half, 2, depth, units), F32),
            struct((half, 2, depth, units), BF16),
        ],
        scratch_shapes=[pltpu.VMEM((features, chunk), F32)],
        compiler_params=params(),
        cost_estimate=cost(4 * count * features * units, 8 * features * units),
        name="feed_grads",
    )(blocks, low, act, upper, hidden)


def project_grad_kernel(
    block_ref, token_ref, low_ref, high_ref, query_ref, key_ref, value_ref, branch_ref,
    attended_ref, keep_ref, send_ref, query_sum, value_sum, scratch,
):
    count = token_ref.shape[0]
    scratch[...] = dot_tn(token_ref[...], query_ref[...])
    spread_rows(block_ref, scratch, keep_ref, send_ref, 0)
    for which, ref in ((1, key_ref), (2, value_ref)):
        scratch[...] = (
            dot_tn(token_ref[...], ref[MAXDOC : MAXDOC + count, :])
            + dot_tn(low_ref[...], ref[PAD:MAXDOC, :])
            + dot_tn(high_ref[...], ref[MAXDOC + count : MAXDOC + count + HALO, :])
        )
        spread_rows(block_ref, scratch, keep_ref, send_ref, which)
    scratch[...] = dot_tn(branch_ref[...], attended_ref[...])
    spread_rows(block_ref, scratch, keep_ref, send_ref, 3)
    query_sum[...] = jnp.sum(query_ref[...].astype(F32), 0, keepdims=True)
    value_sum[...] = jnp.sum(value_ref[...].astype(F32), 0, keepdims=True)


def project_grads(blocks, tokens, low, high, query, key, value, branch, attended):
    count, features = tokens.shape
    width = query.shape[1]
    half = blocks.shape[0] // 2
    depth = features // (2 * half)
    operands = (tokens, low, high, query, key, value, branch, attended)
    return pl.pallas_call(
        project_grad_kernel,
        grid=(1,),
        in_specs=[pl.BlockSpec(memory_space=SMEM)] + [whole(x.shape) for x in operands],
        out_specs=[
            whole((half, 4, depth, width)),
            whole((half, 4, depth, width)),
            whole((1, width)),
            whole((1, width)),
        ],
        out_shape=[
            struct((half, 4, depth, width), F32),
            struct((half, 4, depth, width), BF16),
            struct((1, width), F32),
            struct((1, width), F32),
        ],
        scratch_shapes=[pltpu.VMEM((features, width), F32)],
        compiler_params=params(),
        cost_estimate=cost(2 * features * width * (4 * count + 4 * HALO), 4 << 20),
        name="project_grads",
    )(blocks, *operands)


def token_grad_kernel(query_ref, key_ref, value_ref, weight_ref, low_ref, own_ref, high_ref):
    count = query_ref.shape[0]

    def piece(start, size):
        return dot_nt(key_ref[start : start + size, :], weight_ref[1]) + dot_nt(
            value_ref[start : start + size, :], weight_ref[2]
        )

    for start in range(0, HALO, BLOCK):
        low_ref[start : start + BLOCK, :] = piece(PAD + start, BLOCK).astype(BF16)
        high_ref[start : start + BLOCK, :] = piece(MAXDOC + count + start, BLOCK).astype(BF16)
    for start in range(0, count, BLOCK):
        own_ref[start : start + BLOCK, :] = piece(MAXDOC + start, BLOCK) + dot_nt(
            query_ref[start : start + BLOCK, :], weight_ref[0]
        )


def token_grads(query, key, value, weight):
    count = query.shape[0]
    features = weight.shape[1]
    operands = (query, key, value, weight)
    return pl.pallas_call(
        token_grad_kernel,
        grid=(1,),
        in_specs=[whole(x.shape) for x in operands],
        out_specs=[
            whole((HALO, features)),
            whole((count, features)),
            whole((HALO, features)),
        ],
        out_shape=[
            struct((HALO, features), BF16),
            struct((count, features), F32),
            struct((HALO, features), BF16),
        ],
        compiler_params=params(),
        cost_estimate=cost(2 * features * query.shape[1] * (3 * count + 4 * HALO), 4 << 20),
        name="token_grads",
    )(*operands)


def from_next(x, axis, step):
    count = lax.axis_size(axis)
    return lax.ppermute(x, axis, [((i + step) % count, i) for i in range(count)])


def with_partner(x, bit):
    count = lax.axis_size("row")
    return lax.ppermute(x, "row", [(i, i ^ bit) for i in range(count)])


def others(x):
    return [from_next(x, "col", step) for step in range(1, lax.axis_size("col"))]


def bits_of(count):
    return [1 << place for place in range(count.bit_length() - 1)]


def gather_rows(shard):
    order = bits_of(lax.axis_size("row"))[::-1]
    held = shard[None]
    for bit in order[:-1]:
        held = jnp.concatenate([held, with_partner(held, bit)], 0)
    return held, with_partner(held, order[-1])


def reduce_rows(keep, send):
    for bit in bits_of(lax.axis_size("row")):
        total = keep + with_partner(send, bit).astype(F32)
        half = total.shape[0] // 2
        if half:
            keep, send = total[:half], total[half:].astype(BF16)
    return total[0]


def sum_rows(value):
    for bit in bits_of(lax.axis_size("row")):
        value = value + with_partner(value, bit)
    return value


def exchanged(part):
    arrived = others(part)
    if len(arrived) == 1:
        return arrived[0]
    shift = part.shape[1] // (len(arrived) + 1)
    total = sum(
        jnp.roll(x.astype(F32), step * shift, 1) for step, x in enumerate(arrived, 1)
    )
    return total.astype(BF16)


def on_device(
    tokens,
    prev_logits,
    doc_lengths,
    qkv_weight,
    qv_bias,
    out_weight,
    out_bias,
    up_weight,
    up_bias,
    down_weight,
    norm_gain,
    norm_shift,
    out_grad,
    logit_grad,
):
    count, own = tokens.shape
    width = qkv_weight.shape[2]
    row_count, col_count = lax.axis_size("row"), lax.axis_size("col")
    row_index, col_index = lax.axis_index("row"), lax.axis_index("col")
    token_count = count * row_count
    swap = col_count == 2

    order = bits_of(row_count)
    top = len(order) - 1

    def reversed_bits(x):
        return sum(((x >> place) & 1) << (top - place) for place in range(top + 1))

    places = jnp.arange(row_count, dtype=jnp.int32)
    offset = col_index * (row_count // col_count)
    slots = reversed_bits(((places + offset) % row_count) ^ row_index)
    blocks = ((reversed_bits(places) ^ row_index) - offset) % row_count
    base = (row_index * count)[None]

    tokens_full = jnp.concatenate([tokens] + others(tokens), 1)
    near, far = gather_rows(qkv_weight)
    forward = [(i, i + 1) for i in range(row_count - 1)]
    backward = [(b, a) for a, b in forward]
    low_tokens = lax.ppermute(tokens_full[count - HALO :], "row", forward)
    high_tokens = lax.ppermute(tokens_full[:HALO], "row", backward)
    out_turned = out_weight.T
    out_turned = jnp.concatenate([out_turned] + others(out_turned), 1)
    norms = jnp.concatenate([norm_gain, norm_shift, out_bias], 0)
    norms = jnp.concatenate([norms] + others(norms), 1)
    grad_full = jnp.concatenate([out_grad] + others(out_grad), 1)
    feed_near, feed_far = gather_rows(
        jnp.concatenate([out_turned, up_weight, down_weight.T], 1)
    )

    prev_dense = to_dense(prev_logits, doc_lengths, base, MASKED_SCORE, token_count)
    scores, probs, attended, query, key, value, weight = attend_forward(
        slots, tokens_full, low_tokens, high_tokens, near, far, qv_bias, prev_dense
    )
    attended_other = jnp.concatenate(others(attended), 1)
    logit_dense = to_dense(logit_grad, doc_lengths, base, 0.0, token_count)
    feed = in_order(slots, feed_near, feed_far)

    normed, inverse, upper, act, slope, down_part = feed_first(
        attended, attended_other, tokens_full, feed, norms, up_bias[None]
    )
    down_other = exchanged(down_part)
    new_logits = to_band(scores, True)
    output, res_two, ffn_low, hidden_grad, lower_part, ffn_bias, two_gain, two_shift, hidden_sum = (
        feed_second(swap, own, down_part, down_other, normed, grad_full, slope, feed, norms)
    )
    lower_other = exchanged(lower_part)
    feed_keep, feed_send = feed_grads(blocks, ffn_low, act, upper, hidden_grad)
    branch_low, attended_grad, res_one, one_gain, one_shift, attn_bias = feed_third(
        swap, own, width, lower_part, lower_other, res_two, normed, inverse, feed, norms
    )
    prev_dense_grad, query_grad, key_grad, value_grad = attend_backward(
        attended_grad, query, key, value, probs, logit_dense
    )
    keep, send, query_sum, value_sum = project_grads(
        blocks, tokens_full, low_tokens, high_tokens, query_grad, key_grad, value_grad,
        branch_low, attended,
    )
    feed_grad = reduce_rows(feed_keep, feed_send)
    project_grad = reduce_rows(keep, send)
    low_part, center, high_part = token_grads(query_grad, key_grad, value_grad, weight)
    arrived_low = lax.ppermute(high_part, "row", forward).astype(F32)
    arrived_high = lax.ppermute(low_part, "row", backward).astype(F32)
    rest = ((0, count - HALO), (0, 0))
    center = center + jnp.pad(arrived_low, rest) + jnp.pad(arrived_high, ((count - HALO, 0), (0, 0)))
    tokens_grad = center[:, :own] + res_one
    for step in range(1, col_count):
        part = center[:, step * own : (step + 1) * own].astype(BF16)
        tokens_grad = tokens_grad + from_next(part, "col", -step).astype(F32)
    prev_grad = to_band(prev_dense_grad, False)

    sums = sum_rows(
        jnp.concatenate(
            [
                query_sum, value_sum, attn_bias, ffn_bias, one_gain, two_gain, one_shift,
                two_shift, hidden_sum.reshape(-1, own),
            ],
            0,
        )
    )
    return (
        output,
        new_logits,
        tokens_grad.astype(BF16),
        prev_grad,
        project_grad[:3],
        sums[0:2],
        project_grad[3].T,
        sums[2:4],
        feed_grad[0],
        sums[8:].reshape(-1),
        feed_grad[1].T,
        sums[4:6],
        sums[6:8],
    )


def solution(mesh):
    return jax.shard_map(
        on_device,
        mesh=mesh,
        in_specs=(
            P("row", "col"),
            P("col", "row", None),
            P(),
            P(None, "row", "col"),
            P(None, "col"),
            P("col", "row"),
            P(None, "col"),
            P("row", "col"),
            P("col"),
            P("col", "row"),
            P(None, "col"),
            P(None, "col"),
            P("row", "col"),
            P("col", "row", None),
        ),
        out_specs=(
            P("row", "col"),
            P("col", "row", None),
            P("row", "col"),
            P("col", "row", None),
            P(None, "row", "col"),
            P(None, "col"),
            P("col", "row"),
            P(None, "col"),
            P("row", "col"),
            P("col"),
            P("col", "row"),
            P(None, "col"),
            P(None, "col"),
        ),
        check_vma=False,
    )
```

```python
import functools

import jax
import jax.numpy as jnp
from jax import lax
from jax.experimental import pallas as pl
from jax.experimental.pallas import tpu as pltpu
from jax.sharding import PartitionSpec as P

D = 512
HEAD_DIM = 64
MAXDOC = 512
BAND = 2 * MAXDOC
BLOCK = 128
WINDOW = BAND + BLOCK
HALO = MAXDOC - 128
PAD = MAXDOC - HALO

EPSILON = 1e-05
MASKED_SCORE = -1e30
ERF_RATE = 0.7071067811865476
DENSITY_RATE = 0.3989422804014327

F32 = jnp.float32
BF16 = jnp.bfloat16
SMEM = pltpu.MemorySpace.SMEM
VMEM_LIMIT = 24 << 20
CHUNKS = 2
SUM_ROWS = 16
FLOPS_PER_MICROSECOND = 1.0e9


def dot_nn(a, b):
    return lax.dot_general(a, b, (((1,), (0,)), ((), ())), preferred_element_type=F32)


def dot_nt(a, b):
    return lax.dot_general(a, b, (((1,), (1,)), ((), ())), preferred_element_type=F32)


def dot_tn(a, b):
    return lax.dot_general(a, b, (((0,), (0,)), ((), ())), preferred_element_type=F32)


def params():
    return pltpu.CompilerParams(
        dimension_semantics=("arbitrary",), vmem_limit_bytes=VMEM_LIMIT
    )


def lasting(microseconds):
    return pl.CostEstimate(
        flops=int(microseconds * FLOPS_PER_MICROSECOND), bytes_accessed=0, transcendentals=0
    )


def whole(shape):
    return pl.BlockSpec(shape, lambda b: (0,) * len(shape))


def rows(width, first=0):
    return pl.BlockSpec((BLOCK, width), lambda b: (b + first, 0))


def heads_block(heads, width, first=0):
    return pl.BlockSpec((heads, BLOCK, width), lambda b: (0, b + first, 0))


def struct(shape, dtype):
    return jax.ShapeDtypeStruct(shape, dtype)


def segment_of(positions, lengths_ref, token_count):
    sequences, documents = lengths_ref.shape
    found = jnp.zeros(positions.shape, jnp.int32)
    end = jnp.int32(0)
    for sequence in range(sequences):
        for document in range(documents):
            end = end + lengths_ref[sequence, document]
            found = found + (positions >= end).astype(jnp.int32)
    return jnp.where((positions >= 0) & (positions < token_count), found, -1)


def dense_kernel(fill, token_count, offset, lengths_ref, base_ref, band_ref, dense_ref):
    first = base_ref[0] + (pl.program_id(0) + offset) * BLOCK
    query = first + lax.broadcasted_iota(jnp.int32, (BLOCK, 1), 0)
    key = first - MAXDOC + lax.broadcasted_iota(jnp.int32, (1, WINDOW), 1)
    same = segment_of(query, lengths_ref, token_count) == segment_of(
        key, lengths_ref, token_count
    )
    for head in range(band_ref.shape[0]):
        wide = jnp.concatenate(
            [band_ref[head].astype(F32), jnp.zeros((BLOCK, BLOCK), F32)], 1
        )
        turned = pltpu.roll(wide, 0, 1, stride=1, stride_axis=0)
        dense_ref[head] = jnp.where(same, turned, fill).astype(BF16)


def to_dense(banded, lengths, base, fill, token_count, chunk):
    heads, count, _ = banded.shape
    count //= CHUNKS
    offset = chunk * (count // BLOCK)
    return pl.pallas_call(
        functools.partial(dense_kernel, fill, token_count, offset),
        grid=(count // BLOCK,),
        in_specs=[
            pl.BlockSpec(memory_space=SMEM),
            pl.BlockSpec(memory_space=SMEM),
            heads_block(heads, BAND, offset),
        ],
        out_specs=heads_block(heads, WINDOW),
        out_shape=struct((heads, count, WINDOW), BF16),
        compiler_params=params(),
        cost_estimate=lasting(1.0),
        name="to_dense",
    )(lengths, base, banded)


def band_kernel(masked, *refs):
    dense_refs, band_ref = refs[:-1], refs[-1]
    lane = lax.broadcasted_iota(jnp.int32, (BLOCK, BLOCK), 1)
    row = lax.broadcasted_iota(jnp.int32, (BLOCK, BLOCK), 0)
    source = (lane + row) & (BLOCK - 1)
    near = lane + row < BLOCK
    steps = pl.num_programs(0) // CHUNKS

    def turn(dense_ref):
        for head in range(band_ref.shape[0]):
            pieces = []
            for place in range(WINDOW // BLOCK):
                piece = dense_ref[head, :, place * BLOCK : (place + 1) * BLOCK].astype(F32)
                if masked:
                    piece = jnp.where(piece < 0.5 * MASKED_SCORE, 0.0, piece)
                pieces.append(jnp.take_along_axis(piece, source, axis=1))
            for place in range(BAND // BLOCK):
                band_ref[head, :, place * BLOCK : (place + 1) * BLOCK] = jnp.where(
                    near, pieces[place], pieces[place + 1]
                ).astype(BF16)

    for chunk, dense_ref in enumerate(dense_refs):

        @pl.when(pl.program_id(0) // steps == chunk)
        def _():
            turn(dense_ref)


def to_band(chunks, masked):
    heads, count, _ = chunks[0].shape
    steps = count // BLOCK

    def block_of(chunk):
        return pl.BlockSpec(
            (heads, BLOCK, WINDOW), lambda b: (0, jnp.clip(b - chunk * steps, 0, steps - 1), 0)
        )

    return pl.pallas_call(
        functools.partial(band_kernel, masked),
        grid=(CHUNKS * steps,),
        in_specs=[block_of(chunk) for chunk in range(CHUNKS)],
        out_specs=heads_block(heads, BAND),
        out_shape=struct((heads, CHUNKS * count, BAND), BF16),
        compiler_params=params(),
        cost_estimate=lasting(5.0),
        name="to_band",
    )(*chunks)


def head_split(block, size):
    if size == 1:
        return block
    lane = lax.broadcasted_iota(jnp.int32, block.shape, 1)
    return jnp.concatenate(
        [
            jnp.where((lane >= h * HEAD_DIM) & (lane < (h + 1) * HEAD_DIM), block, 0)
            for h in range(size)
        ],
        0,
    )


def head_join(stacked, size):
    if size == 1:
        return stacked
    height = stacked.shape[0] // size
    joined = stacked[:height]
    lane = lax.broadcasted_iota(jnp.int32, joined.shape, 1)
    for h in range(1, size):
        joined = jnp.where(lane >= h * HEAD_DIM, stacked[h * height : (h + 1) * height], joined)
    return joined


def project_kernel(
    slot_ref, token_ref, low_ref, high_ref, near_ref, far_ref, bias_ref,
    query_ref, key_ref, value_ref, weight_ref,
):
    half, _, depth, width = near_ref.shape
    count = token_ref.shape[0]
    for place in range(2 * half):
        slot = slot_ref[place]

        @pl.when(slot < half)
        def _():
            weight_ref[:, place * depth : (place + 1) * depth, :] = near_ref[slot]

        @pl.when(slot >= half)
        def _():
            weight_ref[:, place * depth : (place + 1) * depth, :] = far_ref[slot - half]

    low_rows, high_rows = low_ref[...], high_ref[...]
    own = token_ref[...]
    empty = jnp.zeros((PAD, width), BF16)
    query = (dot_nn(own, weight_ref[0]) + bias_ref[0:1, :]).astype(BF16)
    query_ref[...] = query * jnp.asarray(HEAD_DIM ** (-0.5), BF16)
    for out_ref, which in ((key_ref, 1), (value_ref, 2)):
        shift = bias_ref[1:2, :] if which == 2 else 0.0
        weight = weight_ref[which]
        out_ref[0:PAD, :] = empty
        out_ref[PAD:MAXDOC, :] = (dot_nn(low_rows, weight) + shift).astype(BF16)
        out_ref[MAXDOC : MAXDOC + count, :] = (dot_nn(own, weight) + shift).astype(BF16)
        out_ref[MAXDOC + count : MAXDOC + count + HALO, :] = (
            dot_nn(high_rows, weight) + shift
        ).astype(BF16)
        out_ref[MAXDOC + count + HALO :, :] = empty


def project(slots, tokens, low, high, near, far, bias):
    count, features = tokens.shape
    width = near.shape[3]
    operands = (tokens, low, high, near, far, bias)
    shapes = ((count, width), (count + BAND, width), (count + BAND, width), (3, features, width))
    return pl.pallas_call(
        project_kernel,
        grid=(1,),
        in_specs=[pl.BlockSpec(memory_space=SMEM)] + [whole(x.shape) for x in operands],
        out_specs=[whole(shape) for shape in shapes],
        out_shape=[struct(shape, BF16) for shape in shapes],
        compiler_params=params(),
        cost_estimate=lasting(2.0),
        name="project",
    )(slots, *operands)


def forward_kernel(
    offset, query_ref, key_ref, value_ref, prev_ref, score_ref, prob_ref, attended_ref
):
    heads = prev_ref.shape[0]
    size = min(2, heads)
    span = size * HEAD_DIM
    window = pl.ds(pl.multiple_of((pl.program_id(0) + offset) * BLOCK, BLOCK), WINDOW)
    for group in range(heads // size):
        lanes = slice(group * span, (group + 1) * span)
        query = head_split(query_ref[:, lanes], size)
        dense = dot_nt(query, key_ref[window, lanes])
        weights = []
        for h in range(size):
            head = group * size + h
            score = dense[h * BLOCK : (h + 1) * BLOCK] + prev_ref[head].astype(F32)
            score_ref[head] = score.astype(BF16)
            peak = jnp.max(score, -1, keepdims=True)
            grown = jnp.exp(score - peak)
            total = jnp.sum(grown, -1, keepdims=True)
            prob = (grown * (1.0 / total)).astype(BF16)
            prob_ref[head] = prob
            weights.append(prob)
        mixed = dot_nn(jnp.concatenate(weights, 0), value_ref[window, lanes])
        attended_ref[:, lanes] = head_join(mixed, size).astype(BF16)


def attend_forward(query, key, value, prev, chunk):
    heads, count, _ = prev.shape
    width = query.shape[1]
    offset = chunk * (count // BLOCK)
    return pl.pallas_call(
        functools.partial(forward_kernel, offset),
        grid=(count // BLOCK,),
        in_specs=[
            rows(width, offset),
            whole(key.shape),
            whole(value.shape),
            heads_block(heads, WINDOW),
        ],
        out_specs=[heads_block(heads, WINDOW), heads_block(heads, WINDOW), rows(width)],
        out_shape=[
            struct((heads, count, WINDOW), BF16),
            struct((heads, count, WINDOW), BF16),
            struct((count, width), BF16),
        ],
        compiler_params=params(),
        cost_estimate=lasting(3.8),
        name="attend_forward",
    )(query, key, value, prev)


def backward_kernel(
    offset, last, grad_ref, query_ref, key_ref, value_ref, prob_ref, logit_ref, *refs
):
    if last:
        key_start, value_start = refs[:2]
        prev_ref, query_grad_ref, key_grad_ref, value_grad_ref, key_sum, value_sum = refs[2:]
    else:
        prev_ref, query_grad_ref, key_sum, value_sum = refs
    step = pl.program_id(0)
    heads = prob_ref.shape[0]
    size = min(2, heads)
    span = size * HEAD_DIM

    @pl.when(step == 0)
    def _():
        if last:
            key_sum[...] = key_start[...]
            value_sum[...] = value_start[...]
        else:
            key_sum[...] = jnp.zeros_like(key_sum)
            value_sum[...] = jnp.zeros_like(value_sum)

    window = pl.ds(pl.multiple_of((step + offset) * BLOCK, BLOCK), WINDOW)
    for group in range(heads // size):
        lanes = slice(group * span, (group + 1) * span)
        query = head_split(query_ref[:, lanes], size)
        grad = head_split(grad_ref[:, lanes], size)
        key = key_ref[window, lanes]
        prob_grad = dot_nt(grad, value_ref[window, lanes])
        probs, scores = [], []
        for h in range(size):
            head = group * size + h
            low = prob_ref[head]
            prob = low.astype(F32)
            slope = prob_grad[h * BLOCK : (h + 1) * BLOCK]
            inner = jnp.sum(prob * slope, -1, keepdims=True)
            score = (prob * (slope - inner) + logit_ref[head].astype(F32)).astype(BF16)
            prev_ref[head] = score
            probs.append(low)
            scores.append(score)
        stacked = jnp.concatenate(scores, 0)
        mixed = head_join(dot_nn(stacked, key), size) * HEAD_DIM ** (-0.5)
        query_grad_ref[:, lanes] = mixed.astype(BF16)
        key_sum[lanes, window] += dot_tn(query, stacked)
        value_sum[lanes, window] += dot_tn(grad, jnp.concatenate(probs, 0))

    if last:

        @pl.when(step == pl.num_programs(0) - 1)
        def _():
            key_grad_ref[...] = key_sum[...].astype(BF16).T
            value_grad_ref[...] = value_sum[...].astype(BF16).T


def attend_backward(grad, query, key, value, prob, logit, chunk, sums):
    heads, count, _ = prob.shape
    extended, width = key.shape
    offset = chunk * (count // BLOCK)
    last = sums is not None
    turned = (width, extended)
    scratch = [pltpu.VMEM(turned, F32), pltpu.VMEM(turned, F32)] if last else []
    ends = [whole((extended, width))] * 2 if last else [whole(turned)] * 2
    end_shapes = [struct((extended, width), BF16)] * 2 if last else [struct(turned, F32)] * 2
    return pl.pallas_call(
        functools.partial(backward_kernel, offset, last),
        grid=(count // BLOCK,),
        in_specs=[
            rows(width),
            rows(width, offset),
            whole((extended, width)),
            whole((extended, width)),
            heads_block(heads, WINDOW),
            heads_block(heads, WINDOW),
        ]
        + ([whole(turned)] * 2 if last else []),
        out_specs=[heads_block(heads, WINDOW), rows(width)] + ends,
        out_shape=[struct((heads, count, WINDOW), BF16), struct((count, width), BF16)]
        + end_shapes,
        scratch_shapes=scratch,
        compiler_params=params(),
        cost_estimate=lasting(1.4),
        name="attend_backward",
    )(grad, query, key, value, prob, logit, *(sums or ()))


def order_kernel(slot_ref, near_ref, far_ref, *out_refs):
    half, depth, _ = near_ref.shape

    def put(place, source_ref, slot):
        first = 0
        for out_ref in out_refs:
            last = first + out_ref.shape[1]
            out_ref[place * depth : (place + 1) * depth, :] = source_ref[slot, :, first:last]
            first = last

    for place in range(2 * half):
        slot = slot_ref[place]

        @pl.when(slot < half)
        def _():
            put(place, near_ref, slot)

        @pl.when(slot >= half)
        def _():
            put(place, far_ref, slot - half)


def in_order(slots, near, far, widths):
    half, depth, _ = near.shape
    shapes = [(2 * half * depth, width) for width in widths]
    return pl.pallas_call(
        order_kernel,
        grid=(1,),
        in_specs=[pl.BlockSpec(memory_space=SMEM), whole(near.shape), whole(far.shape)],
        out_specs=[whole(shape) for shape in shapes],
        out_shape=[struct(shape, BF16) for shape in shapes],
        compiler_params=params(),
        cost_estimate=lasting(0.9),
        name="in_order",
    )(slots, near, far)


def mean_of(x):
    return jnp.sum(x, -1, keepdims=True) * (1.0 / D)


def normalized(hidden):
    mean = mean_of(hidden)
    inverse = lax.rsqrt(mean_of(hidden * hidden) - mean * mean + EPSILON)
    return (hidden - mean) * inverse, inverse


def norm_back(upstream, normed, inverse):
    return inverse * (upstream - mean_of(upstream) - normed * mean_of(upstream * normed))


def added(own_ref, other_ref, swap):
    other = other_ref[...]
    if swap:
        middle = other.shape[1] // 2
        other = jnp.concatenate([other[:, middle:], other[:, :middle]], 1)
    return own_ref[...].astype(F32) + other.astype(F32)


def first_kernel(
    own_ref, other_ref, token_ref, out_ref, up_ref, down_ref, norm_ref, up_bias_ref,
    normed_ref, inverse_ref, upper_ref, act_ref, slope_ref, part_ref,
):
    width = own_ref.shape[1]
    branch = dot_nt(own_ref[...], out_ref[:, :width]) + dot_nt(other_ref[...], out_ref[:, width:])
    hidden = token_ref[...].astype(F32) + branch + norm_ref[4:5, :]
    normed, inverse = normalized(hidden)
    normed_ref[...] = normed
    inverse_ref[...] = inverse
    upper = (normed * norm_ref[0:1, :] + norm_ref[2:3, :]).astype(BF16)
    upper_ref[...] = upper
    pre = dot_nn(upper, up_ref[...]) + up_bias_ref[...]
    share = 0.5 * (1.0 + lax.erf(pre * ERF_RATE))
    act = (pre * share).astype(BF16)
    act_ref[...] = act
    slope_ref[...] = (share + pre * jnp.exp(-0.5 * pre * pre) * DENSITY_RATE).astype(BF16)
    part_ref[...] = dot_nt(act, down_ref[...]).astype(BF16)


def feed_first(own, other, tokens, weights, norms, up_bias, chunk):
    count, width = own.shape
    features = tokens.shape[1]
    units = up_bias.shape[1]
    return pl.pallas_call(
        first_kernel,
        grid=(count // BLOCK,),
        in_specs=[
            rows(width),
            rows(other.shape[1]),
            rows(features, chunk * (count // BLOCK)),
            *weight_blocks(features, units),
            whole(norms.shape),
            whole(up_bias.shape),
        ],
        out_specs=[
            rows(features),
            rows(1),
            rows(features),
            rows(units),
            rows(units),
            rows(features),
        ],
        out_shape=[
            struct((count, features), F32),
            struct((count, 1), F32),
            struct((count, features), BF16),
            struct((count, units), BF16),
            struct((count, units), BF16),
            struct((count, features), BF16),
        ],
        compiler_params=params(),
        cost_estimate=lasting(1.0),
        name="feed_first",
    )(own, other, tokens, *weights, norms, up_bias)


def weight_blocks(features, units):
    return [
        pl.BlockSpec((features, features), lambda b: (0, 0)),
        pl.BlockSpec((features, units), lambda b: (0, 0)),
        pl.BlockSpec((features, units), lambda b: (0, 0)),
    ]


def add_sums(start_ref, sum_ref, first, values):
    @pl.when(pl.program_id(0) == 0)
    def _():
        sum_ref[...] = start_ref[...]

    for place, value in enumerate(values):
        sum_ref[first + place : first + place + 1, :] += jnp.sum(value, 0, keepdims=True)


def second_kernel(
    swap, start_ref, part_ref, recv_ref, normed_ref, grad_ref, slope_ref, up_ref, down_ref,
    norm_ref, *refs,
):
    sum_ref, output_ref, res_ref, low_ref, hidden_ref, lower_ref = refs[-6:]
    own = output_ref.shape[1]
    upper = normed_ref[...] * norm_ref[0:1, :] + norm_ref[2:3, :]
    hidden = upper + added(part_ref, recv_ref, swap) + norm_ref[5:6, :]
    normed, inverse = normalized(hidden)
    output_ref[...] = (
        normed[:, :own] * norm_ref[1:2, :own] + norm_ref[3:4, :own]
    ).astype(BF16)
    grad = grad_ref[...].astype(F32)
    res = norm_back(grad * norm_ref[1:2, :], normed, inverse)
    res_ref[...] = res
    low = res.astype(BF16)
    low_ref[...] = low
    act_grad = dot_nn(low, down_ref[...])
    hidden_grad = (act_grad * slope_ref[...].astype(F32)).astype(BF16)
    hidden_ref[...] = hidden_grad
    lower_ref[...] = dot_nt(hidden_grad, up_ref[...]).astype(BF16)
    wide = hidden_grad.astype(F32)
    add_sums(start_ref, sum_ref, 3, [low[:, :own].astype(F32)])
    for place, value in (
        (5, grad[:, :own] * normed[:, :own]),
        (7, grad[:, :own]),
        *((8 + k, wide[:, k * own : (k + 1) * own]) for k in range(wide.shape[1] // own)),
    ):
        sum_ref[place : place + 1, :] += jnp.sum(value, 0, keepdims=True)


def feed_second(swap, sums, held, part, recv, normed, grad, slope, weights, norms, chunk):
    count, features = part.shape
    own = sums.shape[1]
    units = slope.shape[1]
    offset = chunk * (count // BLOCK)
    return pl.pallas_call(
        functools.partial(second_kernel, swap),
        grid=(count // BLOCK,),
        in_specs=[
            whole(sums.shape),
            rows(features),
            rows(features),
            rows(features),
            rows(features, offset),
            rows(units),
            *weight_blocks(features, units)[1:],
            whole(norms.shape),
            *([] if held is None else [pl.BlockSpec(memory_space=pl.ANY)]),
        ],
        out_specs=[
            whole(sums.shape),
            rows(own, offset),
            rows(features),
            rows(features),
            rows(units),
            rows(features),
        ],
        out_shape=[
            struct(sums.shape, F32),
            struct((CHUNKS * count, own), BF16),
            struct((count, features), F32),
            struct((count, features), BF16),
            struct((count, units), BF16),
            struct((count, features), BF16),
        ],
        input_output_aliases={} if held is None else {9: 1},
        compiler_params=params(),
        cost_estimate=lasting(0.7),
        name="feed_second",
    )(sums, part, recv, normed, grad, slope, *weights[1:], norms, *(() if held is None else (held,)))


def third_kernel(
    swap, start_ref, part_ref, recv_ref, res_ref, normed_ref, inverse_ref, out_ref, norm_ref,
    sum_ref, low_ref, attended_ref, own_ref,
):
    own = own_ref.shape[1]
    grad = added(part_ref, recv_ref, swap) + res_ref[...]
    normed = normed_ref[...]
    res = norm_back(grad * norm_ref[0:1, :], normed, inverse_ref[...])
    own_ref[...] = res[:, :own]
    low = res.astype(BF16)
    low_ref[...] = low
    attended_ref[...] = dot_nn(low, out_ref[:, : attended_ref.shape[1]]).astype(BF16)
    add_sums(start_ref, sum_ref, 2, [low[:, :own].astype(F32)])
    for place, value in ((4, grad[:, :own] * normed[:, :own]), (6, grad[:, :own])):
        sum_ref[place : place + 1, :] += jnp.sum(value, 0, keepdims=True)


def feed_third(swap, sums, width, part, recv, res, normed, inverse, weights, norms):
    count, features = part.shape
    own = sums.shape[1]
    return pl.pallas_call(
        functools.partial(third_kernel, swap),
        grid=(count // BLOCK,),
        in_specs=[
            whole(sums.shape),
            rows(features),
            rows(features),
            rows(features),
            rows(features),
            rows(1),
            whole((features, features)),
            whole(norms.shape),
        ],
        out_specs=[whole(sums.shape), rows(features), rows(width), rows(own)],
        out_shape=[
            struct(sums.shape, F32),
            struct((count, features), BF16),
            struct((count, width), BF16),
            struct((count, own), F32),
        ],
        compiler_params=params(),
        cost_estimate=lasting(0.2),
        name="feed_third",
    )(sums, part, recv, res, normed, inverse, weights[0], norms)


def spread_rows(block_ref, scratch, keep_ref, send_ref, which, kinds):
    features = scratch.shape[0]
    count = block_ref.shape[0]
    depth = features // count
    half = count // 2
    for slot in range(count):
        start = pl.multiple_of(block_ref[slot] * depth, depth)
        piece = scratch[pl.ds(start, depth), :]
        first = ((slot % half) * kinds + which) * depth
        if slot < half:
            keep_ref[first : first + depth, :] = piece
        else:
            send_ref[first : first + depth, :] = piece.astype(BF16)


def split_sums(total):
    high = total.astype(BF16)
    low = (total - high.astype(F32)).astype(BF16)
    return high, low, high.astype(F32) + low.astype(F32)


def feed_grad_kernel(up_block_ref, down_block_ref, *refs):
    low_refs, upper_refs, act_refs, hidden_refs = (
        refs[k * CHUNKS : (k + 1) * CHUNKS] for k in range(4)
    )
    up_keep, up_send, down_keep, down_send, scratch = refs[4 * CHUNKS :]
    scratch[...] = sum(dot_tn(a[...], b[...]) for a, b in zip(upper_refs, hidden_refs))
    spread_rows(up_block_ref, scratch, up_keep, up_send, 0, 1)
    scratch[...] = sum(dot_tn(a[...], b[...]) for a, b in zip(low_refs, act_refs))
    spread_rows(down_block_ref, scratch, down_keep, down_send, 0, 1)


def feed_grads(up_blocks, down_blocks, low, act, upper, hidden):
    count, features = low[0].shape
    units = act[0].shape[1]
    chunk = min(256, units)
    column = pl.BlockSpec((count, chunk), lambda b: (0, b))
    height = features // 2
    result = pl.BlockSpec((height, chunk), lambda b: (0, b))
    return pl.pallas_call(
        feed_grad_kernel,
        grid=(units // chunk,),
        in_specs=[pl.BlockSpec(memory_space=SMEM)] * 2
        + [whole((count, features))] * (2 * CHUNKS)
        + [column] * (2 * CHUNKS),
        out_specs=[result] * 4,
        out_shape=[struct((height, units), F32), struct((height, units), BF16)] * 2,
        scratch_shapes=[pltpu.VMEM((features, chunk), F32)],
        compiler_params=params(),
        cost_estimate=lasting(1.0),
        name="feed_grads",
    )(up_blocks, down_blocks, *low, *upper, *act, *hidden)


def project_grad_kernel(block_ref, start_ref, *refs):
    query_refs, branch_refs, attended_refs = (
        refs[k * CHUNKS : (k + 1) * CHUNKS] for k in range(3)
    )
    token_ref, low_ref, high_ref, key_ref, value_ref = refs[3 * CHUNKS : 3 * CHUNKS + 5]
    keep_ref, send_ref, sum_ref, scratch = refs[3 * CHUNKS + 5 :]
    count = token_ref.shape[0]
    part = count // CHUNKS
    scratch[...] = sum(
        dot_tn(token_ref[k * part : (k + 1) * part, :], ref[...])
        for k, ref in enumerate(query_refs)
    )
    spread_rows(block_ref, scratch, keep_ref, send_ref, 0, 4)
    for which, ref in ((1, key_ref), (2, value_ref)):
        scratch[...] = (
            dot_tn(token_ref[...], ref[MAXDOC : MAXDOC + count, :])
            + dot_tn(low_ref[...], ref[PAD:MAXDOC, :])
            + dot_tn(high_ref[...], ref[MAXDOC + count : MAXDOC + count + HALO, :])
        )
        spread_rows(block_ref, scratch, keep_ref, send_ref, which, 4)
    scratch[...] = sum(dot_tn(a[...], b[...]) for a, b in zip(branch_refs, attended_refs))
    spread_rows(block_ref, scratch, keep_ref, send_ref, 3, 4)
    total = start_ref[...]
    place = lax.broadcasted_iota(jnp.int32, total.shape, 0)
    query_sum = sum(
        jnp.sum(ref[...].astype(F32), 0, keepdims=True) for ref in query_refs
    )
    value_sum = jnp.sum(value_ref[...].astype(F32), 0, keepdims=True)
    total = total + jnp.where(place == 0, query_sum, 0.0) + jnp.where(place == 1, value_sum, 0.0)
    height = keep_ref.shape[0]
    high, low, sum_ref[...] = split_sums(total)
    send_ref[height : height + SUM_ROWS, :] = high
    send_ref[height + SUM_ROWS :, :] = low


def project_grads(blocks, sums, tokens, low, high, query, key, value, branch, attended):
    features = tokens.shape[1]
    width = key.shape[1]
    half = blocks.shape[0] // 2
    depth = features // (2 * half)
    height = half * 4 * depth
    operands = (sums, *query, *branch, *attended, tokens, low, high, key, value)
    return pl.pallas_call(
        project_grad_kernel,
        grid=(1,),
        in_specs=[pl.BlockSpec(memory_space=SMEM)] + [whole(x.shape) for x in operands],
        out_specs=[
            whole((height, width)),
            whole((height + 2 * SUM_ROWS, width)),
            whole(sums.shape),
        ],
        out_shape=[
            struct((height, width), F32),
            struct((height + 2 * SUM_ROWS, width), BF16),
            struct(sums.shape, F32),
        ],
        scratch_shapes=[pltpu.VMEM((features, width), F32)],
        compiler_params=params(),
        cost_estimate=lasting(0.6),
        name="project_grads",
    )(blocks, *operands)


def fold_kernel(arrivals, sends, kinds, *refs):
    keep_ref, *refs = refs
    arrived_refs, refs = refs[:arrivals], refs[arrivals:]
    height = keep_ref.shape[0]
    with_sums = arrived_refs[0].shape[0] > height
    if with_sums:
        start_ref, *refs = refs
    size = height // (sends + 1)

    def total(first):
        parts = [ref[first : first + size, :].astype(F32) for ref in arrived_refs]
        if arrivals == 1:
            return keep_ref[first : first + size, :] + parts[0]
        return (keep_ref[first : first + size, :] + parts[0]) + (parts[1] + parts[2])

    stays = total(0)
    depth = size // kinds
    for kind in range(kinds):
        refs[kind][...] = stays[kind * depth : (kind + 1) * depth, :]
    send_outs = refs[kinds : kinds + sends]
    for place, send_out in enumerate(send_outs):
        send_out[:size, :] = total((place + 1) * size).astype(BF16)
    if with_sums:
        parts = [
            ref[height : height + SUM_ROWS, :].astype(F32)
            + ref[height + SUM_ROWS :, :].astype(F32)
            for ref in arrived_refs
        ]
        summed = start_ref[...] + parts[0]
        if arrivals > 1:
            summed = summed + (parts[1] + parts[2])
        sum_out = refs[kinds + sends]
        if sends:
            high, low, sum_out[...] = split_sums(summed)
            for send_out in send_outs:
                send_out[size : size + SUM_ROWS, :] = high
                send_out[size + SUM_ROWS :, :] = low
        else:
            sum_out[...] = summed


def fold(keep, arrived, sums, sends, kinds):
    height, width = keep.shape
    extra = arrived[0].shape[0] - height
    size = height // (sends + 1)
    operands = (keep, *arrived) + (() if sums is None else (sums,))
    shapes = [struct((size // kinds, width), F32)] * kinds
    shapes += [struct((size + extra, width), BF16)] * sends
    shapes += [] if sums is None else [struct(sums.shape, F32)]
    result = pl.pallas_call(
        functools.partial(fold_kernel, len(arrived), sends, kinds),
        grid=(1,),
        in_specs=[whole(x.shape) for x in operands],
        out_specs=[whole(x.shape) for x in shapes],
        out_shape=shapes,
        compiler_params=params(),
        cost_estimate=lasting(0.2),
        name="fold",
    )(*operands)
    if not sends:
        return result
    return result[0], result[1 : 1 + sends], (None if sums is None else result[-1])


def token_grad_kernel(*refs):
    query_refs, res_refs = refs[:CHUNKS], refs[CHUNKS : 2 * CHUNKS]
    key_ref, value_ref, weight_ref, low_ref, own_ref, high_ref = refs[2 * CHUNKS :]
    count = own_ref.shape[0]
    own = res_refs[0].shape[1]

    def piece(start):
        return dot_nt(key_ref[start : start + BLOCK, :], weight_ref[1]) + dot_nt(
            value_ref[start : start + BLOCK, :], weight_ref[2]
        )

    for start in range(0, HALO, BLOCK):
        low_ref[start : start + BLOCK, :] = piece(PAD + start).astype(BF16)
        high_ref[start : start + BLOCK, :] = piece(MAXDOC + count + start).astype(BF16)
    for start in range(0, count, BLOCK):
        chunk, inside = divmod(start, count // CHUNKS)
        total = piece(MAXDOC + start) + dot_nt(
            query_refs[chunk][inside : inside + BLOCK, :], weight_ref[0]
        )
        own_ref[start : start + BLOCK, :] = total
        own_ref[start : start + BLOCK, :own] += res_refs[chunk][inside : inside + BLOCK, :]


def token_grads(query, res, key, value, weight):
    count = CHUNKS * query[0].shape[0]
    features = weight.shape[1]
    operands = (*query, *res, key, value, weight)
    return pl.pallas_call(
        token_grad_kernel,
        grid=(1,),
        in_specs=[whole(x.shape) for x in operands],
        out_specs=[
            whole((HALO, features)),
            whole((count, features)),
            whole((HALO, features)),
        ],
        out_shape=[
            struct((HALO, features), BF16),
            struct((count, features), F32),
            struct((HALO, features), BF16),
        ],
        compiler_params=params(),
        cost_estimate=lasting(0.6),
        name="token_grads",
    )(*operands)


def from_next(x, axis, step):
    count = lax.axis_size(axis)
    return lax.ppermute(x, axis, [((i + step) % count, i) for i in range(count)])


def with_partner(x, bit):
    count = lax.axis_size("row")
    return lax.ppermute(x, "row", [(i, i ^ bit) for i in range(count)])


def others(x):
    return [from_next(x, "col", step) for step in range(1, lax.axis_size("col"))]


def bits_of(count):
    return [1 << place for place in range(count.bit_length() - 1)]


def after(value, *needed):
    return lax.optimization_barrier((value, *needed))[0]


def high_first(count):
    bits = bits_of(count)[::-1]
    return [bits[:2], *([bit] for bit in bits[2:])]


def high_late(count):
    bits = bits_of(count)[::-1]
    return [*([bit] for bit in bits[2:-1]), bits[:2], bits[-1:]]


def slots_of(steps, distance):
    bits = [bit for step in steps for bit in step]
    return sum(((distance & bit) // bit) << place for place, bit in enumerate(bits))


def distances_of(steps, slots):
    bits = [bit for step in steps for bit in step]
    return sum(((slots >> place) & 1) * bit for place, bit in enumerate(bits))


def partners_of(step):
    return step if len(step) == 1 else (step[0], step[1], step[0] + step[1])


def gather_rows(shard, steps, waits=(), fillers=()):
    waits, fillers, done = list(waits), list(fillers), []
    held = shard[None]
    stages = [held]
    for place, step in enumerate(steps):
        arrived = [with_partner(held, bit) for bit in partners_of(step)]
        if fillers:
            done.append(fillers.pop(0)(held))
            *arrived, done[-1] = lax.optimization_barrier((*arrived, done[-1]))
        if waits:
            needed = waits.pop(0)
            if needed is not None:
                arrived[0] = after(arrived[0], needed)
        if place < len(steps) - 1:
            held = jnp.concatenate([held, *arrived], 0)
            stages.append(held)
    return stages, arrived[0], done


class Gather:
    def __init__(self, shard, steps):
        self.held, self.steps = shard[None], list(steps)
        self.move()

    def move(self):
        self.arrived = [with_partner(self.held, bit) for bit in partners_of(self.steps.pop(0))]

    def put(self, *needed):
        while True:
            arrived = self.arrived
            self.held = jnp.concatenate([after(self.held, *needed), *arrived], 0)
            self.move()
            if len(self.steps) < 2:
                return

    def last(self):
        return self.arrived[0]


class Reduction:
    def __init__(self, steps, keep, send, sums, kinds):
        self.steps = steps[::-1]
        self.keep, self.send, self.sums, self.kinds = keep, send, sums, kinds
        self.arrived = None

    def move(self):
        self.step = self.steps.pop(0)
        self.arrived = [
            with_partner(x, bit) for x, bit in zip(self.send, partners_of(self.step))
        ]

    def add(self, *needed):
        keep = after(self.keep, *needed)
        if not self.steps:
            self.result = fold(keep, self.arrived, self.sums, 0, self.kinds)
            return
        sends = len(partners_of(self.steps[0]))
        self.keep, self.send, self.sums = fold(keep, self.arrived, self.sums, sends, 1)
        self.move()


def exchanged(part):
    arrived = others(part)
    if len(arrived) == 1:
        return arrived[0]
    shift = part.shape[1] // (len(arrived) + 1)
    total = sum(
        jnp.roll(x.astype(F32), step * shift, 1) for step, x in enumerate(arrived, 1)
    )
    return total.astype(BF16)


def on_device(
    tokens,
    prev_logits,
    doc_lengths,
    qkv_weight,
    qv_bias,
    out_weight,
    out_bias,
    up_weight,
    up_bias,
    down_weight,
    norm_gain,
    norm_shift,
    out_grad,
    logit_grad,
):
    count, own = tokens.shape
    width = qkv_weight.shape[2]
    row_count, col_count = lax.axis_size("row"), lax.axis_size("col")
    row_index, col_index = lax.axis_index("row"), lax.axis_index("col")
    token_count = count * row_count
    swap = col_count == 2
    hidden_rows = up_bias.shape[0] // own

    early, late = high_first(row_count), high_late(row_count)
    places = jnp.arange(row_count, dtype=jnp.int32)
    offset = col_index * (row_count // col_count)
    distance = ((places + offset) % row_count) ^ row_index
    slots, late_slots = slots_of(early, distance), slots_of(late, distance)
    blocks = ((distances_of(early, places) ^ row_index) - offset) % row_count
    late_blocks = ((distances_of(late, places) ^ row_index) - offset) % row_count
    base = (row_index * count)[None]

    out_turned = out_weight.T
    norms = jnp.concatenate([norm_gain, norm_shift, out_bias], 0)
    first = norms.astype(BF16)
    rest = norms - first.astype(F32)
    second = rest.astype(BF16)
    third = (rest - second.astype(F32)).astype(BF16)
    mixed = jnp.concatenate([tokens, out_turned, first, second, third], 0)
    arrived = others(mixed)
    depth = out_turned.shape[0]
    tokens_full = jnp.concatenate([tokens] + [x[:count] for x in arrived], 1)
    out_rows = jnp.concatenate([out_turned] + [x[count : count + depth] for x in arrived], 1)
    pieces = [x[count + depth :].astype(F32).reshape(3, -1, own) for x in arrived]
    norms = jnp.concatenate([norms] + [(x[0] + x[1]) + x[2] for x in pieces], 1)

    def dense_of(banded, fill, chunk):
        return lambda held: to_dense(
            after(banded, held), doc_lengths, base, fill, token_count, chunk
        )

    prev_logits = pltpu.with_memory_space_constraint(prev_logits, pltpu.HBM)
    logit_grad = pltpu.with_memory_space_constraint(logit_grad, pltpu.HBM)
    stages, far, prev_dense = gather_rows(
        qkv_weight,
        early,
        (),
        [dense_of(prev_logits, MASKED_SCORE, 0), dense_of(prev_logits, MASKED_SCORE, 1)],
    )
    near = stages[-1]
    forward = [(i, i + 1) for i in range(row_count - 1)]
    backward = [(b, a) for a, b in forward]
    low_tokens = lax.ppermute(tokens_full[count - HALO :], "row", forward)
    high_tokens = lax.ppermute(tokens_full[:HALO], "row", backward)
    grad_full = jnp.concatenate([out_grad] + others(after(out_grad, tokens_full)), 1)

    scores, probs, attended, attended_other, logit_dense = [], [], [], [], []
    up_shard = after(jnp.concatenate([out_rows, up_weight], 1), stages[1])
    down_shard = after(down_weight.T, stages[0])

    up_gather = Gather(up_shard, early)
    down_gather = Gather(down_shard, late)
    up_gather.put()
    down_gather.put()
    query, key, value, weight = project(
        slots, after(tokens_full, up_gather.held, down_gather.held, grad_full), low_tokens,
        high_tokens, near, far, qv_bias,
    )
    for chunk in range(CHUNKS):
        score, prob, mix = attend_forward(query, key, value, prev_dense[chunk], chunk)
        query = after(query, mix)
        scores.append(score)
        probs.append(prob)
        attended.append(mix)
        attended_other.append(jnp.concatenate(others(mix), 1))
    up_gather.put(mix)
    down_gather.put(mix)
    scores_low = after(scores[0], attended_other[0], up_gather.held)
    new_logits = to_band([scores_low, *scores[1:]], True)

    up_near = after(up_gather.held, new_logits)
    weights = in_order(
        slots, up_near, up_gather.last(), (tokens_full.shape[1], up_weight.shape[1])
    )
    down_near = after(down_gather.held, weights[0])
    weights = (
        *weights,
        *in_order(late_slots, down_near, down_gather.last(), (up_weight.shape[1],)),
    )
    ups = up_bias[None]
    firsts = []
    for chunk in range(CHUNKS):
        result = feed_first(
            attended[chunk], attended_other[chunk], tokens_full, weights, norms, ups, chunk
        )
        ups = after(ups, result[-1])
        firsts.append((*result, exchanged(result[-1])))
    normed, inverse, upper, act, slope, down_part, down_other = zip(*firsts)

    logit_dense.append(dense_of(logit_grad, 0.0, 0)(down_part[-1]))
    sums = after(jnp.zeros((SUM_ROWS, own), F32), logit_dense[-1])
    output = None
    seconds = []
    for chunk in range(CHUNKS):
        sums, output, *result = feed_second(
            swap, sums, output, down_part[chunk], down_other[chunk],
            normed[chunk], grad_full, slope[chunk], weights, norms, chunk,
        )
        seconds.append((*result, exchanged(result[-1])))
    res_two, ffn_low, hidden_grad, lower_part, lower_other = zip(*seconds)
    logit_dense.append(dense_of(logit_grad, 0.0, 1)(lower_part[-1]))
    sums = after(sums, logit_dense[-1])

    branch_low, res_one, query_grad, prev_dense_grad = [], [], [], []
    partial = None
    for chunk in range(CHUNKS):
        sums, low, attended_grad, res = feed_third(
            swap, sums, width, lower_part[chunk], lower_other[chunk], res_two[chunk],
            normed[chunk], inverse[chunk], weights, norms,
        )
        branch_low.append(low)
        res_one.append(res)
        if chunk == 0:
            up_keep, up_send, down_keep, down_send = feed_grads(
                late_blocks, blocks, (after(ffn_low[0], low), *ffn_low[1:]), act, upper,
                hidden_grad,
            )
            up_sum = Reduction(late, up_keep, [up_send], None, 1)
            down_sum = Reduction(early, down_keep, [down_send], None, 1)
            up_sum.move()
            down_sum.move()
            attended_grad = after(attended_grad, up_keep)
        prev, query_part, *partial = attend_backward(
            attended_grad, query, key, value, probs[chunk], logit_dense[chunk], chunk, partial
        )
        sums = after(sums, query_part)
        if chunk == 0:
            down_sum.add(query_part)
            up_sum.add(down_sum.keep)
            sums = after(sums, up_sum.keep)
        prev_dense_grad.append(prev)
        query_grad.append(query_part)
    key_grad, value_grad = partial
    low_part, center, high_part = token_grads(query_grad, res_one, key_grad, value_grad, weight)
    arrived_low = lax.ppermute(high_part, "row", forward).astype(F32)
    arrived_high = lax.ppermute(low_part, "row", backward).astype(F32)
    down_sum.add(low_part)
    keep, send, sums = project_grads(
        blocks, after(sums, down_sum.keep), tokens_full, low_tokens, high_tokens, query_grad,
        key_grad, value_grad, branch_low, attended,
    )
    last = Reduction(early, keep, [send], sums, 4)
    last.move()
    up_sum.add(keep)
    last.add(up_sum.keep)
    center = center + jnp.pad(after(arrived_low, last.keep), ((0, count - HALO), (0, 0)))
    center = center + jnp.pad(arrived_high, ((count - HALO, 0), (0, 0)))
    tokens_grad = center[:, :own]
    for step in range(1, col_count):
        part = center[:, step * own : (step + 1) * own].astype(BF16)
        tokens_grad = tokens_grad + from_next(part, "col", -step).astype(F32)
    prev_dense_grad[0] = after(prev_dense_grad[0], center)
    prev_grad = to_band(prev_dense_grad, False)
    for sums_of in (last, down_sum, up_sum):
        while not hasattr(sums_of, "result"):
            sums_of.add(prev_grad)
    *project_grad, out_grad_rows, sums = last.result
    feed_grad = (up_sum.result[0], down_sum.result[0])
    return (
        output,
        new_logits,
        tokens_grad.astype(BF16),
        prev_grad,
        jnp.stack(project_grad),
        sums[0:2],
        out_grad_rows.T,
        sums[2:4],
        feed_grad[0],
        sums[8 : 8 + hidden_rows].reshape(-1),
        feed_grad[1].T,
        sums[4:6],
        sums[6:8],
    )


def solution(mesh):
    return jax.shard_map(
        on_device,
        mesh=mesh,
        in_specs=(
            P("row", "col"),
            P("col", "row", None),
            P(),
            P(None, "row", "col"),
            P(None, "col"),
            P("col", "row"),
            P(None, "col"),
            P("row", "col"),
            P("col"),
            P("col", "row"),
            P(None, "col"),
            P(None, "col"),
            P("row", "col"),
            P("col", "row", None),
        ),
        out_specs=(
            P("row", "col"),
            P("col", "row", None),
            P("row", "col"),
            P("col", "row", None),
            P(None, "row", "col"),
            P(None, "col"),
            P("col", "row"),
            P(None, "col"),
            P("row", "col"),
            P("col"),
            P("col", "row"),
            P(None, "col"),
            P(None, "col"),
        ),
        check_vma=False,
    )
```

```python
import functools

import jax
import jax.numpy as jnp
from jax import lax
from jax.experimental import pallas as pl
from jax.experimental.pallas import tpu as pltpu
from jax.sharding import PartitionSpec as P

D = 512
HEAD_DIM = 64
MAXDOC = 512
BAND = 2 * MAXDOC
BLOCK = 128
WINDOW = BAND + BLOCK
HALO = MAXDOC - 128
PAD = MAXDOC - HALO

EPSILON = 1e-05
MASKED_SCORE = -1e30
ERF_RATE = 0.7071067811865476
DENSITY_RATE = 0.3989422804014327

F32 = jnp.float32
BF16 = jnp.bfloat16
SMEM = pltpu.MemorySpace.SMEM
VMEM_LIMIT = 24 << 20
CHUNKS = 2
SUM_ROWS = 16
FLOPS_PER_MICROSECOND = 1.0e9


def dot_nn(a, b):
    return lax.dot_general(a, b, (((1,), (0,)), ((), ())), preferred_element_type=F32)


def dot_nt(a, b):
    return lax.dot_general(a, b, (((1,), (1,)), ((), ())), preferred_element_type=F32)


def dot_tn(a, b):
    return lax.dot_general(a, b, (((0,), (0,)), ((), ())), preferred_element_type=F32)


def params():
    return pltpu.CompilerParams(
        dimension_semantics=("arbitrary",), vmem_limit_bytes=VMEM_LIMIT
    )


def lasting(microseconds):
    return pl.CostEstimate(
        flops=int(microseconds * FLOPS_PER_MICROSECOND), bytes_accessed=0, transcendentals=0
    )


def whole(shape):
    return pl.BlockSpec(shape, lambda b: (0,) * len(shape))


def rows(width, first=0):
    return pl.BlockSpec((BLOCK, width), lambda b: (b + first, 0))


def heads_block(heads, width, first=0):
    return pl.BlockSpec((heads, BLOCK, width), lambda b: (0, b + first, 0))


def struct(shape, dtype):
    return jax.ShapeDtypeStruct(shape, dtype)


def segment_of(positions, lengths_ref, token_count):
    sequences, documents = lengths_ref.shape
    found = jnp.zeros(positions.shape, jnp.int32)
    end = jnp.int32(0)
    for sequence in range(sequences):
        for document in range(documents):
            end = end + lengths_ref[sequence, document]
            found = found + (positions >= end).astype(jnp.int32)
    return jnp.where((positions >= 0) & (positions < token_count), found, -1)


def dense_kernel(fill, token_count, offset, lengths_ref, base_ref, band_ref, dense_ref):
    first = base_ref[0] + (pl.program_id(0) + offset) * BLOCK
    query = first + lax.broadcasted_iota(jnp.int32, (BLOCK, 1), 0)
    key = first - MAXDOC + lax.broadcasted_iota(jnp.int32, (1, WINDOW), 1)
    same = segment_of(query, lengths_ref, token_count) == segment_of(
        key, lengths_ref, token_count
    )
    for head in range(band_ref.shape[0]):
        wide = jnp.concatenate(
            [band_ref[head].astype(F32), jnp.zeros((BLOCK, BLOCK), F32)], 1
        )
        turned = pltpu.roll(wide, 0, 1, stride=1, stride_axis=0)
        dense_ref[head] = jnp.where(same, turned, fill).astype(BF16)


def to_dense(banded, lengths, base, fill, token_count, chunk):
    heads, count, _ = banded.shape
    count //= CHUNKS
    offset = chunk * (count // BLOCK)
    return pl.pallas_call(
        functools.partial(dense_kernel, fill, token_count, offset),
        grid=(count // BLOCK,),
        in_specs=[
            pl.BlockSpec(memory_space=SMEM),
            pl.BlockSpec(memory_space=SMEM),
            heads_block(heads, BAND, offset),
        ],
        out_specs=heads_block(heads, WINDOW),
        out_shape=struct((heads, count, WINDOW), BF16),
        compiler_params=params(),
        cost_estimate=lasting(8.0 if fill else 1.0),
        name="to_dense",
    )(lengths, base, banded)


def band_kernel(masked, *refs):
    dense_refs, band_ref = refs[:-1], refs[-1]
    lane = lax.broadcasted_iota(jnp.int32, (BLOCK, BLOCK), 1)
    row = lax.broadcasted_iota(jnp.int32, (BLOCK, BLOCK), 0)
    source = (lane + row) & (BLOCK - 1)
    near = lane + row < BLOCK
    steps = pl.num_programs(0) // CHUNKS

    def turn(dense_ref):
        for head in range(band_ref.shape[0]):
            pieces = []
            for place in range(WINDOW // BLOCK):
                piece = dense_ref[head, :, place * BLOCK : (place + 1) * BLOCK].astype(F32)
                if masked:
                    piece = jnp.where(piece < 0.5 * MASKED_SCORE, 0.0, piece)
                pieces.append(jnp.take_along_axis(piece, source, axis=1))
            for place in range(BAND // BLOCK):
                band_ref[head, :, place * BLOCK : (place + 1) * BLOCK] = jnp.where(
                    near, pieces[place], pieces[place + 1]
                ).astype(BF16)

    for chunk, dense_ref in enumerate(dense_refs):

        @pl.when(pl.program_id(0) // steps == chunk)
        def _():
            turn(dense_ref)


def to_band(chunks, masked):
    heads, count, _ = chunks[0].shape
    steps = count // BLOCK

    def block_of(chunk):
        return pl.BlockSpec(
            (heads, BLOCK, WINDOW), lambda b: (0, jnp.clip(b - chunk * steps, 0, steps - 1), 0)
        )

    return pl.pallas_call(
        functools.partial(band_kernel, masked),
        grid=(CHUNKS * steps,),
        in_specs=[block_of(chunk) for chunk in range(CHUNKS)],
        out_specs=heads_block(heads, BAND),
        out_shape=struct((heads, CHUNKS * count, BAND), BF16),
        compiler_params=params(),
        cost_estimate=lasting(5.0),
        name="to_band",
    )(*chunks)


def head_split(block, size):
    if size == 1:
        return block
    lane = lax.broadcasted_iota(jnp.int32, block.shape, 1)
    return jnp.concatenate(
        [
            jnp.where((lane >= h * HEAD_DIM) & (lane < (h + 1) * HEAD_DIM), block, 0)
            for h in range(size)
        ],
        0,
    )


def head_join(stacked, size):
    if size == 1:
        return stacked
    height = stacked.shape[0] // size
    joined = stacked[:height]
    lane = lax.broadcasted_iota(jnp.int32, joined.shape, 1)
    for h in range(1, size):
        joined = jnp.where(lane >= h * HEAD_DIM, stacked[h * height : (h + 1) * height], joined)
    return joined


def join_kernel(even_ref, *refs):
    *part_refs, all_ref, inside_ref, across_ref = refs
    count = all_ref.shape[0]
    width = part_refs[0].shape[1]
    even = even_ref[0] == 1
    for place, ref in enumerate(part_refs):
        lanes = slice(place * width, (place + 1) * width)
        all_ref[:, lanes] = ref[...]
        tail, head = ref[count - HALO :, :], ref[:HALO, :]
        inside_ref[:, lanes] = jnp.where(even, tail, head)
        across_ref[:, lanes] = jnp.where(even, head, tail)


def join(even, parts):
    count, width = parts[0].shape
    features = len(parts) * width
    shapes = ((count, features), (HALO, features), (HALO, features))
    return pl.pallas_call(
        join_kernel,
        grid=(1,),
        in_specs=[pl.BlockSpec(memory_space=SMEM)] + [whole(x.shape) for x in parts],
        out_specs=[whole(shape) for shape in shapes],
        out_shape=[struct(shape, BF16) for shape in shapes],
        compiler_params=params(),
        cost_estimate=lasting(0.5),
        name="join",
    )(even, *parts)


def project_kernel(
    slot_ref, even_ref, token_ref, inside_ref, across_ref, near_ref, far_ref, bias_ref,
    query_ref, key_ref, value_ref, low_ref, high_ref, *weight_refs,
):
    half, _, depth, _ = near_ref.shape
    count = token_ref.shape[0]

    def put(place, source_ref, slot):
        for which, ref in enumerate(weight_refs):
            ref[place * depth : (place + 1) * depth, :] = source_ref[slot, which]

    for place in range(2 * half):
        slot = slot_ref[place]

        @pl.when(slot < half)
        def _():
            put(place, near_ref, slot)

        @pl.when(slot >= half)
        def _():
            put(place, far_ref, slot - half)

    even = even_ref[0] == 1
    inside, across = inside_ref[...], across_ref[...]
    low_rows, high_rows = jnp.where(even, across, inside), jnp.where(even, inside, across)
    low_ref[...] = low_rows
    high_ref[...] = high_rows
    own = token_ref[...]
    query = (dot_nn(own, weight_refs[0][...]) + bias_ref[0:1, :]).astype(BF16)
    empty = jnp.zeros((PAD, query.shape[1]), BF16)
    query_ref[...] = query * jnp.asarray(HEAD_DIM ** (-0.5), BF16)
    for out_ref, which in ((key_ref, 1), (value_ref, 2)):
        shift = bias_ref[1:2, :] if which == 2 else 0.0
        weight = weight_refs[which][...]
        out_ref[0:PAD, :] = empty
        out_ref[PAD:MAXDOC, :] = (dot_nn(low_rows, weight) + shift).astype(BF16)
        out_ref[MAXDOC : MAXDOC + count, :] = (dot_nn(own, weight) + shift).astype(BF16)
        out_ref[MAXDOC + count : MAXDOC + count + HALO, :] = (
            dot_nn(high_rows, weight) + shift
        ).astype(BF16)
        out_ref[MAXDOC + count + HALO :, :] = empty


def project(slots, even, tokens, inside, across, near, far, bias):
    count, features = tokens.shape
    width = near.shape[3]
    operands = (tokens, inside, across, near, far, bias)
    extended = (count + BAND, width)
    shapes = [(count, width), extended, extended, inside.shape, across.shape]
    shapes += [(features, width)] * 3
    return pl.pallas_call(
        project_kernel,
        grid=(1,),
        in_specs=[pl.BlockSpec(memory_space=SMEM)] * 2 + [whole(x.shape) for x in operands],
        out_specs=[whole(shape) for shape in shapes],
        out_shape=[struct(shape, BF16) for shape in shapes],
        compiler_params=params(),
        cost_estimate=lasting(2.0),
        name="project",
    )(slots, even, *operands)


def forward_kernel(
    offset, query_ref, key_ref, value_ref, prev_ref, score_ref, prob_ref, attended_ref
):
    heads = prev_ref.shape[0]
    size = min(2, heads)
    span = size * HEAD_DIM
    window = pl.ds(pl.multiple_of((pl.program_id(0) + offset) * BLOCK, BLOCK), WINDOW)
    for group in range(heads // size):
        lanes = slice(group * span, (group + 1) * span)
        query = head_split(query_ref[:, lanes], size)
        dense = dot_nt(query, key_ref[window, lanes])
        weights = []
        for h in range(size):
            head = group * size + h
            score = dense[h * BLOCK : (h + 1) * BLOCK] + prev_ref[head].astype(F32)
            score_ref[head] = score.astype(BF16)
            peak = jnp.max(score, -1, keepdims=True)
            grown = jnp.exp(score - peak)
            total = jnp.sum(grown, -1, keepdims=True)
            prob = (grown * (1.0 / total)).astype(BF16)
            prob_ref[head] = prob
            weights.append(prob)
        mixed = dot_nn(jnp.concatenate(weights, 0), value_ref[window, lanes])
        attended_ref[:, lanes] = head_join(mixed, size).astype(BF16)


def attend_forward(query, key, value, prev, chunk):
    heads, count, _ = prev.shape
    width = query.shape[1]
    offset = chunk * (count // BLOCK)
    return pl.pallas_call(
        functools.partial(forward_kernel, offset),
        grid=(count // BLOCK,),
        in_specs=[
            rows(width, offset),
            whole(key.shape),
            whole(value.shape),
            heads_block(heads, WINDOW),
        ],
        out_specs=[heads_block(heads, WINDOW), heads_block(heads, WINDOW), rows(width)],
        out_shape=[
            struct((heads, count, WINDOW), BF16),
            struct((heads, count, WINDOW), BF16),
            struct((count, width), BF16),
        ],
        compiler_params=params(),
        cost_estimate=lasting(3.8),
        name="attend_forward",
    )(query, key, value, prev)


def backward_kernel(
    offset, last, grad_ref, query_ref, key_ref, value_ref, prob_ref, logit_ref, *refs
):
    if last:
        key_start, value_start = refs[:2]
        prev_ref, query_grad_ref, key_grad_ref, value_grad_ref, key_sum, value_sum = refs[2:]
    else:
        prev_ref, query_grad_ref, key_sum, value_sum = refs
    step = pl.program_id(0)
    heads = prob_ref.shape[0]
    size = min(2, heads)
    span = size * HEAD_DIM

    @pl.when(step == 0)
    def _():
        if last:
            key_sum[...] = key_start[...]
            value_sum[...] = value_start[...]
        else:
            key_sum[...] = jnp.zeros_like(key_sum)
            value_sum[...] = jnp.zeros_like(value_sum)

    window = pl.ds(pl.multiple_of((step + offset) * BLOCK, BLOCK), WINDOW)
    for group in range(heads // size):
        lanes = slice(group * span, (group + 1) * span)
        query = head_split(query_ref[:, lanes], size)
        grad = head_split(grad_ref[:, lanes], size)
        key = key_ref[window, lanes]
        prob_grad = dot_nt(grad, value_ref[window, lanes])
        probs, scores = [], []
        for h in range(size):
            head = group * size + h
            low = prob_ref[head]
            prob = low.astype(F32)
            slope = prob_grad[h * BLOCK : (h + 1) * BLOCK]
            inner = jnp.sum(prob * slope, -1, keepdims=True)
            score = (prob * (slope - inner) + logit_ref[head].astype(F32)).astype(BF16)
            prev_ref[head] = score
            probs.append(low)
            scores.append(score)
        stacked = jnp.concatenate(scores, 0)
        mixed = head_join(dot_nn(stacked, key), size) * HEAD_DIM ** (-0.5)
        query_grad_ref[:, lanes] = mixed.astype(BF16)
        key_sum[lanes, window] += dot_tn(query, stacked)
        value_sum[lanes, window] += dot_tn(grad, jnp.concatenate(probs, 0))

    if last:

        @pl.when(step == pl.num_programs(0) - 1)
        def _():
            key_grad_ref[...] = key_sum[...].astype(BF16).T
            value_grad_ref[...] = value_sum[...].astype(BF16).T


def attend_backward(grad, query, key, value, prob, logit, chunk, sums):
    heads, count, _ = prob.shape
    extended, width = key.shape
    offset = chunk * (count // BLOCK)
    last = sums is not None
    turned = (width, extended)
    scratch = [pltpu.VMEM(turned, F32), pltpu.VMEM(turned, F32)] if last else []
    ends = [whole((extended, width))] * 2 if last else [whole(turned)] * 2
    end_shapes = [struct((extended, width), BF16)] * 2 if last else [struct(turned, F32)] * 2
    return pl.pallas_call(
        functools.partial(backward_kernel, offset, last),
        grid=(count // BLOCK,),
        in_specs=[
            rows(width),
            rows(width, offset),
            whole((extended, width)),
            whole((extended, width)),
            heads_block(heads, WINDOW),
            heads_block(heads, WINDOW),
        ]
        + ([whole(turned)] * 2 if last else []),
        out_specs=[heads_block(heads, WINDOW), rows(width)] + ends,
        out_shape=[struct((heads, count, WINDOW), BF16), struct((count, width), BF16)]
        + end_shapes,
        scratch_shapes=scratch,
        compiler_params=params(),
        cost_estimate=lasting(3.0 if last else 20.0),
        name="attend_backward",
    )(grad, query, key, value, prob, logit, *(sums or ()))


def order_kernel(slot_ref, near_ref, far_ref, *out_refs):
    half, depth, _ = near_ref.shape

    def put(place, source_ref, slot):
        first = 0
        for out_ref in out_refs:
            last = first + out_ref.shape[1]
            out_ref[place * depth : (place + 1) * depth, :] = source_ref[slot, :, first:last]
            first = last

    for place in range(2 * half):
        slot = slot_ref[place]

        @pl.when(slot < half)
        def _():
            put(place, near_ref, slot)

        @pl.when(slot >= half)
        def _():
            put(place, far_ref, slot - half)


def in_order(slots, near, far, widths):
    half, depth, _ = near.shape
    shapes = [(2 * half * depth, width) for width in widths]
    return pl.pallas_call(
        order_kernel,
        grid=(1,),
        in_specs=[pl.BlockSpec(memory_space=SMEM), whole(near.shape), whole(far.shape)],
        out_specs=[whole(shape) for shape in shapes],
        out_shape=[struct(shape, BF16) for shape in shapes],
        compiler_params=params(),
        cost_estimate=lasting(0.9),
        name="in_order",
    )(slots, near, far)


def mean_of(x):
    return jnp.sum(x, -1, keepdims=True) * (1.0 / D)


def normalized(hidden):
    mean = mean_of(hidden)
    inverse = lax.rsqrt(mean_of(hidden * hidden) - mean * mean + EPSILON)
    return (hidden - mean) * inverse, inverse


def norm_back(upstream, normed, inverse):
    return inverse * (upstream - mean_of(upstream) - normed * mean_of(upstream * normed))


def added(own_ref, other_ref, swap):
    other = other_ref[...]
    if swap:
        middle = other.shape[1] // 2
        other = jnp.concatenate([other[:, middle:], other[:, :middle]], 1)
    return own_ref[...].astype(F32) + other.astype(F32)


def first_kernel(
    own_ref, other_ref, token_ref, other_out_ref, out_ref, up_ref, down_ref, norm_ref,
    up_bias_ref, normed_ref, inverse_ref, upper_ref, act_ref, slope_ref, part_ref,
):
    branch = dot_nt(own_ref[...], out_ref[...]) + dot_nt(other_ref[...], other_out_ref[...])
    hidden = token_ref[...].astype(F32) + branch + norm_ref[4:5, :]
    normed, inverse = normalized(hidden)
    normed_ref[...] = normed
    inverse_ref[...] = inverse
    upper = (normed * norm_ref[0:1, :] + norm_ref[2:3, :]).astype(BF16)
    upper_ref[...] = upper
    pre = dot_nn(upper, up_ref[...]) + up_bias_ref[...]
    share = 0.5 * (1.0 + lax.erf(pre * ERF_RATE))
    act = (pre * share).astype(BF16)
    act_ref[...] = act
    slope_ref[...] = (share + pre * jnp.exp(-0.5 * pre * pre) * DENSITY_RATE).astype(BF16)
    part_ref[...] = dot_nt(act, down_ref[...]).astype(BF16)


def feed_first(own, other, tokens, other_out, weights, norms, up_bias, chunk):
    count, width = own.shape
    features = tokens.shape[1]
    units = up_bias.shape[1]
    return pl.pallas_call(
        first_kernel,
        grid=(count // BLOCK,),
        in_specs=[
            rows(width),
            rows(other.shape[1]),
            rows(features, chunk * (count // BLOCK)),
            whole(other_out.shape),
            *(whole(x.shape) for x in weights),
            whole(norms.shape),
            whole(up_bias.shape),
        ],
        out_specs=[
            rows(features),
            rows(1),
            rows(features),
            rows(units),
            rows(units),
            rows(features),
        ],
        out_shape=[
            struct((count, features), F32),
            struct((count, 1), F32),
            struct((count, features), BF16),
            struct((count, units), BF16),
            struct((count, units), BF16),
            struct((count, features), BF16),
        ],
        compiler_params=params(),
        cost_estimate=lasting(1.0),
        name="feed_first",
    )(own, other, tokens, other_out, *weights, norms, up_bias)


def add_sums(start_ref, sum_ref, first, values):
    @pl.when(pl.program_id(0) == 0)
    def _():
        sum_ref[...] = start_ref[...]

    for place, value in enumerate(values):
        sum_ref[first + place : first + place + 1, :] += jnp.sum(value, 0, keepdims=True)


def second_kernel(
    swap, start_ref, part_ref, recv_ref, normed_ref, grad_ref, slope_ref, up_ref, down_ref,
    norm_ref, *refs,
):
    sum_ref, output_ref, res_ref, low_ref, hidden_ref, lower_ref = refs[-6:]
    own = output_ref.shape[1]
    upper = normed_ref[...] * norm_ref[0:1, :] + norm_ref[2:3, :]
    hidden = upper + added(part_ref, recv_ref, swap) + norm_ref[5:6, :]
    normed, inverse = normalized(hidden)
    output_ref[...] = (
        normed[:, :own] * norm_ref[1:2, :own] + norm_ref[3:4, :own]
    ).astype(BF16)
    grad = grad_ref[...].astype(F32)
    res = norm_back(grad * norm_ref[1:2, :], normed, inverse)
    res_ref[...] = res
    low = res.astype(BF16)
    low_ref[...] = low
    act_grad = dot_nn(low, down_ref[...])
    hidden_grad = (act_grad * slope_ref[...].astype(F32)).astype(BF16)
    hidden_ref[...] = hidden_grad
    lower_ref[...] = dot_nt(hidden_grad, up_ref[...]).astype(BF16)
    wide = hidden_grad.astype(F32)
    add_sums(start_ref, sum_ref, 3, [low[:, :own].astype(F32)])
    for place, value in (
        (5, grad[:, :own] * normed[:, :own]),
        (7, grad[:, :own]),
        *((8 + k, wide[:, k * own : (k + 1) * own]) for k in range(wide.shape[1] // own)),
    ):
        sum_ref[place : place + 1, :] += jnp.sum(value, 0, keepdims=True)


def feed_second(swap, sums, held, part, recv, normed, grad, slope, weights, norms, chunk):
    count, features = part.shape
    own = sums.shape[1]
    units = slope.shape[1]
    offset = chunk * (count // BLOCK)
    return pl.pallas_call(
        functools.partial(second_kernel, swap),
        grid=(count // BLOCK,),
        in_specs=[
            whole(sums.shape),
            rows(features),
            rows(features),
            rows(features),
            rows(features, offset),
            rows(units),
            *(whole(x.shape) for x in weights[1:]),
            whole(norms.shape),
            *([] if held is None else [pl.BlockSpec(memory_space=pl.ANY)]),
        ],
        out_specs=[
            whole(sums.shape),
            rows(own, offset),
            rows(features),
            rows(features),
            rows(units),
            rows(features),
        ],
        out_shape=[
            struct(sums.shape, F32),
            struct((CHUNKS * count, own), BF16),
            struct((count, features), F32),
            struct((count, features), BF16),
            struct((count, units), BF16),
            struct((count, features), BF16),
        ],
        input_output_aliases={} if held is None else {9: 1},
        compiler_params=params(),
        cost_estimate=lasting(0.7),
        name="feed_second",
    )(sums, part, recv, normed, grad, slope, *weights[1:], norms, *(() if held is None else (held,)))


def third_kernel(
    swap, start_ref, part_ref, recv_ref, res_ref, normed_ref, inverse_ref, out_ref, norm_ref,
    sum_ref, low_ref, attended_ref, own_ref,
):
    own = own_ref.shape[1]
    grad = added(part_ref, recv_ref, swap) + res_ref[...]
    normed = normed_ref[...]
    res = norm_back(grad * norm_ref[0:1, :], normed, inverse_ref[...])
    own_ref[...] = res[:, :own]
    low = res.astype(BF16)
    low_ref[...] = low
    attended_ref[...] = dot_nn(low, out_ref[...]).astype(BF16)
    add_sums(start_ref, sum_ref, 2, [low[:, :own].astype(F32)])
    for place, value in ((4, grad[:, :own] * normed[:, :own]), (6, grad[:, :own])):
        sum_ref[place : place + 1, :] += jnp.sum(value, 0, keepdims=True)


def feed_third(swap, sums, width, part, recv, res, normed, inverse, weights, norms):
    count, features = part.shape
    own = sums.shape[1]
    return pl.pallas_call(
        functools.partial(third_kernel, swap),
        grid=(count // BLOCK,),
        in_specs=[
            whole(sums.shape),
            rows(features),
            rows(features),
            rows(features),
            rows(features),
            rows(1),
            whole(weights[0].shape),
            whole(norms.shape),
        ],
        out_specs=[whole(sums.shape), rows(features), rows(width), rows(own)],
        out_shape=[
            struct(sums.shape, F32),
            struct((count, features), BF16),
            struct((count, width), BF16),
            struct((count, own), F32),
        ],
        compiler_params=params(),
        cost_estimate=lasting(0.2),
        name="feed_third",
    )(sums, part, recv, res, normed, inverse, weights[0], norms)


def spread_rows(block_ref, scratch, keep_ref, send_ref, which, kinds):
    features = scratch.shape[0]
    count = block_ref.shape[0]
    depth = features // count
    half = count // 2
    for slot in range(count):
        start = pl.multiple_of(block_ref[slot] * depth, depth)
        piece = scratch[pl.ds(start, depth), :]
        first = ((slot % half) * kinds + which) * depth
        if slot < half:
            keep_ref[first : first + depth, :] = piece
        else:
            send_ref[first : first + depth, :] = piece.astype(BF16)


def split_sums(total):
    high = total.astype(BF16)
    low = (total - high.astype(F32)).astype(BF16)
    return high, low, high.astype(F32) + low.astype(F32)


def feed_grad_kernel(block_ref, *refs):
    low_refs, upper_refs, act_refs, hidden_refs = (
        refs[k * CHUNKS : (k + 1) * CHUNKS] for k in range(4)
    )
    keep_ref, send_ref, scratch = refs[4 * CHUNKS :]
    scratch[...] = sum(dot_tn(a[...], b[...]) for a, b in zip(upper_refs, hidden_refs))
    spread_rows(block_ref, scratch, keep_ref, send_ref, 0, 2)
    scratch[...] = sum(dot_tn(a[...], b[...]) for a, b in zip(low_refs, act_refs))
    spread_rows(block_ref, scratch, keep_ref, send_ref, 1, 2)


def feed_grads(blocks, low, act, upper, hidden):
    count, features = low[0].shape
    units = act[0].shape[1]
    chunk = min(256, units)
    column = pl.BlockSpec((count, chunk), lambda b: (0, b))
    result = pl.BlockSpec((features, chunk), lambda b: (0, b))
    return pl.pallas_call(
        feed_grad_kernel,
        grid=(units // chunk,),
        in_specs=[pl.BlockSpec(memory_space=SMEM)]
        + [whole((count, features))] * (2 * CHUNKS)
        + [column] * (2 * CHUNKS),
        out_specs=[result] * 2,
        out_shape=[struct((features, units), F32), struct((features, units), BF16)],
        scratch_shapes=[pltpu.VMEM((features, chunk), F32)],
        compiler_params=params(),
        cost_estimate=lasting(1.0),
        name="feed_grads",
    )(blocks, *low, *upper, *act, *hidden)


def project_grad_kernel(block_ref, start_ref, *refs):
    query_refs, branch_refs, attended_refs = (
        refs[k * CHUNKS : (k + 1) * CHUNKS] for k in range(3)
    )
    token_ref, low_ref, high_ref, key_ref, value_ref = refs[3 * CHUNKS : 3 * CHUNKS + 5]
    keep_ref, send_ref, sum_ref, scratch = refs[3 * CHUNKS + 5 :]
    count = token_ref.shape[0]
    part = count // CHUNKS
    scratch[...] = sum(
        dot_tn(token_ref[k * part : (k + 1) * part, :], ref[...])
        for k, ref in enumerate(query_refs)
    )
    spread_rows(block_ref, scratch, keep_ref, send_ref, 0, 4)
    for which, ref in ((1, key_ref), (2, value_ref)):
        scratch[...] = (
            dot_tn(token_ref[...], ref[MAXDOC : MAXDOC + count, :])
            + dot_tn(low_ref[...], ref[PAD:MAXDOC, :])
            + dot_tn(high_ref[...], ref[MAXDOC + count : MAXDOC + count + HALO, :])
        )
        spread_rows(block_ref, scratch, keep_ref, send_ref, which, 4)
    scratch[...] = sum(dot_tn(a[...], b[...]) for a, b in zip(branch_refs, attended_refs))
    spread_rows(block_ref, scratch, keep_ref, send_ref, 3, 4)
    total = start_ref[...]
    place = lax.broadcasted_iota(jnp.int32, total.shape, 0)
    query_sum = sum(
        jnp.sum(ref[...].astype(F32), 0, keepdims=True) for ref in query_refs
    )
    value_sum = jnp.sum(value_ref[...].astype(F32), 0, keepdims=True)
    total = total + jnp.where(place == 0, query_sum, 0.0) + jnp.where(place == 1, value_sum, 0.0)
    height = keep_ref.shape[0]
    high, low, sum_ref[...] = split_sums(total)
    send_ref[height : height + SUM_ROWS, :] = high
    send_ref[height + SUM_ROWS :, :] = low


def project_grads(blocks, sums, tokens, low, high, query, key, value, branch, attended):
    features = tokens.shape[1]
    width = key.shape[1]
    half = blocks.shape[0] // 2
    depth = features // (2 * half)
    height = half * 4 * depth
    operands = (sums, *query, *branch, *attended, tokens, low, high, key, value)
    return pl.pallas_call(
        project_grad_kernel,
        grid=(1,),
        in_specs=[pl.BlockSpec(memory_space=SMEM)] + [whole(x.shape) for x in operands],
        out_specs=[
            whole((height, width)),
            whole((height + 2 * SUM_ROWS, width)),
            whole(sums.shape),
        ],
        out_shape=[
            struct((height, width), F32),
            struct((height + 2 * SUM_ROWS, width), BF16),
            struct(sums.shape, F32),
        ],
        scratch_shapes=[pltpu.VMEM((features, width), F32)],
        compiler_params=params(),
        cost_estimate=lasting(0.6),
        name="project_grads",
    )(blocks, *operands)


def fold_kernel(with_sums, keep_ref, arrived_ref, *refs):
    height = keep_ref.shape[0]
    size = height // 2
    if with_sums:
        start_ref, keep_out, send_out, sum_out = refs
    else:
        keep_out, send_out = refs
    keep_out[...] = keep_ref[:size, :] + arrived_ref[:size, :].astype(F32)
    send_out[:size, :] = (keep_ref[size:, :] + arrived_ref[size:height, :].astype(F32)).astype(BF16)
    if with_sums:
        high, low, sum_out[...] = split_sums(start_ref[...] + arrived_sums(arrived_ref, height))
        send_out[size : size + SUM_ROWS, :] = high
        send_out[size + SUM_ROWS :, :] = low


def arrived_sums(ref, height):
    return ref[height : height + SUM_ROWS, :].astype(F32) + ref[height + SUM_ROWS :, :].astype(F32)


def fold(keep, arrived, sums):
    height, width = keep.shape
    extra = arrived.shape[0] - height
    operands = (keep, arrived) + (() if sums is None else (sums,))
    shapes = [struct((height // 2, width), F32), struct((height // 2 + extra, width), BF16)]
    shapes += [] if sums is None else [struct(sums.shape, F32)]
    result = pl.pallas_call(
        functools.partial(fold_kernel, sums is not None),
        grid=(1,),
        in_specs=[whole(x.shape) for x in operands],
        out_specs=[whole(x.shape) for x in shapes],
        out_shape=shapes,
        compiler_params=params(),
        cost_estimate=lasting(0.2),
        name="fold",
    )(*operands)
    return result[0], result[1], (None if sums is None else result[2])


def finish_kernel(kinds, sum_kinds, keep_ref, arrived_ref, *refs):
    height = keep_ref.shape[0]
    if sum_kinds:
        start_ref, *refs = refs
    first = 0
    for kind, ref in zip(kinds, refs):
        depth = ref.shape[-2]
        for place in range(kind or 1):
            rows_here = slice(first, first + depth)
            total = keep_ref[rows_here, :] + arrived_ref[rows_here, :].astype(F32)
            if kind:
                ref[place] = total
            else:
                ref[...] = total
            first += depth
    if sum_kinds:
        total = start_ref[...] + arrived_sums(arrived_ref, height)
        first = 0
        for kind, ref in zip(sum_kinds, refs[len(kinds) :]):
            if ref.shape[0] == kind:
                ref[...] = total[first : first + kind, :]
            else:
                ref[...] = jnp.concatenate([total[first + k : first + k + 1] for k in range(kind)], 1)
            first += kind


def finish(keep, arrived, sums, kinds, sum_kinds):
    height, width = keep.shape
    depth = height // sum(kind or 1 for kind in kinds)
    operands = (keep, arrived) + (() if sums is None else (sums,))
    shapes = [struct((kind, depth, width) if kind else (depth, width), F32) for kind in kinds]
    shapes += [
        struct((kind, width) if kind == 2 else (1, kind * width), F32) for kind in sum_kinds
    ]
    return pl.pallas_call(
        functools.partial(finish_kernel, kinds, sum_kinds),
        grid=(1,),
        in_specs=[whole(x.shape) for x in operands],
        out_specs=[whole(x.shape) for x in shapes],
        out_shape=shapes,
        compiler_params=params(),
        cost_estimate=lasting(0.2),
        name="finish",
    )(*operands)


def token_grad_kernel(even_ref, *refs):
    query_refs, res_refs = refs[:CHUNKS], refs[CHUNKS : 2 * CHUNKS]
    key_ref, value_ref, *weight_refs, own_ref, inside_ref, across_ref = refs[2 * CHUNKS :]
    count = own_ref.shape[0]
    own = res_refs[0].shape[1]
    even = even_ref[0] == 1

    def piece(start):
        return dot_nt(key_ref[start : start + BLOCK, :], weight_refs[1][...]) + dot_nt(
            value_ref[start : start + BLOCK, :], weight_refs[2][...]
        )

    for start in range(0, HALO, BLOCK):
        low = piece(PAD + start).astype(BF16)
        high = piece(MAXDOC + count + start).astype(BF16)
        inside_ref[start : start + BLOCK, :] = jnp.where(even, high, low)
        across_ref[start : start + BLOCK, :] = jnp.where(even, low, high)
    for start in range(0, count, BLOCK):
        chunk, inside = divmod(start, count // CHUNKS)
        total = piece(MAXDOC + start) + dot_nt(
            query_refs[chunk][inside : inside + BLOCK, :], weight_refs[0][...]
        )
        own_ref[start : start + BLOCK, :] = total
        own_ref[start : start + BLOCK, :own] += res_refs[chunk][inside : inside + BLOCK, :]


def token_grads(even, query, res, key, value, weights):
    count = CHUNKS * query[0].shape[0]
    features = weights[0].shape[0]
    operands = (*query, *res, key, value, *weights)
    shapes = [struct((count, features), F32)] + [struct((HALO, features), BF16)] * 2
    return pl.pallas_call(
        token_grad_kernel,
        grid=(1,),
        in_specs=[pl.BlockSpec(memory_space=SMEM)] + [whole(x.shape) for x in operands],
        out_specs=[whole(x.shape) for x in shapes],
        out_shape=shapes,
        compiler_params=params(),
        cost_estimate=lasting(0.6),
        name="token_grads",
    )(even, *operands)


def token_sum_kernel(even_ref, own_ref, inside_ref, across_ref, stays_ref, *leave_refs):
    even = even_ref[0] == 1
    width = stays_ref.shape[1]
    inside, across = inside_ref[...].astype(F32), across_ref[...].astype(F32)
    low, high = jnp.where(even, across, inside), jnp.where(even, inside, across)
    rest = own_ref.shape[0] - HALO
    for start in range(0, own_ref.shape[0], BLOCK):
        piece = own_ref[start : start + BLOCK, :]
        if start < HALO:
            piece = piece + low[start : start + BLOCK, :]
        if start >= rest:
            piece = piece + high[start - rest : start - rest + BLOCK, :]
        stays_ref[start : start + BLOCK, :] = piece[:, :width]
        for place, ref in enumerate(leave_refs, 1):
            ref[start : start + BLOCK, :] = piece[:, place * width : (place + 1) * width].astype(
                BF16
            )


def token_sum(even, own, inside, across, width):
    count, features = own.shape
    shapes = [struct((count, width), F32)]
    shapes += [struct((count, width), BF16)] * (features // width - 1)
    return pl.pallas_call(
        token_sum_kernel,
        grid=(1,),
        in_specs=[pl.BlockSpec(memory_space=SMEM)]
        + [whole(x.shape) for x in (own, inside, across)],
        out_specs=[whole(x.shape) for x in shapes],
        out_shape=shapes,
        compiler_params=params(),
        cost_estimate=lasting(0.3),
        name="token_sum",
    )(even, own, inside, across)


def from_next(x, axis, step):
    count = lax.axis_size(axis)
    return lax.ppermute(x, axis, [((i + step) % count, i) for i in range(count)])


def others(x):
    return [from_next(x, "col", step) for step in range(1, lax.axis_size("col"))]


def bits_of(count):
    return [1 << place for place in range(count.bit_length() - 1)]


def orders_of(count):
    high = bits_of(count)[:0:-1]
    return high + [1], high[2:] + high[:2] + [1]


def slots_of(order, distance):
    return sum(((distance & bit) // bit) << place for place, bit in enumerate(order))


def distances_of(order, slots):
    return sum(((slots >> place) & 1) * bit for place, bit in enumerate(order))


def with_partner(x, step):
    count = lax.axis_size("row")
    orders = orders_of(count)
    return lax.ppermute(x, "row", [(i, i ^ orders[i % 2][step]) for i in range(count)])


def with_next(inside, across):
    count = lax.axis_size("row")
    pairs = [(i, i + 1 if i % 2 else i - 1) for i in range(1, count - 1)]
    return (
        lax.ppermute(inside, "row", [(i, i ^ 1) for i in range(count)]),
        lax.ppermute(across, "row", pairs),
    )


def after(value, *needed):
    return lax.optimization_barrier((value, *needed))[0]


class Gather:
    def __init__(self, shard):
        self.held, self.step = shard[None], 0
        self.count = len(bits_of(lax.axis_size("row")))
        self.move()

    def move(self):
        self.arrived = with_partner(self.held, self.step)
        self.step += 1

    def put(self, *needed):
        self.held = jnp.concatenate([after(self.held, *needed), self.arrived], 0)
        self.move()


class Reduction:
    def __init__(self, keep, send, sums, kinds, sum_kinds=()):
        self.step = len(bits_of(lax.axis_size("row")))
        self.keep, self.send, self.sums = keep, send, sums
        self.kinds, self.sum_kinds = kinds, sum_kinds
        self.result = None
        self.move()

    def move(self):
        self.step -= 1
        self.arrived = with_partner(self.send, self.step)

    def add(self, *needed):
        keep = after(self.keep, *needed)
        if self.step == 0:
            self.result = finish(keep, self.arrived, self.sums, self.kinds, self.sum_kinds)
        else:
            self.keep, self.send, self.sums = fold(keep, self.arrived, self.sums)
            self.move()


def exchanged(part):
    arrived = others(part)
    if len(arrived) == 1:
        return arrived[0]
    shift = part.shape[1] // (len(arrived) + 1)
    total = sum(
        jnp.roll(x.astype(F32), step * shift, 1) for step, x in enumerate(arrived, 1)
    )
    return total.astype(BF16)


def on_device(
    tokens,
    prev_logits,
    doc_lengths,
    qkv_weight,
    qv_bias,
    out_weight,
    out_bias,
    up_weight,
    up_bias,
    down_weight,
    norm_gain,
    norm_shift,
    out_grad,
    logit_grad,
):
    count, own = tokens.shape
    width = qkv_weight.shape[2]
    row_count, col_count = lax.axis_size("row"), lax.axis_size("col")
    row_index, col_index = lax.axis_index("row"), lax.axis_index("col")
    token_count = count * row_count
    swap = col_count == 2
    hidden_rows = up_bias.shape[0] // own

    odd = row_index % 2 == 1
    places = jnp.arange(row_count, dtype=jnp.int32)
    offset = col_index * (row_count // col_count)
    distance = ((places + offset) % row_count) ^ row_index
    half = row_count // 2
    even_order, odd_order = (order[:-1] for order in orders_of(row_count))
    turned = odd ^ (distance % 2 == 1)
    slots = jnp.where(turned, slots_of(odd_order, distance), slots_of(even_order, distance))
    slots = slots + half * (distance % 2)
    turned = odd ^ (places >= half)
    met = jnp.where(turned, distances_of(odd_order, places), distances_of(even_order, places))
    blocks = (((met + (places >= half)) ^ row_index) - offset) % row_count
    base = (row_index * count)[None]

    even = 1 - row_index % 2
    even = even.astype(jnp.int32)[None]

    def dense_of(banded, fill, chunk, *needed):
        dense = to_dense(after(banded, *needed), doc_lengths, base, fill, token_count, chunk)
        return dense

    prev_logits = pltpu.with_memory_space_constraint(prev_logits, pltpu.HBM)
    logit_grad = pltpu.with_memory_space_constraint(logit_grad, pltpu.HBM)

    out_turned = out_weight.T
    out_other = others(out_turned)
    qkv_rows = Gather(qkv_weight)
    tokens_full, inside, across = join(even, [tokens] + others(after(tokens, out_turned)))
    feed_rows = Gather(jnp.concatenate([out_turned, *out_other, up_weight, down_weight.T], 1))
    qkv_rows.put()
    norms = jnp.concatenate([norm_gain, norm_shift, out_bias], 0)
    grad_full = jnp.concatenate([out_grad] + others(out_grad), 1)
    prev_dense = [dense_of(prev_logits, MASKED_SCORE, 0, qkv_rows.held, grad_full)]
    inside, across = with_next(inside, across)
    qkv_rows.put(prev_dense[0])
    feed_rows.put(prev_dense[0])
    prev_dense.append(
        dense_of(prev_logits, MASKED_SCORE, 1, qkv_rows.held, feed_rows.held, tokens_full)
    )
    while qkv_rows.step < qkv_rows.count:
        qkv_rows.put(prev_dense[1], inside, across)
    feed_rows.put(qkv_rows.held)
    query, key, value, low_tokens, high_tokens, *projections = project(
        slots, even, after(tokens_full, feed_rows.held), inside, across, qkv_rows.held,
        qkv_rows.arrived, qv_bias,
    )
    scores, probs, attended, attended_other = [], [], [], []
    for chunk in range(CHUNKS):
        score, prob, mix = attend_forward(query, key, value, prev_dense[chunk], chunk)
        query = after(query, mix)
        scores.append(score)
        probs.append(prob)
        attended.append(mix)
        attended_other.append(jnp.concatenate(others(mix), 1))
    norms = jnp.concatenate([norms] + others(after(norms, mix)), 1)
    feed_rows.put(mix, attended_other[0])
    while feed_rows.step < feed_rows.count:
        feed_rows.put()
    new_logits = to_band([after(scores[0], feed_rows.held), *scores[1:]], True)
    other_out, *weights = in_order(
        slots, after(feed_rows.held, new_logits), feed_rows.arrived,
        (width, (col_count - 1) * width, up_weight.shape[1], up_weight.shape[1]),
    )
    weights[0], other_out = other_out, weights[0]
    ups = up_bias[None]
    firsts = []
    for chunk in range(CHUNKS):
        result = feed_first(
            attended[chunk], attended_other[chunk], tokens_full, other_out, weights, norms, ups,
            chunk,
        )
        ups = after(ups, result[-1])
        firsts.append((*result, exchanged(result[-1])))
    normed, inverse, upper, act, slope, down_part, down_other = zip(*firsts)

    logit_dense = [dense_of(logit_grad, 0.0, 0, down_part[-1])]
    sums = after(jnp.zeros((SUM_ROWS, own), F32), logit_dense[0])
    output = None
    seconds = []
    for chunk in range(CHUNKS):
        sums, output, *result = feed_second(
            swap, sums, output, down_part[chunk], down_other[chunk],
            normed[chunk], grad_full, slope[chunk], weights, norms, chunk,
        )
        seconds.append((*result, exchanged(result[-1])))
    res_two, ffn_low, hidden_grad, lower_part, lower_other = zip(*seconds)
    keep, send = feed_grads(blocks, ffn_low, act, upper, hidden_grad)
    feed_sum = Reduction(keep, send, None, (0, 0))
    sums = after(sums, keep)

    branch_low, res_one, query_grad, prev_dense_grad = [], [], [], []
    partial = None
    for chunk in range(CHUNKS):
        sums, low, attended_grad, res = feed_third(
            swap, sums, width, lower_part[chunk], lower_other[chunk], res_two[chunk],
            normed[chunk], inverse[chunk], weights, norms,
        )
        branch_low.append(low)
        res_one.append(res)
        prev, query_part, *partial = attend_backward(
            attended_grad, query, key, value, probs[chunk], logit_dense[chunk], chunk, partial
        )
        if chunk == 0:
            feed_sum.add(query_part)
            logit_dense.append(dense_of(logit_grad, 0.0, 1, feed_sum.keep))
            sums = after(sums, logit_dense[1])
        prev_dense_grad.append(prev)
        query_grad.append(query_part)
    key_grad, value_grad = partial
    feed_sum.add(query_grad[-1])
    keep, send, sums = project_grads(
        blocks, after(sums, feed_sum.keep), tokens_full, low_tokens, high_tokens, query_grad,
        key_grad, value_grad, branch_low, attended,
    )
    last_sum = Reduction(keep, send, sums, (3, 0), (2, 2, 2, 2, hidden_rows))
    center, inside, across = token_grads(
        even, query_grad, res_one, after(key_grad, keep), value_grad, projections
    )
    last_sum.add(center)
    inside, across = with_next(after(inside, last_sum.keep), across)
    prev_dense_grad[0] = after(prev_dense_grad[0], last_sum.keep)
    prev_grad = to_band(prev_dense_grad, False)
    last_sum.add(prev_grad)
    feed_sum.add(last_sum.keep)
    tokens_grad, *parts = token_sum(even, after(center, feed_sum.keep), inside, across, own)
    for step, part in enumerate(parts, 1):
        tokens_grad = tokens_grad + from_next(part, "col", -step).astype(F32)
    last_sum.add(parts[0])
    while feed_sum.result is None:
        feed_sum.add(last_sum.keep)
    while last_sum.result is None:
        last_sum.add(feed_sum.result[0])
    qkv_grad, out_grad_rows, qv_sum, bias_sum, gain_sum, shift_sum, hidden_sum = last_sum.result
    up_grad, down_grad = feed_sum.result
    return (
        output,
        new_logits,
        tokens_grad.astype(BF16),
        prev_grad,
        qkv_grad,
        qv_sum,
        out_grad_rows.T,
        bias_sum,
        up_grad,
        hidden_sum.reshape(-1),
        down_grad.T,
        gain_sum,
        shift_sum,
    )


def solution(mesh):
    return jax.shard_map(
        on_device,
        mesh=mesh,
        in_specs=(
            P("row", "col"),
            P("col", "row", None),
            P(),
            P(None, "row", "col"),
            P(None, "col"),
            P("col", "row"),
            P(None, "col"),
            P("row", "col"),
            P("col"),
            P("col", "row"),
            P(None, "col"),
            P(None, "col"),
            P("row", "col"),
            P("col", "row", None),
        ),
        out_specs=(
            P("row", "col"),
            P("col", "row", None),
            P("row", "col"),
            P("col", "row", None),
            P(None, "row", "col"),
            P(None, "col"),
            P("col", "row"),
            P(None, "col"),
            P("row", "col"),
            P("col"),
            P("col", "row"),
            P(None, "col"),
            P(None, "col"),
        ),
        check_vma=False,
    )
```

```python
import functools

import jax
import jax.numpy as jnp
from jax import lax
from jax.experimental import pallas as pl
from jax.experimental.pallas import tpu as pltpu
from jax.sharding import PartitionSpec as P

D = 512
HEAD_DIM = 64
MAXDOC = 512
BAND = 2 * MAXDOC
BLOCK = 128
WINDOW = BAND + BLOCK
HALO = MAXDOC - 128
PAD = MAXDOC - HALO

EPSILON = 1e-05
MASKED_SCORE = -1e30
ERF_RATE = 0.7071067811865476
DENSITY_RATE = 0.3989422804014327

F32 = jnp.float32
BF16 = jnp.bfloat16
SMEM = pltpu.MemorySpace.SMEM
VMEM_LIMIT = 24 << 20
CHUNKS = 2
SUM_ROWS = 16
FLOPS_PER_MICROSECOND = 1.0e9


def dot_nn(a, b):
    return lax.dot_general(a, b, (((1,), (0,)), ((), ())), preferred_element_type=F32)


def dot_nt(a, b):
    return lax.dot_general(a, b, (((1,), (1,)), ((), ())), preferred_element_type=F32)


def dot_tn(a, b):
    return lax.dot_general(a, b, (((0,), (0,)), ((), ())), preferred_element_type=F32)


def params():
    return pltpu.CompilerParams(
        dimension_semantics=("arbitrary",), vmem_limit_bytes=VMEM_LIMIT
    )


def lasting(microseconds):
    return pl.CostEstimate(
        flops=int(microseconds * FLOPS_PER_MICROSECOND), bytes_accessed=0, transcendentals=0
    )


def whole(shape):
    return pl.BlockSpec(shape, lambda b: (0,) * len(shape))


def rows(width, first=0):
    return pl.BlockSpec((BLOCK, width), lambda b: (b + first, 0))


def heads_block(heads, width, first=0):
    return pl.BlockSpec((heads, BLOCK, width), lambda b: (0, b + first, 0))


def struct(shape, dtype):
    return jax.ShapeDtypeStruct(shape, dtype)


def segment_of(positions, lengths_ref, documents, token_count):
    found = jnp.zeros(positions.shape, jnp.int32)
    end = jnp.int32(0)
    for document in range(documents):
        end = end + lengths_ref[document]
        found = found + (positions >= end).astype(jnp.int32)
    return jnp.where((positions >= 0) & (positions < token_count), found, -1)


def dense_kernel(fill, token_count, offset, lengths_ref, band_ref, dense_ref):
    documents = lengths_ref.shape[0] - 1
    first = lengths_ref[documents] + (pl.program_id(0) + offset) * BLOCK
    query = first + lax.broadcasted_iota(jnp.int32, (BLOCK, 1), 0)
    key = first - MAXDOC + lax.broadcasted_iota(jnp.int32, (1, WINDOW), 1)
    same = segment_of(query, lengths_ref, documents, token_count) == segment_of(
        key, lengths_ref, documents, token_count
    )
    for head in range(band_ref.shape[0]):
        wide = jnp.concatenate(
            [band_ref[head].astype(F32), jnp.zeros((BLOCK, BLOCK), F32)], 1
        )
        turned = pltpu.roll(wide, 0, 1, stride=1, stride_axis=0)
        dense_ref[head] = jnp.where(same, turned, fill).astype(BF16)


def to_dense(banded, lengths, fill, token_count, chunk):
    heads, count, _ = banded.shape
    count //= CHUNKS
    offset = chunk * (count // BLOCK)
    return pl.pallas_call(
        functools.partial(dense_kernel, fill, token_count, offset),
        grid=(count // BLOCK,),
        in_specs=[pl.BlockSpec(memory_space=SMEM), heads_block(heads, BAND, offset)],
        out_specs=heads_block(heads, WINDOW),
        out_shape=struct((heads, count, WINDOW), BF16),
        compiler_params=params(),
        cost_estimate=lasting(8.0 if fill and chunk == 0 else 1.0),
        name="to_dense",
    )(lengths, banded)


def band_kernel(masked, *refs):
    dense_refs, band_ref = refs[:-1], refs[-1]
    lane = lax.broadcasted_iota(jnp.int32, (BLOCK, BLOCK), 1)
    row = lax.broadcasted_iota(jnp.int32, (BLOCK, BLOCK), 0)
    source = (lane + row) & (BLOCK - 1)
    near = lane + row < BLOCK
    steps = pl.num_programs(0) // CHUNKS

    def turn(dense_ref):
        for head in range(band_ref.shape[0]):
            pieces = []
            for place in range(WINDOW // BLOCK):
                piece = dense_ref[head, :, place * BLOCK : (place + 1) * BLOCK].astype(F32)
                if masked:
                    piece = jnp.where(piece < 0.5 * MASKED_SCORE, 0.0, piece)
                pieces.append(jnp.take_along_axis(piece, source, axis=1))
            for place in range(BAND // BLOCK):
                band_ref[head, :, place * BLOCK : (place + 1) * BLOCK] = jnp.where(
                    near, pieces[place], pieces[place + 1]
                ).astype(BF16)

    for chunk, dense_ref in enumerate(dense_refs):

        @pl.when(pl.program_id(0) // steps == chunk)
        def _():
            turn(dense_ref)


def to_band(chunks, masked):
    heads, count, _ = chunks[0].shape
    steps = count // BLOCK

    def block_of(chunk):
        return pl.BlockSpec(
            (heads, BLOCK, WINDOW), lambda b: (0, jnp.clip(b - chunk * steps, 0, steps - 1), 0)
        )

    return pl.pallas_call(
        functools.partial(band_kernel, masked),
        grid=(CHUNKS * steps,),
        in_specs=[block_of(chunk) for chunk in range(CHUNKS)],
        out_specs=heads_block(heads, BAND),
        out_shape=struct((heads, CHUNKS * count, BAND), BF16),
        compiler_params=params(),
        cost_estimate=lasting(5.0 if masked else 0.5),
        name="to_band",
    )(*chunks)


def head_split(block, size):
    if size == 1:
        return block
    lane = lax.broadcasted_iota(jnp.int32, block.shape, 1)
    return jnp.concatenate(
        [
            jnp.where((lane >= h * HEAD_DIM) & (lane < (h + 1) * HEAD_DIM), block, 0)
            for h in range(size)
        ],
        0,
    )


def head_join(stacked, size):
    if size == 1:
        return stacked
    height = stacked.shape[0] // size
    joined = stacked[:height]
    lane = lax.broadcasted_iota(jnp.int32, joined.shape, 1)
    for h in range(1, size):
        joined = jnp.where(lane >= h * HEAD_DIM, stacked[h * height : (h + 1) * height], joined)
    return joined


def join_kernel(even_ref, *refs):
    *part_refs, all_ref, inside_ref, across_ref = refs
    count = all_ref.shape[0]
    width = part_refs[0].shape[1]
    even = even_ref[0] == 1
    for place, ref in enumerate(part_refs):
        lanes = slice(place * width, (place + 1) * width)
        all_ref[:, lanes] = ref[...]
        tail, head = ref[count - HALO :, :], ref[:HALO, :]
        inside_ref[:, lanes] = jnp.where(even, tail, head)
        across_ref[:, lanes] = jnp.where(even, head, tail)


def join(even, parts):
    count, width = parts[0].shape
    features = len(parts) * width
    shapes = ((count, features), (HALO, features), (HALO, features))
    return pl.pallas_call(
        join_kernel,
        grid=(1,),
        in_specs=[pl.BlockSpec(memory_space=SMEM)] + [whole(x.shape) for x in parts],
        out_specs=[whole(shape) for shape in shapes],
        out_shape=[struct(shape, BF16) for shape in shapes],
        compiler_params=params(),
        cost_estimate=lasting(0.5),
        name="join",
    )(even, *parts)


def project_kernel(
    slot_ref, even_ref, token_ref, inside_ref, across_ref, near_ref, far_ref, bias_ref,
    query_ref, key_ref, value_ref, low_ref, high_ref, *weight_refs,
):
    half, _, depth, _ = near_ref.shape
    count = token_ref.shape[0]

    def put(place, source_ref, slot):
        for which, ref in enumerate(weight_refs):
            ref[place * depth : (place + 1) * depth, :] = source_ref[slot, which]

    for place in range(2 * half):
        slot = slot_ref[place]

        @pl.when(slot < half)
        def _():
            put(place, near_ref, slot)

        @pl.when(slot >= half)
        def _():
            put(place, far_ref, slot - half)

    even = even_ref[0] == 1
    inside, across = inside_ref[...], across_ref[...]
    low_rows, high_rows = jnp.where(even, across, inside), jnp.where(even, inside, across)
    low_ref[...] = low_rows
    high_ref[...] = high_rows
    own = token_ref[...]
    query = (dot_nn(own, weight_refs[0][...]) + bias_ref[0:1, :]).astype(BF16)
    empty = jnp.zeros((PAD, query.shape[1]), BF16)
    query_ref[...] = query * jnp.asarray(HEAD_DIM ** (-0.5), BF16)
    for out_ref, which in ((key_ref, 1), (value_ref, 2)):
        shift = bias_ref[1:2, :] if which == 2 else 0.0
        weight = weight_refs[which][...]
        out_ref[0:PAD, :] = empty
        out_ref[PAD:MAXDOC, :] = (dot_nn(low_rows, weight) + shift).astype(BF16)
        out_ref[MAXDOC : MAXDOC + count, :] = (dot_nn(own, weight) + shift).astype(BF16)
        out_ref[MAXDOC + count : MAXDOC + count + HALO, :] = (
            dot_nn(high_rows, weight) + shift
        ).astype(BF16)
        out_ref[MAXDOC + count + HALO :, :] = empty


def project(slots, even, tokens, inside, across, near, far, bias):
    count, features = tokens.shape
    width = near.shape[3]
    operands = (tokens, inside, across, near, far, bias)
    extended = (count + BAND, width)
    shapes = [(count, width), extended, extended, inside.shape, across.shape]
    shapes += [(features, width)] * 3
    return pl.pallas_call(
        project_kernel,
        grid=(1,),
        in_specs=[pl.BlockSpec(memory_space=SMEM)] * 2 + [whole(x.shape) for x in operands],
        out_specs=[whole(shape) for shape in shapes],
        out_shape=[struct(shape, BF16) for shape in shapes],
        compiler_params=params(),
        cost_estimate=lasting(2.0),
        name="project",
    )(slots, even, *operands)


def forward_kernel(
    offset, query_ref, key_ref, value_ref, prev_ref, score_ref, prob_ref, attended_ref
):
    heads = prev_ref.shape[0]
    size = min(2, heads)
    span = size * HEAD_DIM
    window = pl.ds(pl.multiple_of((pl.program_id(0) + offset) * BLOCK, BLOCK), WINDOW)
    for group in range(heads // size):
        lanes = slice(group * span, (group + 1) * span)
        query = head_split(query_ref[:, lanes], size)
        dense = dot_nt(query, key_ref[window, lanes])
        weights = []
        for h in range(size):
            head = group * size + h
            score = dense[h * BLOCK : (h + 1) * BLOCK] + prev_ref[head].astype(F32)
            score_ref[head] = score.astype(BF16)
            peak = jnp.max(score, -1, keepdims=True)
            grown = jnp.exp(score - peak)
            total = jnp.sum(grown, -1, keepdims=True)
            prob = (grown * (1.0 / total)).astype(BF16)
            prob_ref[head] = prob
            weights.append(prob)
        mixed = dot_nn(jnp.concatenate(weights, 0), value_ref[window, lanes])
        attended_ref[:, lanes] = head_join(mixed, size).astype(BF16)


def attend_forward(query, key, value, prev, chunk):
    heads, count, _ = prev.shape
    width = query.shape[1]
    offset = chunk * (count // BLOCK)
    return pl.pallas_call(
        functools.partial(forward_kernel, offset),
        grid=(count // BLOCK,),
        in_specs=[
            rows(width, offset),
            whole(key.shape),
            whole(value.shape),
            heads_block(heads, WINDOW),
        ],
        out_specs=[heads_block(heads, WINDOW), heads_block(heads, WINDOW), rows(width)],
        out_shape=[
            struct((heads, count, WINDOW), BF16),
            struct((heads, count, WINDOW), BF16),
            struct((count, width), BF16),
        ],
        compiler_params=params(),
        cost_estimate=lasting(3.8),
        name="attend_forward",
    )(query, key, value, prev)


def backward_kernel(
    offset, last, grad_ref, query_ref, key_ref, value_ref, prob_ref, logit_ref, *refs
):
    if last:
        key_start, value_start = refs[:2]
        prev_ref, query_grad_ref, key_grad_ref, value_grad_ref, key_sum, value_sum = refs[2:]
    else:
        prev_ref, query_grad_ref, key_sum, value_sum = refs
    step = pl.program_id(0)
    heads = prob_ref.shape[0]
    size = min(2, heads)
    span = size * HEAD_DIM

    @pl.when(step == 0)
    def _():
        if last:
            key_sum[...] = key_start[...]
            value_sum[...] = value_start[...]
        else:
            key_sum[...] = jnp.zeros_like(key_sum)
            value_sum[...] = jnp.zeros_like(value_sum)

    window = pl.ds(pl.multiple_of((step + offset) * BLOCK, BLOCK), WINDOW)
    for group in range(heads // size):
        lanes = slice(group * span, (group + 1) * span)
        query = head_split(query_ref[:, lanes], size)
        grad = head_split(grad_ref[:, lanes], size)
        key = key_ref[window, lanes]
        prob_grad = dot_nt(grad, value_ref[window, lanes])
        probs, scores = [], []
        for h in range(size):
            head = group * size + h
            low = prob_ref[head]
            prob = low.astype(F32)
            slope = prob_grad[h * BLOCK : (h + 1) * BLOCK]
            inner = jnp.sum(prob * slope, -1, keepdims=True)
            score = (prob * (slope - inner) + logit_ref[head].astype(F32)).astype(BF16)
            prev_ref[head] = score
            probs.append(low)
            scores.append(score)
        stacked = jnp.concatenate(scores, 0)
        mixed = head_join(dot_nn(stacked, key), size) * HEAD_DIM ** (-0.5)
        query_grad_ref[:, lanes] = mixed.astype(BF16)
        key_sum[lanes, window] += dot_tn(query, stacked)
        value_sum[lanes, window] += dot_tn(grad, jnp.concatenate(probs, 0))

    if last:

        @pl.when(step == pl.num_programs(0) - 1)
        def _():
            key_grad_ref[...] = key_sum[...].astype(BF16).T
            value_grad_ref[...] = value_sum[...].astype(BF16).T


def attend_backward(grad, query, key, value, prob, logit, chunk, sums):
    heads, count, _ = prob.shape
    extended, width = key.shape
    offset = chunk * (count // BLOCK)
    last = sums is not None
    turned = (width, extended)
    scratch = [pltpu.VMEM(turned, F32), pltpu.VMEM(turned, F32)] if last else []
    ends = [whole((extended, width))] * 2 if last else [whole(turned)] * 2
    end_shapes = [struct((extended, width), BF16)] * 2 if last else [struct(turned, F32)] * 2
    return pl.pallas_call(
        functools.partial(backward_kernel, offset, last),
        grid=(count // BLOCK,),
        in_specs=[
            rows(width),
            rows(width, offset),
            whole((extended, width)),
            whole((extended, width)),
            heads_block(heads, WINDOW),
            heads_block(heads, WINDOW),
        ]
        + ([whole(turned)] * 2 if last else []),
        out_specs=[heads_block(heads, WINDOW), rows(width)] + ends,
        out_shape=[struct((heads, count, WINDOW), BF16), struct((count, width), BF16)]
        + end_shapes,
        scratch_shapes=scratch,
        compiler_params=params(),
        cost_estimate=lasting(3.0 if last else 20.0),
        name="attend_backward",
    )(grad, query, key, value, prob, logit, *(sums or ()))


def order_kernel(slot_ref, near_ref, far_ref, *out_refs):
    half, depth, _ = near_ref.shape

    def put(place, source_ref, slot):
        first = 0
        for out_ref in out_refs:
            last = first + out_ref.shape[1]
            out_ref[place * depth : (place + 1) * depth, :] = source_ref[slot, :, first:last]
            first = last

    for place in range(2 * half):
        slot = slot_ref[place]

        @pl.when(slot < half)
        def _():
            put(place, near_ref, slot)

        @pl.when(slot >= half)
        def _():
            put(place, far_ref, slot - half)


def in_order(slots, near, far, widths):
    half, depth, _ = near.shape
    shapes = [(2 * half * depth, width) for width in widths]
    return pl.pallas_call(
        order_kernel,
        grid=(1,),
        in_specs=[pl.BlockSpec(memory_space=SMEM), whole(near.shape), whole(far.shape)],
        out_specs=[whole(shape) for shape in shapes],
        out_shape=[struct(shape, BF16) for shape in shapes],
        compiler_params=params(),
        cost_estimate=lasting(0.9),
        name="in_order",
    )(slots, near, far)


def mean_of(x):
    return jnp.sum(x, -1, keepdims=True) * (1.0 / D)


def normalized(hidden):
    mean = mean_of(hidden)
    inverse = lax.rsqrt(mean_of(hidden * hidden) - mean * mean + EPSILON)
    return (hidden - mean) * inverse, inverse


def norm_back(upstream, normed, inverse):
    return inverse * (upstream - mean_of(upstream) - normed * mean_of(upstream * normed))


def added(own_ref, other_ref, swap):
    other = other_ref[...]
    if swap:
        middle = other.shape[1] // 2
        other = jnp.concatenate([other[:, middle:], other[:, :middle]], 1)
    return own_ref[...].astype(F32) + other.astype(F32)


def first_kernel(
    own_ref, other_ref, token_ref, other_out_ref, out_ref, up_ref, down_ref, norm_ref,
    up_bias_ref, normed_ref, inverse_ref, upper_ref, act_ref, slope_ref, part_ref,
):
    branch = dot_nt(own_ref[...], out_ref[...]) + dot_nt(other_ref[...], other_out_ref[...])
    hidden = token_ref[...].astype(F32) + branch + norm_ref[4:5, :]
    normed, inverse = normalized(hidden)
    normed_ref[...] = normed
    inverse_ref[...] = inverse
    upper = (normed * norm_ref[0:1, :] + norm_ref[2:3, :]).astype(BF16)
    upper_ref[...] = upper
    pre = dot_nn(upper, up_ref[...]) + up_bias_ref[...]
    share = 0.5 * (1.0 + lax.erf(pre * ERF_RATE))
    act = (pre * share).astype(BF16)
    act_ref[...] = act
    slope_ref[...] = (share + pre * jnp.exp(-0.5 * pre * pre) * DENSITY_RATE).astype(BF16)
    part_ref[...] = dot_nt(act, down_ref[...]).astype(BF16)


def feed_first(own, other, tokens, other_out, weights, norms, up_bias, chunk):
    count, width = own.shape
    features = tokens.shape[1]
    units = up_bias.shape[1]
    return pl.pallas_call(
        first_kernel,
        grid=(count // BLOCK,),
        in_specs=[
            rows(width),
            rows(other.shape[1]),
            rows(features, chunk * (count // BLOCK)),
            whole(other_out.shape),
            *(whole(x.shape) for x in weights),
            whole(norms.shape),
            whole(up_bias.shape),
        ],
        out_specs=[
            rows(features),
            rows(1),
            rows(features),
            rows(units),
            rows(units),
            rows(features),
        ],
        out_shape=[
            struct((count, features), F32),
            struct((count, 1), F32),
            struct((count, features), BF16),
            struct((count, units), BF16),
            struct((count, units), BF16),
            struct((count, features), BF16),
        ],
        compiler_params=params(),
        cost_estimate=lasting(1.0),
        name="feed_first",
    )(own, other, tokens, other_out, *weights, norms, up_bias)


def add_sums(start_ref, sum_ref, first, values):
    @pl.when(pl.program_id(0) == 0)
    def _():
        sum_ref[...] = start_ref[...]

    for place, value in enumerate(values):
        sum_ref[first + place : first + place + 1, :] += jnp.sum(value, 0, keepdims=True)


def second_kernel(
    swap, start_ref, part_ref, recv_ref, normed_ref, grad_ref, slope_ref, up_ref, down_ref,
    norm_ref, *refs,
):
    sum_ref, output_ref, res_ref, low_ref, hidden_ref, lower_ref = refs[-6:]
    own = output_ref.shape[1]
    upper = normed_ref[...] * norm_ref[0:1, :] + norm_ref[2:3, :]
    hidden = upper + added(part_ref, recv_ref, swap) + norm_ref[5:6, :]
    normed, inverse = normalized(hidden)
    output_ref[...] = (
        normed[:, :own] * norm_ref[1:2, :own] + norm_ref[3:4, :own]
    ).astype(BF16)
    grad = grad_ref[...].astype(F32)
    res = norm_back(grad * norm_ref[1:2, :], normed, inverse)
    res_ref[...] = res
    low = res.astype(BF16)
    low_ref[...] = low
    act_grad = dot_nn(low, down_ref[...])
    hidden_grad = (act_grad * slope_ref[...].astype(F32)).astype(BF16)
    hidden_ref[...] = hidden_grad
    lower_ref[...] = dot_nt(hidden_grad, up_ref[...]).astype(BF16)
    wide = hidden_grad.astype(F32)
    add_sums(start_ref, sum_ref, 3, [low[:, :own].astype(F32)])
    for place, value in (
        (5, grad[:, :own] * normed[:, :own]),
        (7, grad[:, :own]),
        *((8 + k, wide[:, k * own : (k + 1) * own]) for k in range(wide.shape[1] // own)),
    ):
        sum_ref[place : place + 1, :] += jnp.sum(value, 0, keepdims=True)


def feed_second(swap, sums, held, part, recv, normed, grad, slope, weights, norms, chunk):
    count, features = part.shape
    own = sums.shape[1]
    units = slope.shape[1]
    offset = chunk * (count // BLOCK)
    return pl.pallas_call(
        functools.partial(second_kernel, swap),
        grid=(count // BLOCK,),
        in_specs=[
            whole(sums.shape),
            rows(features),
            rows(features),
            rows(features),
            rows(features, offset),
            rows(units),
            *(whole(x.shape) for x in weights[1:]),
            whole(norms.shape),
            *([] if held is None else [pl.BlockSpec(memory_space=pl.ANY)]),
        ],
        out_specs=[
            whole(sums.shape),
            rows(own, offset),
            rows(features),
            rows(features),
            rows(units),
            rows(features),
        ],
        out_shape=[
            struct(sums.shape, F32),
            struct((CHUNKS * count, own), BF16),
            struct((count, features), F32),
            struct((count, features), BF16),
            struct((count, units), BF16),
            struct((count, features), BF16),
        ],
        input_output_aliases={} if held is None else {9: 1},
        compiler_params=params(),
        cost_estimate=lasting(0.7),
        name="feed_second",
    )(sums, part, recv, normed, grad, slope, *weights[1:], norms, *(() if held is None else (held,)))


def third_kernel(
    swap, start_ref, part_ref, recv_ref, res_ref, normed_ref, inverse_ref, out_ref, norm_ref,
    sum_ref, low_ref, attended_ref, own_ref,
):
    own = own_ref.shape[1]
    grad = added(part_ref, recv_ref, swap) + res_ref[...]
    normed = normed_ref[...]
    res = norm_back(grad * norm_ref[0:1, :], normed, inverse_ref[...])
    own_ref[...] = res[:, :own]
    low = res.astype(BF16)
    low_ref[...] = low
    attended_ref[...] = dot_nn(low, out_ref[...]).astype(BF16)
    add_sums(start_ref, sum_ref, 2, [low[:, :own].astype(F32)])
    for place, value in ((4, grad[:, :own] * normed[:, :own]), (6, grad[:, :own])):
        sum_ref[place : place + 1, :] += jnp.sum(value, 0, keepdims=True)


def feed_third(swap, sums, width, part, recv, res, normed, inverse, weights, norms):
    count, features = part.shape
    own = sums.shape[1]
    return pl.pallas_call(
        functools.partial(third_kernel, swap),
        grid=(count // BLOCK,),
        in_specs=[
            whole(sums.shape),
            rows(features),
            rows(features),
            rows(features),
            rows(features),
            rows(1),
            whole(weights[0].shape),
            whole(norms.shape),
        ],
        out_specs=[whole(sums.shape), rows(features), rows(width), rows(own)],
        out_shape=[
            struct(sums.shape, F32),
            struct((count, features), BF16),
            struct((count, width), BF16),
            struct((count, own), F32),
        ],
        compiler_params=params(),
        cost_estimate=lasting(0.2),
        name="feed_third",
    )(sums, part, recv, res, normed, inverse, weights[0], norms)


def spread_rows(block_ref, scratch, keep_ref, send_ref, which, kinds):
    features = scratch.shape[0]
    count = block_ref.shape[0]
    depth = features // count
    half = count // 2
    for slot in range(count):
        start = pl.multiple_of(block_ref[slot] * depth, depth)
        piece = scratch[pl.ds(start, depth), :]
        first = ((slot % half) * kinds + which) * depth
        if slot < half:
            keep_ref[first : first + depth, :] = piece
        else:
            send_ref[first : first + depth, :] = piece.astype(BF16)


def split_sums(total):
    high = total.astype(BF16)
    low = (total - high.astype(F32)).astype(BF16)
    return high, low, high.astype(F32) + low.astype(F32)


def feed_grad_kernel(block_ref, *refs):
    low_refs, upper_refs, act_refs, hidden_refs = (
        refs[k * CHUNKS : (k + 1) * CHUNKS] for k in range(4)
    )
    keep_ref, send_ref, scratch = refs[4 * CHUNKS :]
    scratch[...] = sum(dot_tn(a[...], b[...]) for a, b in zip(upper_refs, hidden_refs))
    spread_rows(block_ref, scratch, keep_ref, send_ref, 0, 2)
    scratch[...] = sum(dot_tn(a[...], b[...]) for a, b in zip(low_refs, act_refs))
    spread_rows(block_ref, scratch, keep_ref, send_ref, 1, 2)


def feed_grads(blocks, low, act, upper, hidden):
    count, features = low[0].shape
    units = act[0].shape[1]
    chunk = min(256, units)
    column = pl.BlockSpec((count, chunk), lambda b: (0, b))
    result = pl.BlockSpec((features, chunk), lambda b: (0, b))
    return pl.pallas_call(
        feed_grad_kernel,
        grid=(units // chunk,),
        in_specs=[pl.BlockSpec(memory_space=SMEM)]
        + [whole((count, features))] * (2 * CHUNKS)
        + [column] * (2 * CHUNKS),
        out_specs=[result] * 2,
        out_shape=[struct((features, units), F32), struct((features, units), BF16)],
        scratch_shapes=[pltpu.VMEM((features, chunk), F32)],
        compiler_params=params(),
        cost_estimate=lasting(1.0),
        name="feed_grads",
    )(blocks, *low, *upper, *act, *hidden)


def project_grad_kernel(block_ref, start_ref, *refs):
    query_refs, branch_refs, attended_refs = (
        refs[k * CHUNKS : (k + 1) * CHUNKS] for k in range(3)
    )
    token_ref, low_ref, high_ref, key_ref, value_ref = refs[3 * CHUNKS : 3 * CHUNKS + 5]
    keep_ref, send_ref, sum_ref, scratch = refs[3 * CHUNKS + 5 :]
    count = token_ref.shape[0]
    part = count // CHUNKS
    scratch[...] = sum(
        dot_tn(token_ref[k * part : (k + 1) * part, :], ref[...])
        for k, ref in enumerate(query_refs)
    )
    spread_rows(block_ref, scratch, keep_ref, send_ref, 0, 4)
    for which, ref in ((1, key_ref), (2, value_ref)):
        scratch[...] = (
            dot_tn(token_ref[...], ref[MAXDOC : MAXDOC + count, :])
            + dot_tn(low_ref[...], ref[PAD:MAXDOC, :])
            + dot_tn(high_ref[...], ref[MAXDOC + count : MAXDOC + count + HALO, :])
        )
        spread_rows(block_ref, scratch, keep_ref, send_ref, which, 4)
    scratch[...] = sum(dot_tn(a[...], b[...]) for a, b in zip(branch_refs, attended_refs))
    spread_rows(block_ref, scratch, keep_ref, send_ref, 3, 4)
    total = start_ref[...]
    place = lax.broadcasted_iota(jnp.int32, total.shape, 0)
    query_sum = sum(
        jnp.sum(ref[...].astype(F32), 0, keepdims=True) for ref in query_refs
    )
    value_sum = jnp.sum(value_ref[...].astype(F32), 0, keepdims=True)
    total = total + jnp.where(place == 0, query_sum, 0.0) + jnp.where(place == 1, value_sum, 0.0)
    height = keep_ref.shape[0]
    high, low, sum_ref[...] = split_sums(total)
    send_ref[height : height + SUM_ROWS, :] = high
    send_ref[height + SUM_ROWS :, :] = low


def project_grads(blocks, sums, tokens, low, high, query, key, value, branch, attended):
    features = tokens.shape[1]
    width = key.shape[1]
    half = blocks.shape[0] // 2
    depth = features // (2 * half)
    height = half * 4 * depth
    operands = (sums, *query, *branch, *attended, tokens, low, high, key, value)
    return pl.pallas_call(
        project_grad_kernel,
        grid=(1,),
        in_specs=[pl.BlockSpec(memory_space=SMEM)] + [whole(x.shape) for x in operands],
        out_specs=[
            whole((height, width)),
            whole((height + 2 * SUM_ROWS, width)),
            whole(sums.shape),
        ],
        out_shape=[
            struct((height, width), F32),
            struct((height + 2 * SUM_ROWS, width), BF16),
            struct(sums.shape, F32),
        ],
        scratch_shapes=[pltpu.VMEM((features, width), F32)],
        compiler_params=params(),
        cost_estimate=lasting(0.6),
        name="project_grads",
    )(blocks, *operands)


def fold_kernel(with_sums, keep_ref, arrived_ref, *refs):
    height = keep_ref.shape[0]
    size = height // 2
    if with_sums:
        start_ref, keep_out, send_out, sum_out = refs
    else:
        keep_out, send_out = refs
    keep_out[...] = keep_ref[:size, :] + arrived_ref[:size, :].astype(F32)
    send_out[:size, :] = (keep_ref[size:, :] + arrived_ref[size:height, :].astype(F32)).astype(BF16)
    if with_sums:
        high, low, sum_out[...] = split_sums(start_ref[...] + arrived_sums(arrived_ref, height))
        send_out[size : size + SUM_ROWS, :] = high
        send_out[size + SUM_ROWS :, :] = low


def arrived_sums(ref, height):
    return ref[height : height + SUM_ROWS, :].astype(F32) + ref[height + SUM_ROWS :, :].astype(F32)


def fold(keep, arrived, sums):
    height, width = keep.shape
    extra = arrived.shape[0] - height
    operands = (keep, arrived) + (() if sums is None else (sums,))
    shapes = [struct((height // 2, width), F32), struct((height // 2 + extra, width), BF16)]
    shapes += [] if sums is None else [struct(sums.shape, F32)]
    result = pl.pallas_call(
        functools.partial(fold_kernel, sums is not None),
        grid=(1,),
        in_specs=[whole(x.shape) for x in operands],
        out_specs=[whole(x.shape) for x in shapes],
        out_shape=shapes,
        compiler_params=params(),
        cost_estimate=lasting(0.2),
        name="fold",
    )(*operands)
    return result[0], result[1], (None if sums is None else result[2])


def finish_kernel(kinds, sum_kinds, keep_ref, arrived_ref, *refs):
    height = keep_ref.shape[0]
    if sum_kinds:
        start_ref, *refs = refs
    first = 0
    for kind, ref in zip(kinds, refs):
        depth = ref.shape[-2]
        for place in range(kind or 1):
            rows_here = slice(first, first + depth)
            total = keep_ref[rows_here, :] + arrived_ref[rows_here, :].astype(F32)
            if kind:
                ref[place] = total
            else:
                ref[...] = total
            first += depth
    if sum_kinds:
        total = start_ref[...] + arrived_sums(arrived_ref, height)
        first = 0
        for kind, ref in zip(sum_kinds, refs[len(kinds) :]):
            if ref.shape[0] == kind:
                ref[...] = total[first : first + kind, :]
            else:
                ref[...] = jnp.concatenate([total[first + k : first + k + 1] for k in range(kind)], 1)
            first += kind


def finish(keep, arrived, sums, kinds, sum_kinds):
    height, width = keep.shape
    depth = height // sum(kind or 1 for kind in kinds)
    operands = (keep, arrived) + (() if sums is None else (sums,))
    shapes = [struct((kind, depth, width) if kind else (depth, width), F32) for kind in kinds]
    shapes += [
        struct((kind, width) if kind == 2 else (1, kind * width), F32) for kind in sum_kinds
    ]
    return pl.pallas_call(
        functools.partial(finish_kernel, kinds, sum_kinds),
        grid=(1,),
        in_specs=[whole(x.shape) for x in operands],
        out_specs=[whole(x.shape) for x in shapes],
        out_shape=shapes,
        compiler_params=params(),
        cost_estimate=lasting(0.2),
        name="finish",
    )(*operands)


def token_grad_kernel(even_ref, *refs):
    query_refs, res_refs = refs[:CHUNKS], refs[CHUNKS : 2 * CHUNKS]
    key_ref, value_ref, *weight_refs = refs[2 * CHUNKS : 2 * CHUNKS + 5]
    own_ref, rim_ref, *out_refs = refs[2 * CHUNKS + 5 :]
    own_outs, rim_outs = out_refs[: len(out_refs) // 2], out_refs[len(out_refs) // 2 :]
    count, own = own_ref.shape
    even = even_ref[0] == 1

    def piece(start):
        return dot_nt(key_ref[start : start + BLOCK, :], weight_refs[1][...]) + dot_nt(
            value_ref[start : start + BLOCK, :], weight_refs[2][...]
        )

    def spread(value, start, stays_ref, leave_refs):
        stays_ref[start : start + BLOCK, :] = value[:, :own]
        for place, ref in enumerate(leave_refs, 1):
            lanes = slice(place * own, (place + 1) * own)
            ref[start : start + BLOCK, :] = value[:, lanes].astype(BF16)

    for start in range(0, HALO, BLOCK):
        low, high = piece(PAD + start), piece(MAXDOC + count + start)
        spread(jnp.where(even, high, low), start, rim_ref, rim_outs)
        spread(jnp.where(even, low, high), HALO + start, rim_ref, rim_outs)
    for start in range(0, count, BLOCK):
        chunk, inside = divmod(start, count // CHUNKS)
        total = piece(MAXDOC + start) + dot_nt(
            query_refs[chunk][inside : inside + BLOCK, :], weight_refs[0][...]
        )
        spread(total, start, own_ref, own_outs)
        own_ref[start : start + BLOCK, :] += res_refs[chunk][inside : inside + BLOCK, :]


def token_grads(even, query, res, key, value, weights):
    count = CHUNKS * query[0].shape[0]
    own = res[0].shape[1]
    leave = weights[0].shape[0] // own - 1
    operands = (*query, *res, key, value, *weights)
    shapes = [struct((count, own), F32), struct((2 * HALO, own), F32)]
    shapes += [struct((count, own), BF16)] * leave + [struct((2 * HALO, own), BF16)] * leave
    result = pl.pallas_call(
        token_grad_kernel,
        grid=(1,),
        in_specs=[pl.BlockSpec(memory_space=SMEM)] + [whole(x.shape) for x in operands],
        out_specs=[whole(x.shape) for x in shapes],
        out_shape=shapes,
        compiler_params=params(),
        cost_estimate=lasting(5.0),
        name="token_grads",
    )(even, *operands)
    return result[0], result[1], result[2 : 2 + leave], result[2 + leave :]


def rim_sum_kernel(rim_ref, *refs):
    *arrived_refs, inside_ref, across_ref = refs
    total = rim_ref[...] + sum(ref[...].astype(F32) for ref in arrived_refs)
    inside_ref[...] = total[:HALO].astype(BF16)
    across_ref[...] = total[HALO:].astype(BF16)


def rim_sum(rim, arrived):
    own = rim.shape[1]
    operands = (rim, *arrived)
    return pl.pallas_call(
        rim_sum_kernel,
        grid=(1,),
        in_specs=[whole(x.shape) for x in operands],
        out_specs=[whole((HALO, own))] * 2,
        out_shape=[struct((HALO, own), BF16)] * 2,
        compiler_params=params(),
        cost_estimate=lasting(0.3),
        name="rim_sum",
    )(*operands)


def token_sum_kernel(even_ref, own_ref, inside_ref, across_ref, *refs):
    *arrived_refs, out_ref = refs
    even = even_ref[0] == 1
    inside, across = inside_ref[...].astype(F32), across_ref[...].astype(F32)
    low, high = jnp.where(even, across, inside), jnp.where(even, inside, across)
    rest = own_ref.shape[0] - HALO
    for start in range(0, own_ref.shape[0], BLOCK):
        rows_here = slice(start, start + BLOCK)
        piece = own_ref[rows_here, :] + sum(ref[rows_here, :].astype(F32) for ref in arrived_refs)
        if start < HALO:
            piece = piece + low[rows_here, :]
        if start >= rest:
            piece = piece + high[start - rest : start - rest + BLOCK, :]
        out_ref[rows_here, :] = piece.astype(BF16)


def token_sum(even, own, inside, across, arrived):
    operands = (own, inside, across, *arrived)
    return pl.pallas_call(
        token_sum_kernel,
        grid=(1,),
        in_specs=[pl.BlockSpec(memory_space=SMEM)] + [whole(x.shape) for x in operands],
        out_specs=whole(own.shape),
        out_shape=struct(own.shape, BF16),
        compiler_params=params(),
        cost_estimate=lasting(0.3),
        name="token_sum",
    )(even, *operands)


def from_next(x, axis, step):
    count = lax.axis_size(axis)
    return lax.ppermute(x, axis, [((i + step) % count, i) for i in range(count)])


def others(x):
    return [from_next(x, "col", step) for step in range(1, lax.axis_size("col"))]


def bits_of(count):
    return [1 << place for place in range(count.bit_length() - 1)]


def orders_of(count):
    high = bits_of(count)[:0:-1]
    return high + [1], high[2:] + high[:2] + [1]


def slots_of(order, distance):
    return sum(((distance & bit) // bit) << place for place, bit in enumerate(order))


def distances_of(order, slots):
    return sum(((slots >> place) & 1) * bit for place, bit in enumerate(order))


def with_partner(x, step):
    count = lax.axis_size("row")
    orders = orders_of(count)
    return lax.ppermute(x, "row", [(i, i ^ orders[i % 2][step]) for i in range(count)])


def with_next(inside, across):
    count = lax.axis_size("row")
    pairs = [(i, i + 1 if i % 2 else i - 1) for i in range(1, count - 1)]
    return (
        lax.ppermute(inside, "row", [(i, i ^ 1) for i in range(count)]),
        lax.ppermute(across, "row", pairs),
    )


def after(value, *needed):
    return lax.optimization_barrier((value, *needed))[0]


class Gather:
    def __init__(self, shard):
        self.held, self.step = shard[None], 0
        self.count = len(bits_of(lax.axis_size("row")))
        self.move()

    def move(self):
        self.arrived = with_partner(self.held, self.step)
        self.step += 1

    def put(self, *needed):
        self.held = jnp.concatenate([after(self.held, *needed), self.arrived], 0)
        self.move()


class Reduction:
    def __init__(self, keep, send, sums, kinds, sum_kinds=()):
        self.step = len(bits_of(lax.axis_size("row")))
        self.keep, self.send, self.sums = keep, send, sums
        self.kinds, self.sum_kinds = kinds, sum_kinds
        self.result = None
        self.move()

    def move(self):
        self.step -= 1
        self.arrived = with_partner(self.send, self.step)

    def add(self, *needed):
        keep = after(self.keep, *needed)
        if self.step == 0:
            self.result = finish(keep, self.arrived, self.sums, self.kinds, self.sum_kinds)
        else:
            self.keep, self.send, self.sums = fold(keep, self.arrived, self.sums)
            self.move()


def exchanged(part):
    arrived = others(part)
    if len(arrived) == 1:
        return arrived[0]
    shift = part.shape[1] // (len(arrived) + 1)
    total = sum(
        jnp.roll(x.astype(F32), step * shift, 1) for step, x in enumerate(arrived, 1)
    )
    return total.astype(BF16)


def on_device(
    tokens,
    prev_logits,
    doc_lengths,
    qkv_weight,
    qv_bias,
    out_weight,
    out_bias,
    up_weight,
    up_bias,
    down_weight,
    norm_gain,
    norm_shift,
    out_grad,
    logit_grad,
):
    count, own = tokens.shape
    width = qkv_weight.shape[2]
    row_count, col_count = lax.axis_size("row"), lax.axis_size("col")
    row_index, col_index = lax.axis_index("row"), lax.axis_index("col")
    token_count = count * row_count
    swap = col_count == 2
    hidden_rows = up_bias.shape[0] // own

    odd = row_index % 2 == 1
    places = jnp.arange(row_count, dtype=jnp.int32)
    offset = col_index * (row_count // col_count)
    distance = ((places + offset) % row_count) ^ row_index
    half = row_count // 2
    even_order, odd_order = (order[:-1] for order in orders_of(row_count))
    turned = odd ^ (distance % 2 == 1)
    slots = jnp.where(turned, slots_of(odd_order, distance), slots_of(even_order, distance))
    slots = slots + half * (distance % 2)
    turned = odd ^ (places >= half)
    met = jnp.where(turned, distances_of(odd_order, places), distances_of(even_order, places))
    blocks = (((met + (places >= half)) ^ row_index) - offset) % row_count
    lengths = jnp.concatenate([doc_lengths.reshape(-1), (row_index * count)[None]])

    even = 1 - row_index % 2
    even = even.astype(jnp.int32)[None]

    def dense_of(banded, fill, chunk, *needed):
        dense = to_dense(after(banded, *needed), lengths, fill, token_count, chunk)
        return dense

    prev_logits = pltpu.with_memory_space_constraint(prev_logits, pltpu.HBM)
    logit_grad = pltpu.with_memory_space_constraint(logit_grad, pltpu.HBM)

    out_turned = out_weight.T
    out_other = others(out_turned)
    qkv_rows = Gather(qkv_weight)
    tokens_full, inside, across = join(even, [tokens] + others(after(tokens, out_turned)))
    feed_rows = Gather(jnp.concatenate([out_turned, *out_other, up_weight, down_weight.T], 1))
    qkv_rows.put()
    grad_full = jnp.concatenate([out_grad] + others(out_grad), 1)
    inside, across = with_next(inside, across)
    qkv_rows.put(tokens_full)
    feed_rows.put(qkv_rows.held)
    prev_dense = [
        dense_of(prev_logits, MASKED_SCORE, 0, qkv_rows.held, feed_rows.held, tokens_full)
    ]
    prev_dense.append(dense_of(prev_logits, MASKED_SCORE, 1, prev_dense[0], grad_full))
    while qkv_rows.step < qkv_rows.count:
        qkv_rows.put(prev_dense[1], inside, across)
    feed_rows.put(qkv_rows.held)
    query, key, value, low_tokens, high_tokens, *projections = project(
        slots, even, after(tokens_full, feed_rows.held), inside, across, qkv_rows.held,
        qkv_rows.arrived, qv_bias,
    )
    norms = jnp.concatenate([norm_gain, norm_shift, out_bias], 0)
    norms = jnp.concatenate([norms] + others(after(norms, query)), 1)
    scores, probs, attended, attended_other = [], [], [], []
    for chunk in range(CHUNKS):
        score, prob, mix = attend_forward(query, key, value, prev_dense[chunk], chunk)
        query = after(query, mix, norms)
        scores.append(score)
        probs.append(prob)
        attended.append(mix)
        attended_other.append(jnp.concatenate(others(mix), 1))
    feed_rows.put(mix, attended_other[0])
    while feed_rows.step < feed_rows.count:
        feed_rows.put()
    new_logits = to_band([after(scores[0], feed_rows.held), *scores[1:]], True)
    other_out, *weights = in_order(
        slots, after(feed_rows.held, new_logits), feed_rows.arrived,
        (width, (col_count - 1) * width, up_weight.shape[1], up_weight.shape[1]),
    )
    weights[0], other_out = other_out, weights[0]
    ups = up_bias[None]
    firsts = []
    for chunk in range(CHUNKS):
        result = feed_first(
            attended[chunk], attended_other[chunk], tokens_full, other_out, weights, norms, ups,
            chunk,
        )
        ups = after(ups, result[-1])
        firsts.append((*result, exchanged(result[-1])))
    normed, inverse, upper, act, slope, down_part, down_other = zip(*firsts)

    logit_dense = [dense_of(logit_grad, 0.0, 0, down_part[-1])]
    sums = after(jnp.zeros((SUM_ROWS, own), F32), logit_dense[0])
    output = None
    seconds = []
    for chunk in range(CHUNKS):
        sums, output, *result = feed_second(
            swap, sums, output, down_part[chunk], down_other[chunk],
            normed[chunk], grad_full, slope[chunk], weights, norms, chunk,
        )
        seconds.append((*result, exchanged(result[-1])))
    res_two, ffn_low, hidden_grad, lower_part, lower_other = zip(*seconds)
    keep, send = feed_grads(blocks, ffn_low, act, upper, hidden_grad)
    feed_sum = Reduction(keep, send, None, (0, 0))
    sums = after(sums, keep)

    branch_low, res_one, query_grad, prev_dense_grad = [], [], [], []
    partial = None
    for chunk in range(CHUNKS):
        sums, low, attended_grad, res = feed_third(
            swap, sums, width, lower_part[chunk], lower_other[chunk], res_two[chunk],
            normed[chunk], inverse[chunk], weights, norms,
        )
        branch_low.append(low)
        res_one.append(res)
        prev, query_part, *partial = attend_backward(
            attended_grad, query, key, value, probs[chunk], logit_dense[chunk], chunk, partial
        )
        if chunk == 0:
            feed_sum.add(query_part)
            logit_dense.append(dense_of(logit_grad, 0.0, 1, feed_sum.keep))
            sums = after(sums, logit_dense[1])
        prev_dense_grad.append(prev)
        query_grad.append(query_part)
    key_grad, value_grad = partial
    feed_sum.add(query_grad[-1])
    keep, send, sums = project_grads(
        blocks, after(sums, feed_sum.keep), tokens_full, low_tokens, high_tokens, query_grad,
        key_grad, value_grad, branch_low, attended,
    )
    last_sum = Reduction(keep, send, sums, (3, 0), (2, 2, 2, 2, hidden_rows))
    center, rim, center_parts, rim_parts = token_grads(
        even, query_grad, res_one, after(key_grad, keep), value_grad, projections
    )

    def spread_over(parts):
        return [from_next(part, "col", -step) for step, part in enumerate(parts, 1)]

    last_sum.add(center)
    rim_parts = spread_over(rim_parts)
    center_parts = spread_over(after(x, rim) for x in center_parts)
    prev_dense_grad[0] = after(prev_dense_grad[0], last_sum.keep)
    prev_grad = to_band(prev_dense_grad, False)
    last_sum.add(prev_grad)
    inside, across = rim_sum(after(rim, last_sum.keep), rim_parts)
    feed_sum.add(inside)
    inside, across = with_next(inside, across)
    last_sum.add(feed_sum.keep)
    tokens_grad = token_sum(even, after(center, last_sum.keep), inside, across, center_parts)
    while feed_sum.result is None:
        feed_sum.add(tokens_grad)
    while last_sum.result is None:
        last_sum.add(feed_sum.result[0])
    qkv_grad, out_grad_rows, qv_sum, bias_sum, gain_sum, shift_sum, hidden_sum = last_sum.result
    up_grad, down_grad = feed_sum.result
    return (
        output,
        new_logits,
        tokens_grad,
        prev_grad,
        qkv_grad,
        qv_sum,
        out_grad_rows.T,
        bias_sum,
        up_grad,
        hidden_sum.reshape(-1),
        down_grad.T,
        gain_sum,
        shift_sum,
    )


def solution(mesh):
    return jax.shard_map(
        on_device,
        mesh=mesh,
        in_specs=(
            P("row", "col"),
            P("col", "row", None),
            P(),
            P(None, "row", "col"),
            P(None, "col"),
            P("col", "row"),
            P(None, "col"),
            P("row", "col"),
            P("col"),
            P("col", "row"),
            P(None, "col"),
            P(None, "col"),
            P("row", "col"),
            P("col", "row", None),
        ),
        out_specs=(
            P("row", "col"),
            P("col", "row", None),
            P("row", "col"),
            P("col", "row", None),
            P(None, "row", "col"),
            P(None, "col"),
            P("col", "row"),
            P(None, "col"),
            P("row", "col"),
            P("col"),
            P("col", "row"),
            P(None, "col"),
            P(None, "col"),
        ),
        check_vma=False,
    )
```

```python
import functools

import jax
import jax.numpy as jnp
from jax import lax
from jax.experimental import pallas as pl
from jax.experimental.pallas import tpu as pltpu
from jax.sharding import PartitionSpec as P

D = 512
HEAD_DIM = 64
MAXDOC = 512
BAND = 2 * MAXDOC
BLOCK = 128
WINDOW = BAND + BLOCK
HALO = MAXDOC - 128
PAD = MAXDOC - HALO

EPSILON = 1e-05
MASKED_SCORE = -1e30
ERF_RATE = 0.7071067811865476
DENSITY_RATE = 0.3989422804014327

F32 = jnp.float32
BF16 = jnp.bfloat16
SMEM = pltpu.MemorySpace.SMEM
VMEM_LIMIT = 24 << 20
CHUNKS = 2
SUM_ROWS = 16
FLOPS_PER_MICROSECOND = 1.0e9


def dot_nn(a, b):
    return lax.dot_general(a, b, (((1,), (0,)), ((), ())), preferred_element_type=F32)


def dot_nt(a, b):
    return lax.dot_general(a, b, (((1,), (1,)), ((), ())), preferred_element_type=F32)


def dot_tn(a, b):
    return lax.dot_general(a, b, (((0,), (0,)), ((), ())), preferred_element_type=F32)


def params():
    return pltpu.CompilerParams(
        dimension_semantics=("arbitrary",), vmem_limit_bytes=VMEM_LIMIT
    )


def lasting(microseconds):
    return pl.CostEstimate(
        flops=int(microseconds * FLOPS_PER_MICROSECOND), bytes_accessed=0, transcendentals=0
    )


def whole(shape):
    return pl.BlockSpec(shape, lambda b: (0,) * len(shape))


def rows(width, first=0):
    return pl.BlockSpec((BLOCK, width), lambda b: (b + first, 0))


def heads_block(heads, width, first=0):
    return pl.BlockSpec((heads, BLOCK, width), lambda b: (0, b + first, 0))


def struct(shape, dtype):
    return jax.ShapeDtypeStruct(shape, dtype)


def segment_of(positions, lengths_ref, documents, token_count):
    found = jnp.zeros(positions.shape, jnp.int32)
    end = jnp.int32(0)
    for document in range(documents):
        end = end + lengths_ref[document]
        found = found + (positions >= end).astype(jnp.int32)
    return jnp.where((positions >= 0) & (positions < token_count), found, -1)


def dense_kernel(fill, token_count, offset, lengths_ref, band_ref, dense_ref):
    documents = lengths_ref.shape[0] - 1
    first = lengths_ref[documents] + (pl.program_id(0) + offset) * BLOCK
    query = first + lax.broadcasted_iota(jnp.int32, (BLOCK, 1), 0)
    key = first - MAXDOC + lax.broadcasted_iota(jnp.int32, (1, WINDOW), 1)
    same = segment_of(query, lengths_ref, documents, token_count) == segment_of(
        key, lengths_ref, documents, token_count
    )
    for head in range(band_ref.shape[0]):
        wide = jnp.concatenate(
            [band_ref[head].astype(F32), jnp.zeros((BLOCK, BLOCK), F32)], 1
        )
        turned = pltpu.roll(wide, 0, 1, stride=1, stride_axis=0)
        dense_ref[head] = jnp.where(same, turned, fill).astype(BF16)


def to_dense(banded, lengths, fill, token_count, chunk):
    heads, count, _ = banded.shape
    count //= CHUNKS
    offset = chunk * (count // BLOCK)
    return pl.pallas_call(
        functools.partial(dense_kernel, fill, token_count, offset),
        grid=(count // BLOCK,),
        in_specs=[pl.BlockSpec(memory_space=SMEM), heads_block(heads, BAND, offset)],
        out_specs=heads_block(heads, WINDOW),
        out_shape=struct((heads, count, WINDOW), BF16),
        compiler_params=params(),
        cost_estimate=lasting(8.0 if fill and chunk == 0 else 1.0),
        name="to_dense",
    )(lengths, banded)


def band_kernel(masked, *refs):
    dense_refs, band_ref = refs[:-1], refs[-1]
    lane = lax.broadcasted_iota(jnp.int32, (BLOCK, BLOCK), 1)
    row = lax.broadcasted_iota(jnp.int32, (BLOCK, BLOCK), 0)
    source = (lane + row) & (BLOCK - 1)
    near = lane + row < BLOCK
    steps = pl.num_programs(0) // CHUNKS

    def turn(dense_ref):
        for head in range(band_ref.shape[0]):
            pieces = []
            for place in range(WINDOW // BLOCK):
                piece = dense_ref[head, :, place * BLOCK : (place + 1) * BLOCK].astype(F32)
                if masked:
                    piece = jnp.where(piece < 0.5 * MASKED_SCORE, 0.0, piece)
                pieces.append(jnp.take_along_axis(piece, source, axis=1))
            for place in range(BAND // BLOCK):
                band_ref[head, :, place * BLOCK : (place + 1) * BLOCK] = jnp.where(
                    near, pieces[place], pieces[place + 1]
                ).astype(BF16)

    for chunk, dense_ref in enumerate(dense_refs):

        @pl.when(pl.program_id(0) // steps == chunk)
        def _():
            turn(dense_ref)


def to_band(chunks, masked):
    heads, count, _ = chunks[0].shape
    steps = count // BLOCK

    def block_of(chunk):
        return pl.BlockSpec(
            (heads, BLOCK, WINDOW), lambda b: (0, jnp.clip(b - chunk * steps, 0, steps - 1), 0)
        )

    return pl.pallas_call(
        functools.partial(band_kernel, masked),
        grid=(CHUNKS * steps,),
        in_specs=[block_of(chunk) for chunk in range(CHUNKS)],
        out_specs=heads_block(heads, BAND),
        out_shape=struct((heads, CHUNKS * count, BAND), BF16),
        compiler_params=params(),
        cost_estimate=lasting(5.0 if masked else 0.5),
        name="to_band",
    )(*chunks)


def head_split(block, size):
    if size == 1:
        return block
    lane = lax.broadcasted_iota(jnp.int32, block.shape, 1)
    return jnp.concatenate(
        [
            jnp.where((lane >= h * HEAD_DIM) & (lane < (h + 1) * HEAD_DIM), block, 0)
            for h in range(size)
        ],
        0,
    )


def head_join(stacked, size):
    if size == 1:
        return stacked
    height = stacked.shape[0] // size
    joined = stacked[:height]
    lane = lax.broadcasted_iota(jnp.int32, joined.shape, 1)
    for h in range(1, size):
        joined = jnp.where(lane >= h * HEAD_DIM, stacked[h * height : (h + 1) * height], joined)
    return joined


def project_kernel(
    parts, slot_ref, even_ref, near_ref, far_ref, bias_ref, *refs
):
    token_refs, inside_refs, across_refs = (refs[k * parts : (k + 1) * parts] for k in range(3))
    all_ref, query_ref, key_ref, value_ref, low_ref, high_ref, *weight_refs = refs[3 * parts :]
    half, _, depth, _ = near_ref.shape
    count, width = token_refs[0].shape

    def put(place, source_ref, slot):
        for which, ref in enumerate(weight_refs):
            ref[place * depth : (place + 1) * depth, :] = source_ref[slot, which]

    for place in range(2 * half):
        slot = slot_ref[place]

        @pl.when(slot < half)
        def _():
            put(place, near_ref, slot)

        @pl.when(slot >= half)
        def _():
            put(place, far_ref, slot - half)

    even = even_ref[0] == 1
    for place, (own_ref, inside_ref, across_ref) in enumerate(
        zip(token_refs, inside_refs, across_refs)
    ):
        lanes = slice(place * width, (place + 1) * width)
        inside, across = inside_ref[...], across_ref[...]
        all_ref[:, lanes] = own_ref[...]
        low_ref[:, lanes] = jnp.where(even, across, inside)
        high_ref[:, lanes] = jnp.where(even, inside, across)
    own, low_rows, high_rows = all_ref[...], low_ref[...], high_ref[...]
    query = (dot_nn(own, weight_refs[0][...]) + bias_ref[0:1, :]).astype(BF16)
    empty = jnp.zeros((PAD, query.shape[1]), BF16)
    query_ref[...] = query * jnp.asarray(HEAD_DIM ** (-0.5), BF16)
    for out_ref, which in ((key_ref, 1), (value_ref, 2)):
        shift = bias_ref[1:2, :] if which == 2 else 0.0
        weight = weight_refs[which][...]
        out_ref[0:PAD, :] = empty
        out_ref[PAD:MAXDOC, :] = (dot_nn(low_rows, weight) + shift).astype(BF16)
        out_ref[MAXDOC : MAXDOC + count, :] = (dot_nn(own, weight) + shift).astype(BF16)
        out_ref[MAXDOC + count : MAXDOC + count + HALO, :] = (
            dot_nn(high_rows, weight) + shift
        ).astype(BF16)
        out_ref[MAXDOC + count + HALO :, :] = empty


def project(slots, even, near, far, bias, tokens, inside, across):
    count, part = tokens[0].shape
    features = len(tokens) * part
    width = near.shape[3]
    operands = (near, far, bias, *tokens, *inside, *across)
    extended = (count + BAND, width)
    shapes = [(count, features), (count, width), extended, extended]
    shapes += [(HALO, features)] * 2 + [(features, width)] * 3
    return pl.pallas_call(
        functools.partial(project_kernel, len(tokens)),
        grid=(1,),
        in_specs=[pl.BlockSpec(memory_space=SMEM)] * 2 + [whole(x.shape) for x in operands],
        out_specs=[whole(shape) for shape in shapes],
        out_shape=[struct(shape, BF16) for shape in shapes],
        compiler_params=params(),
        cost_estimate=lasting(2.0),
        name="project",
    )(slots, even, *operands)


def forward_kernel(
    offset, query_ref, key_ref, value_ref, prev_ref, score_ref, prob_ref, attended_ref
):
    heads = prev_ref.shape[0]
    size = min(2, heads)
    span = size * HEAD_DIM
    window = pl.ds(pl.multiple_of((pl.program_id(0) + offset) * BLOCK, BLOCK), WINDOW)
    for group in range(heads // size):
        lanes = slice(group * span, (group + 1) * span)
        query = head_split(query_ref[:, lanes], size)
        dense = dot_nt(query, key_ref[window, lanes])
        weights = []
        for h in range(size):
            head = group * size + h
            score = dense[h * BLOCK : (h + 1) * BLOCK] + prev_ref[head].astype(F32)
            score_ref[head] = score.astype(BF16)
            peak = jnp.max(score, -1, keepdims=True)
            grown = jnp.exp(score - peak)
            total = jnp.sum(grown, -1, keepdims=True)
            prob = (grown * (1.0 / total)).astype(BF16)
            prob_ref[head] = prob
            weights.append(prob)
        mixed = dot_nn(jnp.concatenate(weights, 0), value_ref[window, lanes])
        attended_ref[:, lanes] = head_join(mixed, size).astype(BF16)


def attend_forward(query, key, value, prev, chunk):
    heads, count, _ = prev.shape
    width = query.shape[1]
    offset = chunk * (count // BLOCK)
    return pl.pallas_call(
        functools.partial(forward_kernel, offset),
        grid=(count // BLOCK,),
        in_specs=[
            rows(width, offset),
            whole(key.shape),
            whole(value.shape),
            heads_block(heads, WINDOW),
        ],
        out_specs=[heads_block(heads, WINDOW), heads_block(heads, WINDOW), rows(width)],
        out_shape=[
            struct((heads, count, WINDOW), BF16),
            struct((heads, count, WINDOW), BF16),
            struct((count, width), BF16),
        ],
        compiler_params=params(),
        cost_estimate=lasting(3.8),
        name="attend_forward",
    )(query, key, value, prev)


def backward_kernel(
    offset, last, grad_ref, query_ref, key_ref, value_ref, prob_ref, logit_ref, *refs
):
    if last:
        key_start, value_start = refs[:2]
        prev_ref, query_grad_ref, key_grad_ref, value_grad_ref, key_sum, value_sum = refs[2:]
    else:
        prev_ref, query_grad_ref, key_sum, value_sum = refs
    step = pl.program_id(0)
    heads = prob_ref.shape[0]
    size = min(2, heads)
    span = size * HEAD_DIM

    @pl.when(step == 0)
    def _():
        if last:
            key_sum[...] = key_start[...]
            value_sum[...] = value_start[...]
        else:
            key_sum[...] = jnp.zeros_like(key_sum)
            value_sum[...] = jnp.zeros_like(value_sum)

    window = pl.ds(pl.multiple_of((step + offset) * BLOCK, BLOCK), WINDOW)
    for group in range(heads // size):
        lanes = slice(group * span, (group + 1) * span)
        query = head_split(query_ref[:, lanes], size)
        grad = head_split(grad_ref[:, lanes], size)
        key = key_ref[window, lanes]
        prob_grad = dot_nt(grad, value_ref[window, lanes])
        probs, scores = [], []
        for h in range(size):
            head = group * size + h
            low = prob_ref[head]
            prob = low.astype(F32)
            slope = prob_grad[h * BLOCK : (h + 1) * BLOCK]
            inner = jnp.sum(prob * slope, -1, keepdims=True)
            score = (prob * (slope - inner) + logit_ref[head].astype(F32)).astype(BF16)
            prev_ref[head] = score
            probs.append(low)
            scores.append(score)
        stacked = jnp.concatenate(scores, 0)
        mixed = head_join(dot_nn(stacked, key), size) * HEAD_DIM ** (-0.5)
        query_grad_ref[:, lanes] = mixed.astype(BF16)
        key_sum[lanes, window] += dot_tn(query, stacked)
        value_sum[lanes, window] += dot_tn(grad, jnp.concatenate(probs, 0))

    if last:

        @pl.when(step == pl.num_programs(0) - 1)
        def _():
            key_grad_ref[...] = key_sum[...].astype(BF16).T
            value_grad_ref[...] = value_sum[...].astype(BF16).T


def attend_backward(grad, query, key, value, prob, logit, chunk, sums):
    heads, count, _ = prob.shape
    extended, width = key.shape
    offset = chunk * (count // BLOCK)
    last = sums is not None
    turned = (width, extended)
    scratch = [pltpu.VMEM(turned, F32), pltpu.VMEM(turned, F32)] if last else []
    ends = [whole((extended, width))] * 2 if last else [whole(turned)] * 2
    end_shapes = [struct((extended, width), BF16)] * 2 if last else [struct(turned, F32)] * 2
    return pl.pallas_call(
        functools.partial(backward_kernel, offset, last),
        grid=(count // BLOCK,),
        in_specs=[
            rows(width),
            rows(width, offset),
            whole((extended, width)),
            whole((extended, width)),
            heads_block(heads, WINDOW),
            heads_block(heads, WINDOW),
        ]
        + ([whole(turned)] * 2 if last else []),
        out_specs=[heads_block(heads, WINDOW), rows(width)] + ends,
        out_shape=[struct((heads, count, WINDOW), BF16), struct((count, width), BF16)]
        + end_shapes,
        scratch_shapes=scratch,
        compiler_params=params(),
        cost_estimate=lasting(3.0 if last else 20.0),
        name="attend_backward",
    )(grad, query, key, value, prob, logit, *(sums or ()))


def order_kernel(slot_ref, near_ref, far_ref, *out_refs):
    half, depth, _ = near_ref.shape

    def put(place, source_ref, slot):
        first = 0
        for out_ref in out_refs:
            last = first + out_ref.shape[1]
            out_ref[place * depth : (place + 1) * depth, :] = source_ref[slot, :, first:last]
            first = last

    for place in range(2 * half):
        slot = slot_ref[place]

        @pl.when(slot < half)
        def _():
            put(place, near_ref, slot)

        @pl.when(slot >= half)
        def _():
            put(place, far_ref, slot - half)


def in_order(slots, near, far, widths):
    half, depth, _ = near.shape
    shapes = [(2 * half * depth, width) for width in widths]
    return pl.pallas_call(
        order_kernel,
        grid=(1,),
        in_specs=[pl.BlockSpec(memory_space=SMEM), whole(near.shape), whole(far.shape)],
        out_specs=[whole(shape) for shape in shapes],
        out_shape=[struct(shape, BF16) for shape in shapes],
        compiler_params=params(),
        cost_estimate=lasting(0.9),
        name="in_order",
    )(slots, near, far)


def mean_of(x):
    return jnp.sum(x, -1, keepdims=True) * (1.0 / D)


def normalized(hidden):
    mean = mean_of(hidden)
    inverse = lax.rsqrt(mean_of(hidden * hidden) - mean * mean + EPSILON)
    return (hidden - mean) * inverse, inverse


def norm_back(upstream, normed, inverse):
    return inverse * (upstream - mean_of(upstream) - normed * mean_of(upstream * normed))


def added(own_ref, other_ref, swap):
    other = other_ref[...]
    if swap:
        middle = other.shape[1] // 2
        other = jnp.concatenate([other[:, middle:], other[:, :middle]], 1)
    return own_ref[...].astype(F32) + other.astype(F32)


def first_kernel(
    own_ref, other_ref, token_ref, other_out_ref, out_ref, up_ref, down_ref, norm_ref,
    up_bias_ref, normed_ref, inverse_ref, upper_ref, act_ref, slope_ref, part_ref,
):
    branch = dot_nt(own_ref[...], out_ref[...]) + dot_nt(other_ref[...], other_out_ref[...])
    hidden = token_ref[...].astype(F32) + branch + norm_ref[4:5, :]
    normed, inverse = normalized(hidden)
    normed_ref[...] = normed
    inverse_ref[...] = inverse
    upper = (normed * norm_ref[0:1, :] + norm_ref[2:3, :]).astype(BF16)
    upper_ref[...] = upper
    pre = dot_nn(upper, up_ref[...]) + up_bias_ref[...]
    share = 0.5 * (1.0 + lax.erf(pre * ERF_RATE))
    act = (pre * share).astype(BF16)
    act_ref[...] = act
    slope_ref[...] = (share + pre * jnp.exp(-0.5 * pre * pre) * DENSITY_RATE).astype(BF16)
    part_ref[...] = dot_nt(act, down_ref[...]).astype(BF16)


def feed_first(own, other, tokens, other_out, weights, norms, up_bias, chunk):
    count, width = own.shape
    features = tokens.shape[1]
    units = up_bias.shape[1]
    return pl.pallas_call(
        first_kernel,
        grid=(count // BLOCK,),
        in_specs=[
            rows(width),
            rows(other.shape[1]),
            rows(features, chunk * (count // BLOCK)),
            whole(other_out.shape),
            *(whole(x.shape) for x in weights),
            whole(norms.shape),
            whole(up_bias.shape),
        ],
        out_specs=[
            rows(features),
            rows(1),
            rows(features),
            rows(units),
            rows(units),
            rows(features),
        ],
        out_shape=[
            struct((count, features), F32),
            struct((count, 1), F32),
            struct((count, features), BF16),
            struct((count, units), BF16),
            struct((count, units), BF16),
            struct((count, features), BF16),
        ],
        compiler_params=params(),
        cost_estimate=lasting(1.0),
        name="feed_first",
    )(own, other, tokens, other_out, *weights, norms, up_bias)


def add_sums(start_ref, sum_ref, first, values):
    @pl.when(pl.program_id(0) == 0)
    def _():
        sum_ref[...] = start_ref[...]

    for place, value in enumerate(values):
        sum_ref[first + place : first + place + 1, :] += jnp.sum(value, 0, keepdims=True)


def second_kernel(
    swap, start_ref, part_ref, recv_ref, normed_ref, grad_ref, slope_ref, up_ref, down_ref,
    norm_ref, *refs,
):
    sum_ref, output_ref, res_ref, low_ref, hidden_ref, lower_ref = refs[-6:]
    own = output_ref.shape[1]
    upper = normed_ref[...] * norm_ref[0:1, :] + norm_ref[2:3, :]
    hidden = upper + added(part_ref, recv_ref, swap) + norm_ref[5:6, :]
    normed, inverse = normalized(hidden)
    output_ref[...] = (
        normed[:, :own] * norm_ref[1:2, :own] + norm_ref[3:4, :own]
    ).astype(BF16)
    grad = grad_ref[...].astype(F32)
    res = norm_back(grad * norm_ref[1:2, :], normed, inverse)
    res_ref[...] = res
    low = res.astype(BF16)
    low_ref[...] = low
    act_grad = dot_nn(low, down_ref[...])
    hidden_grad = (act_grad * slope_ref[...].astype(F32)).astype(BF16)
    hidden_ref[...] = hidden_grad
    lower_ref[...] = dot_nt(hidden_grad, up_ref[...]).astype(BF16)
    wide = hidden_grad.astype(F32)
    add_sums(start_ref, sum_ref, 3, [low[:, :own].astype(F32)])
    for place, value in (
        (5, grad[:, :own] * normed[:, :own]),
        (7, grad[:, :own]),
        *((8 + k, wide[:, k * own : (k + 1) * own]) for k in range(wide.shape[1] // own)),
    ):
        sum_ref[place : place + 1, :] += jnp.sum(value, 0, keepdims=True)


def feed_second(swap, sums, held, part, recv, normed, grad, slope, weights, norms, chunk):
    count, features = part.shape
    own = sums.shape[1]
    units = slope.shape[1]
    offset = chunk * (count // BLOCK)
    return pl.pallas_call(
        functools.partial(second_kernel, swap),
        grid=(count // BLOCK,),
        in_specs=[
            whole(sums.shape),
            rows(features),
            rows(features),
            rows(features),
            rows(features, offset),
            rows(units),
            *(whole(x.shape) for x in weights[1:]),
            whole(norms.shape),
            *([] if held is None else [pl.BlockSpec(memory_space=pl.ANY)]),
        ],
        out_specs=[
            whole(sums.shape),
            rows(own, offset),
            rows(features),
            rows(features),
            rows(units),
            rows(features),
        ],
        out_shape=[
            struct(sums.shape, F32),
            struct((CHUNKS * count, own), BF16),
            struct((count, features), F32),
            struct((count, features), BF16),
            struct((count, units), BF16),
            struct((count, features), BF16),
        ],
        input_output_aliases={} if held is None else {9: 1},
        compiler_params=params(),
        cost_estimate=lasting(0.7),
        name="feed_second",
    )(sums, part, recv, normed, grad, slope, *weights[1:], norms, *(() if held is None else (held,)))


def third_kernel(
    swap, start_ref, part_ref, recv_ref, res_ref, normed_ref, inverse_ref, out_ref, norm_ref,
    sum_ref, low_ref, attended_ref, own_ref,
):
    own = own_ref.shape[1]
    grad = added(part_ref, recv_ref, swap) + res_ref[...]
    normed = normed_ref[...]
    res = norm_back(grad * norm_ref[0:1, :], normed, inverse_ref[...])
    own_ref[...] = res[:, :own]
    low = res.astype(BF16)
    low_ref[...] = low
    attended_ref[...] = dot_nn(low, out_ref[...]).astype(BF16)
    add_sums(start_ref, sum_ref, 2, [low[:, :own].astype(F32)])
    for place, value in ((4, grad[:, :own] * normed[:, :own]), (6, grad[:, :own])):
        sum_ref[place : place + 1, :] += jnp.sum(value, 0, keepdims=True)


def feed_third(swap, sums, width, part, recv, res, normed, inverse, weights, norms):
    count, features = part.shape
    own = sums.shape[1]
    return pl.pallas_call(
        functools.partial(third_kernel, swap),
        grid=(count // BLOCK,),
        in_specs=[
            whole(sums.shape),
            rows(features),
            rows(features),
            rows(features),
            rows(features),
            rows(1),
            whole(weights[0].shape),
            whole(norms.shape),
        ],
        out_specs=[whole(sums.shape), rows(features), rows(width), rows(own)],
        out_shape=[
            struct(sums.shape, F32),
            struct((count, features), BF16),
            struct((count, width), BF16),
            struct((count, own), F32),
        ],
        compiler_params=params(),
        cost_estimate=lasting(0.2),
        name="feed_third",
    )(sums, part, recv, res, normed, inverse, weights[0], norms)


def spread_rows(block_ref, scratch, keep_ref, send_ref, which, kinds):
    features = scratch.shape[0]
    count = block_ref.shape[0]
    depth = features // count
    half = count // 2
    for slot in range(count):
        start = pl.multiple_of(block_ref[slot] * depth, depth)
        piece = scratch[pl.ds(start, depth), :]
        first = ((slot % half) * kinds + which) * depth
        if slot < half:
            keep_ref[first : first + depth, :] = piece
        else:
            send_ref[first : first + depth, :] = piece.astype(BF16)


def split_sums(total):
    high = total.astype(BF16)
    low = (total - high.astype(F32)).astype(BF16)
    return high, low, high.astype(F32) + low.astype(F32)


def feed_grad_kernel(block_ref, *refs):
    low_refs, upper_refs, act_refs, hidden_refs = (
        refs[k * CHUNKS : (k + 1) * CHUNKS] for k in range(4)
    )
    keep_ref, send_ref, scratch = refs[4 * CHUNKS :]
    scratch[...] = sum(dot_tn(a[...], b[...]) for a, b in zip(upper_refs, hidden_refs))
    spread_rows(block_ref, scratch, keep_ref, send_ref, 0, 2)
    scratch[...] = sum(dot_tn(a[...], b[...]) for a, b in zip(low_refs, act_refs))
    spread_rows(block_ref, scratch, keep_ref, send_ref, 1, 2)


def feed_grads(blocks, low, act, upper, hidden):
    count, features = low[0].shape
    units = act[0].shape[1]
    chunk = min(256, units)
    column = pl.BlockSpec((count, chunk), lambda b: (0, b))
    result = pl.BlockSpec((features, chunk), lambda b: (0, b))
    return pl.pallas_call(
        feed_grad_kernel,
        grid=(units // chunk,),
        in_specs=[pl.BlockSpec(memory_space=SMEM)]
        + [whole((count, features))] * (2 * CHUNKS)
        + [column] * (2 * CHUNKS),
        out_specs=[result] * 2,
        out_shape=[struct((features, units), F32), struct((features, units), BF16)],
        scratch_shapes=[pltpu.VMEM((features, chunk), F32)],
        compiler_params=params(),
        cost_estimate=lasting(1.0),
        name="feed_grads",
    )(blocks, *low, *upper, *act, *hidden)


def project_grad_kernel(block_ref, start_ref, *refs):
    query_refs, branch_refs, attended_refs = (
        refs[k * CHUNKS : (k + 1) * CHUNKS] for k in range(3)
    )
    token_ref, low_ref, high_ref, key_ref, value_ref = refs[3 * CHUNKS : 3 * CHUNKS + 5]
    keep_ref, send_ref, sum_ref, scratch = refs[3 * CHUNKS + 5 :]
    count = token_ref.shape[0]
    part = count // CHUNKS
    scratch[...] = sum(
        dot_tn(token_ref[k * part : (k + 1) * part, :], ref[...])
        for k, ref in enumerate(query_refs)
    )
    spread_rows(block_ref, scratch, keep_ref, send_ref, 0, 4)
    for which, ref in ((1, key_ref), (2, value_ref)):
        scratch[...] = (
            dot_tn(token_ref[...], ref[MAXDOC : MAXDOC + count, :])
            + dot_tn(low_ref[...], ref[PAD:MAXDOC, :])
            + dot_tn(high_ref[...], ref[MAXDOC + count : MAXDOC + count + HALO, :])
        )
        spread_rows(block_ref, scratch, keep_ref, send_ref, which, 4)
    scratch[...] = sum(dot_tn(a[...], b[...]) for a, b in zip(branch_refs, attended_refs))
    spread_rows(block_ref, scratch, keep_ref, send_ref, 3, 4)
    total = start_ref[...]
    place = lax.broadcasted_iota(jnp.int32, total.shape, 0)
    query_sum = sum(
        jnp.sum(ref[...].astype(F32), 0, keepdims=True) for ref in query_refs
    )
    value_sum = jnp.sum(value_ref[...].astype(F32), 0, keepdims=True)
    total = total + jnp.where(place == 0, query_sum, 0.0) + jnp.where(place == 1, value_sum, 0.0)
    height = keep_ref.shape[0]
    high, low, sum_ref[...] = split_sums(total)
    send_ref[height : height + SUM_ROWS, :] = high
    send_ref[height + SUM_ROWS :, :] = low


def project_grads(blocks, sums, tokens, low, high, query, key, value, branch, attended):
    features = tokens.shape[1]
    width = key.shape[1]
    half = blocks.shape[0] // 2
    depth = features // (2 * half)
    height = half * 4 * depth
    operands = (sums, *query, *branch, *attended, tokens, low, high, key, value)
    return pl.pallas_call(
        project_grad_kernel,
        grid=(1,),
        in_specs=[pl.BlockSpec(memory_space=SMEM)] + [whole(x.shape) for x in operands],
        out_specs=[
            whole((height, width)),
            whole((height + 2 * SUM_ROWS, width)),
            whole(sums.shape),
        ],
        out_shape=[
            struct((height, width), F32),
            struct((height + 2 * SUM_ROWS, width), BF16),
            struct(sums.shape, F32),
        ],
        scratch_shapes=[pltpu.VMEM((features, width), F32)],
        compiler_params=params(),
        cost_estimate=lasting(0.6),
        name="project_grads",
    )(blocks, *operands)


def fold_kernel(with_sums, keep_ref, arrived_ref, *refs):
    height = keep_ref.shape[0]
    size = height // 2
    if with_sums:
        start_ref, keep_out, send_out, sum_out = refs
    else:
        keep_out, send_out = refs
    keep_out[...] = keep_ref[:size, :] + arrived_ref[:size, :].astype(F32)
    send_out[:size, :] = (keep_ref[size:, :] + arrived_ref[size:height, :].astype(F32)).astype(BF16)
    if with_sums:
        high, low, sum_out[...] = split_sums(start_ref[...] + arrived_sums(arrived_ref, height))
        send_out[size : size + SUM_ROWS, :] = high
        send_out[size + SUM_ROWS :, :] = low


def arrived_sums(ref, height):
    return ref[height : height + SUM_ROWS, :].astype(F32) + ref[height + SUM_ROWS :, :].astype(F32)


def fold(keep, arrived, sums):
    height, width = keep.shape
    extra = arrived.shape[0] - height
    operands = (keep, arrived) + (() if sums is None else (sums,))
    shapes = [struct((height // 2, width), F32), struct((height // 2 + extra, width), BF16)]
    shapes += [] if sums is None else [struct(sums.shape, F32)]
    result = pl.pallas_call(
        functools.partial(fold_kernel, sums is not None),
        grid=(1,),
        in_specs=[whole(x.shape) for x in operands],
        out_specs=[whole(x.shape) for x in shapes],
        out_shape=shapes,
        compiler_params=params(),
        cost_estimate=lasting(0.2),
        name="fold",
    )(*operands)
    return result[0], result[1], (None if sums is None else result[2])


def finish_kernel(kinds, sum_kinds, keep_ref, arrived_ref, *refs):
    height = keep_ref.shape[0]
    if sum_kinds:
        start_ref, *refs = refs
    first = 0
    for kind, ref in zip(kinds, refs):
        depth = ref.shape[-2]
        for place in range(kind or 1):
            rows_here = slice(first, first + depth)
            total = keep_ref[rows_here, :] + arrived_ref[rows_here, :].astype(F32)
            if kind:
                ref[place] = total
            else:
                ref[...] = total
            first += depth
    if sum_kinds:
        total = start_ref[...] + arrived_sums(arrived_ref, height)
        first = 0
        for kind, ref in zip(sum_kinds, refs[len(kinds) :]):
            if ref.shape[0] == kind:
                ref[...] = total[first : first + kind, :]
            else:
                ref[...] = jnp.concatenate([total[first + k : first + k + 1] for k in range(kind)], 1)
            first += kind


def finish(keep, arrived, sums, kinds, sum_kinds):
    height, width = keep.shape
    depth = height // sum(kind or 1 for kind in kinds)
    operands = (keep, arrived) + (() if sums is None else (sums,))
    shapes = [struct((kind, depth, width) if kind else (depth, width), F32) for kind in kinds]
    shapes += [
        struct((kind, width) if kind == 2 else (1, kind * width), F32) for kind in sum_kinds
    ]
    return pl.pallas_call(
        functools.partial(finish_kernel, kinds, sum_kinds),
        grid=(1,),
        in_specs=[whole(x.shape) for x in operands],
        out_specs=[whole(x.shape) for x in shapes],
        out_shape=shapes,
        compiler_params=params(),
        cost_estimate=lasting(0.2),
        name="finish",
    )(*operands)


def token_grad_kernel(even_ref, *refs):
    query_refs, res_refs = refs[:CHUNKS], refs[CHUNKS : 2 * CHUNKS]
    key_ref, value_ref, *weight_refs = refs[2 * CHUNKS : 2 * CHUNKS + 5]
    own_ref, rim_ref, *out_refs = refs[2 * CHUNKS + 5 :]
    own_outs, rim_outs = out_refs[: len(out_refs) // 2], out_refs[len(out_refs) // 2 :]
    count, own = own_ref.shape
    even = even_ref[0] == 1

    def piece(start):
        return dot_nt(key_ref[start : start + BLOCK, :], weight_refs[1][...]) + dot_nt(
            value_ref[start : start + BLOCK, :], weight_refs[2][...]
        )

    def spread(value, start, stays_ref, leave_refs):
        stays_ref[start : start + BLOCK, :] = value[:, :own]
        for place, ref in enumerate(leave_refs, 1):
            lanes = slice(place * own, (place + 1) * own)
            ref[start : start + BLOCK, :] = value[:, lanes].astype(BF16)

    for start in range(0, HALO, BLOCK):
        low, high = piece(PAD + start), piece(MAXDOC + count + start)
        spread(jnp.where(even, high, low), start, rim_ref, rim_outs)
        spread(jnp.where(even, low, high), HALO + start, rim_ref, rim_outs)
    for start in range(0, count, BLOCK):
        chunk, inside = divmod(start, count // CHUNKS)
        total = piece(MAXDOC + start) + dot_nt(
            query_refs[chunk][inside : inside + BLOCK, :], weight_refs[0][...]
        )
        spread(total, start, own_ref, own_outs)
        own_ref[start : start + BLOCK, :] += res_refs[chunk][inside : inside + BLOCK, :]


def token_grads(even, query, res, key, value, weights):
    count = CHUNKS * query[0].shape[0]
    own = res[0].shape[1]
    leave = weights[0].shape[0] // own - 1
    operands = (*query, *res, key, value, *weights)
    shapes = [struct((count, own), F32), struct((2 * HALO, own), F32)]
    shapes += [struct((count, own), BF16)] * leave + [struct((2 * HALO, own), BF16)] * leave
    result = pl.pallas_call(
        token_grad_kernel,
        grid=(1,),
        in_specs=[pl.BlockSpec(memory_space=SMEM)] + [whole(x.shape) for x in operands],
        out_specs=[whole(x.shape) for x in shapes],
        out_shape=shapes,
        compiler_params=params(),
        cost_estimate=lasting(5.0),
        name="token_grads",
    )(even, *operands)
    return result[0], result[1], result[2 : 2 + leave], result[2 + leave :]


def rim_sum_kernel(rim_ref, *refs):
    *arrived_refs, inside_ref, across_ref = refs
    total = rim_ref[...] + sum(ref[...].astype(F32) for ref in arrived_refs)
    inside_ref[...] = total[:HALO].astype(BF16)
    across_ref[...] = total[HALO:].astype(BF16)


def rim_sum(rim, arrived):
    own = rim.shape[1]
    operands = (rim, *arrived)
    return pl.pallas_call(
        rim_sum_kernel,
        grid=(1,),
        in_specs=[whole(x.shape) for x in operands],
        out_specs=[whole((HALO, own))] * 2,
        out_shape=[struct((HALO, own), BF16)] * 2,
        compiler_params=params(),
        cost_estimate=lasting(0.3),
        name="rim_sum",
    )(*operands)


def token_sum_kernel(even_ref, own_ref, inside_ref, across_ref, *refs):
    *arrived_refs, out_ref = refs
    even = even_ref[0] == 1
    inside, across = inside_ref[...].astype(F32), across_ref[...].astype(F32)
    low, high = jnp.where(even, across, inside), jnp.where(even, inside, across)
    rest = own_ref.shape[0] - HALO
    for start in range(0, own_ref.shape[0], BLOCK):
        rows_here = slice(start, start + BLOCK)
        piece = own_ref[rows_here, :] + sum(ref[rows_here, :].astype(F32) for ref in arrived_refs)
        if start < HALO:
            piece = piece + low[rows_here, :]
        if start >= rest:
            piece = piece + high[start - rest : start - rest + BLOCK, :]
        out_ref[rows_here, :] = piece.astype(BF16)


def token_sum(even, own, inside, across, arrived):
    operands = (own, inside, across, *arrived)
    return pl.pallas_call(
        token_sum_kernel,
        grid=(1,),
        in_specs=[pl.BlockSpec(memory_space=SMEM)] + [whole(x.shape) for x in operands],
        out_specs=whole(own.shape),
        out_shape=struct(own.shape, BF16),
        compiler_params=params(),
        cost_estimate=lasting(0.3),
        name="token_sum",
    )(even, *operands)


def from_next(x, axis, step):
    count = lax.axis_size(axis)
    return lax.ppermute(x, axis, [((i + step) % count, i) for i in range(count)])


def others(x):
    return [from_next(x, "col", step) for step in range(1, lax.axis_size("col"))]


def bits_of(count):
    return [1 << place for place in range(count.bit_length() - 1)]


def orders_of(count):
    high = bits_of(count)[:0:-1]
    return high + [1], high[2:] + high[:2] + [1]


def slots_of(order, distance):
    return sum(((distance & bit) // bit) << place for place, bit in enumerate(order))


def distances_of(order, slots):
    return sum(((slots >> place) & 1) * bit for place, bit in enumerate(order))


def with_partner(x, step):
    count = lax.axis_size("row")
    orders = orders_of(count)
    return lax.ppermute(x, "row", [(i, i ^ orders[i % 2][step]) for i in range(count)])


def with_next(inside, across):
    count = lax.axis_size("row")
    pairs = [(i, i + 1 if i % 2 else i - 1) for i in range(1, count - 1)]
    return (
        lax.ppermute(inside, "row", [(i, i ^ 1) for i in range(count)]),
        lax.ppermute(across, "row", pairs),
    )


def after(value, *needed):
    return lax.optimization_barrier((value, *needed))[0]


class Gather:
    def __init__(self, shard):
        self.held, self.step = shard[None], 0
        self.count = len(bits_of(lax.axis_size("row")))
        self.move()

    def move(self):
        self.arrived = with_partner(self.held, self.step)
        self.step += 1

    def put(self, *needed):
        self.held = jnp.concatenate([after(self.held, *needed), self.arrived], 0)
        self.move()


class Reduction:
    def __init__(self, keep, send, sums, kinds, sum_kinds=()):
        self.step = len(bits_of(lax.axis_size("row")))
        self.keep, self.send, self.sums = keep, send, sums
        self.kinds, self.sum_kinds = kinds, sum_kinds
        self.result = None
        self.move()

    def move(self):
        self.step -= 1
        self.arrived = with_partner(self.send, self.step)

    def add(self, *needed):
        keep = after(self.keep, *needed)
        if self.step == 0:
            self.result = finish(keep, self.arrived, self.sums, self.kinds, self.sum_kinds)
        else:
            self.keep, self.send, self.sums = fold(keep, self.arrived, self.sums)
            self.move()


def exchanged(part):
    arrived = others(part)
    if len(arrived) == 1:
        return arrived[0]
    shift = part.shape[1] // (len(arrived) + 1)
    total = sum(
        jnp.roll(x.astype(F32), step * shift, 1) for step, x in enumerate(arrived, 1)
    )
    return total.astype(BF16)


def on_device(
    tokens,
    prev_logits,
    doc_lengths,
    qkv_weight,
    qv_bias,
    out_weight,
    out_bias,
    up_weight,
    up_bias,
    down_weight,
    norm_gain,
    norm_shift,
    out_grad,
    logit_grad,
):
    count, own = tokens.shape
    width = qkv_weight.shape[2]
    row_count, col_count = lax.axis_size("row"), lax.axis_size("col")
    row_index, col_index = lax.axis_index("row"), lax.axis_index("col")
    token_count = count * row_count
    swap = col_count == 2
    hidden_rows = up_bias.shape[0] // own

    odd = row_index % 2 == 1
    places = jnp.arange(row_count, dtype=jnp.int32)
    offset = col_index * (row_count // col_count)
    distance = ((places + offset) % row_count) ^ row_index
    half = row_count // 2
    even_order, odd_order = (order[:-1] for order in orders_of(row_count))
    turned = odd ^ (distance % 2 == 1)
    slots = jnp.where(turned, slots_of(odd_order, distance), slots_of(even_order, distance))
    slots = slots + half * (distance % 2)
    turned = odd ^ (places >= half)
    met = jnp.where(turned, distances_of(odd_order, places), distances_of(even_order, places))
    blocks = (((met + (places >= half)) ^ row_index) - offset) % row_count

    even = 1 - row_index % 2
    even = even.astype(jnp.int32)[None]

    def dense_of(banded, fill, chunk, *needed):
        dense = to_dense(after(banded, *needed), lengths, fill, token_count, chunk)
        return dense

    prev_logits = pltpu.with_memory_space_constraint(prev_logits, pltpu.HBM)
    logit_grad = pltpu.with_memory_space_constraint(logit_grad, pltpu.HBM)

    out_turned = out_weight.T
    out_other = others(out_turned)
    qkv_rows = Gather(qkv_weight)
    tokens_other = others(after(tokens, out_turned))
    feed_rows = Gather(jnp.concatenate([out_turned, *out_other, up_weight, down_weight.T], 1))
    tail = row_index % 2 * (count - HALO)
    ready = after(tokens, feed_rows.held)
    inside, across = with_next(
        lax.dynamic_slice_in_dim(ready, count - HALO - tail, HALO, 0),
        lax.dynamic_slice_in_dim(ready, tail, HALO, 0),
    )
    qkv_rows.put(feed_rows.held)
    inside_other, across_other = others(inside), others(across)
    feed_rows.put(qkv_rows.held)
    qkv_rows.put(feed_rows.held, *tokens_other)
    lengths = jnp.concatenate(
        [after(doc_lengths, qkv_rows.held).reshape(-1), (row_index * count)[None]]
    )
    prev_dense = [
        dense_of(prev_logits, MASKED_SCORE, 0, qkv_rows.held, feed_rows.held, inside, across)
    ]
    grad_other = others(after(out_grad, *inside_other))
    while qkv_rows.step < qkv_rows.count:
        qkv_rows.put(prev_dense[0], *inside_other, *across_other)
    feed_rows.put(qkv_rows.held)
    tokens_full, query, key, value, low_tokens, high_tokens, *projections = project(
        slots, even, qkv_rows.held, qkv_rows.arrived, qv_bias, [after(tokens, feed_rows.held), *tokens_other],
        [inside, *inside_other], [across, *across_other],
    )
    grad_full = jnp.concatenate([after(out_grad, query)] + grad_other, 1)
    norms = jnp.concatenate([after(norm_gain, query), norm_shift, out_bias], 0)
    norms = jnp.concatenate([norms] + others(norms), 1)
    scores, probs, attended, attended_other = [], [], [], []
    for chunk in range(CHUNKS):
        score, prob, mix = attend_forward(
            after(query, feed_rows.held) if chunk else query, key, value, prev_dense[chunk], chunk
        )
        scores.append(score)
        probs.append(prob)
        attended.append(mix)
        attended_other.append(jnp.concatenate(others(mix), 1))
        if chunk == 0:
            prev_dense.append(dense_of(prev_logits, MASKED_SCORE, 1, mix, norms, grad_full))
            while feed_rows.step < feed_rows.count:
                feed_rows.put(prev_dense[1], attended_other[0])
    other_out, *weights = in_order(
        slots, after(feed_rows.held, mix), feed_rows.arrived,
        (width, (col_count - 1) * width, up_weight.shape[1], up_weight.shape[1]),
    )
    weights[0], other_out = other_out, weights[0]
    ups = up_bias[None]
    firsts, logit_dense = [], []
    for chunk in range(CHUNKS):
        result = feed_first(
            attended[chunk], attended_other[chunk], tokens_full, other_out, weights, norms, ups,
            chunk,
        )
        if chunk == 0:
            logit_dense.append(dense_of(logit_grad, 0.0, 0, result[-1]))
            ups = after(ups, logit_dense[0])
        firsts.append((*result, exchanged(result[-1])))
    normed, inverse, upper, act, slope, down_part, down_other = zip(*firsts)

    new_logits = to_band([after(scores[0], down_part[-1]), *scores[1:]], True)
    sums = after(jnp.zeros((SUM_ROWS, own), F32), new_logits)
    output = None
    seconds = []
    for chunk in range(CHUNKS):
        sums, output, *result = feed_second(
            swap, sums, output, down_part[chunk], down_other[chunk],
            normed[chunk], grad_full, slope[chunk], weights, norms, chunk,
        )
        seconds.append((*result, exchanged(result[-1])))
    res_two, ffn_low, hidden_grad, lower_part, lower_other = zip(*seconds)
    keep, send = feed_grads(blocks, ffn_low, act, upper, hidden_grad)
    feed_sum = Reduction(keep, send, None, (0, 0))
    sums = after(sums, keep)

    branch_low, res_one, query_grad, prev_dense_grad = [], [], [], []
    partial = None
    for chunk in range(CHUNKS):
        sums, low, attended_grad, res = feed_third(
            swap, sums, width, lower_part[chunk], lower_other[chunk], res_two[chunk],
            normed[chunk], inverse[chunk], weights, norms,
        )
        branch_low.append(low)
        res_one.append(res)
        prev, query_part, *partial = attend_backward(
            attended_grad, query, key, value, probs[chunk], logit_dense[chunk], chunk, partial
        )
        if chunk == 0:
            feed_sum.add(query_part)
            logit_dense.append(dense_of(logit_grad, 0.0, 1, feed_sum.keep))
            sums = after(sums, logit_dense[1])
        prev_dense_grad.append(prev)
        query_grad.append(query_part)
    key_grad, value_grad = partial
    feed_sum.add(query_grad[-1])
    keep, send, sums = project_grads(
        blocks, after(sums, feed_sum.keep), tokens_full, low_tokens, high_tokens, query_grad,
        key_grad, value_grad, branch_low, attended,
    )
    last_sum = Reduction(keep, send, sums, (3, 0), (2, 2, 2, 2, hidden_rows))
    center, rim, center_parts, rim_parts = token_grads(
        even, query_grad, res_one, after(key_grad, keep), value_grad, projections
    )

    def spread_over(parts):
        return [from_next(part, "col", -step) for step, part in enumerate(parts, 1)]

    last_sum.add(center)
    rim_parts = spread_over(rim_parts)
    center_parts = spread_over(after(x, rim) for x in center_parts)
    prev_dense_grad[0] = after(prev_dense_grad[0], last_sum.keep)
    prev_grad = to_band(prev_dense_grad, False)
    last_sum.add(prev_grad)
    inside, across = rim_sum(after(rim, last_sum.keep), rim_parts)
    feed_sum.add(inside)
    inside, across = with_next(inside, across)
    last_sum.add(feed_sum.keep)
    tokens_grad = token_sum(even, after(center, last_sum.keep), inside, across, center_parts)
    while feed_sum.result is None:
        feed_sum.add(tokens_grad)
    while last_sum.result is None:
        last_sum.add(feed_sum.result[0])
    qkv_grad, out_grad_rows, qv_sum, bias_sum, gain_sum, shift_sum, hidden_sum = last_sum.result
    up_grad, down_grad = feed_sum.result
    return (
        output,
        new_logits,
        tokens_grad,
        prev_grad,
        qkv_grad,
        qv_sum,
        out_grad_rows.T,
        bias_sum,
        up_grad,
        hidden_sum.reshape(-1),
        down_grad.T,
        gain_sum,
        shift_sum,
    )


def solution(mesh):
    return jax.shard_map(
        on_device,
        mesh=mesh,
        in_specs=(
            P("row", "col"),
            P("col", "row", None),
            P(),
            P(None, "row", "col"),
            P(None, "col"),
            P("col", "row"),
            P(None, "col"),
            P("row", "col"),
            P("col"),
            P("col", "row"),
            P(None, "col"),
            P(None, "col"),
            P("row", "col"),
            P("col", "row", None),
        ),
        out_specs=(
            P("row", "col"),
            P("col", "row", None),
            P("row", "col"),
            P("col", "row", None),
            P(None, "row", "col"),
            P(None, "col"),
            P("col", "row"),
            P(None, "col"),
            P("row", "col"),
            P("col"),
            P("col", "row"),
            P(None, "col"),
            P(None, "col"),
        ),
        check_vma=False,
    )
```

```python
import functools

import jax
import jax.numpy as jnp
from jax import lax
from jax.experimental import pallas as pl
from jax.experimental.pallas import tpu as pltpu
from jax.sharding import PartitionSpec as P

D = 512
HEAD_DIM = 64
MAXDOC = 512
BAND = 2 * MAXDOC
BLOCK = 128
WINDOW = BAND + BLOCK
HALO = MAXDOC - 128
PAD = MAXDOC - HALO

EPSILON = 1e-05
MASKED_SCORE = -1e30
ERF_RATE = 0.7071067811865476
DENSITY_RATE = 0.3989422804014327

F32 = jnp.float32
BF16 = jnp.bfloat16
SMEM = pltpu.MemorySpace.SMEM
VMEM_LIMIT = 24 << 20
CHUNKS = 2
SUM_ROWS = 16
FLOPS_PER_MICROSECOND = 1.0e9


def dot_nn(a, b):
    return lax.dot_general(a, b, (((1,), (0,)), ((), ())), preferred_element_type=F32)


def dot_nt(a, b):
    return lax.dot_general(a, b, (((1,), (1,)), ((), ())), preferred_element_type=F32)


def dot_tn(a, b):
    return lax.dot_general(a, b, (((0,), (0,)), ((), ())), preferred_element_type=F32)


def params():
    return pltpu.CompilerParams(
        dimension_semantics=("arbitrary",), vmem_limit_bytes=VMEM_LIMIT
    )


def lasting(microseconds):
    return pl.CostEstimate(
        flops=int(microseconds * FLOPS_PER_MICROSECOND), bytes_accessed=0, transcendentals=0
    )


def whole(shape):
    return pl.BlockSpec(shape, lambda b: (0,) * len(shape))


def rows(width, first=0):
    return pl.BlockSpec((BLOCK, width), lambda b: (b + first, 0))


def heads_block(heads, width, first=0):
    return pl.BlockSpec((heads, BLOCK, width), lambda b: (0, b + first, 0))


def struct(shape, dtype):
    return jax.ShapeDtypeStruct(shape, dtype)


def segment_of(positions, lengths_ref, documents, token_count):
    found = jnp.zeros(positions.shape, jnp.int32)
    end = jnp.int32(0)
    for document in range(documents):
        end = end + lengths_ref[document]
        found = found + (positions >= end).astype(jnp.int32)
    return jnp.where((positions >= 0) & (positions < token_count), found, -1)


def dense_kernel(fill, token_count, offset, lengths_ref, band_ref, dense_ref):
    documents = lengths_ref.shape[0] - 1
    first = lengths_ref[documents] + (pl.program_id(0) + offset) * BLOCK
    query = first + lax.broadcasted_iota(jnp.int32, (BLOCK, 1), 0)
    key = first - MAXDOC + lax.broadcasted_iota(jnp.int32, (1, WINDOW), 1)
    same = segment_of(query, lengths_ref, documents, token_count) == segment_of(
        key, lengths_ref, documents, token_count
    )
    for head in range(band_ref.shape[0]):
        wide = jnp.concatenate(
            [band_ref[head].astype(F32), jnp.zeros((BLOCK, BLOCK), F32)], 1
        )
        turned = pltpu.roll(wide, 0, 1, stride=1, stride_axis=0)
        dense_ref[head] = jnp.where(same, turned, fill).astype(BF16)


def to_dense(banded, lengths, fill, token_count, chunk):
    heads, count, _ = banded.shape
    count //= CHUNKS
    offset = chunk * (count // BLOCK)
    return pl.pallas_call(
        functools.partial(dense_kernel, fill, token_count, offset),
        grid=(count // BLOCK,),
        in_specs=[pl.BlockSpec(memory_space=SMEM), heads_block(heads, BAND, offset)],
        out_specs=heads_block(heads, WINDOW),
        out_shape=struct((heads, count, WINDOW), BF16),
        compiler_params=params(),
        cost_estimate=lasting(8.0 if fill and chunk == 0 else 1.0),
        name="to_dense",
    )(lengths, banded)


def band_kernel(masked, chunks, *refs):
    dense_refs, band_ref = refs[:chunks], refs[-1]
    lane = lax.broadcasted_iota(jnp.int32, (BLOCK, BLOCK), 1)
    row = lax.broadcasted_iota(jnp.int32, (BLOCK, BLOCK), 0)
    source = (lane + row) & (BLOCK - 1)
    near = lane + row < BLOCK
    steps = pl.num_programs(0) // chunks

    def turn(dense_ref):
        for head in range(band_ref.shape[0]):
            pieces = []
            for place in range(WINDOW // BLOCK):
                piece = dense_ref[head, :, place * BLOCK : (place + 1) * BLOCK].astype(F32)
                if masked:
                    piece = jnp.where(piece < 0.5 * MASKED_SCORE, 0.0, piece)
                pieces.append(jnp.take_along_axis(piece, source, axis=1))
            for place in range(BAND // BLOCK):
                band_ref[head, :, place * BLOCK : (place + 1) * BLOCK] = jnp.where(
                    near, pieces[place], pieces[place + 1]
                ).astype(BF16)

    for chunk, dense_ref in enumerate(dense_refs):

        @pl.when(pl.program_id(0) // steps == chunk)
        def _():
            turn(dense_ref)


def to_band(chunks, masked, first=0, held=None):
    heads, count, _ = chunks[0].shape
    steps = count // BLOCK

    def block_of(chunk):
        return pl.BlockSpec(
            (heads, BLOCK, WINDOW), lambda b: (0, jnp.clip(b - chunk * steps, 0, steps - 1), 0)
        )

    return pl.pallas_call(
        functools.partial(band_kernel, masked, len(chunks)),
        grid=(len(chunks) * steps,),
        in_specs=[block_of(chunk) for chunk in range(len(chunks))]
        + ([] if held is None else [pl.BlockSpec(memory_space=pl.ANY)]),
        out_specs=heads_block(heads, BAND, first * steps),
        out_shape=struct((heads, CHUNKS * count, BAND), BF16),
        input_output_aliases={} if held is None else {len(chunks): 0},
        compiler_params=params(),
        cost_estimate=lasting(5.0 if masked and held is None else 0.3),
        name="to_band",
    )(*chunks, *(() if held is None else (held,)))


def head_split(block, size):
    if size == 1:
        return block
    lane = lax.broadcasted_iota(jnp.int32, block.shape, 1)
    return jnp.concatenate(
        [
            jnp.where((lane >= h * HEAD_DIM) & (lane < (h + 1) * HEAD_DIM), block, 0)
            for h in range(size)
        ],
        0,
    )


def head_join(stacked, size):
    if size == 1:
        return stacked
    height = stacked.shape[0] // size
    joined = stacked[:height]
    lane = lax.broadcasted_iota(jnp.int32, joined.shape, 1)
    for h in range(1, size):
        joined = jnp.where(lane >= h * HEAD_DIM, stacked[h * height : (h + 1) * height], joined)
    return joined


def project_kernel(
    parts, slot_ref, even_ref, near_ref, far_ref, bias_ref, *refs
):
    token_refs, inside_refs, across_refs = (refs[k * parts : (k + 1) * parts] for k in range(3))
    all_ref, query_ref, key_ref, value_ref, low_ref, high_ref, *weight_refs = refs[3 * parts :]
    half, _, depth, _ = near_ref.shape
    count, width = token_refs[0].shape

    def put(place, source_ref, slot):
        for which, ref in enumerate(weight_refs):
            ref[place * depth : (place + 1) * depth, :] = source_ref[slot, which]

    for place in range(2 * half):
        slot = slot_ref[place]

        @pl.when(slot < half)
        def _():
            put(place, near_ref, slot)

        @pl.when(slot >= half)
        def _():
            put(place, far_ref, slot - half)

    even = even_ref[0] == 1
    for place, (own_ref, inside_ref, across_ref) in enumerate(
        zip(token_refs, inside_refs, across_refs)
    ):
        lanes = slice(place * width, (place + 1) * width)
        inside, across = inside_ref[...], across_ref[...]
        all_ref[:, lanes] = own_ref[...]
        low_ref[:, lanes] = jnp.where(even, across, inside)
        high_ref[:, lanes] = jnp.where(even, inside, across)
    own, low_rows, high_rows = all_ref[...], low_ref[...], high_ref[...]
    query = (dot_nn(own, weight_refs[0][...]) + bias_ref[0:1, :]).astype(BF16)
    empty = jnp.zeros((PAD, query.shape[1]), BF16)
    query_ref[...] = query * jnp.asarray(HEAD_DIM ** (-0.5), BF16)
    for out_ref, which in ((key_ref, 1), (value_ref, 2)):
        shift = bias_ref[1:2, :] if which == 2 else 0.0
        weight = weight_refs[which][...]
        out_ref[0:PAD, :] = empty
        out_ref[PAD:MAXDOC, :] = (dot_nn(low_rows, weight) + shift).astype(BF16)
        out_ref[MAXDOC : MAXDOC + count, :] = (dot_nn(own, weight) + shift).astype(BF16)
        out_ref[MAXDOC + count : MAXDOC + count + HALO, :] = (
            dot_nn(high_rows, weight) + shift
        ).astype(BF16)
        out_ref[MAXDOC + count + HALO :, :] = empty


def project(slots, even, near, far, bias, tokens, inside, across):
    count, part = tokens[0].shape
    features = len(tokens) * part
    width = near.shape[3]
    operands = (near, far, bias, *tokens, *inside, *across)
    extended = (count + BAND, width)
    shapes = [(count, features), (count, width), extended, extended]
    shapes += [(HALO, features)] * 2 + [(features, width)] * 3
    return pl.pallas_call(
        functools.partial(project_kernel, len(tokens)),
        grid=(1,),
        in_specs=[pl.BlockSpec(memory_space=SMEM)] * 2 + [whole(x.shape) for x in operands],
        out_specs=[whole(shape) for shape in shapes],
        out_shape=[struct(shape, BF16) for shape in shapes],
        compiler_params=params(),
        cost_estimate=lasting(2.0),
        name="project",
    )(slots, even, *operands)


def forward_kernel(
    offset, query_ref, key_ref, value_ref, prev_ref, score_ref, prob_ref, attended_ref
):
    heads = prev_ref.shape[0]
    size = min(2, heads)
    span = size * HEAD_DIM
    window = pl.ds(pl.multiple_of((pl.program_id(0) + offset) * BLOCK, BLOCK), WINDOW)
    for group in range(heads // size):
        lanes = slice(group * span, (group + 1) * span)
        query = head_split(query_ref[:, lanes], size)
        dense = dot_nt(query, key_ref[window, lanes])
        weights = []
        for h in range(size):
            head = group * size + h
            score = dense[h * BLOCK : (h + 1) * BLOCK] + prev_ref[head].astype(F32)
            score_ref[head] = score.astype(BF16)
            peak = jnp.max(score, -1, keepdims=True)
            grown = jnp.exp(score - peak)
            total = jnp.sum(grown, -1, keepdims=True)
            prob = (grown * (1.0 / total)).astype(BF16)
            prob_ref[head] = prob
            weights.append(prob)
        mixed = dot_nn(jnp.concatenate(weights, 0), value_ref[window, lanes])
        attended_ref[:, lanes] = head_join(mixed, size).astype(BF16)


def attend_forward(query, key, value, prev, chunk):
    heads, count, _ = prev.shape
    width = query.shape[1]
    offset = chunk * (count // BLOCK)
    return pl.pallas_call(
        functools.partial(forward_kernel, offset),
        grid=(count // BLOCK,),
        in_specs=[
            rows(width, offset),
            whole(key.shape),
            whole(value.shape),
            heads_block(heads, WINDOW),
        ],
        out_specs=[heads_block(heads, WINDOW), heads_block(heads, WINDOW), rows(width)],
        out_shape=[
            struct((heads, count, WINDOW), BF16),
            struct((heads, count, WINDOW), BF16),
            struct((count, width), BF16),
        ],
        compiler_params=params(),
        cost_estimate=lasting(3.8),
        name="attend_forward",
    )(query, key, value, prev)


def backward_kernel(
    offset, last, grad_ref, query_ref, key_ref, value_ref, prob_ref, logit_ref, *refs
):
    if last:
        key_start, value_start = refs[:2]
        prev_ref, query_grad_ref, key_grad_ref, value_grad_ref, key_sum, value_sum = refs[2:]
    else:
        prev_ref, query_grad_ref, key_sum, value_sum = refs
    step = pl.program_id(0)
    heads = prob_ref.shape[0]
    size = min(2, heads)
    span = size * HEAD_DIM

    @pl.when(step == 0)
    def _():
        if last:
            key_sum[...] = key_start[...]
            value_sum[...] = value_start[...]
        else:
            key_sum[...] = jnp.zeros_like(key_sum)
            value_sum[...] = jnp.zeros_like(value_sum)

    window = pl.ds(pl.multiple_of((step + offset) * BLOCK, BLOCK), WINDOW)
    for group in range(heads // size):
        lanes = slice(group * span, (group + 1) * span)
        query = head_split(query_ref[:, lanes], size)
        grad = head_split(grad_ref[:, lanes], size)
        key = key_ref[window, lanes]
        prob_grad = dot_nt(grad, value_ref[window, lanes])
        probs, scores = [], []
        for h in range(size):
            head = group * size + h
            low = prob_ref[head]
            prob = low.astype(F32)
            slope = prob_grad[h * BLOCK : (h + 1) * BLOCK]
            inner = jnp.sum(prob * slope, -1, keepdims=True)
            score = (prob * (slope - inner) + logit_ref[head].astype(F32)).astype(BF16)
            prev_ref[head] = score
            probs.append(low)
            scores.append(score)
        stacked = jnp.concatenate(scores, 0)
        mixed = head_join(dot_nn(stacked, key), size) * HEAD_DIM ** (-0.5)
        query_grad_ref[:, lanes] = mixed.astype(BF16)
        key_sum[lanes, window] += dot_tn(query, stacked)
        value_sum[lanes, window] += dot_tn(grad, jnp.concatenate(probs, 0))

    if last:

        @pl.when(step == pl.num_programs(0) - 1)
        def _():
            key_grad_ref[...] = key_sum[...].astype(BF16).T
            value_grad_ref[...] = value_sum[...].astype(BF16).T


def attend_backward(grad, query, key, value, prob, logit, chunk, sums):
    heads, count, _ = prob.shape
    extended, width = key.shape
    offset = chunk * (count // BLOCK)
    last = sums is not None
    turned = (width, extended)
    scratch = [pltpu.VMEM(turned, F32), pltpu.VMEM(turned, F32)] if last else []
    ends = [whole((extended, width))] * 2 if last else [whole(turned)] * 2
    end_shapes = [struct((extended, width), BF16)] * 2 if last else [struct(turned, F32)] * 2
    return pl.pallas_call(
        functools.partial(backward_kernel, offset, last),
        grid=(count // BLOCK,),
        in_specs=[
            rows(width),
            rows(width, offset),
            whole((extended, width)),
            whole((extended, width)),
            heads_block(heads, WINDOW),
            heads_block(heads, WINDOW),
        ]
        + ([whole(turned)] * 2 if last else []),
        out_specs=[heads_block(heads, WINDOW), rows(width)] + ends,
        out_shape=[struct((heads, count, WINDOW), BF16), struct((count, width), BF16)]
        + end_shapes,
        scratch_shapes=scratch,
        compiler_params=params(),
        cost_estimate=lasting(3.0 if last else 20.0),
        name="attend_backward",
    )(grad, query, key, value, prob, logit, *(sums or ()))


def order_kernel(slot_ref, near_ref, far_ref, *out_refs):
    half, depth, _ = near_ref.shape

    def put(place, source_ref, slot):
        first = 0
        for out_ref in out_refs:
            last = first + out_ref.shape[1]
            out_ref[place * depth : (place + 1) * depth, :] = source_ref[slot, :, first:last]
            first = last

    for place in range(2 * half):
        slot = slot_ref[place]

        @pl.when(slot < half)
        def _():
            put(place, near_ref, slot)

        @pl.when(slot >= half)
        def _():
            put(place, far_ref, slot - half)


def in_order(slots, near, far, widths):
    half, depth, _ = near.shape
    shapes = [(2 * half * depth, width) for width in widths]
    return pl.pallas_call(
        order_kernel,
        grid=(1,),
        in_specs=[pl.BlockSpec(memory_space=SMEM), whole(near.shape), whole(far.shape)],
        out_specs=[whole(shape) for shape in shapes],
        out_shape=[struct(shape, BF16) for shape in shapes],
        compiler_params=params(),
        cost_estimate=lasting(0.9),
        name="in_order",
    )(slots, near, far)


def mean_of(x):
    return jnp.sum(x, -1, keepdims=True) * (1.0 / D)


def normalized(hidden):
    mean = mean_of(hidden)
    inverse = lax.rsqrt(mean_of(hidden * hidden) - mean * mean + EPSILON)
    return (hidden - mean) * inverse, inverse


def norm_back(upstream, normed, inverse):
    return inverse * (upstream - mean_of(upstream) - normed * mean_of(upstream * normed))


def added(own_ref, other_ref, swap):
    other = other_ref[...]
    if swap:
        middle = other.shape[1] // 2
        other = jnp.concatenate([other[:, middle:], other[:, :middle]], 1)
    return own_ref[...].astype(F32) + other.astype(F32)


def first_kernel(
    own_ref, other_ref, token_ref, other_out_ref, out_ref, up_ref, down_ref, norm_ref,
    up_bias_ref, normed_ref, inverse_ref, upper_ref, act_ref, slope_ref, part_ref,
):
    branch = dot_nt(own_ref[...], out_ref[...]) + dot_nt(other_ref[...], other_out_ref[...])
    hidden = token_ref[...].astype(F32) + branch + norm_ref[4:5, :]
    normed, inverse = normalized(hidden)
    normed_ref[...] = normed
    inverse_ref[...] = inverse
    upper = (normed * norm_ref[0:1, :] + norm_ref[2:3, :]).astype(BF16)
    upper_ref[...] = upper
    pre = dot_nn(upper, up_ref[...]) + up_bias_ref[...]
    share = 0.5 * (1.0 + lax.erf(pre * ERF_RATE))
    act = (pre * share).astype(BF16)
    act_ref[...] = act
    slope_ref[...] = (share + pre * jnp.exp(-0.5 * pre * pre) * DENSITY_RATE).astype(BF16)
    part_ref[...] = dot_nt(act, down_ref[...]).astype(BF16)


def feed_first(own, other, tokens, other_out, weights, norms, up_bias, chunk):
    count, width = own.shape
    features = tokens.shape[1]
    units = up_bias.shape[1]
    return pl.pallas_call(
        first_kernel,
        grid=(count // BLOCK,),
        in_specs=[
            rows(width),
            rows(other.shape[1]),
            rows(features, chunk * (count // BLOCK)),
            whole(other_out.shape),
            *(whole(x.shape) for x in weights),
            whole(norms.shape),
            whole(up_bias.shape),
        ],
        out_specs=[
            rows(features),
            rows(1),
            rows(features),
            rows(units),
            rows(units),
            rows(features),
        ],
        out_shape=[
            struct((count, features), F32),
            struct((count, 1), F32),
            struct((count, features), BF16),
            struct((count, units), BF16),
            struct((count, units), BF16),
            struct((count, features), BF16),
        ],
        compiler_params=params(),
        cost_estimate=lasting(1.0),
        name="feed_first",
    )(own, other, tokens, other_out, *weights, norms, up_bias)


def add_sums(start_ref, sum_ref, first, values):
    @pl.when(pl.program_id(0) == 0)
    def _():
        sum_ref[...] = start_ref[...]

    for place, value in enumerate(values):
        sum_ref[first + place : first + place + 1, :] += jnp.sum(value, 0, keepdims=True)


def second_kernel(
    swap, start_ref, part_ref, recv_ref, normed_ref, grad_ref, slope_ref, up_ref, down_ref,
    norm_ref, *refs,
):
    sum_ref, output_ref, res_ref, low_ref, hidden_ref, lower_ref = refs[-6:]
    own = output_ref.shape[1]
    upper = normed_ref[...] * norm_ref[0:1, :] + norm_ref[2:3, :]
    hidden = upper + added(part_ref, recv_ref, swap) + norm_ref[5:6, :]
    normed, inverse = normalized(hidden)
    output_ref[...] = (
        normed[:, :own] * norm_ref[1:2, :own] + norm_ref[3:4, :own]
    ).astype(BF16)
    grad = grad_ref[...].astype(F32)
    res = norm_back(grad * norm_ref[1:2, :], normed, inverse)
    res_ref[...] = res
    low = res.astype(BF16)
    low_ref[...] = low
    act_grad = dot_nn(low, down_ref[...])
    hidden_grad = (act_grad * slope_ref[...].astype(F32)).astype(BF16)
    hidden_ref[...] = hidden_grad
    lower_ref[...] = dot_nt(hidden_grad, up_ref[...]).astype(BF16)
    wide = hidden_grad.astype(F32)
    add_sums(start_ref, sum_ref, 3, [low[:, :own].astype(F32)])
    for place, value in (
        (5, grad[:, :own] * normed[:, :own]),
        (7, grad[:, :own]),
        *((8 + k, wide[:, k * own : (k + 1) * own]) for k in range(wide.shape[1] // own)),
    ):
        sum_ref[place : place + 1, :] += jnp.sum(value, 0, keepdims=True)


def feed_second(swap, sums, held, part, recv, normed, grad, slope, weights, norms, chunk):
    count, features = part.shape
    own = sums.shape[1]
    units = slope.shape[1]
    offset = chunk * (count // BLOCK)
    return pl.pallas_call(
        functools.partial(second_kernel, swap),
        grid=(count // BLOCK,),
        in_specs=[
            whole(sums.shape),
            rows(features),
            rows(features),
            rows(features),
            rows(features, offset),
            rows(units),
            *(whole(x.shape) for x in weights[1:]),
            whole(norms.shape),
            *([] if held is None else [pl.BlockSpec(memory_space=pl.ANY)]),
        ],
        out_specs=[
            whole(sums.shape),
            rows(own, offset),
            rows(features),
            rows(features),
            rows(units),
            rows(features),
        ],
        out_shape=[
            struct(sums.shape, F32),
            struct((CHUNKS * count, own), BF16),
            struct((count, features), F32),
            struct((count, features), BF16),
            struct((count, units), BF16),
            struct((count, features), BF16),
        ],
        input_output_aliases={} if held is None else {9: 1},
        compiler_params=params(),
        cost_estimate=lasting(0.7),
        name="feed_second",
    )(sums, part, recv, normed, grad, slope, *weights[1:], norms, *(() if held is None else (held,)))


def third_kernel(
    swap, start_ref, part_ref, recv_ref, res_ref, normed_ref, inverse_ref, out_ref, norm_ref,
    sum_ref, low_ref, attended_ref, own_ref,
):
    own = own_ref.shape[1]
    grad = added(part_ref, recv_ref, swap) + res_ref[...]
    normed = normed_ref[...]
    res = norm_back(grad * norm_ref[0:1, :], normed, inverse_ref[...])
    own_ref[...] = res[:, :own]
    low = res.astype(BF16)
    low_ref[...] = low
    attended_ref[...] = dot_nn(low, out_ref[...]).astype(BF16)
    add_sums(start_ref, sum_ref, 2, [low[:, :own].astype(F32)])
    for place, value in ((4, grad[:, :own] * normed[:, :own]), (6, grad[:, :own])):
        sum_ref[place : place + 1, :] += jnp.sum(value, 0, keepdims=True)


def feed_third(swap, sums, width, part, recv, res, normed, inverse, weights, norms):
    count, features = part.shape
    own = sums.shape[1]
    return pl.pallas_call(
        functools.partial(third_kernel, swap),
        grid=(count // BLOCK,),
        in_specs=[
            whole(sums.shape),
            rows(features),
            rows(features),
            rows(features),
            rows(features),
            rows(1),
            whole(weights[0].shape),
            whole(norms.shape),
        ],
        out_specs=[whole(sums.shape), rows(features), rows(width), rows(own)],
        out_shape=[
            struct(sums.shape, F32),
            struct((count, features), BF16),
            struct((count, width), BF16),
            struct((count, own), F32),
        ],
        compiler_params=params(),
        cost_estimate=lasting(0.2),
        name="feed_third",
    )(sums, part, recv, res, normed, inverse, weights[0], norms)


def spread_rows(block_ref, scratch, keep_ref, send_ref, which, kinds):
    features = scratch.shape[0]
    count = block_ref.shape[0]
    depth = features // count
    half = count // 2
    for slot in range(count):
        start = pl.multiple_of(block_ref[slot] * depth, depth)
        piece = scratch[pl.ds(start, depth), :]
        first = ((slot % half) * kinds + which) * depth
        if slot < half:
            keep_ref[first : first + depth, :] = piece
        else:
            send_ref[first : first + depth, :] = piece.astype(BF16)


def split_sums(total):
    high = total.astype(BF16)
    low = (total - high.astype(F32)).astype(BF16)
    return high, low, high.astype(F32) + low.astype(F32)


def feed_grad_kernel(block_ref, *refs):
    low_refs, upper_refs, act_refs, hidden_refs = (
        refs[k * CHUNKS : (k + 1) * CHUNKS] for k in range(4)
    )
    keep_ref, send_ref, scratch = refs[4 * CHUNKS :]
    scratch[...] = sum(dot_tn(a[...], b[...]) for a, b in zip(upper_refs, hidden_refs))
    spread_rows(block_ref, scratch, keep_ref, send_ref, 0, 2)
    scratch[...] = sum(dot_tn(a[...], b[...]) for a, b in zip(low_refs, act_refs))
    spread_rows(block_ref, scratch, keep_ref, send_ref, 1, 2)


def feed_grads(blocks, low, act, upper, hidden):
    count, features = low[0].shape
    units = act[0].shape[1]
    chunk = min(256, units)
    column = pl.BlockSpec((count, chunk), lambda b: (0, b))
    result = pl.BlockSpec((features, chunk), lambda b: (0, b))
    return pl.pallas_call(
        feed_grad_kernel,
        grid=(units // chunk,),
        in_specs=[pl.BlockSpec(memory_space=SMEM)]
        + [whole((count, features))] * (2 * CHUNKS)
        + [column] * (2 * CHUNKS),
        out_specs=[result] * 2,
        out_shape=[struct((features, units), F32), struct((features, units), BF16)],
        scratch_shapes=[pltpu.VMEM((features, chunk), F32)],
        compiler_params=params(),
        cost_estimate=lasting(1.0),
        name="feed_grads",
    )(blocks, *low, *upper, *act, *hidden)


def project_grad_kernel(block_ref, start_ref, *refs):
    query_refs, branch_refs, attended_refs = (
        refs[k * CHUNKS : (k + 1) * CHUNKS] for k in range(3)
    )
    token_ref, low_ref, high_ref, key_ref, value_ref = refs[3 * CHUNKS : 3 * CHUNKS + 5]
    keep_ref, send_ref, sum_ref, scratch = refs[3 * CHUNKS + 5 :]
    count = token_ref.shape[0]
    part = count // CHUNKS
    scratch[...] = sum(
        dot_tn(token_ref[k * part : (k + 1) * part, :], ref[...])
        for k, ref in enumerate(query_refs)
    )
    spread_rows(block_ref, scratch, keep_ref, send_ref, 0, 4)
    for which, ref in ((1, key_ref), (2, value_ref)):
        scratch[...] = (
            dot_tn(token_ref[...], ref[MAXDOC : MAXDOC + count, :])
            + dot_tn(low_ref[...], ref[PAD:MAXDOC, :])
            + dot_tn(high_ref[...], ref[MAXDOC + count : MAXDOC + count + HALO, :])
        )
        spread_rows(block_ref, scratch, keep_ref, send_ref, which, 4)
    scratch[...] = sum(dot_tn(a[...], b[...]) for a, b in zip(branch_refs, attended_refs))
    spread_rows(block_ref, scratch, keep_ref, send_ref, 3, 4)
    total = start_ref[...]
    place = lax.broadcasted_iota(jnp.int32, total.shape, 0)
    query_sum = sum(
        jnp.sum(ref[...].astype(F32), 0, keepdims=True) for ref in query_refs
    )
    value_sum = jnp.sum(value_ref[...].astype(F32), 0, keepdims=True)
    total = total + jnp.where(place == 0, query_sum, 0.0) + jnp.where(place == 1, value_sum, 0.0)
    height = keep_ref.shape[0]
    high, low, sum_ref[...] = split_sums(total)
    send_ref[height : height + SUM_ROWS, :] = high
    send_ref[height + SUM_ROWS :, :] = low


def project_grads(blocks, sums, tokens, low, high, query, key, value, branch, attended):
    features = tokens.shape[1]
    width = key.shape[1]
    half = blocks.shape[0] // 2
    depth = features // (2 * half)
    height = half * 4 * depth
    operands = (sums, *query, *branch, *attended, tokens, low, high, key, value)
    return pl.pallas_call(
        project_grad_kernel,
        grid=(1,),
        in_specs=[pl.BlockSpec(memory_space=SMEM)] + [whole(x.shape) for x in operands],
        out_specs=[
            whole((height, width)),
            whole((height + 2 * SUM_ROWS, width)),
            whole(sums.shape),
        ],
        out_shape=[
            struct((height, width), F32),
            struct((height + 2 * SUM_ROWS, width), BF16),
            struct(sums.shape, F32),
        ],
        scratch_shapes=[pltpu.VMEM((features, width), F32)],
        compiler_params=params(),
        cost_estimate=lasting(0.6),
        name="project_grads",
    )(blocks, *operands)


def fold_kernel(with_sums, keep_ref, arrived_ref, *refs):
    height = keep_ref.shape[0]
    size = height // 2
    if with_sums:
        start_ref, keep_out, send_out, sum_out = refs
    else:
        keep_out, send_out = refs
    keep_out[...] = keep_ref[:size, :] + arrived_ref[:size, :].astype(F32)
    send_out[:size, :] = (keep_ref[size:, :] + arrived_ref[size:height, :].astype(F32)).astype(BF16)
    if with_sums:
        high, low, sum_out[...] = split_sums(start_ref[...] + arrived_sums(arrived_ref, height))
        send_out[size : size + SUM_ROWS, :] = high
        send_out[size + SUM_ROWS :, :] = low


def arrived_sums(ref, height):
    return ref[height : height + SUM_ROWS, :].astype(F32) + ref[height + SUM_ROWS :, :].astype(F32)


def fold(keep, arrived, sums):
    height, width = keep.shape
    extra = arrived.shape[0] - height
    operands = (keep, arrived) + (() if sums is None else (sums,))
    shapes = [struct((height // 2, width), F32), struct((height // 2 + extra, width), BF16)]
    shapes += [] if sums is None else [struct(sums.shape, F32)]
    result = pl.pallas_call(
        functools.partial(fold_kernel, sums is not None),
        grid=(1,),
        in_specs=[whole(x.shape) for x in operands],
        out_specs=[whole(x.shape) for x in shapes],
        out_shape=shapes,
        compiler_params=params(),
        cost_estimate=lasting(0.2),
        name="fold",
    )(*operands)
    return result[0], result[1], (None if sums is None else result[2])


def finish_kernel(kinds, sum_kinds, keep_ref, arrived_ref, *refs):
    height = keep_ref.shape[0]
    if sum_kinds:
        start_ref, *refs = refs
    first = 0
    for kind, ref in zip(kinds, refs):
        depth = ref.shape[-2]
        for place in range(kind or 1):
            rows_here = slice(first, first + depth)
            total = keep_ref[rows_here, :] + arrived_ref[rows_here, :].astype(F32)
            if kind:
                ref[place] = total
            else:
                ref[...] = total
            first += depth
    if sum_kinds:
        total = start_ref[...] + arrived_sums(arrived_ref, height)
        first = 0
        for kind, ref in zip(sum_kinds, refs[len(kinds) :]):
            if ref.shape[0] == kind:
                ref[...] = total[first : first + kind, :]
            else:
                ref[...] = jnp.concatenate([total[first + k : first + k + 1] for k in range(kind)], 1)
            first += kind


def finish(keep, arrived, sums, kinds, sum_kinds):
    height, width = keep.shape
    depth = height // sum(kind or 1 for kind in kinds)
    operands = (keep, arrived) + (() if sums is None else (sums,))
    shapes = [struct((kind, depth, width) if kind else (depth, width), F32) for kind in kinds]
    shapes += [
        struct((kind, width) if kind == 2 else (1, kind * width), F32) for kind in sum_kinds
    ]
    return pl.pallas_call(
        functools.partial(finish_kernel, kinds, sum_kinds),
        grid=(1,),
        in_specs=[whole(x.shape) for x in operands],
        out_specs=[whole(x.shape) for x in shapes],
        out_shape=shapes,
        compiler_params=params(),
        cost_estimate=lasting(0.2),
        name="finish",
    )(*operands)


def token_grad_kernel(even_ref, *refs):
    query_refs, res_refs = refs[:CHUNKS], refs[CHUNKS : 2 * CHUNKS]
    key_ref, value_ref, *weight_refs = refs[2 * CHUNKS : 2 * CHUNKS + 5]
    own_ref, rim_ref, *out_refs = refs[2 * CHUNKS + 5 :]
    own_outs, rim_outs = out_refs[: len(out_refs) // 2], out_refs[len(out_refs) // 2 :]
    count, own = own_ref.shape
    even = even_ref[0] == 1

    def piece(start):
        return dot_nt(key_ref[start : start + BLOCK, :], weight_refs[1][...]) + dot_nt(
            value_ref[start : start + BLOCK, :], weight_refs[2][...]
        )

    def spread(value, start, stays_ref, leave_refs):
        stays_ref[start : start + BLOCK, :] = value[:, :own]
        for place, ref in enumerate(leave_refs, 1):
            lanes = slice(place * own, (place + 1) * own)
            ref[start : start + BLOCK, :] = value[:, lanes].astype(BF16)

    for start in range(0, HALO, BLOCK):
        low, high = piece(PAD + start), piece(MAXDOC + count + start)
        spread(jnp.where(even, high, low), start, rim_ref, rim_outs)
        spread(jnp.where(even, low, high), HALO + start, rim_ref, rim_outs)
    for start in range(0, count, BLOCK):
        chunk, inside = divmod(start, count // CHUNKS)
        total = piece(MAXDOC + start) + dot_nt(
            query_refs[chunk][inside : inside + BLOCK, :], weight_refs[0][...]
        )
        spread(total, start, own_ref, own_outs)
        own_ref[start : start + BLOCK, :] += res_refs[chunk][inside : inside + BLOCK, :]


def token_grads(even, query, res, key, value, weights):
    count = CHUNKS * query[0].shape[0]
    own = res[0].shape[1]
    leave = weights[0].shape[0] // own - 1
    operands = (*query, *res, key, value, *weights)
    shapes = [struct((count, own), F32), struct((2 * HALO, own), F32)]
    shapes += [struct((count, own), BF16)] * leave + [struct((2 * HALO, own), BF16)] * leave
    result = pl.pallas_call(
        token_grad_kernel,
        grid=(1,),
        in_specs=[pl.BlockSpec(memory_space=SMEM)] + [whole(x.shape) for x in operands],
        out_specs=[whole(x.shape) for x in shapes],
        out_shape=shapes,
        compiler_params=params(),
        cost_estimate=lasting(5.0),
        name="token_grads",
    )(even, *operands)
    return result[0], result[1], result[2 : 2 + leave], result[2 + leave :]


def rim_sum_kernel(rim_ref, *refs):
    *arrived_refs, inside_ref, across_ref = refs
    total = rim_ref[...] + sum(ref[...].astype(F32) for ref in arrived_refs)
    inside_ref[...] = total[:HALO].astype(BF16)
    across_ref[...] = total[HALO:].astype(BF16)


def rim_sum(rim, arrived):
    own = rim.shape[1]
    operands = (rim, *arrived)
    return pl.pallas_call(
        rim_sum_kernel,
        grid=(1,),
        in_specs=[whole(x.shape) for x in operands],
        out_specs=[whole((HALO, own))] * 2,
        out_shape=[struct((HALO, own), BF16)] * 2,
        compiler_params=params(),
        cost_estimate=lasting(0.3),
        name="rim_sum",
    )(*operands)


def token_sum_kernel(even_ref, own_ref, inside_ref, across_ref, *refs):
    *arrived_refs, out_ref = refs
    even = even_ref[0] == 1
    inside, across = inside_ref[...].astype(F32), across_ref[...].astype(F32)
    low, high = jnp.where(even, across, inside), jnp.where(even, inside, across)
    rest = own_ref.shape[0] - HALO
    for start in range(0, own_ref.shape[0], BLOCK):
        rows_here = slice(start, start + BLOCK)
        piece = own_ref[rows_here, :] + sum(ref[rows_here, :].astype(F32) for ref in arrived_refs)
        if start < HALO:
            piece = piece + low[rows_here, :]
        if start >= rest:
            piece = piece + high[start - rest : start - rest + BLOCK, :]
        out_ref[rows_here, :] = piece.astype(BF16)


def token_sum(even, own, inside, across, arrived):
    operands = (own, inside, across, *arrived)
    return pl.pallas_call(
        token_sum_kernel,
        grid=(1,),
        in_specs=[pl.BlockSpec(memory_space=SMEM)] + [whole(x.shape) for x in operands],
        out_specs=whole(own.shape),
        out_shape=struct(own.shape, BF16),
        compiler_params=params(),
        cost_estimate=lasting(0.3),
        name="token_sum",
    )(even, *operands)


def from_next(x, axis, step):
    count = lax.axis_size(axis)
    return lax.ppermute(x, axis, [((i + step) % count, i) for i in range(count)])


def others(x):
    return [from_next(x, "col", step) for step in range(1, lax.axis_size("col"))]


def bits_of(count):
    return [1 << place for place in range(count.bit_length() - 1)]


def orders_of(count):
    high = bits_of(count)[:0:-1]
    return high + [1], high[2:] + high[:2] + [1]


def slots_of(order, distance):
    return sum(((distance & bit) // bit) << place for place, bit in enumerate(order))


def distances_of(order, slots):
    return sum(((slots >> place) & 1) * bit for place, bit in enumerate(order))


def with_partner(x, step):
    count = lax.axis_size("row")
    orders = orders_of(count)
    return lax.ppermute(x, "row", [(i, i ^ orders[i % 2][step]) for i in range(count)])


def with_next(inside, across):
    count = lax.axis_size("row")
    pairs = [(i, i + 1 if i % 2 else i - 1) for i in range(1, count - 1)]
    return (
        lax.ppermute(inside, "row", [(i, i ^ 1) for i in range(count)]),
        lax.ppermute(across, "row", pairs),
    )


def after(value, *needed):
    return lax.optimization_barrier((value, *needed))[0]


class Gather:
    def __init__(self, shard):
        self.held, self.step = shard[None], 0
        self.count = len(bits_of(lax.axis_size("row")))
        self.move()

    def move(self):
        self.arrived = with_partner(self.held, self.step)
        self.step += 1

    def put(self, *needed):
        self.held = jnp.concatenate([after(self.held, *needed), self.arrived], 0)
        self.move()


class Reduction:
    def __init__(self, keep, send, sums, kinds, sum_kinds=()):
        self.step = len(bits_of(lax.axis_size("row")))
        self.keep, self.send, self.sums = keep, send, sums
        self.kinds, self.sum_kinds = kinds, sum_kinds
        self.result = None
        self.move()

    def move(self):
        self.step -= 1
        self.arrived = with_partner(self.send, self.step)

    def add(self, *needed):
        keep = after(self.keep, *needed)
        if self.step == 0:
            self.result = finish(keep, self.arrived, self.sums, self.kinds, self.sum_kinds)
        else:
            self.keep, self.send, self.sums = fold(keep, self.arrived, self.sums)
            self.move()


def exchanged(part):
    arrived = others(part)
    if len(arrived) == 1:
        return arrived[0]
    shift = part.shape[1] // (len(arrived) + 1)
    total = sum(
        jnp.roll(x.astype(F32), step * shift, 1) for step, x in enumerate(arrived, 1)
    )
    return total.astype(BF16)


def on_device(
    tokens,
    prev_logits,
    doc_lengths,
    qkv_weight,
    qv_bias,
    out_weight,
    out_bias,
    up_weight,
    up_bias,
    down_weight,
    norm_gain,
    norm_shift,
    out_grad,
    logit_grad,
):
    count, own = tokens.shape
    width = qkv_weight.shape[2]
    row_count, col_count = lax.axis_size("row"), lax.axis_size("col")
    row_index, col_index = lax.axis_index("row"), lax.axis_index("col")
    token_count = count * row_count
    swap = col_count == 2
    hidden_rows = up_bias.shape[0] // own

    odd = row_index % 2 == 1
    places = jnp.arange(row_count, dtype=jnp.int32)
    offset = col_index * (row_count // col_count)
    distance = ((places + offset) % row_count) ^ row_index
    half = row_count // 2
    even_order, odd_order = (order[:-1] for order in orders_of(row_count))
    turned = odd ^ (distance % 2 == 1)
    slots = jnp.where(turned, slots_of(odd_order, distance), slots_of(even_order, distance))
    slots = slots + half * (distance % 2)
    turned = odd ^ (places >= half)
    met = jnp.where(turned, distances_of(odd_order, places), distances_of(even_order, places))
    blocks = (((met + (places >= half)) ^ row_index) - offset) % row_count

    even = 1 - row_index % 2
    even = even.astype(jnp.int32)[None]

    def dense_of(banded, fill, chunk, *needed):
        dense = to_dense(after(banded, *needed), lengths, fill, token_count, chunk)
        return dense

    prev_logits = pltpu.with_memory_space_constraint(prev_logits, pltpu.HBM)
    logit_grad = pltpu.with_memory_space_constraint(logit_grad, pltpu.HBM)

    out_turned = out_weight.T
    out_other = others(out_turned)
    qkv_rows = Gather(qkv_weight)
    tokens_other = others(after(tokens, out_turned))
    feed_rows = Gather(jnp.concatenate([out_turned, *out_other, up_weight, down_weight.T], 1))
    tail = row_index % 2 * (count - HALO)
    ready = after(tokens, feed_rows.held)
    inside, across = with_next(
        lax.dynamic_slice_in_dim(ready, count - HALO - tail, HALO, 0),
        lax.dynamic_slice_in_dim(ready, tail, HALO, 0),
    )
    qkv_rows.put(feed_rows.held)
    inside_other, across_other = others(inside), others(across)
    feed_rows.put(qkv_rows.held)
    qkv_rows.put(feed_rows.held, *tokens_other)
    lengths = jnp.concatenate(
        [after(doc_lengths, qkv_rows.held).reshape(-1), (row_index * count)[None]]
    )
    prev_dense = [
        dense_of(prev_logits, MASKED_SCORE, 0, qkv_rows.held, feed_rows.held, inside, across)
    ]
    grad_other = others(after(out_grad, *inside_other))
    while qkv_rows.step < qkv_rows.count:
        qkv_rows.put(prev_dense[0], *inside_other, *across_other)
    feed_rows.put(qkv_rows.held)
    tokens_full, query, key, value, low_tokens, high_tokens, *projections = project(
        slots, even, qkv_rows.held, qkv_rows.arrived, qv_bias, [after(tokens, feed_rows.held), *tokens_other],
        [inside, *inside_other], [across, *across_other],
    )
    grad_full = jnp.concatenate([after(out_grad, query)] + grad_other, 1)
    norms = jnp.concatenate([after(norm_gain, query), norm_shift, out_bias], 0)
    norms = jnp.concatenate([norms] + others(norms), 1)
    scores, probs, attended, attended_other = [], [], [], []
    for chunk in range(CHUNKS):
        score, prob, mix = attend_forward(
            after(query, feed_rows.held) if chunk else query, key, value, prev_dense[chunk], chunk
        )
        scores.append(score)
        probs.append(prob)
        attended.append(mix)
        attended_other.append(jnp.concatenate(others(mix), 1))
        if chunk == 0:
            prev_dense.append(dense_of(prev_logits, MASKED_SCORE, 1, mix, norms, grad_full))
            while feed_rows.step < feed_rows.count:
                feed_rows.put(prev_dense[1], attended_other[0])
    other_out, *weights = in_order(
        slots, after(feed_rows.held, mix), feed_rows.arrived,
        (width, (col_count - 1) * width, up_weight.shape[1], up_weight.shape[1]),
    )
    weights[0], other_out = other_out, weights[0]
    ups = up_bias[None]
    firsts, logit_dense = [], []
    for chunk in range(CHUNKS):
        result = feed_first(
            attended[chunk], attended_other[chunk], tokens_full, other_out, weights, norms, ups,
            chunk,
        )
        if chunk == 0:
            logit_dense.append(dense_of(logit_grad, 0.0, 0, result[-1]))
            ups = after(ups, logit_dense[0])
        firsts.append((*result, exchanged(result[-1])))
    normed, inverse, upper, act, slope, down_part, down_other = zip(*firsts)

    new_logits = to_band([after(scores[0], down_part[-1])], True)
    sums = after(jnp.zeros((SUM_ROWS, own), F32), new_logits)
    output = None
    seconds = []
    for chunk in range(CHUNKS):
        sums, output, *result = feed_second(
            swap, sums, output, down_part[chunk], down_other[chunk],
            normed[chunk], grad_full, slope[chunk], weights, norms, chunk,
        )
        seconds.append((*result, exchanged(result[-1])))
    res_two, ffn_low, hidden_grad, lower_part, lower_other = zip(*seconds)
    keep, send = feed_grads(blocks, ffn_low, act, upper, hidden_grad)
    feed_sum = Reduction(keep, send, None, (0, 0))
    sums = after(sums, keep)

    branch_low, res_one, query_grad, prev_dense_grad = [], [], [], []
    partial = None
    for chunk in range(CHUNKS):
        sums, low, attended_grad, res = feed_third(
            swap, sums, width, lower_part[chunk], lower_other[chunk], res_two[chunk],
            normed[chunk], inverse[chunk], weights, norms,
        )
        branch_low.append(low)
        res_one.append(res)
        prev, query_part, *partial = attend_backward(
            attended_grad, query, key, value, probs[chunk], logit_dense[chunk], chunk, partial
        )
        if chunk == 0:
            feed_sum.add(query_part)
            logit_dense.append(dense_of(logit_grad, 0.0, 1, feed_sum.keep))
            sums = after(sums, logit_dense[1])
        prev_dense_grad.append(prev)
        query_grad.append(query_part)
    key_grad, value_grad = partial
    feed_sum.add(query_grad[-1])
    keep, send, sums = project_grads(
        blocks, after(sums, feed_sum.keep), tokens_full, low_tokens, high_tokens, query_grad,
        key_grad, value_grad, branch_low, attended,
    )
    last_sum = Reduction(keep, send, sums, (3, 0), (2, 2, 2, 2, hidden_rows))
    center, rim, center_parts, rim_parts = token_grads(
        even, query_grad, res_one, after(key_grad, keep), value_grad, projections
    )

    def spread_over(parts):
        return [from_next(part, "col", -step) for step, part in enumerate(parts, 1)]

    last_sum.add(center)
    rim_parts = spread_over(rim_parts)
    center_parts = spread_over(after(x, rim) for x in center_parts)
    prev_dense_grad[0] = after(prev_dense_grad[0], last_sum.keep)
    prev_grad = to_band(prev_dense_grad, False)
    last_sum.add(prev_grad)
    inside, across = rim_sum(after(rim, last_sum.keep), rim_parts)
    feed_sum.add(inside)
    inside, across = with_next(inside, across)
    last_sum.add(feed_sum.keep)
    for chunk in range(1, CHUNKS):
        new_logits = to_band([after(scores[chunk], last_sum.keep)], True, chunk, new_logits)
    tokens_grad = token_sum(even, after(center, new_logits), inside, across, center_parts)
    while feed_sum.result is None:
        feed_sum.add(tokens_grad)
    while last_sum.result is None:
        last_sum.add(feed_sum.result[0])
    qkv_grad, out_grad_rows, qv_sum, bias_sum, gain_sum, shift_sum, hidden_sum = last_sum.result
    up_grad, down_grad = feed_sum.result
    return (
        output,
        new_logits,
        tokens_grad,
        prev_grad,
        qkv_grad,
        qv_sum,
        out_grad_rows.T,
        bias_sum,
        up_grad,
        hidden_sum.reshape(-1),
        down_grad.T,
        gain_sum,
        shift_sum,
    )


def solution(mesh):
    return jax.shard_map(
        on_device,
        mesh=mesh,
        in_specs=(
            P("row", "col"),
            P("col", "row", None),
            P(),
            P(None, "row", "col"),
            P(None, "col"),
            P("col", "row"),
            P(None, "col"),
            P("row", "col"),
            P("col"),
            P("col", "row"),
            P(None, "col"),
            P(None, "col"),
            P("row", "col"),
            P("col", "row", None),
        ),
        out_specs=(
            P("row", "col"),
            P("col", "row", None),
            P("row", "col"),
            P("col", "row", None),
            P(None, "row", "col"),
            P(None, "col"),
            P("col", "row"),
            P(None, "col"),
            P("row", "col"),
            P("col"),
            P("col", "row"),
            P(None, "col"),
            P(None, "col"),
        ),
        check_vma=False,
    )
```

```python
import functools

import jax
import jax.numpy as jnp
from jax import lax
from jax.experimental import pallas as pl
from jax.experimental.pallas import tpu as pltpu
from jax.sharding import PartitionSpec as P

D = 512
HEAD_DIM = 64
MAXDOC = 512
BAND = 2 * MAXDOC
BLOCK = 128
WINDOW = BAND + BLOCK
HALO = MAXDOC - 128
PAD = MAXDOC - HALO

EPSILON = 1e-05
MASKED_SCORE = -1e30
ERF_RATE = 0.7071067811865476
DENSITY_RATE = 0.3989422804014327

F32 = jnp.float32
BF16 = jnp.bfloat16
SMEM = pltpu.MemorySpace.SMEM
VMEM_LIMIT = 24 << 20
CHUNKS = 2
SUM_ROWS = 16
FLOPS_PER_MICROSECOND = 1.0e9


def dot_nn(a, b):
    return lax.dot_general(a, b, (((1,), (0,)), ((), ())), preferred_element_type=F32)


def dot_nt(a, b):
    return lax.dot_general(a, b, (((1,), (1,)), ((), ())), preferred_element_type=F32)


def dot_tn(a, b):
    return lax.dot_general(a, b, (((0,), (0,)), ((), ())), preferred_element_type=F32)


def params():
    return pltpu.CompilerParams(
        dimension_semantics=("arbitrary",), vmem_limit_bytes=VMEM_LIMIT
    )


def lasting(microseconds):
    return pl.CostEstimate(
        flops=int(microseconds * FLOPS_PER_MICROSECOND), bytes_accessed=0, transcendentals=0
    )


def whole(shape):
    return pl.BlockSpec(shape, lambda b: (0,) * len(shape))


def rows(width, first=0):
    return pl.BlockSpec((BLOCK, width), lambda b: (b + first, 0))


def heads_block(heads, width, first=0):
    return pl.BlockSpec((heads, BLOCK, width), lambda b: (0, b + first, 0))


def struct(shape, dtype):
    return jax.ShapeDtypeStruct(shape, dtype)


def segment_of(positions, lengths_ref, documents, token_count):
    found = jnp.zeros(positions.shape, jnp.int32)
    end = jnp.int32(0)
    for document in range(documents):
        end = end + lengths_ref[document]
        found = found + (positions >= end).astype(jnp.int32)
    return jnp.where((positions >= 0) & (positions < token_count), found, -1)


def dense_kernel(fill, token_count, offset, lengths_ref, band_ref, dense_ref):
    documents = lengths_ref.shape[0] - 1
    first = lengths_ref[documents] + (pl.program_id(0) + offset) * BLOCK
    query = first + lax.broadcasted_iota(jnp.int32, (BLOCK, 1), 0)
    key = first - MAXDOC + lax.broadcasted_iota(jnp.int32, (1, WINDOW), 1)
    same = segment_of(query, lengths_ref, documents, token_count) == segment_of(
        key, lengths_ref, documents, token_count
    )
    for head in range(band_ref.shape[0]):
        wide = jnp.concatenate(
            [band_ref[head].astype(F32), jnp.zeros((BLOCK, BLOCK), F32)], 1
        )
        turned = pltpu.roll(wide, 0, 1, stride=1, stride_axis=0)
        dense_ref[head] = jnp.where(same, turned, fill).astype(BF16)


def to_dense(banded, lengths, fill, token_count, chunk):
    heads, count, _ = banded.shape
    count //= CHUNKS
    offset = chunk * (count // BLOCK)
    return pl.pallas_call(
        functools.partial(dense_kernel, fill, token_count, offset),
        grid=(count // BLOCK,),
        in_specs=[pl.BlockSpec(memory_space=SMEM), heads_block(heads, BAND, offset)],
        out_specs=heads_block(heads, WINDOW),
        out_shape=struct((heads, count, WINDOW), BF16),
        compiler_params=params(),
        cost_estimate=lasting(8.0 if fill and chunk == 0 else 1.0),
        name="to_dense",
    )(lengths, banded)


def band_kernel(masked, chunks, *refs):
    dense_refs, band_ref = refs[:chunks], refs[-1]
    lane = lax.broadcasted_iota(jnp.int32, (BLOCK, BLOCK), 1)
    row = lax.broadcasted_iota(jnp.int32, (BLOCK, BLOCK), 0)
    source = (lane + row) & (BLOCK - 1)
    near = lane + row < BLOCK
    steps = pl.num_programs(0) // chunks

    def turn(dense_ref):
        for head in range(band_ref.shape[0]):
            pieces = []
            for place in range(WINDOW // BLOCK):
                piece = dense_ref[head, :, place * BLOCK : (place + 1) * BLOCK].astype(F32)
                if masked:
                    piece = jnp.where(piece < 0.5 * MASKED_SCORE, 0.0, piece)
                pieces.append(jnp.take_along_axis(piece, source, axis=1))
            for place in range(BAND // BLOCK):
                band_ref[head, :, place * BLOCK : (place + 1) * BLOCK] = jnp.where(
                    near, pieces[place], pieces[place + 1]
                ).astype(BF16)

    for chunk, dense_ref in enumerate(dense_refs):

        @pl.when(pl.program_id(0) // steps == chunk)
        def _():
            turn(dense_ref)


def to_band(chunks, masked, first=0, held=None):
    heads, count, _ = chunks[0].shape
    steps = count // BLOCK

    def block_of(chunk):
        return pl.BlockSpec(
            (heads, BLOCK, WINDOW), lambda b: (0, jnp.clip(b - chunk * steps, 0, steps - 1), 0)
        )

    return pl.pallas_call(
        functools.partial(band_kernel, masked, len(chunks)),
        grid=(len(chunks) * steps,),
        in_specs=[block_of(chunk) for chunk in range(len(chunks))]
        + ([] if held is None else [pl.BlockSpec(memory_space=pl.ANY)]),
        out_specs=heads_block(heads, BAND, first * steps),
        out_shape=struct((heads, CHUNKS * count, BAND), BF16),
        input_output_aliases={} if held is None else {len(chunks): 0},
        compiler_params=params(),
        cost_estimate=lasting(5.0 if masked and held is None else 0.3),
        name="to_band",
    )(*chunks, *(() if held is None else (held,)))


def head_split(block, size):
    if size == 1:
        return block
    lane = lax.broadcasted_iota(jnp.int32, block.shape, 1)
    return jnp.concatenate(
        [
            jnp.where((lane >= h * HEAD_DIM) & (lane < (h + 1) * HEAD_DIM), block, 0)
            for h in range(size)
        ],
        0,
    )


def head_join(stacked, size):
    if size == 1:
        return stacked
    height = stacked.shape[0] // size
    joined = stacked[:height]
    lane = lax.broadcasted_iota(jnp.int32, joined.shape, 1)
    for h in range(1, size):
        joined = jnp.where(lane >= h * HEAD_DIM, stacked[h * height : (h + 1) * height], joined)
    return joined


def project_kernel(
    parts, slot_ref, even_ref, near_ref, far_ref, bias_ref, *refs
):
    token_refs, inside_refs, across_refs = (refs[k * parts : (k + 1) * parts] for k in range(3))
    all_ref, query_ref, key_ref, value_ref, low_ref, high_ref, *weight_refs = refs[3 * parts :]
    half, _, depth, _ = near_ref.shape
    count, width = token_refs[0].shape

    def put(place, source_ref, slot):
        for which, ref in enumerate(weight_refs):
            ref[place * depth : (place + 1) * depth, :] = source_ref[slot, which]

    for place in range(2 * half):
        slot = slot_ref[place]

        @pl.when(slot < half)
        def _():
            put(place, near_ref, slot)

        @pl.when(slot >= half)
        def _():
            put(place, far_ref, slot - half)

    even = even_ref[0] == 1
    for place, (own_ref, inside_ref, across_ref) in enumerate(
        zip(token_refs, inside_refs, across_refs)
    ):
        lanes = slice(place * width, (place + 1) * width)
        inside, across = inside_ref[...], across_ref[...]
        all_ref[:, lanes] = own_ref[...]
        low_ref[:, lanes] = jnp.where(even, across, inside)
        high_ref[:, lanes] = jnp.where(even, inside, across)
    own, low_rows, high_rows = all_ref[...], low_ref[...], high_ref[...]
    query = (dot_nn(own, weight_refs[0][...]) + bias_ref[0:1, :]).astype(BF16)
    empty = jnp.zeros((PAD, query.shape[1]), BF16)
    query_ref[...] = query * jnp.asarray(HEAD_DIM ** (-0.5), BF16)
    for out_ref, which in ((key_ref, 1), (value_ref, 2)):
        shift = bias_ref[1:2, :] if which == 2 else 0.0
        weight = weight_refs[which][...]
        out_ref[0:PAD, :] = empty
        out_ref[PAD:MAXDOC, :] = (dot_nn(low_rows, weight) + shift).astype(BF16)
        out_ref[MAXDOC : MAXDOC + count, :] = (dot_nn(own, weight) + shift).astype(BF16)
        out_ref[MAXDOC + count : MAXDOC + count + HALO, :] = (
            dot_nn(high_rows, weight) + shift
        ).astype(BF16)
        out_ref[MAXDOC + count + HALO :, :] = empty


def project(slots, even, near, far, bias, tokens, inside, across):
    count, part = tokens[0].shape
    features = len(tokens) * part
    width = near.shape[3]
    operands = (near, far, bias, *tokens, *inside, *across)
    extended = (count + BAND, width)
    shapes = [(count, features), (count, width), extended, extended]
    shapes += [(HALO, features)] * 2 + [(features, width)] * 3
    return pl.pallas_call(
        functools.partial(project_kernel, len(tokens)),
        grid=(1,),
        in_specs=[pl.BlockSpec(memory_space=SMEM)] * 2 + [whole(x.shape) for x in operands],
        out_specs=[whole(shape) for shape in shapes],
        out_shape=[struct(shape, BF16) for shape in shapes],
        compiler_params=params(),
        cost_estimate=lasting(2.0),
        name="project",
    )(slots, even, *operands)


def by_edge(block, last, body):
    edge = (block == 0) | (block == last)

    @pl.when(edge)
    def _():
        body(BLOCK, WINDOW - 2 * BLOCK)

    @pl.when(jnp.logical_not(edge))
    def _():
        body(0, WINDOW)


def forward_kernel(
    offset, query_ref, key_ref, value_ref, prev_ref, score_ref, prob_ref, attended_ref
):
    heads = prev_ref.shape[0]
    size = min(2, heads)
    span = size * HEAD_DIM
    block = pl.program_id(0) + offset

    def body(first, width):
        window = pl.ds(pl.multiple_of(block * BLOCK + first, BLOCK), width)
        inside = slice(first, first + width)
        for group in range(heads // size):
            lanes = slice(group * span, (group + 1) * span)
            query = head_split(query_ref[:, lanes], size)
            dense = dot_nt(query, key_ref[window, lanes])
            weights = []
            for h in range(size):
                head = group * size + h
                score = dense[h * BLOCK : (h + 1) * BLOCK] + prev_ref[head, :, inside].astype(F32)
                score_ref[head, :, inside] = score.astype(BF16)
                if first:
                    empty = jnp.full((BLOCK, first), MASKED_SCORE, BF16)
                    score_ref[head, :, :first] = empty
                    score_ref[head, :, first + width :] = empty
                peak = jnp.max(score, -1, keepdims=True)
                grown = jnp.exp(score - peak)
                total = jnp.sum(grown, -1, keepdims=True)
                prob = (grown * (1.0 / total)).astype(BF16)
                prob_ref[head, :, inside] = prob
                weights.append(prob)
            mixed = dot_nn(jnp.concatenate(weights, 0), value_ref[window, lanes])
            attended_ref[:, lanes] = head_join(mixed, size).astype(BF16)

    by_edge(block, key_ref.shape[0] // BLOCK - WINDOW // BLOCK, body)


def attend_forward(query, key, value, prev, chunk):
    heads, count, _ = prev.shape
    width = query.shape[1]
    offset = chunk * (count // BLOCK)
    return pl.pallas_call(
        functools.partial(forward_kernel, offset),
        grid=(count // BLOCK,),
        in_specs=[
            rows(width, offset),
            whole(key.shape),
            whole(value.shape),
            heads_block(heads, WINDOW),
        ],
        out_specs=[heads_block(heads, WINDOW), heads_block(heads, WINDOW), rows(width)],
        out_shape=[
            struct((heads, count, WINDOW), BF16),
            struct((heads, count, WINDOW), BF16),
            struct((count, width), BF16),
        ],
        compiler_params=params(),
        cost_estimate=lasting(3.8),
        name="attend_forward",
    )(query, key, value, prev)


def backward_kernel(
    offset, last, grad_ref, query_ref, key_ref, value_ref, prob_ref, logit_ref, *refs
):
    if last:
        key_start, value_start = refs[:2]
        prev_ref, query_grad_ref, key_grad_ref, value_grad_ref, key_sum, value_sum = refs[2:]
    else:
        prev_ref, query_grad_ref, key_sum, value_sum = refs
    step = pl.program_id(0)
    heads = prob_ref.shape[0]
    size = min(2, heads)
    span = size * HEAD_DIM

    @pl.when(step == 0)
    def _():
        if last:
            key_sum[...] = key_start[...]
            value_sum[...] = value_start[...]
        else:
            key_sum[...] = jnp.zeros_like(key_sum)
            value_sum[...] = jnp.zeros_like(value_sum)

    block = step + offset

    def body(first, width):
        window = pl.ds(pl.multiple_of(block * BLOCK + first, BLOCK), width)
        inside = slice(first, first + width)
        for group in range(heads // size):
            lanes = slice(group * span, (group + 1) * span)
            query = head_split(query_ref[:, lanes], size)
            grad = head_split(grad_ref[:, lanes], size)
            key = key_ref[window, lanes]
            prob_grad = dot_nt(grad, value_ref[window, lanes])
            probs, scores = [], []
            for h in range(size):
                head = group * size + h
                low = prob_ref[head, :, inside]
                prob = low.astype(F32)
                slope = prob_grad[h * BLOCK : (h + 1) * BLOCK]
                inner = jnp.sum(prob * slope, -1, keepdims=True)
                score = prob * (slope - inner) + logit_ref[head, :, inside].astype(F32)
                score = score.astype(BF16)
                prev_ref[head, :, inside] = score
                if first:
                    empty = jnp.zeros((BLOCK, first), BF16)
                    prev_ref[head, :, :first] = empty
                    prev_ref[head, :, first + width :] = empty
                probs.append(low)
                scores.append(score)
            stacked = jnp.concatenate(scores, 0)
            mixed = head_join(dot_nn(stacked, key), size) * HEAD_DIM ** (-0.5)
            query_grad_ref[:, lanes] = mixed.astype(BF16)
            key_sum[lanes, window] += dot_tn(query, stacked)
            value_sum[lanes, window] += dot_tn(grad, jnp.concatenate(probs, 0))

    by_edge(block, key_ref.shape[0] // BLOCK - WINDOW // BLOCK, body)

    if last:

        @pl.when(step == pl.num_programs(0) - 1)
        def _():
            key_grad_ref[...] = key_sum[...].astype(BF16).T
            value_grad_ref[...] = value_sum[...].astype(BF16).T


def attend_backward(grad, query, key, value, prob, logit, chunk, sums):
    heads, count, _ = prob.shape
    extended, width = key.shape
    offset = chunk * (count // BLOCK)
    last = sums is not None
    turned = (width, extended)
    scratch = [pltpu.VMEM(turned, F32), pltpu.VMEM(turned, F32)] if last else []
    ends = [whole((extended, width))] * 2 if last else [whole(turned)] * 2
    end_shapes = [struct((extended, width), BF16)] * 2 if last else [struct(turned, F32)] * 2
    return pl.pallas_call(
        functools.partial(backward_kernel, offset, last),
        grid=(count // BLOCK,),
        in_specs=[
            rows(width),
            rows(width, offset),
            whole((extended, width)),
            whole((extended, width)),
            heads_block(heads, WINDOW),
            heads_block(heads, WINDOW),
        ]
        + ([whole(turned)] * 2 if last else []),
        out_specs=[heads_block(heads, WINDOW), rows(width)] + ends,
        out_shape=[struct((heads, count, WINDOW), BF16), struct((count, width), BF16)]
        + end_shapes,
        scratch_shapes=scratch,
        compiler_params=params(),
        cost_estimate=lasting(3.0 if last else 20.0),
        name="attend_backward",
    )(grad, query, key, value, prob, logit, *(sums or ()))


def order_kernel(slot_ref, near_ref, far_ref, *out_refs):
    half, depth, _ = near_ref.shape

    def put(place, source_ref, slot):
        first = 0
        for out_ref in out_refs:
            last = first + out_ref.shape[1]
            out_ref[place * depth : (place + 1) * depth, :] = source_ref[slot, :, first:last]
            first = last

    for place in range(2 * half):
        slot = slot_ref[place]

        @pl.when(slot < half)
        def _():
            put(place, near_ref, slot)

        @pl.when(slot >= half)
        def _():
            put(place, far_ref, slot - half)


def in_order(slots, near, far, widths):
    half, depth, _ = near.shape
    shapes = [(2 * half * depth, width) for width in widths]
    return pl.pallas_call(
        order_kernel,
        grid=(1,),
        in_specs=[pl.BlockSpec(memory_space=SMEM), whole(near.shape), whole(far.shape)],
        out_specs=[whole(shape) for shape in shapes],
        out_shape=[struct(shape, BF16) for shape in shapes],
        compiler_params=params(),
        cost_estimate=lasting(0.9),
        name="in_order",
    )(slots, near, far)


def mean_of(x):
    return jnp.sum(x, -1, keepdims=True) * (1.0 / D)


def normalized(hidden):
    mean = mean_of(hidden)
    inverse = lax.rsqrt(mean_of(hidden * hidden) - mean * mean + EPSILON)
    return (hidden - mean) * inverse, inverse


def norm_back(upstream, normed, inverse):
    return inverse * (upstream - mean_of(upstream) - normed * mean_of(upstream * normed))


def added(own_ref, other_ref, swap):
    other = other_ref[...]
    if swap:
        middle = other.shape[1] // 2
        other = jnp.concatenate([other[:, middle:], other[:, :middle]], 1)
    return own_ref[...].astype(F32) + other.astype(F32)


def first_kernel(
    own_ref, other_ref, token_ref, other_out_ref, out_ref, up_ref, down_ref, norm_ref,
    up_bias_ref, normed_ref, inverse_ref, upper_ref, act_ref, slope_ref, part_ref,
):
    branch = dot_nt(own_ref[...], out_ref[...]) + dot_nt(other_ref[...], other_out_ref[...])
    hidden = token_ref[...].astype(F32) + branch + norm_ref[4:5, :]
    normed, inverse = normalized(hidden)
    normed_ref[...] = normed
    inverse_ref[...] = inverse
    upper = (normed * norm_ref[0:1, :] + norm_ref[2:3, :]).astype(BF16)
    upper_ref[...] = upper
    pre = dot_nn(upper, up_ref[...]) + up_bias_ref[...]
    share = 0.5 * (1.0 + lax.erf(pre * ERF_RATE))
    act = (pre * share).astype(BF16)
    act_ref[...] = act
    slope_ref[...] = (share + pre * jnp.exp(-0.5 * pre * pre) * DENSITY_RATE).astype(BF16)
    part_ref[...] = dot_nt(act, down_ref[...]).astype(BF16)


def feed_first(own, other, tokens, other_out, weights, norms, up_bias, chunk):
    count, width = own.shape
    features = tokens.shape[1]
    units = up_bias.shape[1]
    return pl.pallas_call(
        first_kernel,
        grid=(count // BLOCK,),
        in_specs=[
            rows(width),
            rows(other.shape[1]),
            rows(features, chunk * (count // BLOCK)),
            whole(other_out.shape),
            *(whole(x.shape) for x in weights),
            whole(norms.shape),
            whole(up_bias.shape),
        ],
        out_specs=[
            rows(features),
            rows(1),
            rows(features),
            rows(units),
            rows(units),
            rows(features),
        ],
        out_shape=[
            struct((count, features), F32),
            struct((count, 1), F32),
            struct((count, features), BF16),
            struct((count, units), BF16),
            struct((count, units), BF16),
            struct((count, features), BF16),
        ],
        compiler_params=params(),
        cost_estimate=lasting(1.0),
        name="feed_first",
    )(own, other, tokens, other_out, *weights, norms, up_bias)


def add_sums(start_ref, sum_ref, first, values):
    @pl.when(pl.program_id(0) == 0)
    def _():
        sum_ref[...] = start_ref[...]

    for place, value in enumerate(values):
        sum_ref[first + place : first + place + 1, :] += jnp.sum(value, 0, keepdims=True)


def second_kernel(
    swap, start_ref, part_ref, recv_ref, normed_ref, grad_ref, slope_ref, up_ref, down_ref,
    norm_ref, *refs,
):
    sum_ref, output_ref, res_ref, low_ref, hidden_ref, lower_ref = refs[-6:]
    own = output_ref.shape[1]
    upper = normed_ref[...] * norm_ref[0:1, :] + norm_ref[2:3, :]
    hidden = upper + added(part_ref, recv_ref, swap) + norm_ref[5:6, :]
    normed, inverse = normalized(hidden)
    output_ref[...] = (
        normed[:, :own] * norm_ref[1:2, :own] + norm_ref[3:4, :own]
    ).astype(BF16)
    grad = grad_ref[...].astype(F32)
    res = norm_back(grad * norm_ref[1:2, :], normed, inverse)
    res_ref[...] = res
    low = res.astype(BF16)
    low_ref[...] = low
    act_grad = dot_nn(low, down_ref[...])
    hidden_grad = (act_grad * slope_ref[...].astype(F32)).astype(BF16)
    hidden_ref[...] = hidden_grad
    lower_ref[...] = dot_nt(hidden_grad, up_ref[...]).astype(BF16)
    wide = hidden_grad.astype(F32)
    add_sums(start_ref, sum_ref, 3, [low[:, :own].astype(F32)])
    for place, value in (
        (5, grad[:, :own] * normed[:, :own]),
        (7, grad[:, :own]),
        *((8 + k, wide[:, k * own : (k + 1) * own]) for k in range(wide.shape[1] // own)),
    ):
        sum_ref[place : place + 1, :] += jnp.sum(value, 0, keepdims=True)


def feed_second(swap, sums, held, part, recv, normed, grad, slope, weights, norms, chunk):
    count, features = part.shape
    own = sums.shape[1]
    units = slope.shape[1]
    offset = chunk * (count // BLOCK)
    return pl.pallas_call(
        functools.partial(second_kernel, swap),
        grid=(count // BLOCK,),
        in_specs=[
            whole(sums.shape),
            rows(features),
            rows(features),
            rows(features),
            rows(features, offset),
            rows(units),
            *(whole(x.shape) for x in weights[1:]),
            whole(norms.shape),
            *([] if held is None else [pl.BlockSpec(memory_space=pl.ANY)]),
        ],
        out_specs=[
            whole(sums.shape),
            rows(own, offset),
            rows(features),
            rows(features),
            rows(units),
            rows(features),
        ],
        out_shape=[
            struct(sums.shape, F32),
            struct((CHUNKS * count, own), BF16),
            struct((count, features), F32),
            struct((count, features), BF16),
            struct((count, units), BF16),
            struct((count, features), BF16),
        ],
        input_output_aliases={} if held is None else {9: 1},
        compiler_params=params(),
        cost_estimate=lasting(0.7),
        name="feed_second",
    )(sums, part, recv, normed, grad, slope, *weights[1:], norms, *(() if held is None else (held,)))


def third_kernel(
    swap, start_ref, part_ref, recv_ref, res_ref, normed_ref, inverse_ref, out_ref, norm_ref,
    sum_ref, low_ref, attended_ref, own_ref,
):
    own = own_ref.shape[1]
    grad = added(part_ref, recv_ref, swap) + res_ref[...]
    normed = normed_ref[...]
    res = norm_back(grad * norm_ref[0:1, :], normed, inverse_ref[...])
    own_ref[...] = res[:, :own]
    low = res.astype(BF16)
    low_ref[...] = low
    attended_ref[...] = dot_nn(low, out_ref[...]).astype(BF16)
    add_sums(start_ref, sum_ref, 2, [low[:, :own].astype(F32)])
    for place, value in ((4, grad[:, :own] * normed[:, :own]), (6, grad[:, :own])):
        sum_ref[place : place + 1, :] += jnp.sum(value, 0, keepdims=True)


def feed_third(swap, sums, width, part, recv, res, normed, inverse, weights, norms):
    count, features = part.shape
    own = sums.shape[1]
    return pl.pallas_call(
        functools.partial(third_kernel, swap),
        grid=(count // BLOCK,),
        in_specs=[
            whole(sums.shape),
            rows(features),
            rows(features),
            rows(features),
            rows(features),
            rows(1),
            whole(weights[0].shape),
            whole(norms.shape),
        ],
        out_specs=[whole(sums.shape), rows(features), rows(width), rows(own)],
        out_shape=[
            struct(sums.shape, F32),
            struct((count, features), BF16),
            struct((count, width), BF16),
            struct((count, own), F32),
        ],
        compiler_params=params(),
        cost_estimate=lasting(0.2),
        name="feed_third",
    )(sums, part, recv, res, normed, inverse, weights[0], norms)


def spread_rows(block_ref, scratch, keep_ref, send_ref, which, kinds):
    features = scratch.shape[0]
    count = block_ref.shape[0]
    depth = features // count
    half = count // 2
    for slot in range(count):
        start = pl.multiple_of(block_ref[slot] * depth, depth)
        piece = scratch[pl.ds(start, depth), :]
        first = ((slot % half) * kinds + which) * depth
        if slot < half:
            keep_ref[first : first + depth, :] = piece
        else:
            send_ref[first : first + depth, :] = piece.astype(BF16)


def split_sums(total):
    high = total.astype(BF16)
    low = (total - high.astype(F32)).astype(BF16)
    return high, low, high.astype(F32) + low.astype(F32)


def feed_grad_kernel(block_ref, *refs):
    low_refs, upper_refs, act_refs, hidden_refs = (
        refs[k * CHUNKS : (k + 1) * CHUNKS] for k in range(4)
    )
    keep_ref, send_ref, scratch = refs[4 * CHUNKS :]
    scratch[...] = sum(dot_tn(a[...], b[...]) for a, b in zip(upper_refs, hidden_refs))
    spread_rows(block_ref, scratch, keep_ref, send_ref, 0, 2)
    scratch[...] = sum(dot_tn(a[...], b[...]) for a, b in zip(low_refs, act_refs))
    spread_rows(block_ref, scratch, keep_ref, send_ref, 1, 2)


def feed_grads(blocks, low, act, upper, hidden):
    count, features = low[0].shape
    units = act[0].shape[1]
    chunk = min(256, units)
    column = pl.BlockSpec((count, chunk), lambda b: (0, b))
    result = pl.BlockSpec((features, chunk), lambda b: (0, b))
    return pl.pallas_call(
        feed_grad_kernel,
        grid=(units // chunk,),
        in_specs=[pl.BlockSpec(memory_space=SMEM)]
        + [whole((count, features))] * (2 * CHUNKS)
        + [column] * (2 * CHUNKS),
        out_specs=[result] * 2,
        out_shape=[struct((features, units), F32), struct((features, units), BF16)],
        scratch_shapes=[pltpu.VMEM((features, chunk), F32)],
        compiler_params=params(),
        cost_estimate=lasting(1.0),
        name="feed_grads",
    )(blocks, *low, *upper, *act, *hidden)


def project_grad_kernel(block_ref, start_ref, *refs):
    query_refs, branch_refs, attended_refs = (
        refs[k * CHUNKS : (k + 1) * CHUNKS] for k in range(3)
    )
    token_ref, low_ref, high_ref, key_ref, value_ref = refs[3 * CHUNKS : 3 * CHUNKS + 5]
    keep_ref, send_ref, sum_ref, scratch = refs[3 * CHUNKS + 5 :]
    count = token_ref.shape[0]
    part = count // CHUNKS
    scratch[...] = sum(
        dot_tn(token_ref[k * part : (k + 1) * part, :], ref[...])
        for k, ref in enumerate(query_refs)
    )
    spread_rows(block_ref, scratch, keep_ref, send_ref, 0, 4)
    for which, ref in ((1, key_ref), (2, value_ref)):
        scratch[...] = (
            dot_tn(token_ref[...], ref[MAXDOC : MAXDOC + count, :])
            + dot_tn(low_ref[...], ref[PAD:MAXDOC, :])
            + dot_tn(high_ref[...], ref[MAXDOC + count : MAXDOC + count + HALO, :])
        )
        spread_rows(block_ref, scratch, keep_ref, send_ref, which, 4)
    scratch[...] = sum(dot_tn(a[...], b[...]) for a, b in zip(branch_refs, attended_refs))
    spread_rows(block_ref, scratch, keep_ref, send_ref, 3, 4)
    total = start_ref[...]
    place = lax.broadcasted_iota(jnp.int32, total.shape, 0)
    query_sum = sum(
        jnp.sum(ref[...].astype(F32), 0, keepdims=True) for ref in query_refs
    )
    value_sum = jnp.sum(value_ref[...].astype(F32), 0, keepdims=True)
    total = total + jnp.where(place == 0, query_sum, 0.0) + jnp.where(place == 1, value_sum, 0.0)
    height = keep_ref.shape[0]
    high, low, sum_ref[...] = split_sums(total)
    send_ref[height : height + SUM_ROWS, :] = high
    send_ref[height + SUM_ROWS :, :] = low


def project_grads(blocks, sums, tokens, low, high, query, key, value, branch, attended):
    features = tokens.shape[1]
    width = key.shape[1]
    half = blocks.shape[0] // 2
    depth = features // (2 * half)
    height = half * 4 * depth
    operands = (sums, *query, *branch, *attended, tokens, low, high, key, value)
    return pl.pallas_call(
        project_grad_kernel,
        grid=(1,),
        in_specs=[pl.BlockSpec(memory_space=SMEM)] + [whole(x.shape) for x in operands],
        out_specs=[
            whole((height, width)),
            whole((height + 2 * SUM_ROWS, width)),
            whole(sums.shape),
        ],
        out_shape=[
            struct((height, width), F32),
            struct((height + 2 * SUM_ROWS, width), BF16),
            struct(sums.shape, F32),
        ],
        scratch_shapes=[pltpu.VMEM((features, width), F32)],
        compiler_params=params(),
        cost_estimate=lasting(0.6),
        name="project_grads",
    )(blocks, *operands)


def fold_kernel(with_sums, keep_ref, arrived_ref, *refs):
    height = keep_ref.shape[0]
    size = height // 2
    if with_sums:
        start_ref, keep_out, send_out, sum_out = refs
    else:
        keep_out, send_out = refs
    keep_out[...] = keep_ref[:size, :] + arrived_ref[:size, :].astype(F32)
    send_out[:size, :] = (keep_ref[size:, :] + arrived_ref[size:height, :].astype(F32)).astype(BF16)
    if with_sums:
        high, low, sum_out[...] = split_sums(start_ref[...] + arrived_sums(arrived_ref, height))
        send_out[size : size + SUM_ROWS, :] = high
        send_out[size + SUM_ROWS :, :] = low


def arrived_sums(ref, height):
    return ref[height : height + SUM_ROWS, :].astype(F32) + ref[height + SUM_ROWS :, :].astype(F32)


def fold(keep, arrived, sums):
    height, width = keep.shape
    extra = arrived.shape[0] - height
    operands = (keep, arrived) + (() if sums is None else (sums,))
    shapes = [struct((height // 2, width), F32), struct((height // 2 + extra, width), BF16)]
    shapes += [] if sums is None else [struct(sums.shape, F32)]
    result = pl.pallas_call(
        functools.partial(fold_kernel, sums is not None),
        grid=(1,),
        in_specs=[whole(x.shape) for x in operands],
        out_specs=[whole(x.shape) for x in shapes],
        out_shape=shapes,
        compiler_params=params(),
        cost_estimate=lasting(0.2),
        name="fold",
    )(*operands)
    return result[0], result[1], (None if sums is None else result[2])


def finish_kernel(kinds, sum_kinds, keep_ref, arrived_ref, *refs):
    height = keep_ref.shape[0]
    if sum_kinds:
        start_ref, *refs = refs
    first = 0
    for kind, ref in zip(kinds, refs):
        depth = ref.shape[-2]
        for place in range(kind or 1):
            rows_here = slice(first, first + depth)
            total = keep_ref[rows_here, :] + arrived_ref[rows_here, :].astype(F32)
            if kind:
                ref[place] = total
            else:
                ref[...] = total
            first += depth
    if sum_kinds:
        total = start_ref[...] + arrived_sums(arrived_ref, height)
        first = 0
        for kind, ref in zip(sum_kinds, refs[len(kinds) :]):
            if ref.shape[0] == kind:
                ref[...] = total[first : first + kind, :]
            else:
                ref[...] = jnp.concatenate([total[first + k : first + k + 1] for k in range(kind)], 1)
            first += kind


def finish(keep, arrived, sums, kinds, sum_kinds):
    height, width = keep.shape
    depth = height // sum(kind or 1 for kind in kinds)
    operands = (keep, arrived) + (() if sums is None else (sums,))
    shapes = [struct((kind, depth, width) if kind else (depth, width), F32) for kind in kinds]
    shapes += [
        struct((kind, width) if kind == 2 else (1, kind * width), F32) for kind in sum_kinds
    ]
    return pl.pallas_call(
        functools.partial(finish_kernel, kinds, sum_kinds),
        grid=(1,),
        in_specs=[whole(x.shape) for x in operands],
        out_specs=[whole(x.shape) for x in shapes],
        out_shape=shapes,
        compiler_params=params(),
        cost_estimate=lasting(0.2),
        name="finish",
    )(*operands)


def token_grad_kernel(even_ref, *refs):
    query_refs, res_refs = refs[:CHUNKS], refs[CHUNKS : 2 * CHUNKS]
    key_ref, value_ref, *weight_refs = refs[2 * CHUNKS : 2 * CHUNKS + 5]
    own_ref, rim_ref, *out_refs = refs[2 * CHUNKS + 5 :]
    own_outs, rim_outs = out_refs[: len(out_refs) // 2], out_refs[len(out_refs) // 2 :]
    count, own = own_ref.shape
    even = even_ref[0] == 1

    def piece(start):
        return dot_nt(key_ref[start : start + BLOCK, :], weight_refs[1][...]) + dot_nt(
            value_ref[start : start + BLOCK, :], weight_refs[2][...]
        )

    def spread(value, start, stays_ref, leave_refs):
        stays_ref[start : start + BLOCK, :] = value[:, :own]
        for place, ref in enumerate(leave_refs, 1):
            lanes = slice(place * own, (place + 1) * own)
            ref[start : start + BLOCK, :] = value[:, lanes].astype(BF16)

    for start in range(0, HALO, BLOCK):
        low, high = piece(PAD + start), piece(MAXDOC + count + start)
        spread(jnp.where(even, high, low), start, rim_ref, rim_outs)
        spread(jnp.where(even, low, high), HALO + start, rim_ref, rim_outs)
    for start in range(0, count, BLOCK):
        chunk, inside = divmod(start, count // CHUNKS)
        total = piece(MAXDOC + start) + dot_nt(
            query_refs[chunk][inside : inside + BLOCK, :], weight_refs[0][...]
        )
        spread(total, start, own_ref, own_outs)
        own_ref[start : start + BLOCK, :] += res_refs[chunk][inside : inside + BLOCK, :]


def token_grads(even, query, res, key, value, weights):
    count = CHUNKS * query[0].shape[0]
    own = res[0].shape[1]
    leave = weights[0].shape[0] // own - 1
    operands = (*query, *res, key, value, *weights)
    shapes = [struct((count, own), F32), struct((2 * HALO, own), F32)]
    shapes += [struct((count, own), BF16)] * leave + [struct((2 * HALO, own), BF16)] * leave
    result = pl.pallas_call(
        token_grad_kernel,
        grid=(1,),
        in_specs=[pl.BlockSpec(memory_space=SMEM)] + [whole(x.shape) for x in operands],
        out_specs=[whole(x.shape) for x in shapes],
        out_shape=shapes,
        compiler_params=params(),
        cost_estimate=lasting(5.0),
        name="token_grads",
    )(even, *operands)
    return result[0], result[1], result[2 : 2 + leave], result[2 + leave :]


def rim_sum_kernel(rim_ref, *refs):
    *arrived_refs, inside_ref, across_ref = refs
    total = rim_ref[...] + sum(ref[...].astype(F32) for ref in arrived_refs)
    inside_ref[...] = total[:HALO].astype(BF16)
    across_ref[...] = total[HALO:].astype(BF16)


def rim_sum(rim, arrived):
    own = rim.shape[1]
    operands = (rim, *arrived)
    return pl.pallas_call(
        rim_sum_kernel,
        grid=(1,),
        in_specs=[whole(x.shape) for x in operands],
        out_specs=[whole((HALO, own))] * 2,
        out_shape=[struct((HALO, own), BF16)] * 2,
        compiler_params=params(),
        cost_estimate=lasting(0.3),
        name="rim_sum",
    )(*operands)


def token_sum_kernel(even_ref, own_ref, inside_ref, across_ref, *refs):
    *arrived_refs, out_ref = refs
    even = even_ref[0] == 1
    inside, across = inside_ref[...].astype(F32), across_ref[...].astype(F32)
    low, high = jnp.where(even, across, inside), jnp.where(even, inside, across)
    rest = own_ref.shape[0] - HALO
    for start in range(0, own_ref.shape[0], BLOCK):
        rows_here = slice(start, start + BLOCK)
        piece = own_ref[rows_here, :] + sum(ref[rows_here, :].astype(F32) for ref in arrived_refs)
        if start < HALO:
            piece = piece + low[rows_here, :]
        if start >= rest:
            piece = piece + high[start - rest : start - rest + BLOCK, :]
        out_ref[rows_here, :] = piece.astype(BF16)


def token_sum(even, own, inside, across, arrived):
    operands = (own, inside, across, *arrived)
    return pl.pallas_call(
        token_sum_kernel,
        grid=(1,),
        in_specs=[pl.BlockSpec(memory_space=SMEM)] + [whole(x.shape) for x in operands],
        out_specs=whole(own.shape),
        out_shape=struct(own.shape, BF16),
        compiler_params=params(),
        cost_estimate=lasting(0.3),
        name="token_sum",
    )(even, *operands)


def from_next(x, axis, step):
    count = lax.axis_size(axis)
    return lax.ppermute(x, axis, [((i + step) % count, i) for i in range(count)])


def others(x):
    return [from_next(x, "col", step) for step in range(1, lax.axis_size("col"))]


def bits_of(count):
    return [1 << place for place in range(count.bit_length() - 1)]


def orders_of(count):
    high = bits_of(count)[:0:-1]
    return high + [1], high[2:] + high[:2] + [1]


def slots_of(order, distance):
    return sum(((distance & bit) // bit) << place for place, bit in enumerate(order))


def distances_of(order, slots):
    return sum(((slots >> place) & 1) * bit for place, bit in enumerate(order))


def with_partner(x, step):
    count = lax.axis_size("row")
    orders = orders_of(count)
    return lax.ppermute(x, "row", [(i, i ^ orders[i % 2][step]) for i in range(count)])


def with_next(inside, across):
    count = lax.axis_size("row")
    pairs = [(i, i + 1 if i % 2 else i - 1) for i in range(1, count - 1)]
    return (
        lax.ppermute(inside, "row", [(i, i ^ 1) for i in range(count)]),
        lax.ppermute(across, "row", pairs),
    )


def after(value, *needed):
    return lax.optimization_barrier((value, *needed))[0]


class Gather:
    def __init__(self, shard):
        self.held, self.step = shard[None], 0
        self.count = len(bits_of(lax.axis_size("row")))
        self.move()

    def move(self):
        self.arrived = with_partner(self.held, self.step)
        self.step += 1

    def put(self, *needed):
        self.held = jnp.concatenate([after(self.held, *needed), self.arrived], 0)
        self.move()


class Reduction:
    def __init__(self, keep, send, sums, kinds, sum_kinds=()):
        self.step = len(bits_of(lax.axis_size("row")))
        self.keep, self.send, self.sums = keep, send, sums
        self.kinds, self.sum_kinds = kinds, sum_kinds
        self.result = None
        self.move()

    def move(self):
        self.step -= 1
        self.arrived = with_partner(self.send, self.step)

    def add(self, *needed):
        keep = after(self.keep, *needed)
        if self.step == 0:
            self.result = finish(keep, self.arrived, self.sums, self.kinds, self.sum_kinds)
        else:
            self.keep, self.send, self.sums = fold(keep, self.arrived, self.sums)
            self.move()


def exchanged(part):
    arrived = others(part)
    if len(arrived) == 1:
        return arrived[0]
    shift = part.shape[1] // (len(arrived) + 1)
    total = sum(
        jnp.roll(x.astype(F32), step * shift, 1) for step, x in enumerate(arrived, 1)
    )
    return total.astype(BF16)


def on_device(
    tokens,
    prev_logits,
    doc_lengths,
    qkv_weight,
    qv_bias,
    out_weight,
    out_bias,
    up_weight,
    up_bias,
    down_weight,
    norm_gain,
    norm_shift,
    out_grad,
    logit_grad,
):
    count, own = tokens.shape
    width = qkv_weight.shape[2]
    row_count, col_count = lax.axis_size("row"), lax.axis_size("col")
    row_index, col_index = lax.axis_index("row"), lax.axis_index("col")
    token_count = count * row_count
    swap = col_count == 2
    hidden_rows = up_bias.shape[0] // own

    odd = row_index % 2 == 1
    places = jnp.arange(row_count, dtype=jnp.int32)
    offset = col_index * (row_count // col_count)
    distance = ((places + offset) % row_count) ^ row_index
    half = row_count // 2
    even_order, odd_order = (order[:-1] for order in orders_of(row_count))
    turned = odd ^ (distance % 2 == 1)
    slots = jnp.where(turned, slots_of(odd_order, distance), slots_of(even_order, distance))
    slots = slots + half * (distance % 2)
    turned = odd ^ (places >= half)
    met = jnp.where(turned, distances_of(odd_order, places), distances_of(even_order, places))
    blocks = (((met + (places >= half)) ^ row_index) - offset) % row_count

    even = 1 - row_index % 2
    even = even.astype(jnp.int32)[None]

    def dense_of(banded, fill, chunk, *needed):
        dense = to_dense(after(banded, *needed), lengths, fill, token_count, chunk)
        return dense

    prev_logits = pltpu.with_memory_space_constraint(prev_logits, pltpu.HBM)
    logit_grad = pltpu.with_memory_space_constraint(logit_grad, pltpu.HBM)

    out_turned = out_weight.T
    out_other = others(out_turned)
    qkv_rows = Gather(qkv_weight)
    tokens_other = others(after(tokens, out_turned))
    feed_rows = Gather(jnp.concatenate([out_turned, *out_other, up_weight, down_weight.T], 1))
    tail = row_index % 2 * (count - HALO)
    ready = after(tokens, feed_rows.held)
    inside, across = with_next(
        lax.dynamic_slice_in_dim(ready, count - HALO - tail, HALO, 0),
        lax.dynamic_slice_in_dim(ready, tail, HALO, 0),
    )
    qkv_rows.put(feed_rows.held)
    inside_other, across_other = others(inside), others(across)
    feed_rows.put(qkv_rows.held)
    qkv_rows.put(feed_rows.held, *tokens_other)
    lengths = jnp.concatenate(
        [after(doc_lengths, qkv_rows.held).reshape(-1), (row_index * count)[None]]
    )
    prev_dense = [
        dense_of(prev_logits, MASKED_SCORE, 0, qkv_rows.held, feed_rows.held, inside, across)
    ]
    grad_other = others(after(out_grad, *inside_other))
    while qkv_rows.step < qkv_rows.count:
        qkv_rows.put(prev_dense[0], *inside_other, *across_other)
    feed_rows.put(qkv_rows.held)
    tokens_full, query, key, value, low_tokens, high_tokens, *projections = project(
        slots, even, qkv_rows.held, qkv_rows.arrived, qv_bias, [after(tokens, feed_rows.held), *tokens_other],
        [inside, *inside_other], [across, *across_other],
    )
    grad_full = jnp.concatenate([after(out_grad, query)] + grad_other, 1)
    norms = jnp.concatenate([after(norm_gain, query), norm_shift, out_bias], 0)
    norms = jnp.concatenate([norms] + others(norms), 1)
    scores, probs, attended, attended_other = [], [], [], []
    for chunk in range(CHUNKS):
        score, prob, mix = attend_forward(
            after(query, feed_rows.held) if chunk else query, key, value, prev_dense[chunk], chunk
        )
        scores.append(score)
        probs.append(prob)
        attended.append(mix)
        attended_other.append(jnp.concatenate(others(mix), 1))
        if chunk == 0:
            prev_dense.append(dense_of(prev_logits, MASKED_SCORE, 1, mix, norms, grad_full))
            while feed_rows.step < feed_rows.count:
                feed_rows.put(prev_dense[1], attended_other[0])
    other_out, *weights = in_order(
        slots, after(feed_rows.held, mix), feed_rows.arrived,
        (width, (col_count - 1) * width, up_weight.shape[1], up_weight.shape[1]),
    )
    weights[0], other_out = other_out, weights[0]
    ups = up_bias[None]
    firsts, logit_dense = [], []
    for chunk in range(CHUNKS):
        result = feed_first(
            attended[chunk], attended_other[chunk], tokens_full, other_out, weights, norms, ups,
            chunk,
        )
        if chunk == 0:
            logit_dense.append(dense_of(logit_grad, 0.0, 0, result[-1]))
            ups = after(ups, logit_dense[0])
        firsts.append((*result, exchanged(result[-1])))
    normed, inverse, upper, act, slope, down_part, down_other = zip(*firsts)

    new_logits = to_band([after(scores[0], down_part[-1])], True)
    sums = after(jnp.zeros((SUM_ROWS, own), F32), new_logits)
    output = None
    seconds = []
    for chunk in range(CHUNKS):
        sums, output, *result = feed_second(
            swap, sums, output, down_part[chunk], down_other[chunk],
            normed[chunk], grad_full, slope[chunk], weights, norms, chunk,
        )
        seconds.append((*result, exchanged(result[-1])))
    res_two, ffn_low, hidden_grad, lower_part, lower_other = zip(*seconds)
    keep, send = feed_grads(blocks, ffn_low, act, upper, hidden_grad)
    feed_sum = Reduction(keep, send, None, (0, 0))
    sums = after(sums, keep)

    branch_low, res_one, query_grad, prev_dense_grad = [], [], [], []
    partial = None
    for chunk in range(CHUNKS):
        sums, low, attended_grad, res = feed_third(
            swap, sums, width, lower_part[chunk], lower_other[chunk], res_two[chunk],
            normed[chunk], inverse[chunk], weights, norms,
        )
        branch_low.append(low)
        res_one.append(res)
        prev, query_part, *partial = attend_backward(
            attended_grad, query, key, value, probs[chunk], logit_dense[chunk], chunk, partial
        )
        if chunk == 0:
            feed_sum.add(query_part)
            logit_dense.append(dense_of(logit_grad, 0.0, 1, feed_sum.keep))
            sums = after(sums, logit_dense[1])
        prev_dense_grad.append(prev)
        query_grad.append(query_part)
    key_grad, value_grad = partial
    feed_sum.add(query_grad[-1])
    keep, send, sums = project_grads(
        blocks, after(sums, feed_sum.keep), tokens_full, low_tokens, high_tokens, query_grad,
        key_grad, value_grad, branch_low, attended,
    )
    last_sum = Reduction(keep, send, sums, (3, 0), (2, 2, 2, 2, hidden_rows))
    center, rim, center_parts, rim_parts = token_grads(
        even, query_grad, res_one, after(key_grad, keep), value_grad, projections
    )

    def spread_over(parts):
        return [from_next(part, "col", -step) for step, part in enumerate(parts, 1)]

    last_sum.add(center)
    rim_parts = spread_over(rim_parts)
    center_parts = spread_over(after(x, rim) for x in center_parts)
    prev_dense_grad[0] = after(prev_dense_grad[0], last_sum.keep)
    prev_grad = to_band(prev_dense_grad, False)
    last_sum.add(prev_grad)
    inside, across = rim_sum(after(rim, last_sum.keep), rim_parts)
    feed_sum.add(inside)
    inside, across = with_next(inside, across)
    last_sum.add(feed_sum.keep)
    for chunk in range(1, CHUNKS):
        new_logits = to_band([after(scores[chunk], last_sum.keep)], True, chunk, new_logits)
    tokens_grad = token_sum(even, after(center, new_logits), inside, across, center_parts)
    while feed_sum.result is None:
        feed_sum.add(tokens_grad)
    while last_sum.result is None:
        last_sum.add(feed_sum.result[0])
    qkv_grad, out_grad_rows, qv_sum, bias_sum, gain_sum, shift_sum, hidden_sum = last_sum.result
    up_grad, down_grad = feed_sum.result
    return (
        output,
        new_logits,
        tokens_grad,
        prev_grad,
        qkv_grad,
        qv_sum,
        out_grad_rows.T,
        bias_sum,
        up_grad,
        hidden_sum.reshape(-1),
        down_grad.T,
        gain_sum,
        shift_sum,
    )


def solution(mesh):
    return jax.shard_map(
        on_device,
        mesh=mesh,
        in_specs=(
            P("row", "col"),
            P("col", "row", None),
            P(),
            P(None, "row", "col"),
            P(None, "col"),
            P("col", "row"),
            P(None, "col"),
            P("row", "col"),
            P("col"),
            P("col", "row"),
            P(None, "col"),
            P(None, "col"),
            P("row", "col"),
            P("col", "row", None),
        ),
        out_specs=(
            P("row", "col"),
            P("col", "row", None),
            P("row", "col"),
            P("col", "row", None),
            P(None, "row", "col"),
            P(None, "col"),
            P("col", "row"),
            P(None, "col"),
            P("row", "col"),
            P("col"),
            P("col", "row"),
            P(None, "col"),
            P(None, "col"),
        ),
        check_vma=False,
    )
```

```python
import functools

import jax
import jax.numpy as jnp
from jax import lax
from jax.experimental import pallas as pl
from jax.experimental.pallas import tpu as pltpu
from jax.sharding import PartitionSpec as P

D = 512
HEAD_DIM = 64
MAXDOC = 512
BAND = 2 * MAXDOC
BLOCK = 128
WINDOW = BAND + BLOCK
HALO = MAXDOC - 128
PAD = MAXDOC - HALO

EPSILON = 1e-05
MASKED_SCORE = -1e30
ERF_RATE = 0.7071067811865476
DENSITY_RATE = 0.3989422804014327

F32 = jnp.float32
BF16 = jnp.bfloat16
SMEM = pltpu.MemorySpace.SMEM
VMEM_LIMIT = 24 << 20
CHUNKS = 2
SUM_ROWS = 16
FLOPS_PER_MICROSECOND = 1.0e9


def dot_nn(a, b):
    return lax.dot_general(a, b, (((1,), (0,)), ((), ())), preferred_element_type=F32)


def dot_nt(a, b):
    return lax.dot_general(a, b, (((1,), (1,)), ((), ())), preferred_element_type=F32)


def dot_tn(a, b):
    return lax.dot_general(a, b, (((0,), (0,)), ((), ())), preferred_element_type=F32)


def params():
    return pltpu.CompilerParams(
        dimension_semantics=("arbitrary",), vmem_limit_bytes=VMEM_LIMIT
    )


def lasting(microseconds):
    return pl.CostEstimate(
        flops=int(microseconds * FLOPS_PER_MICROSECOND), bytes_accessed=0, transcendentals=0
    )


def whole(shape):
    return pl.BlockSpec(shape, lambda b: (0,) * len(shape))


def rows(width, first=0):
    return pl.BlockSpec((BLOCK, width), lambda b: (b + first, 0))


def heads_block(heads, width, first=0):
    return pl.BlockSpec((heads, BLOCK, width), lambda b: (0, b + first, 0))


def struct(shape, dtype):
    return jax.ShapeDtypeStruct(shape, dtype)


def segment_of(positions, lengths_ref, documents, token_count):
    found = jnp.zeros(positions.shape, jnp.int32)
    end = jnp.int32(0)
    for document in range(documents):
        end = end + lengths_ref[document]
        found = found + (positions >= end).astype(jnp.int32)
    return jnp.where((positions >= 0) & (positions < token_count), found, -1)


def dense_kernel(fill, token_count, offset, lengths_ref, band_ref, dense_ref):
    documents = lengths_ref.shape[0] - 1
    first = lengths_ref[documents] + (pl.program_id(0) + offset) * BLOCK
    query = first + lax.broadcasted_iota(jnp.int32, (BLOCK, 1), 0)
    key = first - MAXDOC + lax.broadcasted_iota(jnp.int32, (1, WINDOW), 1)
    same = segment_of(query, lengths_ref, documents, token_count) == segment_of(
        key, lengths_ref, documents, token_count
    )
    for head in range(band_ref.shape[0]):
        wide = jnp.concatenate(
            [band_ref[head].astype(F32), jnp.zeros((BLOCK, BLOCK), F32)], 1
        )
        turned = pltpu.roll(wide, 0, 1, stride=1, stride_axis=0)
        dense_ref[head] = jnp.where(same, turned, fill).astype(BF16)


def to_dense(banded, lengths, fill, token_count, chunk):
    heads, count, _ = banded.shape
    count //= CHUNKS
    offset = chunk * (count // BLOCK)
    return pl.pallas_call(
        functools.partial(dense_kernel, fill, token_count, offset),
        grid=(count // BLOCK,),
        in_specs=[pl.BlockSpec(memory_space=SMEM), heads_block(heads, BAND, offset)],
        out_specs=heads_block(heads, WINDOW),
        out_shape=struct((heads, count, WINDOW), BF16),
        compiler_params=params(),
        cost_estimate=lasting(8.0 if fill and chunk == 0 else 1.0),
        name="to_dense",
    )(lengths, banded)


def band_kernel(masked, chunks, *refs):
    dense_refs, band_ref = refs[:chunks], refs[-1]
    lane = lax.broadcasted_iota(jnp.int32, (BLOCK, BLOCK), 1)
    row = lax.broadcasted_iota(jnp.int32, (BLOCK, BLOCK), 0)
    source = (lane + row) & (BLOCK - 1)
    near = lane + row < BLOCK
    steps = pl.num_programs(0) // chunks

    def turn(dense_ref):
        for head in range(band_ref.shape[0]):
            pieces = []
            for place in range(WINDOW // BLOCK):
                piece = dense_ref[head, :, place * BLOCK : (place + 1) * BLOCK].astype(F32)
                if masked:
                    piece = jnp.where(piece < 0.5 * MASKED_SCORE, 0.0, piece)
                pieces.append(jnp.take_along_axis(piece, source, axis=1))
            for place in range(BAND // BLOCK):
                band_ref[head, :, place * BLOCK : (place + 1) * BLOCK] = jnp.where(
                    near, pieces[place], pieces[place + 1]
                ).astype(BF16)

    for chunk, dense_ref in enumerate(dense_refs):

        @pl.when(pl.program_id(0) // steps == chunk)
        def _():
            turn(dense_ref)


def to_band(chunks, masked, first=0, held=None):
    heads, count, _ = chunks[0].shape
    steps = count // BLOCK

    def block_of(chunk):
        return pl.BlockSpec(
            (heads, BLOCK, WINDOW), lambda b: (0, jnp.clip(b - chunk * steps, 0, steps - 1), 0)
        )

    return pl.pallas_call(
        functools.partial(band_kernel, masked, len(chunks)),
        grid=(len(chunks) * steps,),
        in_specs=[block_of(chunk) for chunk in range(len(chunks))]
        + ([] if held is None else [pl.BlockSpec(memory_space=pl.ANY)]),
        out_specs=heads_block(heads, BAND, first * steps),
        out_shape=struct((heads, CHUNKS * count, BAND), BF16),
        input_output_aliases={} if held is None else {len(chunks): 0},
        compiler_params=params(),
        cost_estimate=lasting(5.0 if masked and held is None else 0.3),
        name="to_band",
    )(*chunks, *(() if held is None else (held,)))


def head_split(block, size):
    if size == 1:
        return block
    lane = lax.broadcasted_iota(jnp.int32, block.shape, 1)
    return jnp.concatenate(
        [
            jnp.where((lane >= h * HEAD_DIM) & (lane < (h + 1) * HEAD_DIM), block, 0)
            for h in range(size)
        ],
        0,
    )


def head_join(stacked, size):
    if size == 1:
        return stacked
    height = stacked.shape[0] // size
    joined = stacked[:height]
    lane = lax.broadcasted_iota(jnp.int32, joined.shape, 1)
    for h in range(1, size):
        joined = jnp.where(lane >= h * HEAD_DIM, stacked[h * height : (h + 1) * height], joined)
    return joined


def project_kernel(
    parts, slot_ref, even_ref, near_ref, far_ref, bias_ref, *refs
):
    token_refs, inside_refs, across_refs = (refs[k * parts : (k + 1) * parts] for k in range(3))
    all_ref, query_ref, key_ref, value_ref, low_ref, high_ref, *weight_refs = refs[3 * parts :]
    half, _, depth, _ = near_ref.shape
    count, width = token_refs[0].shape

    def put(place, source_ref, slot):
        for which, ref in enumerate(weight_refs):
            ref[place * depth : (place + 1) * depth, :] = source_ref[slot, which]

    for place in range(2 * half):
        slot = slot_ref[place]

        @pl.when(slot < half)
        def _():
            put(place, near_ref, slot)

        @pl.when(slot >= half)
        def _():
            put(place, far_ref, slot - half)

    even = even_ref[0] == 1
    for place, (own_ref, inside_ref, across_ref) in enumerate(
        zip(token_refs, inside_refs, across_refs)
    ):
        lanes = slice(place * width, (place + 1) * width)
        inside, across = inside_ref[...], across_ref[...]
        all_ref[:, lanes] = own_ref[...]
        low_ref[:, lanes] = jnp.where(even, across, inside)
        high_ref[:, lanes] = jnp.where(even, inside, across)
    own, low_rows, high_rows = all_ref[...], low_ref[...], high_ref[...]
    query = (dot_nn(own, weight_refs[0][...]) + bias_ref[0:1, :]).astype(BF16)
    empty = jnp.zeros((PAD, query.shape[1]), BF16)
    query_ref[...] = query * jnp.asarray(HEAD_DIM ** (-0.5), BF16)
    for out_ref, which in ((key_ref, 1), (value_ref, 2)):
        shift = bias_ref[1:2, :] if which == 2 else 0.0
        weight = weight_refs[which][...]
        out_ref[0:PAD, :] = empty
        out_ref[PAD:MAXDOC, :] = (dot_nn(low_rows, weight) + shift).astype(BF16)
        out_ref[MAXDOC : MAXDOC + count, :] = (dot_nn(own, weight) + shift).astype(BF16)
        out_ref[MAXDOC + count : MAXDOC + count + HALO, :] = (
            dot_nn(high_rows, weight) + shift
        ).astype(BF16)
        out_ref[MAXDOC + count + HALO :, :] = empty


def project(slots, even, near, far, bias, tokens, inside, across):
    count, part = tokens[0].shape
    features = len(tokens) * part
    width = near.shape[3]
    operands = (near, far, bias, *tokens, *inside, *across)
    extended = (count + BAND, width)
    shapes = [(count, features), (count, width), extended, extended]
    shapes += [(HALO, features)] * 2 + [(features, width)] * 3
    return pl.pallas_call(
        functools.partial(project_kernel, len(tokens)),
        grid=(1,),
        in_specs=[pl.BlockSpec(memory_space=SMEM)] * 2 + [whole(x.shape) for x in operands],
        out_specs=[whole(shape) for shape in shapes],
        out_shape=[struct(shape, BF16) for shape in shapes],
        compiler_params=params(),
        cost_estimate=lasting(2.0),
        name="project",
    )(slots, even, *operands)


def by_edge(block, last, body):
    edge = (block == 0) | (block == last)

    @pl.when(edge)
    def _():
        body(BLOCK, WINDOW - 2 * BLOCK)

    @pl.when(jnp.logical_not(edge))
    def _():
        body(0, WINDOW)


def forward_kernel(
    offset, query_ref, key_ref, value_ref, prev_ref, score_ref, prob_ref, attended_ref
):
    heads = prev_ref.shape[0]
    size = min(2, heads)
    span = size * HEAD_DIM
    block = pl.program_id(0) + offset

    def body(first, width):
        window = pl.ds(pl.multiple_of(block * BLOCK + first, BLOCK), width)
        inside = slice(first, first + width)
        for group in range(heads // size):
            lanes = slice(group * span, (group + 1) * span)
            query = head_split(query_ref[:, lanes], size)
            dense = dot_nt(query, key_ref[window, lanes])
            weights = []
            for h in range(size):
                head = group * size + h
                score = dense[h * BLOCK : (h + 1) * BLOCK] + prev_ref[head, :, inside].astype(F32)
                score_ref[head, :, inside] = score.astype(BF16)
                if first:
                    empty = jnp.full((BLOCK, first), MASKED_SCORE, BF16)
                    score_ref[head, :, :first] = empty
                    score_ref[head, :, first + width :] = empty
                peak = jnp.max(score, -1, keepdims=True)
                grown = jnp.exp(score - peak)
                total = jnp.sum(grown, -1, keepdims=True)
                prob = (grown * (1.0 / total)).astype(BF16)
                prob_ref[head, :, inside] = prob
                weights.append(prob)
            mixed = dot_nn(jnp.concatenate(weights, 0), value_ref[window, lanes])
            attended_ref[:, lanes] = head_join(mixed, size).astype(BF16)

    by_edge(block, key_ref.shape[0] // BLOCK - WINDOW // BLOCK, body)


def attend_forward(query, key, value, prev, chunk):
    heads, count, _ = prev.shape
    width = query.shape[1]
    offset = chunk * (count // BLOCK)
    return pl.pallas_call(
        functools.partial(forward_kernel, offset),
        grid=(count // BLOCK,),
        in_specs=[
            rows(width, offset),
            whole(key.shape),
            whole(value.shape),
            heads_block(heads, WINDOW),
        ],
        out_specs=[heads_block(heads, WINDOW), heads_block(heads, WINDOW), rows(width)],
        out_shape=[
            struct((heads, count, WINDOW), BF16),
            struct((heads, count, WINDOW), BF16),
            struct((count, width), BF16),
        ],
        compiler_params=params(),
        cost_estimate=lasting(3.8),
        name="attend_forward",
    )(query, key, value, prev)


def backward_kernel(
    offset, last, grad_ref, query_ref, key_ref, value_ref, prob_ref, logit_ref, *refs
):
    if last:
        key_start, value_start = refs[:2]
        prev_ref, query_grad_ref, key_grad_ref, value_grad_ref, key_sum, value_sum = refs[2:]
    else:
        prev_ref, query_grad_ref, key_sum, value_sum = refs
    step = pl.program_id(0)
    heads = prob_ref.shape[0]
    size = min(2, heads)
    span = size * HEAD_DIM

    @pl.when(step == 0)
    def _():
        if last:
            key_sum[...] = key_start[...]
            value_sum[...] = value_start[...]
        else:
            key_sum[...] = jnp.zeros_like(key_sum)
            value_sum[...] = jnp.zeros_like(value_sum)

    block = step + offset

    def body(first, width):
        window = pl.ds(pl.multiple_of(block * BLOCK + first, BLOCK), width)
        inside = slice(first, first + width)
        for group in range(heads // size):
            lanes = slice(group * span, (group + 1) * span)
            query = head_split(query_ref[:, lanes], size)
            grad = head_split(grad_ref[:, lanes], size)
            key = key_ref[window, lanes]
            prob_grad = dot_nt(grad, value_ref[window, lanes])
            probs, scores = [], []
            for h in range(size):
                head = group * size + h
                low = prob_ref[head, :, inside]
                prob = low.astype(F32)
                slope = prob_grad[h * BLOCK : (h + 1) * BLOCK]
                inner = jnp.sum(prob * slope, -1, keepdims=True)
                score = prob * (slope - inner) + logit_ref[head, :, inside].astype(F32)
                score = score.astype(BF16)
                prev_ref[head, :, inside] = score
                if first:
                    empty = jnp.zeros((BLOCK, first), BF16)
                    prev_ref[head, :, :first] = empty
                    prev_ref[head, :, first + width :] = empty
                probs.append(low)
                scores.append(score)
            stacked = jnp.concatenate(scores, 0)
            mixed = head_join(dot_nn(stacked, key), size) * HEAD_DIM ** (-0.5)
            query_grad_ref[:, lanes] = mixed.astype(BF16)
            key_sum[lanes, window] += dot_tn(query, stacked)
            value_sum[lanes, window] += dot_tn(grad, jnp.concatenate(probs, 0))

    by_edge(block, key_ref.shape[0] // BLOCK - WINDOW // BLOCK, body)

    if last:

        @pl.when(step == pl.num_programs(0) - 1)
        def _():
            key_grad_ref[...] = key_sum[...].astype(BF16).T
            value_grad_ref[...] = value_sum[...].astype(BF16).T


def attend_backward(grad, query, key, value, prob, logit, chunk, sums):
    heads, count, _ = prob.shape
    extended, width = key.shape
    offset = chunk * (count // BLOCK)
    last = sums is not None
    turned = (width, extended)
    scratch = [pltpu.VMEM(turned, F32), pltpu.VMEM(turned, F32)] if last else []
    ends = [whole((extended, width))] * 2 if last else [whole(turned)] * 2
    end_shapes = [struct((extended, width), BF16)] * 2 if last else [struct(turned, F32)] * 2
    return pl.pallas_call(
        functools.partial(backward_kernel, offset, last),
        grid=(count // BLOCK,),
        in_specs=[
            rows(width),
            rows(width, offset),
            whole((extended, width)),
            whole((extended, width)),
            heads_block(heads, WINDOW),
            heads_block(heads, WINDOW),
        ]
        + ([whole(turned)] * 2 if last else []),
        out_specs=[heads_block(heads, WINDOW), rows(width)] + ends,
        out_shape=[struct((heads, count, WINDOW), BF16), struct((count, width), BF16)]
        + end_shapes,
        scratch_shapes=scratch,
        compiler_params=params(),
        cost_estimate=lasting(3.0 if last else 20.0),
        name="attend_backward",
    )(grad, query, key, value, prob, logit, *(sums or ()))


def order_kernel(slot_ref, near_ref, far_ref, *out_refs):
    half, depth, _ = near_ref.shape

    def put(place, source_ref, slot):
        first = 0
        for out_ref in out_refs:
            last = first + out_ref.shape[1]
            out_ref[place * depth : (place + 1) * depth, :] = source_ref[slot, :, first:last]
            first = last

    for place in range(2 * half):
        slot = slot_ref[place]

        @pl.when(slot < half)
        def _():
            put(place, near_ref, slot)

        @pl.when(slot >= half)
        def _():
            put(place, far_ref, slot - half)


def in_order(slots, near, far, widths):
    half, depth, _ = near.shape
    shapes = [(2 * half * depth, width) for width in widths]
    return pl.pallas_call(
        order_kernel,
        grid=(1,),
        in_specs=[pl.BlockSpec(memory_space=SMEM), whole(near.shape), whole(far.shape)],
        out_specs=[whole(shape) for shape in shapes],
        out_shape=[struct(shape, BF16) for shape in shapes],
        compiler_params=params(),
        cost_estimate=lasting(0.9),
        name="in_order",
    )(slots, near, far)


def mean_of(x):
    return jnp.sum(x, -1, keepdims=True) * (1.0 / D)


def normalized(hidden):
    mean = mean_of(hidden)
    inverse = lax.rsqrt(mean_of(hidden * hidden) - mean * mean + EPSILON)
    return (hidden - mean) * inverse, inverse


def norm_back(upstream, normed, inverse):
    return inverse * (upstream - mean_of(upstream) - normed * mean_of(upstream * normed))


def added(own_ref, other_ref, swap):
    other = other_ref[...]
    if swap:
        middle = other.shape[1] // 2
        other = jnp.concatenate([other[:, middle:], other[:, :middle]], 1)
    return own_ref[...].astype(F32) + other.astype(F32)


def first_kernel(
    own_ref, other_ref, token_ref, other_out_ref, out_ref, up_ref, down_ref, norm_ref,
    up_bias_ref, normed_ref, inverse_ref, upper_ref, act_ref, slope_ref, part_ref,
):
    branch = dot_nt(own_ref[...], out_ref[...]) + dot_nt(other_ref[...], other_out_ref[...])
    hidden = token_ref[...].astype(F32) + branch + norm_ref[4:5, :]
    normed, inverse = normalized(hidden)
    normed_ref[...] = normed
    inverse_ref[...] = inverse
    upper = (normed * norm_ref[0:1, :] + norm_ref[2:3, :]).astype(BF16)
    upper_ref[...] = upper
    pre = dot_nn(upper, up_ref[...]) + up_bias_ref[...]
    share = 0.5 * (1.0 + lax.erf(pre * ERF_RATE))
    act = (pre * share).astype(BF16)
    act_ref[...] = act
    slope_ref[...] = (share + pre * jnp.exp(-0.5 * pre * pre) * DENSITY_RATE).astype(BF16)
    part_ref[...] = dot_nt(act, down_ref[...]).astype(BF16)


def feed_first(own, other, tokens, other_out, weights, norms, up_bias, chunk):
    count, width = own.shape
    features = tokens.shape[1]
    units = up_bias.shape[1]
    return pl.pallas_call(
        first_kernel,
        grid=(count // BLOCK,),
        in_specs=[
            rows(width),
            rows(other.shape[1]),
            rows(features, chunk * (count // BLOCK)),
            whole(other_out.shape),
            *(whole(x.shape) for x in weights),
            whole(norms.shape),
            whole(up_bias.shape),
        ],
        out_specs=[
            rows(features),
            rows(1),
            rows(features),
            rows(units),
            rows(units),
            rows(features),
        ],
        out_shape=[
            struct((count, features), F32),
            struct((count, 1), F32),
            struct((count, features), BF16),
            struct((count, units), BF16),
            struct((count, units), BF16),
            struct((count, features), BF16),
        ],
        compiler_params=params(),
        cost_estimate=lasting(1.0),
        name="feed_first",
    )(own, other, tokens, other_out, *weights, norms, up_bias)


def add_sums(start_ref, sum_ref, first, values):
    @pl.when(pl.program_id(0) == 0)
    def _():
        sum_ref[...] = start_ref[...]

    for place, value in enumerate(values):
        sum_ref[first + place : first + place + 1, :] += jnp.sum(value, 0, keepdims=True)


def second_kernel(
    swap, start_ref, part_ref, recv_ref, normed_ref, grad_ref, slope_ref, up_ref, down_ref,
    norm_ref, *refs,
):
    sum_ref, output_ref, res_ref, low_ref, hidden_ref, lower_ref = refs[-6:]
    own = output_ref.shape[1]
    upper = normed_ref[...] * norm_ref[0:1, :] + norm_ref[2:3, :]
    hidden = upper + added(part_ref, recv_ref, swap) + norm_ref[5:6, :]
    normed, inverse = normalized(hidden)
    output_ref[...] = (
        normed[:, :own] * norm_ref[1:2, :own] + norm_ref[3:4, :own]
    ).astype(BF16)
    grad = grad_ref[...].astype(F32)
    res = norm_back(grad * norm_ref[1:2, :], normed, inverse)
    res_ref[...] = res
    low = res.astype(BF16)
    low_ref[...] = low
    act_grad = dot_nn(low, down_ref[...])
    hidden_grad = (act_grad * slope_ref[...].astype(F32)).astype(BF16)
    hidden_ref[...] = hidden_grad
    lower_ref[...] = dot_nt(hidden_grad, up_ref[...]).astype(BF16)
    wide = hidden_grad.astype(F32)
    add_sums(start_ref, sum_ref, 3, [low[:, :own].astype(F32)])
    for place, value in (
        (5, grad[:, :own] * normed[:, :own]),
        (7, grad[:, :own]),
        *((8 + k, wide[:, k * own : (k + 1) * own]) for k in range(wide.shape[1] // own)),
    ):
        sum_ref[place : place + 1, :] += jnp.sum(value, 0, keepdims=True)


def feed_second(swap, sums, held, part, recv, normed, grad, slope, weights, norms, chunk):
    count, features = part.shape
    own = sums.shape[1]
    units = slope.shape[1]
    offset = chunk * (count // BLOCK)
    return pl.pallas_call(
        functools.partial(second_kernel, swap),
        grid=(count // BLOCK,),
        in_specs=[
            whole(sums.shape),
            rows(features),
            rows(features),
            rows(features),
            rows(features, offset),
            rows(units),
            *(whole(x.shape) for x in weights[1:]),
            whole(norms.shape),
            *([] if held is None else [pl.BlockSpec(memory_space=pl.ANY)]),
        ],
        out_specs=[
            whole(sums.shape),
            rows(own, offset),
            rows(features),
            rows(features),
            rows(units),
            rows(features),
        ],
        out_shape=[
            struct(sums.shape, F32),
            struct((CHUNKS * count, own), BF16),
            struct((count, features), F32),
            struct((count, features), BF16),
            struct((count, units), BF16),
            struct((count, features), BF16),
        ],
        input_output_aliases={} if held is None else {9: 1},
        compiler_params=params(),
        cost_estimate=lasting(0.7),
        name="feed_second",
    )(sums, part, recv, normed, grad, slope, *weights[1:], norms, *(() if held is None else (held,)))


def third_kernel(
    swap, start_ref, part_ref, recv_ref, res_ref, normed_ref, inverse_ref, out_ref, norm_ref,
    sum_ref, low_ref, attended_ref, own_ref,
):
    own = own_ref.shape[1]
    grad = added(part_ref, recv_ref, swap) + res_ref[...]
    normed = normed_ref[...]
    res = norm_back(grad * norm_ref[0:1, :], normed, inverse_ref[...])
    own_ref[...] = res[:, :own]
    low = res.astype(BF16)
    low_ref[...] = low
    attended_ref[...] = dot_nn(low, out_ref[...]).astype(BF16)
    add_sums(start_ref, sum_ref, 2, [low[:, :own].astype(F32)])
    for place, value in ((4, grad[:, :own] * normed[:, :own]), (6, grad[:, :own])):
        sum_ref[place : place + 1, :] += jnp.sum(value, 0, keepdims=True)


def feed_third(swap, sums, width, part, recv, res, normed, inverse, weights, norms):
    count, features = part.shape
    own = sums.shape[1]
    return pl.pallas_call(
        functools.partial(third_kernel, swap),
        grid=(count // BLOCK,),
        in_specs=[
            whole(sums.shape),
            rows(features),
            rows(features),
            rows(features),
            rows(features),
            rows(1),
            whole(weights[0].shape),
            whole(norms.shape),
        ],
        out_specs=[whole(sums.shape), rows(features), rows(width), rows(own)],
        out_shape=[
            struct(sums.shape, F32),
            struct((count, features), BF16),
            struct((count, width), BF16),
            struct((count, own), F32),
        ],
        compiler_params=params(),
        cost_estimate=lasting(0.2),
        name="feed_third",
    )(sums, part, recv, res, normed, inverse, weights[0], norms)


def spread_rows(block_ref, scratch, keep_ref, send_ref, which, kinds):
    features = scratch.shape[0]
    count = block_ref.shape[0]
    depth = features // count
    half = count // 2
    for slot in range(count):
        start = pl.multiple_of(block_ref[slot] * depth, depth)
        piece = scratch[pl.ds(start, depth), :]
        first = ((slot % half) * kinds + which) * depth
        if slot < half:
            keep_ref[first : first + depth, :] = piece
        else:
            send_ref[first : first + depth, :] = piece.astype(BF16)


def split_sums(total):
    high = total.astype(BF16)
    low = (total - high.astype(F32)).astype(BF16)
    return high, low, high.astype(F32) + low.astype(F32)


def feed_grad_kernel(block_ref, *refs):
    low_refs, upper_refs, act_refs, hidden_refs = (
        refs[k * CHUNKS : (k + 1) * CHUNKS] for k in range(4)
    )
    keep_ref, send_ref, scratch = refs[4 * CHUNKS :]
    scratch[...] = sum(dot_tn(a[...], b[...]) for a, b in zip(upper_refs, hidden_refs))
    spread_rows(block_ref, scratch, keep_ref, send_ref, 0, 2)
    scratch[...] = sum(dot_tn(a[...], b[...]) for a, b in zip(low_refs, act_refs))
    spread_rows(block_ref, scratch, keep_ref, send_ref, 1, 2)


def feed_grads(blocks, low, act, upper, hidden):
    count, features = low[0].shape
    units = act[0].shape[1]
    chunk = min(256, units)
    column = pl.BlockSpec((count, chunk), lambda b: (0, b))
    result = pl.BlockSpec((features, chunk), lambda b: (0, b))
    return pl.pallas_call(
        feed_grad_kernel,
        grid=(units // chunk,),
        in_specs=[pl.BlockSpec(memory_space=SMEM)]
        + [whole((count, features))] * (2 * CHUNKS)
        + [column] * (2 * CHUNKS),
        out_specs=[result] * 2,
        out_shape=[struct((features, units), F32), struct((features, units), BF16)],
        scratch_shapes=[pltpu.VMEM((features, chunk), F32)],
        compiler_params=params(),
        cost_estimate=lasting(1.0),
        name="feed_grads",
    )(blocks, *low, *upper, *act, *hidden)


def project_grad_kernel(block_ref, start_ref, *refs):
    query_refs, branch_refs, attended_refs = (
        refs[k * CHUNKS : (k + 1) * CHUNKS] for k in range(3)
    )
    token_ref, low_ref, high_ref, key_ref, value_ref = refs[3 * CHUNKS : 3 * CHUNKS + 5]
    keep_ref, send_ref, sum_ref, scratch = refs[3 * CHUNKS + 5 :]
    count = token_ref.shape[0]
    part = count // CHUNKS
    scratch[...] = sum(
        dot_tn(token_ref[k * part : (k + 1) * part, :], ref[...])
        for k, ref in enumerate(query_refs)
    )
    spread_rows(block_ref, scratch, keep_ref, send_ref, 0, 4)
    for which, ref in ((1, key_ref), (2, value_ref)):
        scratch[...] = (
            dot_tn(token_ref[...], ref[MAXDOC : MAXDOC + count, :])
            + dot_tn(low_ref[...], ref[PAD:MAXDOC, :])
            + dot_tn(high_ref[...], ref[MAXDOC + count : MAXDOC + count + HALO, :])
        )
        spread_rows(block_ref, scratch, keep_ref, send_ref, which, 4)
    scratch[...] = sum(dot_tn(a[...], b[...]) for a, b in zip(branch_refs, attended_refs))
    spread_rows(block_ref, scratch, keep_ref, send_ref, 3, 4)
    total = start_ref[...]
    place = lax.broadcasted_iota(jnp.int32, total.shape, 0)
    query_sum = sum(
        jnp.sum(ref[...].astype(F32), 0, keepdims=True) for ref in query_refs
    )
    value_sum = jnp.sum(value_ref[...].astype(F32), 0, keepdims=True)
    total = total + jnp.where(place == 0, query_sum, 0.0) + jnp.where(place == 1, value_sum, 0.0)
    height = keep_ref.shape[0]
    high, low, sum_ref[...] = split_sums(total)
    send_ref[height : height + SUM_ROWS, :] = high
    send_ref[height + SUM_ROWS :, :] = low


def project_grads(blocks, sums, tokens, low, high, query, key, value, branch, attended):
    features = tokens.shape[1]
    width = key.shape[1]
    half = blocks.shape[0] // 2
    depth = features // (2 * half)
    height = half * 4 * depth
    operands = (sums, *query, *branch, *attended, tokens, low, high, key, value)
    return pl.pallas_call(
        project_grad_kernel,
        grid=(1,),
        in_specs=[pl.BlockSpec(memory_space=SMEM)] + [whole(x.shape) for x in operands],
        out_specs=[
            whole((height, width)),
            whole((height + 2 * SUM_ROWS, width)),
            whole(sums.shape),
        ],
        out_shape=[
            struct((height, width), F32),
            struct((height + 2 * SUM_ROWS, width), BF16),
            struct(sums.shape, F32),
        ],
        scratch_shapes=[pltpu.VMEM((features, width), F32)],
        compiler_params=params(),
        cost_estimate=lasting(0.6),
        name="project_grads",
    )(blocks, *operands)


def fold_kernel(with_sums, keep_ref, arrived_ref, *refs):
    height = keep_ref.shape[0]
    size = height // 2
    if with_sums:
        start_ref, keep_out, send_out, sum_out = refs
    else:
        keep_out, send_out = refs
    keep_out[...] = keep_ref[:size, :] + arrived_ref[:size, :].astype(F32)
    send_out[:size, :] = (keep_ref[size:, :] + arrived_ref[size:height, :].astype(F32)).astype(BF16)
    if with_sums:
        high, low, sum_out[...] = split_sums(start_ref[...] + arrived_sums(arrived_ref, height))
        send_out[size : size + SUM_ROWS, :] = high
        send_out[size + SUM_ROWS :, :] = low


def arrived_sums(ref, height):
    return ref[height : height + SUM_ROWS, :].astype(F32) + ref[height + SUM_ROWS :, :].astype(F32)


def fold(keep, arrived, sums):
    height, width = keep.shape
    extra = arrived.shape[0] - height
    operands = (keep, arrived) + (() if sums is None else (sums,))
    shapes = [struct((height // 2, width), F32), struct((height // 2 + extra, width), BF16)]
    shapes += [] if sums is None else [struct(sums.shape, F32)]
    result = pl.pallas_call(
        functools.partial(fold_kernel, sums is not None),
        grid=(1,),
        in_specs=[whole(x.shape) for x in operands],
        out_specs=[whole(x.shape) for x in shapes],
        out_shape=shapes,
        compiler_params=params(),
        cost_estimate=lasting(0.2),
        name="fold",
    )(*operands)
    return result[0], result[1], (None if sums is None else result[2])


def finish_kernel(kinds, sum_kinds, keep_ref, arrived_ref, *refs):
    height = keep_ref.shape[0]
    if sum_kinds:
        start_ref, *refs = refs
    first = 0
    for kind, ref in zip(kinds, refs):
        depth = ref.shape[-2]
        for place in range(kind or 1):
            rows_here = slice(first, first + depth)
            total = keep_ref[rows_here, :] + arrived_ref[rows_here, :].astype(F32)
            if kind:
                ref[place] = total
            else:
                ref[...] = total
            first += depth
    if sum_kinds:
        total = start_ref[...] + arrived_sums(arrived_ref, height)
        first = 0
        for kind, ref in zip(sum_kinds, refs[len(kinds) :]):
            if ref.shape[0] == kind:
                ref[...] = total[first : first + kind, :]
            else:
                ref[...] = jnp.concatenate([total[first + k : first + k + 1] for k in range(kind)], 1)
            first += kind


def finish(keep, arrived, sums, kinds, sum_kinds):
    height, width = keep.shape
    depth = height // sum(kind or 1 for kind in kinds)
    operands = (keep, arrived) + (() if sums is None else (sums,))
    shapes = [struct((kind, depth, width) if kind else (depth, width), F32) for kind in kinds]
    shapes += [
        struct((kind, width) if kind == 2 else (1, kind * width), F32) for kind in sum_kinds
    ]
    return pl.pallas_call(
        functools.partial(finish_kernel, kinds, sum_kinds),
        grid=(1,),
        in_specs=[whole(x.shape) for x in operands],
        out_specs=[whole(x.shape) for x in shapes],
        out_shape=shapes,
        compiler_params=params(),
        cost_estimate=lasting(0.2),
        name="finish",
    )(*operands)


def token_grad_kernel(even_ref, *refs):
    query_refs, res_refs = refs[:CHUNKS], refs[CHUNKS : 2 * CHUNKS]
    key_ref, value_ref, *weight_refs = refs[2 * CHUNKS : 2 * CHUNKS + 5]
    own_ref, rim_ref, *out_refs = refs[2 * CHUNKS + 5 :]
    own_outs, rim_outs = out_refs[: len(out_refs) // 2], out_refs[len(out_refs) // 2 :]
    count, own = own_ref.shape
    even = even_ref[0] == 1

    def piece(start):
        return dot_nt(key_ref[start : start + BLOCK, :], weight_refs[1][...]) + dot_nt(
            value_ref[start : start + BLOCK, :], weight_refs[2][...]
        )

    def spread(value, start, stays_ref, leave_refs):
        stays_ref[start : start + BLOCK, :] = value[:, :own]
        for place, ref in enumerate(leave_refs, 1):
            lanes = slice(place * own, (place + 1) * own)
            ref[start : start + BLOCK, :] = value[:, lanes].astype(BF16)

    for start in range(0, HALO, BLOCK):
        low, high = piece(PAD + start), piece(MAXDOC + count + start)
        spread(jnp.where(even, high, low), start, rim_ref, rim_outs)
        spread(jnp.where(even, low, high), HALO + start, rim_ref, rim_outs)
    for start in range(0, count, BLOCK):
        chunk, inside = divmod(start, count // CHUNKS)
        total = piece(MAXDOC + start) + dot_nt(
            query_refs[chunk][inside : inside + BLOCK, :], weight_refs[0][...]
        )
        spread(total, start, own_ref, own_outs)
        own_ref[start : start + BLOCK, :] += res_refs[chunk][inside : inside + BLOCK, :]


def token_grads(even, query, res, key, value, weights):
    count = CHUNKS * query[0].shape[0]
    own = res[0].shape[1]
    leave = weights[0].shape[0] // own - 1
    operands = (*query, *res, key, value, *weights)
    shapes = [struct((count, own), F32), struct((2 * HALO, own), F32)]
    shapes += [struct((count, own), BF16)] * leave + [struct((2 * HALO, own), BF16)] * leave
    result = pl.pallas_call(
        token_grad_kernel,
        grid=(1,),
        in_specs=[pl.BlockSpec(memory_space=SMEM)] + [whole(x.shape) for x in operands],
        out_specs=[whole(x.shape) for x in shapes],
        out_shape=shapes,
        compiler_params=params(),
        cost_estimate=lasting(5.0),
        name="token_grads",
    )(even, *operands)
    return result[0], result[1], result[2 : 2 + leave], result[2 + leave :]


def rim_sum_kernel(rim_ref, *refs):
    *arrived_refs, inside_ref, across_ref = refs
    total = rim_ref[...] + sum(ref[...].astype(F32) for ref in arrived_refs)
    inside_ref[...] = total[:HALO].astype(BF16)
    across_ref[...] = total[HALO:].astype(BF16)


def rim_sum(rim, arrived):
    own = rim.shape[1]
    operands = (rim, *arrived)
    return pl.pallas_call(
        rim_sum_kernel,
        grid=(1,),
        in_specs=[whole(x.shape) for x in operands],
        out_specs=[whole((HALO, own))] * 2,
        out_shape=[struct((HALO, own), BF16)] * 2,
        compiler_params=params(),
        cost_estimate=lasting(0.3),
        name="rim_sum",
    )(*operands)


def token_sum_kernel(even_ref, own_ref, inside_ref, across_ref, *refs):
    *arrived_refs, out_ref = refs
    even = even_ref[0] == 1
    inside, across = inside_ref[...].astype(F32), across_ref[...].astype(F32)
    low, high = jnp.where(even, across, inside), jnp.where(even, inside, across)
    rest = own_ref.shape[0] - HALO
    for start in range(0, own_ref.shape[0], BLOCK):
        rows_here = slice(start, start + BLOCK)
        piece = own_ref[rows_here, :] + sum(ref[rows_here, :].astype(F32) for ref in arrived_refs)
        if start < HALO:
            piece = piece + low[rows_here, :]
        if start >= rest:
            piece = piece + high[start - rest : start - rest + BLOCK, :]
        out_ref[rows_here, :] = piece.astype(BF16)


def token_sum(even, own, inside, across, arrived):
    operands = (own, inside, across, *arrived)
    return pl.pallas_call(
        token_sum_kernel,
        grid=(1,),
        in_specs=[pl.BlockSpec(memory_space=SMEM)] + [whole(x.shape) for x in operands],
        out_specs=whole(own.shape),
        out_shape=struct(own.shape, BF16),
        compiler_params=params(),
        cost_estimate=lasting(0.3),
        name="token_sum",
    )(even, *operands)


def from_next(x, axis, step):
    count = lax.axis_size(axis)
    return lax.ppermute(x, axis, [((i + step) % count, i) for i in range(count)])


def others(x):
    return [from_next(x, "col", step) for step in range(1, lax.axis_size("col"))]


def bits_of(count):
    return [1 << place for place in range(count.bit_length() - 1)]


def orders_of(count):
    high = bits_of(count)[:0:-1]
    return high + [1], high[2:] + high[:2] + [1]


def slots_of(order, distance):
    return sum(((distance & bit) // bit) << place for place, bit in enumerate(order))


def distances_of(order, slots):
    return sum(((slots >> place) & 1) * bit for place, bit in enumerate(order))


def with_partner(x, step):
    count = lax.axis_size("row")
    orders = orders_of(count)
    return lax.ppermute(x, "row", [(i, i ^ orders[i % 2][step]) for i in range(count)])


def with_next(inside, across):
    count = lax.axis_size("row")
    pairs = [(i, i + 1 if i % 2 else i - 1) for i in range(1, count - 1)]
    return (
        lax.ppermute(inside, "row", [(i, i ^ 1) for i in range(count)]),
        lax.ppermute(across, "row", pairs),
    )


def after(value, *needed):
    return lax.optimization_barrier((value, *needed))[0]


class Gather:
    def __init__(self, shard):
        self.held, self.step = shard[None], 0
        self.count = len(bits_of(lax.axis_size("row")))
        self.move()

    def move(self):
        self.arrived = with_partner(self.held, self.step)
        self.step += 1

    def put(self, *needed):
        self.held = jnp.concatenate([after(self.held, *needed), self.arrived], 0)
        self.move()


class Reduction:
    def __init__(self, keep, send, sums, kinds, sum_kinds=()):
        self.step = len(bits_of(lax.axis_size("row")))
        self.keep, self.send, self.sums = keep, send, sums
        self.kinds, self.sum_kinds = kinds, sum_kinds
        self.result = None
        self.move()

    def move(self):
        self.step -= 1
        self.arrived = with_partner(self.send, self.step)

    def add(self, *needed):
        keep = after(self.keep, *needed)
        if self.step == 0:
            self.result = finish(keep, self.arrived, self.sums, self.kinds, self.sum_kinds)
        else:
            self.keep, self.send, self.sums = fold(keep, self.arrived, self.sums)
            self.move()


def exchanged(part):
    arrived = others(part)
    if len(arrived) == 1:
        return arrived[0]
    shift = part.shape[1] // (len(arrived) + 1)
    total = sum(
        jnp.roll(x.astype(F32), step * shift, 1) for step, x in enumerate(arrived, 1)
    )
    return total.astype(BF16)


def on_device(
    tokens,
    prev_logits,
    doc_lengths,
    qkv_weight,
    qv_bias,
    out_weight,
    out_bias,
    up_weight,
    up_bias,
    down_weight,
    norm_gain,
    norm_shift,
    out_grad,
    logit_grad,
):
    count, own = tokens.shape
    width = qkv_weight.shape[2]
    row_count, col_count = lax.axis_size("row"), lax.axis_size("col")
    row_index, col_index = lax.axis_index("row"), lax.axis_index("col")
    token_count = count * row_count
    swap = col_count == 2
    hidden_rows = up_bias.shape[0] // own

    odd = row_index % 2 == 1
    places = jnp.arange(row_count, dtype=jnp.int32)
    offset = col_index * (row_count // col_count)
    distance = ((places + offset) % row_count) ^ row_index
    half = row_count // 2
    even_order, odd_order = (order[:-1] for order in orders_of(row_count))
    turned = odd ^ (distance % 2 == 1)
    slots = jnp.where(turned, slots_of(odd_order, distance), slots_of(even_order, distance))
    slots = slots + half * (distance % 2)
    turned = odd ^ (places >= half)
    met = jnp.where(turned, distances_of(odd_order, places), distances_of(even_order, places))
    blocks = (((met + (places >= half)) ^ row_index) - offset) % row_count

    even = 1 - row_index % 2
    even = even.astype(jnp.int32)[None]

    def dense_of(banded, fill, chunk, *needed):
        dense = to_dense(after(banded, *needed), lengths, fill, token_count, chunk)
        return dense

    prev_logits = pltpu.with_memory_space_constraint(prev_logits, pltpu.HBM)

    out_turned = out_weight.T
    out_other = others(out_turned)
    qkv_rows = Gather(qkv_weight)
    tokens_other = others(after(tokens, out_turned))
    feed_rows = Gather(jnp.concatenate([out_turned, *out_other, up_weight, down_weight.T], 1))
    tail = row_index % 2 * (count - HALO)
    ready = after(tokens, feed_rows.held)
    inside, across = with_next(
        lax.dynamic_slice_in_dim(ready, count - HALO - tail, HALO, 0),
        lax.dynamic_slice_in_dim(ready, tail, HALO, 0),
    )
    qkv_rows.put(feed_rows.held)
    inside_other, across_other = others(inside), others(across)
    feed_rows.put(qkv_rows.held)
    qkv_rows.put(feed_rows.held, *tokens_other)
    lengths = jnp.concatenate(
        [after(doc_lengths, qkv_rows.held).reshape(-1), (row_index * count)[None]]
    )
    prev_dense = [
        dense_of(prev_logits, MASKED_SCORE, 0, qkv_rows.held, feed_rows.held, inside, across)
    ]
    grad_other = others(after(out_grad, *inside_other))
    while qkv_rows.step < qkv_rows.count:
        qkv_rows.put(prev_dense[0], *inside_other, *across_other)
    feed_rows.put(qkv_rows.held)
    tokens_full, query, key, value, low_tokens, high_tokens, *projections = project(
        slots, even, qkv_rows.held, qkv_rows.arrived, qv_bias, [after(tokens, feed_rows.held), *tokens_other],
        [inside, *inside_other], [across, *across_other],
    )
    grad_full = jnp.concatenate([after(out_grad, query)] + grad_other, 1)
    norms = jnp.concatenate([after(norm_gain, query), norm_shift, out_bias], 0)
    norms = jnp.concatenate([norms] + others(norms), 1)
    scores, probs, attended, attended_other = [], [], [], []
    for chunk in range(CHUNKS):
        score, prob, mix = attend_forward(
            after(query, feed_rows.held) if chunk else query, key, value, prev_dense[chunk], chunk
        )
        scores.append(score)
        probs.append(prob)
        attended.append(mix)
        attended_other.append(jnp.concatenate(others(mix), 1))
        if chunk == 0:
            prev_dense.append(dense_of(prev_logits, MASKED_SCORE, 1, mix, norms, grad_full))
            while feed_rows.step < feed_rows.count:
                feed_rows.put(prev_dense[1], attended_other[0])
    other_out, *weights = in_order(
        slots, after(feed_rows.held, mix), feed_rows.arrived,
        (width, (col_count - 1) * width, up_weight.shape[1], up_weight.shape[1]),
    )
    weights[0], other_out = other_out, weights[0]
    ups = up_bias[None]
    firsts, logit_dense = [], []
    for chunk in range(CHUNKS):
        result = feed_first(
            attended[chunk], attended_other[chunk], tokens_full, other_out, weights, norms, ups,
            chunk,
        )
        if chunk == 0:
            logit_dense.append(dense_of(logit_grad, 0.0, 0, result[-1]))
            ups = after(ups, logit_dense[0])
        firsts.append((*result, exchanged(result[-1])))
    normed, inverse, upper, act, slope, down_part, down_other = zip(*firsts)

    new_logits = to_band([after(scores[0], down_part[-1])], True)
    sums = after(jnp.zeros((SUM_ROWS, own), F32), new_logits)
    output = None
    seconds = []
    for chunk in range(CHUNKS):
        sums, output, *result = feed_second(
            swap, sums, output, down_part[chunk], down_other[chunk],
            normed[chunk], grad_full, slope[chunk], weights, norms, chunk,
        )
        seconds.append((*result, exchanged(result[-1])))
    res_two, ffn_low, hidden_grad, lower_part, lower_other = zip(*seconds)
    keep, send = feed_grads(blocks, ffn_low, act, upper, hidden_grad)
    feed_sum = Reduction(keep, send, None, (0, 0))
    sums = after(sums, keep)

    branch_low, res_one, query_grad, prev_dense_grad = [], [], [], []
    partial = None
    for chunk in range(CHUNKS):
        sums, low, attended_grad, res = feed_third(
            swap, sums, width, lower_part[chunk], lower_other[chunk], res_two[chunk],
            normed[chunk], inverse[chunk], weights, norms,
        )
        branch_low.append(low)
        res_one.append(res)
        prev, query_part, *partial = attend_backward(
            attended_grad, query, key, value, probs[chunk], logit_dense[chunk], chunk, partial
        )
        if chunk == 0:
            feed_sum.add(query_part)
            logit_dense.append(dense_of(logit_grad, 0.0, 1, feed_sum.keep))
            sums = after(sums, logit_dense[1])
        prev_dense_grad.append(prev)
        query_grad.append(query_part)
    key_grad, value_grad = partial
    feed_sum.add(query_grad[-1])
    keep, send, sums = project_grads(
        blocks, after(sums, feed_sum.keep), tokens_full, low_tokens, high_tokens, query_grad,
        key_grad, value_grad, branch_low, attended,
    )
    last_sum = Reduction(keep, send, sums, (3, 0), (2, 2, 2, 2, hidden_rows))
    center, rim, center_parts, rim_parts = token_grads(
        even, query_grad, res_one, after(key_grad, keep), value_grad, projections
    )

    def spread_over(parts):
        return [from_next(part, "col", -step) for step, part in enumerate(parts, 1)]

    last_sum.add(center)
    rim_parts = spread_over(rim_parts)
    center_parts = spread_over(after(x, rim) for x in center_parts)
    prev_dense_grad[0] = after(prev_dense_grad[0], last_sum.keep)
    prev_grad = to_band(prev_dense_grad, False)
    last_sum.add(prev_grad)
    inside, across = rim_sum(after(rim, last_sum.keep), rim_parts)
    feed_sum.add(inside)
    inside, across = with_next(inside, across)
    last_sum.add(feed_sum.keep)
    for chunk in range(1, CHUNKS):
        new_logits = to_band([after(scores[chunk], last_sum.keep)], True, chunk, new_logits)
    tokens_grad = token_sum(even, after(center, new_logits), inside, across, center_parts)
    while feed_sum.result is None:
        feed_sum.add(tokens_grad)
    while last_sum.result is None:
        last_sum.add(feed_sum.result[0])
    qkv_grad, out_grad_rows, qv_sum, bias_sum, gain_sum, shift_sum, hidden_sum = last_sum.result
    up_grad, down_grad = feed_sum.result
    return (
        output,
        new_logits,
        tokens_grad,
        prev_grad,
        qkv_grad,
        qv_sum,
        out_grad_rows.T,
        bias_sum,
        up_grad,
        hidden_sum.reshape(-1),
        down_grad.T,
        gain_sum,
        shift_sum,
    )


def solution(mesh):
    return jax.shard_map(
        on_device,
        mesh=mesh,
        in_specs=(
            P("row", "col"),
            P("col", "row", None),
            P(),
            P(None, "row", "col"),
            P(None, "col"),
            P("col", "row"),
            P(None, "col"),
            P("row", "col"),
            P("col"),
            P("col", "row"),
            P(None, "col"),
            P(None, "col"),
            P("row", "col"),
            P("col", "row", None),
        ),
        out_specs=(
            P("row", "col"),
            P("col", "row", None),
            P("row", "col"),
            P("col", "row", None),
            P(None, "row", "col"),
            P(None, "col"),
            P("col", "row"),
            P(None, "col"),
            P("row", "col"),
            P("col"),
            P("col", "row"),
            P(None, "col"),
            P(None, "col"),
        ),
        check_vma=False,
    )
```

```python
import functools

import jax
import jax.numpy as jnp
from jax import lax
from jax.experimental import pallas as pl
from jax.experimental.pallas import tpu as pltpu
from jax.sharding import PartitionSpec as P

D = 512
HEAD_DIM = 64
MAXDOC = 512
BAND = 2 * MAXDOC
BLOCK = 128
WINDOW = BAND + BLOCK
HALO = MAXDOC - 128
PAD = MAXDOC - HALO

EPSILON = 1e-05
MASKED_SCORE = -1e30
ERF_RATE = 0.7071067811865476
DENSITY_RATE = 0.3989422804014327

F32 = jnp.float32
BF16 = jnp.bfloat16
SMEM = pltpu.MemorySpace.SMEM
VMEM_LIMIT = 24 << 20
CHUNKS = 2
SUM_ROWS = 16
FLOPS_PER_MICROSECOND = 1.0e9


def dot_nn(a, b):
    return lax.dot_general(a, b, (((1,), (0,)), ((), ())), preferred_element_type=F32)


def dot_nt(a, b):
    return lax.dot_general(a, b, (((1,), (1,)), ((), ())), preferred_element_type=F32)


def dot_tn(a, b):
    return lax.dot_general(a, b, (((0,), (0,)), ((), ())), preferred_element_type=F32)


def params():
    return pltpu.CompilerParams(
        dimension_semantics=("arbitrary",), vmem_limit_bytes=VMEM_LIMIT
    )


def lasting(microseconds):
    return pl.CostEstimate(
        flops=int(microseconds * FLOPS_PER_MICROSECOND), bytes_accessed=0, transcendentals=0
    )


def whole(shape):
    return pl.BlockSpec(shape, lambda b: (0,) * len(shape))


def rows(width, first=0):
    return pl.BlockSpec((BLOCK, width), lambda b: (b + first, 0))


def heads_block(heads, width, first=0):
    return pl.BlockSpec((heads, BLOCK, width), lambda b: (0, b + first, 0))


def struct(shape, dtype):
    return jax.ShapeDtypeStruct(shape, dtype)


def segment_of(positions, lengths_ref, documents, token_count):
    found = jnp.zeros(positions.shape, jnp.int32)
    end = jnp.int32(0)
    for document in range(documents):
        end = end + lengths_ref[document]
        found = found + (positions >= end).astype(jnp.int32)
    return jnp.where((positions >= 0) & (positions < token_count), found, -1)


def dense_kernel(fill, token_count, offset, lengths_ref, band_ref, dense_ref):
    documents = lengths_ref.shape[0] - 1
    first = lengths_ref[documents] + (pl.program_id(0) + offset) * BLOCK
    query = first + lax.broadcasted_iota(jnp.int32, (BLOCK, 1), 0)
    key = first - MAXDOC + lax.broadcasted_iota(jnp.int32, (1, WINDOW), 1)
    same = segment_of(query, lengths_ref, documents, token_count) == segment_of(
        key, lengths_ref, documents, token_count
    )
    for head in range(band_ref.shape[0]):
        wide = jnp.concatenate(
            [band_ref[head].astype(F32), jnp.zeros((BLOCK, BLOCK), F32)], 1
        )
        turned = pltpu.roll(wide, 0, 1, stride=1, stride_axis=0)
        dense_ref[head] = jnp.where(same, turned, fill).astype(BF16)


def to_dense(banded, lengths, fill, token_count, chunk):
    heads, count, _ = banded.shape
    count //= CHUNKS
    offset = chunk * (count // BLOCK)
    return pl.pallas_call(
        functools.partial(dense_kernel, fill, token_count, offset),
        grid=(count // BLOCK,),
        in_specs=[pl.BlockSpec(memory_space=SMEM), heads_block(heads, BAND, offset)],
        out_specs=heads_block(heads, WINDOW),
        out_shape=struct((heads, count, WINDOW), BF16),
        compiler_params=params(),
        cost_estimate=lasting(8.0 if fill and chunk == 0 else 1.0),
        name="to_dense",
    )(lengths, banded)


def band_kernel(masked, chunks, *refs):
    dense_refs, band_ref = refs[:chunks], refs[-1]
    lane = lax.broadcasted_iota(jnp.int32, (BLOCK, BLOCK), 1)
    row = lax.broadcasted_iota(jnp.int32, (BLOCK, BLOCK), 0)
    source = (lane + row) & (BLOCK - 1)
    near = lane + row < BLOCK
    steps = pl.num_programs(0) // chunks

    def turn(dense_ref):
        for head in range(band_ref.shape[0]):
            pieces = []
            for place in range(WINDOW // BLOCK):
                piece = dense_ref[head, :, place * BLOCK : (place + 1) * BLOCK].astype(F32)
                if masked:
                    piece = jnp.where(piece < 0.5 * MASKED_SCORE, 0.0, piece)
                pieces.append(jnp.take_along_axis(piece, source, axis=1))
            for place in range(BAND // BLOCK):
                band_ref[head, :, place * BLOCK : (place + 1) * BLOCK] = jnp.where(
                    near, pieces[place], pieces[place + 1]
                ).astype(BF16)

    for chunk, dense_ref in enumerate(dense_refs):

        @pl.when(pl.program_id(0) // steps == chunk)
        def _():
            turn(dense_ref)


def to_band(chunks, masked, first=0, held=None):
    heads, count, _ = chunks[0].shape
    steps = count // BLOCK

    def block_of(chunk):
        return pl.BlockSpec(
            (heads, BLOCK, WINDOW), lambda b: (0, jnp.clip(b - chunk * steps, 0, steps - 1), 0)
        )

    return pl.pallas_call(
        functools.partial(band_kernel, masked, len(chunks)),
        grid=(len(chunks) * steps,),
        in_specs=[block_of(chunk) for chunk in range(len(chunks))]
        + ([] if held is None else [pl.BlockSpec(memory_space=pl.ANY)]),
        out_specs=heads_block(heads, BAND, first * steps),
        out_shape=struct((heads, CHUNKS * count, BAND), BF16),
        input_output_aliases={} if held is None else {len(chunks): 0},
        compiler_params=params(),
        cost_estimate=lasting(5.0 if masked and held is None else 0.3),
        name="to_band",
    )(*chunks, *(() if held is None else (held,)))


def head_split(block, size):
    if size == 1:
        return block
    lane = lax.broadcasted_iota(jnp.int32, block.shape, 1)
    return jnp.concatenate(
        [
            jnp.where((lane >= h * HEAD_DIM) & (lane < (h + 1) * HEAD_DIM), block, 0)
            for h in range(size)
        ],
        0,
    )


def head_join(stacked, size):
    if size == 1:
        return stacked
    height = stacked.shape[0] // size
    joined = stacked[:height]
    lane = lax.broadcasted_iota(jnp.int32, joined.shape, 1)
    for h in range(1, size):
        joined = jnp.where(lane >= h * HEAD_DIM, stacked[h * height : (h + 1) * height], joined)
    return joined


def project_kernel(
    parts, slot_ref, even_ref, near_ref, far_ref, bias_ref, *refs
):
    token_refs, inside_refs, across_refs = (refs[k * parts : (k + 1) * parts] for k in range(3))
    all_ref, query_ref, key_ref, value_ref, low_ref, high_ref, *weight_refs = refs[3 * parts :]
    half, _, depth, _ = near_ref.shape
    count, width = token_refs[0].shape

    def put(place, source_ref, slot):
        for which, ref in enumerate(weight_refs):
            ref[place * depth : (place + 1) * depth, :] = source_ref[slot, which]

    for place in range(2 * half):
        slot = slot_ref[place]

        @pl.when(slot < half)
        def _():
            put(place, near_ref, slot)

        @pl.when(slot >= half)
        def _():
            put(place, far_ref, slot - half)

    even = even_ref[0] == 1
    for place, (own_ref, inside_ref, across_ref) in enumerate(
        zip(token_refs, inside_refs, across_refs)
    ):
        lanes = slice(place * width, (place + 1) * width)
        inside, across = inside_ref[...], across_ref[...]
        all_ref[:, lanes] = own_ref[...]
        low_ref[:, lanes] = jnp.where(even, across, inside)
        high_ref[:, lanes] = jnp.where(even, inside, across)
    own, low_rows, high_rows = all_ref[...], low_ref[...], high_ref[...]
    query = (dot_nn(own, weight_refs[0][...]) + bias_ref[0:1, :]).astype(BF16)
    empty = jnp.zeros((PAD, query.shape[1]), BF16)
    query_ref[...] = query * jnp.asarray(HEAD_DIM ** (-0.5), BF16)
    for out_ref, which in ((key_ref, 1), (value_ref, 2)):
        shift = bias_ref[1:2, :] if which == 2 else 0.0
        weight = weight_refs[which][...]
        out_ref[0:PAD, :] = empty
        out_ref[PAD:MAXDOC, :] = (dot_nn(low_rows, weight) + shift).astype(BF16)
        out_ref[MAXDOC : MAXDOC + count, :] = (dot_nn(own, weight) + shift).astype(BF16)
        out_ref[MAXDOC + count : MAXDOC + count + HALO, :] = (
            dot_nn(high_rows, weight) + shift
        ).astype(BF16)
        out_ref[MAXDOC + count + HALO :, :] = empty


def project(slots, even, near, far, bias, tokens, inside, across):
    count, part = tokens[0].shape
    features = len(tokens) * part
    width = near.shape[3]
    operands = (near, far, bias, *tokens, *inside, *across)
    extended = (count + BAND, width)
    shapes = [(count, features), (count, width), extended, extended]
    shapes += [(HALO, features)] * 2 + [(features, width)] * 3
    return pl.pallas_call(
        functools.partial(project_kernel, len(tokens)),
        grid=(1,),
        in_specs=[pl.BlockSpec(memory_space=SMEM)] * 2 + [whole(x.shape) for x in operands],
        out_specs=[whole(shape) for shape in shapes],
        out_shape=[struct(shape, BF16) for shape in shapes],
        compiler_params=params(),
        cost_estimate=lasting(2.0),
        name="project",
    )(slots, even, *operands)


def by_edge(block, last, body):
    edge = (block == 0) | (block == last)

    @pl.when(edge)
    def _():
        body(BLOCK, WINDOW - 2 * BLOCK)

    @pl.when(jnp.logical_not(edge))
    def _():
        body(0, WINDOW)


def forward_kernel(
    offset, query_ref, key_ref, value_ref, prev_ref, score_ref, prob_ref, attended_ref
):
    heads = prev_ref.shape[0]
    size = min(2, heads)
    span = size * HEAD_DIM
    block = pl.program_id(0) + offset

    def body(first, width):
        window = pl.ds(pl.multiple_of(block * BLOCK + first, BLOCK), width)
        inside = slice(first, first + width)
        for group in range(heads // size):
            lanes = slice(group * span, (group + 1) * span)
            query = head_split(query_ref[:, lanes], size)
            dense = dot_nt(query, key_ref[window, lanes])
            weights = []
            for h in range(size):
                head = group * size + h
                score = dense[h * BLOCK : (h + 1) * BLOCK] + prev_ref[head, :, inside].astype(F32)
                score_ref[head, :, inside] = score.astype(BF16)
                if first:
                    empty = jnp.full((BLOCK, first), MASKED_SCORE, BF16)
                    score_ref[head, :, :first] = empty
                    score_ref[head, :, first + width :] = empty
                peak = jnp.max(score, -1, keepdims=True)
                grown = jnp.exp(score - peak)
                total = jnp.sum(grown, -1, keepdims=True)
                prob = (grown * (1.0 / total)).astype(BF16)
                prob_ref[head, :, inside] = prob
                weights.append(prob)
            mixed = dot_nn(jnp.concatenate(weights, 0), value_ref[window, lanes])
            attended_ref[:, lanes] = head_join(mixed, size).astype(BF16)

    by_edge(block, key_ref.shape[0] // BLOCK - WINDOW // BLOCK, body)


def attend_forward(query, key, value, prev, chunk):
    heads, count, _ = prev.shape
    width = query.shape[1]
    offset = chunk * (count // BLOCK)
    return pl.pallas_call(
        functools.partial(forward_kernel, offset),
        grid=(count // BLOCK,),
        in_specs=[
            rows(width, offset),
            whole(key.shape),
            whole(value.shape),
            heads_block(heads, WINDOW),
        ],
        out_specs=[heads_block(heads, WINDOW), heads_block(heads, WINDOW), rows(width)],
        out_shape=[
            struct((heads, count, WINDOW), BF16),
            struct((heads, count, WINDOW), BF16),
            struct((count, width), BF16),
        ],
        compiler_params=params(),
        cost_estimate=lasting(3.8),
        name="attend_forward",
    )(query, key, value, prev)


def backward_kernel(
    offset, last, grad_ref, query_ref, key_ref, value_ref, prob_ref, logit_ref, *refs
):
    if last:
        key_start, value_start = refs[:2]
        prev_ref, query_grad_ref, key_grad_ref, value_grad_ref, key_sum, value_sum = refs[2:]
    else:
        prev_ref, query_grad_ref, key_sum, value_sum = refs
    step = pl.program_id(0)
    heads = prob_ref.shape[0]
    size = min(2, heads)
    span = size * HEAD_DIM

    @pl.when(step == 0)
    def _():
        if last:
            key_sum[...] = key_start[...]
            value_sum[...] = value_start[...]
        else:
            key_sum[...] = jnp.zeros_like(key_sum)
            value_sum[...] = jnp.zeros_like(value_sum)

    block = step + offset

    def body(first, width):
        window = pl.ds(pl.multiple_of(block * BLOCK + first, BLOCK), width)
        inside = slice(first, first + width)
        for group in range(heads // size):
            lanes = slice(group * span, (group + 1) * span)
            query = head_split(query_ref[:, lanes], size)
            grad = head_split(grad_ref[:, lanes], size)
            key = key_ref[window, lanes]
            prob_grad = dot_nt(grad, value_ref[window, lanes])
            probs, scores = [], []
            for h in range(size):
                head = group * size + h
                low = prob_ref[head, :, inside]
                prob = low.astype(F32)
                slope = prob_grad[h * BLOCK : (h + 1) * BLOCK]
                inner = jnp.sum(prob * slope, -1, keepdims=True)
                score = prob * (slope - inner) + logit_ref[head, :, inside].astype(F32)
                score = score.astype(BF16)
                prev_ref[head, :, inside] = score
                if first:
                    empty = jnp.zeros((BLOCK, first), BF16)
                    prev_ref[head, :, :first] = empty
                    prev_ref[head, :, first + width :] = empty
                probs.append(low)
                scores.append(score)
            stacked = jnp.concatenate(scores, 0)
            mixed = head_join(dot_nn(stacked, key), size) * HEAD_DIM ** (-0.5)
            query_grad_ref[:, lanes] = mixed.astype(BF16)
            key_sum[lanes, window] += dot_tn(query, stacked)
            value_sum[lanes, window] += dot_tn(grad, jnp.concatenate(probs, 0))

    by_edge(block, key_ref.shape[0] // BLOCK - WINDOW // BLOCK, body)

    if last:

        @pl.when(step == pl.num_programs(0) - 1)
        def _():
            key_grad_ref[...] = key_sum[...].astype(BF16).T
            value_grad_ref[...] = value_sum[...].astype(BF16).T


def attend_backward(grad, query, key, value, prob, logit, chunk, sums):
    heads, count, _ = prob.shape
    extended, width = key.shape
    offset = chunk * (count // BLOCK)
    last = sums is not None
    turned = (width, extended)
    scratch = [pltpu.VMEM(turned, F32), pltpu.VMEM(turned, F32)] if last else []
    ends = [whole((extended, width))] * 2 if last else [whole(turned)] * 2
    end_shapes = [struct((extended, width), BF16)] * 2 if last else [struct(turned, F32)] * 2
    return pl.pallas_call(
        functools.partial(backward_kernel, offset, last),
        grid=(count // BLOCK,),
        in_specs=[
            rows(width),
            rows(width, offset),
            whole((extended, width)),
            whole((extended, width)),
            heads_block(heads, WINDOW),
            heads_block(heads, WINDOW),
        ]
        + ([whole(turned)] * 2 if last else []),
        out_specs=[heads_block(heads, WINDOW), rows(width)] + ends,
        out_shape=[struct((heads, count, WINDOW), BF16), struct((count, width), BF16)]
        + end_shapes,
        scratch_shapes=scratch,
        compiler_params=params(),
        cost_estimate=lasting(3.0 if last else 20.0),
        name="attend_backward",
    )(grad, query, key, value, prob, logit, *(sums or ()))


def order_kernel(slot_ref, near_ref, far_ref, *out_refs):
    half, depth, _ = near_ref.shape

    def put(place, source_ref, slot):
        first = 0
        for out_ref in out_refs:
            last = first + out_ref.shape[1]
            out_ref[place * depth : (place + 1) * depth, :] = source_ref[slot, :, first:last]
            first = last

    for place in range(2 * half):
        slot = slot_ref[place]

        @pl.when(slot < half)
        def _():
            put(place, near_ref, slot)

        @pl.when(slot >= half)
        def _():
            put(place, far_ref, slot - half)


def in_order(slots, near, far, widths):
    half, depth, _ = near.shape
    shapes = [(2 * half * depth, width) for width in widths]
    return pl.pallas_call(
        order_kernel,
        grid=(1,),
        in_specs=[pl.BlockSpec(memory_space=SMEM), whole(near.shape), whole(far.shape)],
        out_specs=[whole(shape) for shape in shapes],
        out_shape=[struct(shape, BF16) for shape in shapes],
        compiler_params=params(),
        cost_estimate=lasting(0.9),
        name="in_order",
    )(slots, near, far)


def mean_of(x):
    return jnp.sum(x, -1, keepdims=True) * (1.0 / D)


def normalized(hidden):
    mean = mean_of(hidden)
    inverse = lax.rsqrt(mean_of(hidden * hidden) - mean * mean + EPSILON)
    return (hidden - mean) * inverse, inverse


def norm_back(upstream, normed, inverse):
    return inverse * (upstream - mean_of(upstream) - normed * mean_of(upstream * normed))


def added(own_ref, other_ref, swap):
    other = other_ref[...]
    if swap:
        middle = other.shape[1] // 2
        other = jnp.concatenate([other[:, middle:], other[:, :middle]], 1)
    return own_ref[...].astype(F32) + other.astype(F32)


def first_kernel(
    own_ref, other_ref, token_ref, other_out_ref, out_ref, up_ref, down_ref, norm_ref,
    up_bias_ref, normed_ref, inverse_ref, upper_ref, act_ref, slope_ref, part_ref,
):
    branch = dot_nt(own_ref[...], out_ref[...]) + dot_nt(other_ref[...], other_out_ref[...])
    hidden = token_ref[...].astype(F32) + branch + norm_ref[4:5, :]
    normed, inverse = normalized(hidden)
    normed_ref[...] = normed
    inverse_ref[...] = inverse
    upper = (normed * norm_ref[0:1, :] + norm_ref[2:3, :]).astype(BF16)
    upper_ref[...] = upper
    pre = dot_nn(upper, up_ref[...]) + up_bias_ref[...]
    share = 0.5 * (1.0 + lax.erf(pre * ERF_RATE))
    act = (pre * share).astype(BF16)
    act_ref[...] = act
    slope_ref[...] = (share + pre * jnp.exp(-0.5 * pre * pre) * DENSITY_RATE).astype(BF16)
    part_ref[...] = dot_nt(act, down_ref[...]).astype(BF16)


def feed_first(own, other, tokens, other_out, weights, norms, up_bias, chunk):
    count, width = own.shape
    features = tokens.shape[1]
    units = up_bias.shape[1]
    return pl.pallas_call(
        first_kernel,
        grid=(count // BLOCK,),
        in_specs=[
            rows(width),
            rows(other.shape[1]),
            rows(features, chunk * (count // BLOCK)),
            whole(other_out.shape),
            *(whole(x.shape) for x in weights),
            whole(norms.shape),
            whole(up_bias.shape),
        ],
        out_specs=[
            rows(features),
            rows(1),
            rows(features),
            rows(units),
            rows(units),
            rows(features),
        ],
        out_shape=[
            struct((count, features), F32),
            struct((count, 1), F32),
            struct((count, features), BF16),
            struct((count, units), BF16),
            struct((count, units), BF16),
            struct((count, features), BF16),
        ],
        compiler_params=params(),
        cost_estimate=lasting(1.0),
        name="feed_first",
    )(own, other, tokens, other_out, *weights, norms, up_bias)


def add_sums(start_ref, sum_ref, first, values):
    @pl.when(pl.program_id(0) == 0)
    def _():
        sum_ref[...] = start_ref[...]

    for place, value in enumerate(values):
        sum_ref[first + place : first + place + 1, :] += jnp.sum(value, 0, keepdims=True)


def second_kernel(
    swap, start_ref, part_ref, recv_ref, normed_ref, grad_ref, slope_ref, up_ref, down_ref,
    norm_ref, *refs,
):
    sum_ref, output_ref, res_ref, low_ref, hidden_ref, lower_ref = refs[-6:]
    own = output_ref.shape[1]
    upper = normed_ref[...] * norm_ref[0:1, :] + norm_ref[2:3, :]
    hidden = upper + added(part_ref, recv_ref, swap) + norm_ref[5:6, :]
    normed, inverse = normalized(hidden)
    output_ref[...] = (
        normed[:, :own] * norm_ref[1:2, :own] + norm_ref[3:4, :own]
    ).astype(BF16)
    grad = grad_ref[...].astype(F32)
    res = norm_back(grad * norm_ref[1:2, :], normed, inverse)
    res_ref[...] = res
    low = res.astype(BF16)
    low_ref[...] = low
    act_grad = dot_nn(low, down_ref[...])
    hidden_grad = (act_grad * slope_ref[...].astype(F32)).astype(BF16)
    hidden_ref[...] = hidden_grad
    lower_ref[...] = dot_nt(hidden_grad, up_ref[...]).astype(BF16)
    wide = hidden_grad.astype(F32)
    add_sums(start_ref, sum_ref, 3, [low[:, :own].astype(F32)])
    for place, value in (
        (5, grad[:, :own] * normed[:, :own]),
        (7, grad[:, :own]),
        *((8 + k, wide[:, k * own : (k + 1) * own]) for k in range(wide.shape[1] // own)),
    ):
        sum_ref[place : place + 1, :] += jnp.sum(value, 0, keepdims=True)


def feed_second(swap, sums, held, part, recv, normed, grad, slope, weights, norms, chunk):
    count, features = part.shape
    own = sums.shape[1]
    units = slope.shape[1]
    offset = chunk * (count // BLOCK)
    return pl.pallas_call(
        functools.partial(second_kernel, swap),
        grid=(count // BLOCK,),
        in_specs=[
            whole(sums.shape),
            rows(features),
            rows(features),
            rows(features),
            rows(features, offset),
            rows(units),
            *(whole(x.shape) for x in weights[1:]),
            whole(norms.shape),
            *([] if held is None else [pl.BlockSpec(memory_space=pl.ANY)]),
        ],
        out_specs=[
            whole(sums.shape),
            rows(own, offset),
            rows(features),
            rows(features),
            rows(units),
            rows(features),
        ],
        out_shape=[
            struct(sums.shape, F32),
            struct((CHUNKS * count, own), BF16),
            struct((count, features), F32),
            struct((count, features), BF16),
            struct((count, units), BF16),
            struct((count, features), BF16),
        ],
        input_output_aliases={} if held is None else {9: 1},
        compiler_params=params(),
        cost_estimate=lasting(0.7),
        name="feed_second",
    )(sums, part, recv, normed, grad, slope, *weights[1:], norms, *(() if held is None else (held,)))


def third_kernel(
    swap, start_ref, part_ref, recv_ref, res_ref, normed_ref, inverse_ref, out_ref, norm_ref,
    sum_ref, low_ref, attended_ref, own_ref,
):
    own = own_ref.shape[1]
    grad = added(part_ref, recv_ref, swap) + res_ref[...]
    normed = normed_ref[...]
    res = norm_back(grad * norm_ref[0:1, :], normed, inverse_ref[...])
    own_ref[...] = res[:, :own]
    low = res.astype(BF16)
    low_ref[...] = low
    attended_ref[...] = dot_nn(low, out_ref[...]).astype(BF16)
    add_sums(start_ref, sum_ref, 2, [low[:, :own].astype(F32)])
    for place, value in ((4, grad[:, :own] * normed[:, :own]), (6, grad[:, :own])):
        sum_ref[place : place + 1, :] += jnp.sum(value, 0, keepdims=True)


def feed_third(swap, sums, width, part, recv, res, normed, inverse, weights, norms):
    count, features = part.shape
    own = sums.shape[1]
    return pl.pallas_call(
        functools.partial(third_kernel, swap),
        grid=(count // BLOCK,),
        in_specs=[
            whole(sums.shape),
            rows(features),
            rows(features),
            rows(features),
            rows(features),
            rows(1),
            whole(weights[0].shape),
            whole(norms.shape),
        ],
        out_specs=[whole(sums.shape), rows(features), rows(width), rows(own)],
        out_shape=[
            struct(sums.shape, F32),
            struct((count, features), BF16),
            struct((count, width), BF16),
            struct((count, own), F32),
        ],
        compiler_params=params(),
        cost_estimate=lasting(0.2),
        name="feed_third",
    )(sums, part, recv, res, normed, inverse, weights[0], norms)


def spread_rows(block_ref, scratch, keep_ref, send_ref, which, kinds):
    features = scratch.shape[0]
    count = block_ref.shape[0]
    depth = features // count
    half = count // 2
    for slot in range(count):
        start = pl.multiple_of(block_ref[slot] * depth, depth)
        piece = scratch[pl.ds(start, depth), :]
        first = ((slot % half) * kinds + which) * depth
        if slot < half:
            keep_ref[first : first + depth, :] = piece
        else:
            send_ref[first : first + depth, :] = piece.astype(BF16)


def split_sums(total):
    high = total.astype(BF16)
    low = (total - high.astype(F32)).astype(BF16)
    return high, low, high.astype(F32) + low.astype(F32)


def feed_grad_kernel(block_ref, *refs):
    low_refs, upper_refs, act_refs, hidden_refs = (
        refs[k * CHUNKS : (k + 1) * CHUNKS] for k in range(4)
    )
    keep_ref, send_ref, scratch = refs[4 * CHUNKS :]
    scratch[...] = sum(dot_tn(a[...], b[...]) for a, b in zip(upper_refs, hidden_refs))
    spread_rows(block_ref, scratch, keep_ref, send_ref, 0, 2)
    scratch[...] = sum(dot_tn(a[...], b[...]) for a, b in zip(low_refs, act_refs))
    spread_rows(block_ref, scratch, keep_ref, send_ref, 1, 2)


def feed_grads(blocks, low, act, upper, hidden):
    count, features = low[0].shape
    units = act[0].shape[1]
    chunk = min(256, units)
    column = pl.BlockSpec((count, chunk), lambda b: (0, b))
    result = pl.BlockSpec((features, chunk), lambda b: (0, b))
    return pl.pallas_call(
        feed_grad_kernel,
        grid=(units // chunk,),
        in_specs=[pl.BlockSpec(memory_space=SMEM)]
        + [whole((count, features))] * (2 * CHUNKS)
        + [column] * (2 * CHUNKS),
        out_specs=[result] * 2,
        out_shape=[struct((features, units), F32), struct((features, units), BF16)],
        scratch_shapes=[pltpu.VMEM((features, chunk), F32)],
        compiler_params=params(),
        cost_estimate=lasting(1.0),
        name="feed_grads",
    )(blocks, *low, *upper, *act, *hidden)


def project_grad_kernel(block_ref, start_ref, *refs):
    query_refs, branch_refs, attended_refs = (
        refs[k * CHUNKS : (k + 1) * CHUNKS] for k in range(3)
    )
    token_ref, low_ref, high_ref, key_ref, value_ref = refs[3 * CHUNKS : 3 * CHUNKS + 5]
    keep_ref, send_ref, sum_ref, scratch = refs[3 * CHUNKS + 5 :]
    count = token_ref.shape[0]
    part = count // CHUNKS
    scratch[...] = sum(
        dot_tn(token_ref[k * part : (k + 1) * part, :], ref[...])
        for k, ref in enumerate(query_refs)
    )
    spread_rows(block_ref, scratch, keep_ref, send_ref, 0, 4)
    for which, ref in ((1, key_ref), (2, value_ref)):
        scratch[...] = (
            dot_tn(token_ref[...], ref[MAXDOC : MAXDOC + count, :])
            + dot_tn(low_ref[...], ref[PAD:MAXDOC, :])
            + dot_tn(high_ref[...], ref[MAXDOC + count : MAXDOC + count + HALO, :])
        )
        spread_rows(block_ref, scratch, keep_ref, send_ref, which, 4)
    scratch[...] = sum(dot_tn(a[...], b[...]) for a, b in zip(branch_refs, attended_refs))
    spread_rows(block_ref, scratch, keep_ref, send_ref, 3, 4)
    total = start_ref[...]
    place = lax.broadcasted_iota(jnp.int32, total.shape, 0)
    query_sum = sum(
        jnp.sum(ref[...].astype(F32), 0, keepdims=True) for ref in query_refs
    )
    value_sum = jnp.sum(value_ref[...].astype(F32), 0, keepdims=True)
    total = total + jnp.where(place == 0, query_sum, 0.0) + jnp.where(place == 1, value_sum, 0.0)
    height = keep_ref.shape[0]
    high, low, sum_ref[...] = split_sums(total)
    send_ref[height : height + SUM_ROWS, :] = high
    send_ref[height + SUM_ROWS :, :] = low


def project_grads(blocks, sums, tokens, low, high, query, key, value, branch, attended):
    features = tokens.shape[1]
    width = key.shape[1]
    half = blocks.shape[0] // 2
    depth = features // (2 * half)
    height = half * 4 * depth
    operands = (sums, *query, *branch, *attended, tokens, low, high, key, value)
    return pl.pallas_call(
        project_grad_kernel,
        grid=(1,),
        in_specs=[pl.BlockSpec(memory_space=SMEM)] + [whole(x.shape) for x in operands],
        out_specs=[
            whole((height, width)),
            whole((height + 2 * SUM_ROWS, width)),
            whole(sums.shape),
        ],
        out_shape=[
            struct((height, width), F32),
            struct((height + 2 * SUM_ROWS, width), BF16),
            struct(sums.shape, F32),
        ],
        scratch_shapes=[pltpu.VMEM((features, width), F32)],
        compiler_params=params(),
        cost_estimate=lasting(0.6),
        name="project_grads",
    )(blocks, *operands)


def fold_kernel(with_sums, keep_ref, arrived_ref, *refs):
    height = keep_ref.shape[0]
    size = height // 2
    if with_sums:
        start_ref, keep_out, send_out, sum_out = refs
    else:
        keep_out, send_out = refs
    keep_out[...] = keep_ref[:size, :] + arrived_ref[:size, :].astype(F32)
    send_out[:size, :] = (keep_ref[size:, :] + arrived_ref[size:height, :].astype(F32)).astype(BF16)
    if with_sums:
        high, low, sum_out[...] = split_sums(start_ref[...] + arrived_sums(arrived_ref, height))
        send_out[size : size + SUM_ROWS, :] = high
        send_out[size + SUM_ROWS :, :] = low


def arrived_sums(ref, height):
    return ref[height : height + SUM_ROWS, :].astype(F32) + ref[height + SUM_ROWS :, :].astype(F32)


def fold(keep, arrived, sums):
    height, width = keep.shape
    extra = arrived.shape[0] - height
    operands = (keep, arrived) + (() if sums is None else (sums,))
    shapes = [struct((height // 2, width), F32), struct((height // 2 + extra, width), BF16)]
    shapes += [] if sums is None else [struct(sums.shape, F32)]
    result = pl.pallas_call(
        functools.partial(fold_kernel, sums is not None),
        grid=(1,),
        in_specs=[whole(x.shape) for x in operands],
        out_specs=[whole(x.shape) for x in shapes],
        out_shape=shapes,
        compiler_params=params(),
        cost_estimate=lasting(0.2),
        name="fold",
    )(*operands)
    return result[0], result[1], (None if sums is None else result[2])


def finish_kernel(kinds, sum_kinds, keep_ref, arrived_ref, *refs):
    height = keep_ref.shape[0]
    if sum_kinds:
        start_ref, *refs = refs
    first = 0
    for kind, ref in zip(kinds, refs):
        depth = ref.shape[-2]
        for place in range(kind or 1):
            rows_here = slice(first, first + depth)
            total = keep_ref[rows_here, :] + arrived_ref[rows_here, :].astype(F32)
            if kind:
                ref[place] = total
            else:
                ref[...] = total
            first += depth
    if sum_kinds:
        total = start_ref[...] + arrived_sums(arrived_ref, height)
        first = 0
        for kind, ref in zip(sum_kinds, refs[len(kinds) :]):
            if ref.shape[0] == kind:
                ref[...] = total[first : first + kind, :]
            else:
                ref[...] = jnp.concatenate([total[first + k : first + k + 1] for k in range(kind)], 1)
            first += kind


def finish(keep, arrived, sums, kinds, sum_kinds):
    height, width = keep.shape
    depth = height // sum(kind or 1 for kind in kinds)
    operands = (keep, arrived) + (() if sums is None else (sums,))
    shapes = [struct((kind, depth, width) if kind else (depth, width), F32) for kind in kinds]
    shapes += [
        struct((kind, width) if kind == 2 else (1, kind * width), F32) for kind in sum_kinds
    ]
    return pl.pallas_call(
        functools.partial(finish_kernel, kinds, sum_kinds),
        grid=(1,),
        in_specs=[whole(x.shape) for x in operands],
        out_specs=[whole(x.shape) for x in shapes],
        out_shape=shapes,
        compiler_params=params(),
        cost_estimate=lasting(0.2),
        name="finish",
    )(*operands)


def token_grad_kernel(even_ref, *refs):
    query_refs, res_refs = refs[:CHUNKS], refs[CHUNKS : 2 * CHUNKS]
    key_ref, value_ref, *weight_refs = refs[2 * CHUNKS : 2 * CHUNKS + 5]
    own_ref, rim_ref, *out_refs = refs[2 * CHUNKS + 5 :]
    own_outs, rim_outs = out_refs[: len(out_refs) // 2], out_refs[len(out_refs) // 2 :]
    count, own = own_ref.shape
    even = even_ref[0] == 1

    def piece(start):
        return dot_nt(key_ref[start : start + BLOCK, :], weight_refs[1][...]) + dot_nt(
            value_ref[start : start + BLOCK, :], weight_refs[2][...]
        )

    def spread(value, start, stays_ref, leave_refs):
        stays_ref[start : start + BLOCK, :] = value[:, :own]
        for place, ref in enumerate(leave_refs, 1):
            lanes = slice(place * own, (place + 1) * own)
            ref[start : start + BLOCK, :] = value[:, lanes].astype(BF16)

    for start in range(0, HALO, BLOCK):
        low, high = piece(PAD + start), piece(MAXDOC + count + start)
        spread(jnp.where(even, high, low), start, rim_ref, rim_outs)
        spread(jnp.where(even, low, high), HALO + start, rim_ref, rim_outs)
    for start in range(0, count, BLOCK):
        chunk, inside = divmod(start, count // CHUNKS)
        total = piece(MAXDOC + start) + dot_nt(
            query_refs[chunk][inside : inside + BLOCK, :], weight_refs[0][...]
        )
        spread(total, start, own_ref, own_outs)
        own_ref[start : start + BLOCK, :] += res_refs[chunk][inside : inside + BLOCK, :]


def token_grads(even, query, res, key, value, weights):
    count = CHUNKS * query[0].shape[0]
    own = res[0].shape[1]
    leave = weights[0].shape[0] // own - 1
    operands = (*query, *res, key, value, *weights)
    shapes = [struct((count, own), F32), struct((2 * HALO, own), F32)]
    shapes += [struct((count, own), BF16)] * leave + [struct((2 * HALO, own), BF16)] * leave
    result = pl.pallas_call(
        token_grad_kernel,
        grid=(1,),
        in_specs=[pl.BlockSpec(memory_space=SMEM)] + [whole(x.shape) for x in operands],
        out_specs=[whole(x.shape) for x in shapes],
        out_shape=shapes,
        compiler_params=params(),
        cost_estimate=lasting(5.0),
        name="token_grads",
    )(even, *operands)
    return result[0], result[1], result[2 : 2 + leave], result[2 + leave :]


def rim_sum_kernel(rim_ref, *refs):
    *arrived_refs, inside_ref, across_ref = refs
    total = rim_ref[...] + sum(ref[...].astype(F32) for ref in arrived_refs)
    inside_ref[...] = total[:HALO].astype(BF16)
    across_ref[...] = total[HALO:].astype(BF16)


def rim_sum(rim, arrived):
    own = rim.shape[1]
    operands = (rim, *arrived)
    return pl.pallas_call(
        rim_sum_kernel,
        grid=(1,),
        in_specs=[whole(x.shape) for x in operands],
        out_specs=[whole((HALO, own))] * 2,
        out_shape=[struct((HALO, own), BF16)] * 2,
        compiler_params=params(),
        cost_estimate=lasting(0.3),
        name="rim_sum",
    )(*operands)


def token_sum_kernel(even_ref, own_ref, inside_ref, across_ref, *refs):
    *arrived_refs, out_ref = refs
    even = even_ref[0] == 1
    inside, across = inside_ref[...].astype(F32), across_ref[...].astype(F32)
    low, high = jnp.where(even, across, inside), jnp.where(even, inside, across)
    rest = own_ref.shape[0] - HALO
    for start in range(0, own_ref.shape[0], BLOCK):
        rows_here = slice(start, start + BLOCK)
        piece = own_ref[rows_here, :] + sum(ref[rows_here, :].astype(F32) for ref in arrived_refs)
        if start < HALO:
            piece = piece + low[rows_here, :]
        if start >= rest:
            piece = piece + high[start - rest : start - rest + BLOCK, :]
        out_ref[rows_here, :] = piece.astype(BF16)


def token_sum(even, own, inside, across, arrived):
    operands = (own, inside, across, *arrived)
    return pl.pallas_call(
        token_sum_kernel,
        grid=(1,),
        in_specs=[pl.BlockSpec(memory_space=SMEM)] + [whole(x.shape) for x in operands],
        out_specs=whole(own.shape),
        out_shape=struct(own.shape, BF16),
        compiler_params=params(),
        cost_estimate=lasting(0.3),
        name="token_sum",
    )(even, *operands)


def from_next(x, axis, step):
    count = lax.axis_size(axis)
    return lax.ppermute(x, axis, [((i + step) % count, i) for i in range(count)])


def others(x):
    return [from_next(x, "col", step) for step in range(1, lax.axis_size("col"))]


def bits_of(count):
    return [1 << place for place in range(count.bit_length() - 1)]


def orders_of(count):
    high = bits_of(count)[:0:-1]
    return high + [1], high[2:] + high[:2] + [1]


def slots_of(order, distance):
    return sum(((distance & bit) // bit) << place for place, bit in enumerate(order))


def distances_of(order, slots):
    return sum(((slots >> place) & 1) * bit for place, bit in enumerate(order))


def with_partner(x, step):
    count = lax.axis_size("row")
    orders = orders_of(count)
    return lax.ppermute(x, "row", [(i, i ^ orders[i % 2][step]) for i in range(count)])


def with_next(inside, across):
    count = lax.axis_size("row")
    pairs = [(i, i + 1 if i % 2 else i - 1) for i in range(1, count - 1)]
    return (
        lax.ppermute(inside, "row", [(i, i ^ 1) for i in range(count)]),
        lax.ppermute(across, "row", pairs),
    )


def after(value, *needed):
    return lax.optimization_barrier((value, *needed))[0]


class Gather:
    def __init__(self, shard):
        self.held, self.step = shard[None], 0
        self.count = len(bits_of(lax.axis_size("row")))
        self.move()

    def move(self):
        self.arrived = with_partner(self.held, self.step)
        self.step += 1

    def put(self, *needed):
        self.held = jnp.concatenate([after(self.held, *needed), self.arrived], 0)
        self.move()


class Reduction:
    def __init__(self, keep, send, sums, kinds, sum_kinds=()):
        self.step = len(bits_of(lax.axis_size("row")))
        self.keep, self.send, self.sums = keep, send, sums
        self.kinds, self.sum_kinds = kinds, sum_kinds
        self.result = None
        self.move()

    def move(self):
        self.step -= 1
        self.arrived = with_partner(self.send, self.step)

    def add(self, *needed):
        keep = after(self.keep, *needed)
        if self.step == 0:
            self.result = finish(keep, self.arrived, self.sums, self.kinds, self.sum_kinds)
        else:
            self.keep, self.send, self.sums = fold(keep, self.arrived, self.sums)
            self.move()


def exchanged(part):
    arrived = others(part)
    if len(arrived) == 1:
        return arrived[0]
    shift = part.shape[1] // (len(arrived) + 1)
    total = sum(
        jnp.roll(x.astype(F32), step * shift, 1) for step, x in enumerate(arrived, 1)
    )
    return total.astype(BF16)


def on_device(
    tokens,
    prev_logits,
    doc_lengths,
    qkv_weight,
    qv_bias,
    out_weight,
    out_bias,
    up_weight,
    up_bias,
    down_weight,
    norm_gain,
    norm_shift,
    out_grad,
    logit_grad,
):
    count, own = tokens.shape
    width = qkv_weight.shape[2]
    row_count, col_count = lax.axis_size("row"), lax.axis_size("col")
    row_index, col_index = lax.axis_index("row"), lax.axis_index("col")
    token_count = count * row_count
    swap = col_count == 2
    hidden_rows = up_bias.shape[0] // own

    odd = row_index % 2 == 1
    places = jnp.arange(row_count, dtype=jnp.int32)
    offset = col_index * (row_count // col_count)
    distance = ((places + offset) % row_count) ^ row_index
    half = row_count // 2
    even_order, odd_order = (order[:-1] for order in orders_of(row_count))
    turned = odd ^ (distance % 2 == 1)
    slots = jnp.where(turned, slots_of(odd_order, distance), slots_of(even_order, distance))
    slots = slots + half * (distance % 2)
    turned = odd ^ (places >= half)
    met = jnp.where(turned, distances_of(odd_order, places), distances_of(even_order, places))
    blocks = (((met + (places >= half)) ^ row_index) - offset) % row_count

    even = 1 - row_index % 2
    even = even.astype(jnp.int32)[None]

    def dense_of(banded, fill, chunk, *needed):
        dense = to_dense(after(banded, *needed), lengths, fill, token_count, chunk)
        return dense


    out_turned = out_weight.T
    out_other = others(out_turned)
    qkv_rows = Gather(qkv_weight)
    tokens_other = others(after(tokens, out_turned))
    feed_rows = Gather(jnp.concatenate([out_turned, *out_other, up_weight, down_weight.T], 1))
    tail = row_index % 2 * (count - HALO)
    ready = after(tokens, feed_rows.held)
    inside, across = with_next(
        lax.dynamic_slice_in_dim(ready, count - HALO - tail, HALO, 0),
        lax.dynamic_slice_in_dim(ready, tail, HALO, 0),
    )
    qkv_rows.put(feed_rows.held)
    inside_other, across_other = others(inside), others(across)
    feed_rows.put(qkv_rows.held)
    qkv_rows.put(feed_rows.held, *tokens_other)
    lengths = jnp.concatenate(
        [after(doc_lengths, qkv_rows.held).reshape(-1), (row_index * count)[None]]
    )
    prev_dense = [
        dense_of(prev_logits, MASKED_SCORE, 0, qkv_rows.held, feed_rows.held, inside, across)
    ]
    grad_other = others(after(out_grad, *inside_other))
    while qkv_rows.step < qkv_rows.count:
        qkv_rows.put(prev_dense[0], *inside_other, *across_other)
    feed_rows.put(qkv_rows.held)
    tokens_full, query, key, value, low_tokens, high_tokens, *projections = project(
        slots, even, qkv_rows.held, qkv_rows.arrived, qv_bias, [after(tokens, feed_rows.held), *tokens_other],
        [inside, *inside_other], [across, *across_other],
    )
    grad_full = jnp.concatenate([after(out_grad, query)] + grad_other, 1)
    norms = jnp.concatenate([after(norm_gain, query), norm_shift, out_bias], 0)
    norms = jnp.concatenate([norms] + others(norms), 1)
    scores, probs, attended, attended_other = [], [], [], []
    for chunk in range(CHUNKS):
        score, prob, mix = attend_forward(
            after(query, feed_rows.held) if chunk else query, key, value, prev_dense[chunk], chunk
        )
        scores.append(score)
        probs.append(prob)
        attended.append(mix)
        attended_other.append(jnp.concatenate(others(mix), 1))
        if chunk == 0:
            prev_dense.append(dense_of(prev_logits, MASKED_SCORE, 1, mix, norms, grad_full))
            while feed_rows.step < feed_rows.count:
                feed_rows.put(prev_dense[1], attended_other[0])
    other_out, *weights = in_order(
        slots, after(feed_rows.held, mix), feed_rows.arrived,
        (width, (col_count - 1) * width, up_weight.shape[1], up_weight.shape[1]),
    )
    weights[0], other_out = other_out, weights[0]
    ups = up_bias[None]
    firsts, logit_dense = [], []
    for chunk in range(CHUNKS):
        result = feed_first(
            attended[chunk], attended_other[chunk], tokens_full, other_out, weights, norms, ups,
            chunk,
        )
        if chunk == 0:
            logit_dense.append(dense_of(logit_grad, 0.0, 0, result[-1]))
            ups = after(ups, logit_dense[0])
        firsts.append((*result, exchanged(result[-1])))
    normed, inverse, upper, act, slope, down_part, down_other = zip(*firsts)

    new_logits = to_band([after(scores[0], down_part[-1])], True)
    sums = after(jnp.zeros((SUM_ROWS, own), F32), new_logits)
    output = None
    seconds = []
    for chunk in range(CHUNKS):
        sums, output, *result = feed_second(
            swap, sums, output, down_part[chunk], down_other[chunk],
            normed[chunk], grad_full, slope[chunk], weights, norms, chunk,
        )
        seconds.append((*result, exchanged(result[-1])))
    res_two, ffn_low, hidden_grad, lower_part, lower_other = zip(*seconds)
    keep, send = feed_grads(blocks, ffn_low, act, upper, hidden_grad)
    feed_sum = Reduction(keep, send, None, (0, 0))
    sums = after(sums, keep)

    branch_low, res_one, query_grad, prev_dense_grad = [], [], [], []
    partial = None
    for chunk in range(CHUNKS):
        sums, low, attended_grad, res = feed_third(
            swap, sums, width, lower_part[chunk], lower_other[chunk], res_two[chunk],
            normed[chunk], inverse[chunk], weights, norms,
        )
        branch_low.append(low)
        res_one.append(res)
        prev, query_part, *partial = attend_backward(
            attended_grad, query, key, value, probs[chunk], logit_dense[chunk], chunk, partial
        )
        if chunk == 0:
            feed_sum.add(query_part)
            logit_dense.append(dense_of(logit_grad, 0.0, 1, feed_sum.keep))
            sums = after(sums, logit_dense[1])
        prev_dense_grad.append(prev)
        query_grad.append(query_part)
    key_grad, value_grad = partial
    feed_sum.add(query_grad[-1])
    keep, send, sums = project_grads(
        blocks, after(sums, feed_sum.keep), tokens_full, low_tokens, high_tokens, query_grad,
        key_grad, value_grad, branch_low, attended,
    )
    last_sum = Reduction(keep, send, sums, (3, 0), (2, 2, 2, 2, hidden_rows))
    center, rim, center_parts, rim_parts = token_grads(
        even, query_grad, res_one, after(key_grad, keep), value_grad, projections
    )

    def spread_over(parts):
        return [from_next(part, "col", -step) for step, part in enumerate(parts, 1)]

    last_sum.add(center)
    rim_parts = spread_over(rim_parts)
    center_parts = spread_over(after(x, rim) for x in center_parts)
    prev_dense_grad[0] = after(prev_dense_grad[0], last_sum.keep)
    prev_grad = to_band(prev_dense_grad, False)
    last_sum.add(prev_grad)
    inside, across = rim_sum(after(rim, last_sum.keep), rim_parts)
    feed_sum.add(inside)
    inside, across = with_next(inside, across)
    last_sum.add(feed_sum.keep)
    for chunk in range(1, CHUNKS):
        new_logits = to_band([after(scores[chunk], last_sum.keep)], True, chunk, new_logits)
    tokens_grad = token_sum(even, after(center, new_logits), inside, across, center_parts)
    while feed_sum.result is None:
        feed_sum.add(tokens_grad)
    while last_sum.result is None:
        last_sum.add(feed_sum.result[0])
    qkv_grad, out_grad_rows, qv_sum, bias_sum, gain_sum, shift_sum, hidden_sum = last_sum.result
    up_grad, down_grad = feed_sum.result
    return (
        output,
        new_logits,
        tokens_grad,
        prev_grad,
        qkv_grad,
        qv_sum,
        out_grad_rows.T,
        bias_sum,
        up_grad,
        hidden_sum.reshape(-1),
        down_grad.T,
        gain_sum,
        shift_sum,
    )


def solution(mesh):
    return jax.shard_map(
        on_device,
        mesh=mesh,
        in_specs=(
            P("row", "col"),
            P("col", "row", None),
            P(),
            P(None, "row", "col"),
            P(None, "col"),
            P("col", "row"),
            P(None, "col"),
            P("row", "col"),
            P("col"),
            P("col", "row"),
            P(None, "col"),
            P(None, "col"),
            P("row", "col"),
            P("col", "row", None),
        ),
        out_specs=(
            P("row", "col"),
            P("col", "row", None),
            P("row", "col"),
            P("col", "row", None),
            P(None, "row", "col"),
            P(None, "col"),
            P("col", "row"),
            P(None, "col"),
            P("row", "col"),
            P("col"),
            P("col", "row"),
            P(None, "col"),
            P(None, "col"),
        ),
        check_vma=False,
    )
```
